32 devices in a mesh: wide: 16 (over z, y, x), narrow: 2 (over core).
Axes of the slice: x: 2, y: 2, z: 4, core: 2. Of those that a mesh axis runs over, the one named last changes fastest.
Arguments:
- tokens: bfloat16 [16384, 1024], P(('wide', 'narrow')), may hold values from -6 to 6
- cotangent: bfloat16 [16384, 1024], P(('wide', 'narrow'))
- pages: int32 [16384], P('wide'), may hold values from 0 to 3, as said below
- boxes: int32 [2, 16384], P(None, 'wide'), may hold values from 0 to 1000, as said below
- gain_attn: bfloat16 [1024], replicated, may hold values from 0.099609375 to 1.8984375
- gain_ffn: bfloat16 [1024], replicated, may hold values from 0.099609375 to 1.8984375
- bias_tables: bfloat16 [96, 16], replicated, may hold values from -4 to 4
- w_query: bfloat16 [1024, 1024], P('wide', 'narrow'), may hold values from -0.046875 to 0.046875
- w_key: bfloat16 [1024, 1024], P('wide', 'narrow'), may hold values from -0.1875 to 0.1875
- w_value: bfloat16 [1024, 1024], P('wide', 'narrow'), may hold values from -0.1875 to 0.1875
- w_out: bfloat16 [1024, 1024], P('narrow', 'wide'), may hold values from -1 to 1
- w_gate: bfloat16 [1024, 2816], P('wide', 'narrow'), may hold values from -0.1875 to 0.1875
- w_up: bfloat16 [1024, 2816], P('wide', 'narrow'), may hold values from -0.1875 to 0.1875
- w_down: bfloat16 [2816, 1024], P('narrow', 'wide'), may hold values from -0.109375 to 0.109375
Outputs:
- output: bfloat16 [16384, 1024], P(('wide', 'narrow'))
- grad_tokens: float32 [16384, 1024], P(('wide', 'narrow'))
- grad_gain_attn: float32 [1024], replicated
- grad_gain_ffn: float32 [1024], replicated
- grad_bias_tables: float32 [96, 16], replicated
- grad_w_query: float32 [1024, 1024], P('wide', 'narrow')
- grad_w_key: float32 [1024, 1024], P('wide', 'narrow')
- grad_w_value: float32 [1024, 1024], P('wide', 'narrow')
- grad_w_out: float32 [1024, 1024], P('narrow', 'wide')
- grad_w_gate: float32 [1024, 2816], P('wide', 'narrow')
- grad_w_up: float32 [1024, 2816], P('wide', 'narrow')
- grad_w_down: float32 [2816, 1024], P('narrow', 'wide')
The draws below stay inside these ranges and needn't reach their ends.
Inputs may be any that keep to these rules, and one draw needn't show every extreme that they name: Each aligned block of 1024 rows holds one page of up to 1024 rows or two pages of up to 512 rows each, the second starting at row 512 of the block; a value is the page's number within its block, 0 or 1, plus 2 on padding rows. A page has its patch rows first (784 of them for a page of the whole block, 196 otherwise), then text rows ending in an end token, then padding. Some block holds two pages. `boxes`: row 0 is the horizontal and row 1 the vertical centre of a row's box in thousandths of the page: patch rows carry the centre of their grid cell, text rows their word's box, end tokens 1000 and padding 0.
All inputs are finite; a program needn't handle non-finite values.
Results may differ from the reference program's by a relative error of at most 0.018.
Values may be sent and summed in bfloat16 or wider, within the bound.
A program may use at most 256 MiB of HBM per device.

```python
from functools import partial
import jax
import jax.numpy as jnp
from jax import lax

D = 1024
HEADS = 16
HEAD_DIM = 64
FF = 2816
INNER = 1024
BUCKETS = 32
PAGE = 512
GRID = 14
TOKENS = 16384


def page_layout(key):
    slot_count = TOKENS // (2 * PAGE)
    base_key = jax.random.fold_in(key, 7)
    kind_key, text_key, word_key, forced_key = jax.random.split(base_key, 4)
    slot_kinds = jax.random.randint(kind_key, (slot_count,), 0, 2)
    forced = jax.random.randint(forced_key, (), 0, slot_count)
    slot_kinds = jnp.where(jnp.arange(slot_count) == forced, 1, slot_kinds)
    small_text = jax.random.randint(text_key, (slot_count, 2), 1, PAGE - GRID * GRID)
    large_text = jax.random.randint(jax.random.fold_in(text_key, 1), (slot_count,), 1, 2 * PAGE - 4 * GRID * GRID)
    position = jnp.arange(2 * PAGE, dtype=jnp.int32)[None, :]
    two_pages = slot_kinds[:, None] == 1
    page_number = jnp.where(two_pages, position // PAGE, 0)
    in_page = jnp.where(two_pages, position % PAGE, position)
    lattice_length = jnp.where(two_pages, GRID, 2 * GRID)
    patch_count = lattice_length * lattice_length
    text_count = jnp.where(two_pages, jnp.where(page_number == 0, small_text[:, 0:1], small_text[:, 1:2]), large_text[:, None])
    valid_length = patch_count + text_count
    is_valid = in_page < valid_length
    is_patch = in_page < patch_count
    is_end = in_page == valid_length - 1
    column = in_page % lattice_length
    grid_row = in_page // lattice_length
    word_across = jax.random.randint(word_key, (slot_count, 2 * PAGE), 0, 1001)
    word_upward = jax.random.randint(jax.random.fold_in(word_key, 1), (slot_count, 2 * PAGE), 0, 1001)
    box_across = jnp.where(is_patch, (2 * column + 1) * 500 // lattice_length, jnp.where(is_end, 1000, jnp.where(is_valid, word_across, 0)))
    box_upward = jnp.where(is_patch, (2 * grid_row + 1) * 500 // lattice_length, jnp.where(is_end, 1000, jnp.where(is_valid, word_upward, 0)))
    page_values = page_number + 2 * (1 - is_valid.astype(jnp.int32))
    return (page_values.reshape(TOKENS).astype(jnp.int32), jnp.stack([box_across.reshape(TOKENS), box_upward.reshape(TOKENS)]).astype(jnp.int32))


def draw_pages(key, part):
    return page_layout(key)[0]


def draw_boxes(key, part):
    return page_layout(key)[1]


def draw_cotangent(key, part):
    row_ids = jnp.arange(TOKENS, dtype=jnp.float32)[:, None]
    ramp = 0.5 + row_ids / TOKENS
    values = jax.random.normal(key, (TOKENS, D), jnp.float32) * ramp
    return values.astype(jnp.bfloat16)


def levels(key, dims, shards, low, largest):
    def one(axis_at, shards_of):
        draws = jax.random.uniform(jax.random.fold_in(jax.random.fold_in(key, 6), axis_at), (shards_of,), jnp.float32, low / len(shards), largest / len(shards))
        return jnp.repeat(jnp.exp(draws), dims[axis_at] // shards_of).reshape((-1,) + (1,) * (len(dims) - axis_at - 1))

    gain = one(*shards[0])
    for cut in shards[1:]:
        gain = gain * one(*cut)
    return gain


def bell_draw(own_key, dims, scale, reach, shards=(), kind=jnp.bfloat16):
    loudness = levels(own_key, dims, shards, -0.22, 0.18) if shards else 1.0
    values = jax.random.normal(own_key, dims, jnp.float32) * scale * loudness
    return jnp.minimum(jnp.maximum(values, -reach), reach).astype(kind)


def setup_inputs(seed: int = 0) -> dict:
    arg_keys = jax.random.split(jax.random.key(seed), 15)
    return {
        "tokens": bell_draw(arg_keys[0], (TOKENS, D), 1.0, 6.0, ((0, 32),)),
        "cotangent": draw_cotangent(jax.random.fold_in(arg_keys[14], 71), 0),
        "pages": draw_pages(jax.random.fold_in(arg_keys[14], 71), 0),
        "boxes": draw_boxes(jax.random.fold_in(arg_keys[14], 71), 0),
        "gain_attn": jnp.clip(1.0 + 0.18 * jax.random.normal(arg_keys[4], (D,), jnp.float32), 0.099609375, 1.8984375).astype(jnp.bfloat16),
        "gain_ffn": jnp.clip(1.0 + 0.18 * jax.random.normal(arg_keys[5], (D,), jnp.float32), 0.099609375, 1.8984375).astype(jnp.bfloat16),
        "bias_tables": bell_draw(arg_keys[6], (3 * BUCKETS, HEADS), 0.7, 4.0),
        "w_query": bell_draw(arg_keys[7], (D, INNER), (16 * D) ** -0.5, 0.046875, ((0, 16), (1, 2))),
        "w_key": bell_draw(arg_keys[8], (D, INNER), D ** -0.5, 0.1875, ((0, 16), (1, 2))),
        "w_value": bell_draw(arg_keys[9], (D, INNER), D ** -0.5, 0.1875, ((0, 16), (1, 2))),
        "w_out": bell_draw(arg_keys[10], (INNER, D), (INNER // 32) ** -0.5, 1.0, ((0, 2), (1, 16))),
        "w_gate": bell_draw(arg_keys[11], (D, FF), D ** -0.5, 0.1875, ((0, 16), (1, 2))),
        "w_up": bell_draw(arg_keys[12], (D, FF), D ** -0.5, 0.1875, ((0, 16), (1, 2))),
        "w_down": bell_draw(arg_keys[13], (FF, D), FF ** -0.5, 0.109375, ((0, 2), (1, 16))),
    }


epsilon = 1e-06
bucket_edges = (1, 2, 3, 4, 5, 6, 7, 8, 12, 16, 23, 32, 46, 64, 91)
layout_stretch = 4

@jax.custom_vjp
def low(v):
    return lax.optimization_barrier(v.astype(jnp.bfloat16)).astype(jnp.float32)

@jax.custom_vjp
def low_back(v):
    return v

def low_keep(v):
    return (low(v), None)

def low_pass(kept, grad):
    return (grad,)

def back_keep(v):
    return (v, None)

def back_low(kept, grad):
    return (low(grad),)
low.defvjp(low_keep, low_pass)
low_back.defvjp(back_keep, back_low)

def bucket_of(spacing, stretch_factor):
    magnitude = jnp.abs(spacing)
    counted = jnp.zeros(spacing.shape, jnp.int32)
    for border in bucket_edges:
        counted = counted + (magnitude >= border * stretch_factor).astype(jnp.int32)
    return counted + BUCKETS // 2 * (spacing > 0).astype(jnp.int32)

def matmul(left_side, right_side):
    return jnp.dot(left_side, right_side, precision=lax.Precision.HIGHEST, preferred_element_type=jnp.float32)

def rms_norm(values, gain_row):
    factor = lax.rsqrt(lax.optimization_barrier(jnp.mean(values * values, axis=-1, keepdims=True)) + epsilon)
    return low(values * factor * gain_row)

def slot_attention(tables, pieces):
    query_rows, key_rows, value_rows, page_row, box_rows = pieces
    places = jnp.arange(page_row.shape[0], dtype=jnp.int32)
    linear_ids = bucket_of(places[None, :] - places[:, None], 1)
    across = bucket_of(box_rows[0][None, :] - box_rows[0][:, None], layout_stretch)
    upward = bucket_of(box_rows[1][None, :] - box_rows[1][:, None], layout_stretch)
    bias_sum = tables[linear_ids] + tables[BUCKETS + across] + tables[2 * BUCKETS + upward]
    scores = jnp.einsum('qhd,khd->hqk', query_rows, key_rows, precision=lax.Precision.HIGHEST)
    scores = low_back(scores + jnp.transpose(bias_sum, (2, 0, 1)))
    allowed = page_row[None, :] == page_row[:, None] % 2
    masked = jnp.where(allowed[None], scores, -1e+30)
    weights_low = low(jax.nn.softmax(masked, axis=-1))
    return jnp.einsum('hqk,khd->qhd', weights_low, value_rows, precision=lax.Precision.HIGHEST)

def forward(tokens, gain_attn, gain_ffn, bias_tables, w_query, w_key, w_value, w_out, w_gate, w_up, w_down, pages, boxes):
    row_total = tokens.shape[0]
    slot_count = row_total // (2 * PAGE)
    normed = rms_norm(tokens, gain_attn)

    def project(weight):
        return low_back(low(matmul(normed, weight))).reshape(slot_count, 2 * PAGE, HEADS, HEAD_DIM)
    query_rows = project(w_query)
    key_rows = project(w_key)
    value_rows = project(w_value)
    page_slots = pages.reshape(slot_count, 2 * PAGE)
    box_slots = jnp.transpose(boxes.reshape(2, slot_count, 2 * PAGE), (1, 0, 2))
    attend = jax.checkpoint(partial(slot_attention, bias_tables))
    attended = lax.map(attend, (query_rows, key_rows, value_rows, page_slots, box_slots))
    attended = low_back(low(attended.reshape(row_total, INNER)))
    hidden = tokens + low_back(matmul(attended, w_out))
    normed_two = rms_norm(hidden, gain_ffn)
    gate_pre = low_back(matmul(normed_two, w_gate))
    up_pre = low_back(matmul(normed_two, w_up))
    hidden_ff = low(jax.nn.gelu(gate_pre, approximate=True) * up_pre)
    return hidden + low_back(matmul(hidden_ff, w_down))

def reference(tokens, cotangent, pages, boxes, gain_attn, gain_ffn, bias_tables, w_query, w_key, w_value, w_out, w_gate, w_up, w_down):
    floats = [array_item.astype(jnp.float32) for array_item in (tokens, gain_attn, gain_ffn, bias_tables, w_query, w_key, w_value, w_out, w_gate, w_up, w_down)]

    def closed_interval(*arrays):
        return forward(*arrays, pages, boxes)
    output, pullback = jax.vjp(closed_interval, *floats)
    grads = pullback(cotangent.astype(jnp.float32))
    return (output.astype(jnp.bfloat16), grads[0], grads[1], grads[2], grads[3], grads[4], grads[5], grads[6], grads[7], grads[8], grads[9], grads[10])
```

```python
import functools

import jax
import jax.numpy as jnp
from jax import lax
from jax.experimental import pallas as pl
from jax.experimental.pallas import tpu as pltpu
from jax.sharding import PartitionSpec as P

f32, bf16 = jnp.float32, jnp.bfloat16
MESH = pl.DeviceIdType.MESH


EDGES = (1, 2, 3, 4, 5, 6, 7, 8, 12, 16, 23, 32, 46, 64, 91)
NT = (((1,), (1,)), ((), ()))
VM = 56 * 2**20

def lane_take(table, idx):
    return jnp.take_along_axis(table, idx, axis=1, mode="promise_in_bounds")

def bias_kernel(heads, rows, n, steps_ref, tab_ref, box_col, box_row, page_col, page_row, bias_ref, ids_ref):
    start = pl.program_id(0) * rows
    steps = jnp.broadcast_to(steps_ref[...], (rows, 128))
    allowed_col = jnp.broadcast_to(page_col[...] % 2, (rows, 128))
    cols = [jnp.broadcast_to(box_col[:, t:t + 1], (rows, 128)) for t in range(2)]
    own = lax.broadcasted_iota(jnp.int32, (rows, 128), 0) + start
    for c in range(n // 128):
        lanes = pl.ds(c * 128, 128)
        lane_id = lax.broadcasted_iota(jnp.int32, (rows, 128), 1) + c * 128
        ids = []
        for t in range(3):
            gap = (lane_id - own) if t == 0 else (jnp.broadcast_to(box_row[t - 1:t, lanes], (rows, 128)) - cols[t - 1])
            size = jnp.abs(gap)
            if t > 0:
                size = size >> 2
            bucket = lane_take(steps, jnp.minimum(size, 91)) + jnp.where(gap > 0, 16, 0)
            ids.append(bucket)
            ids_ref[t, :, lanes] = bucket.astype(ids_ref.dtype)
        ok = jnp.broadcast_to(page_row[:, lanes], (rows, 128)) == allowed_col
        for h in range(heads):
            total = None
            for t in range(3):
                table = jnp.broadcast_to(tab_ref[t * heads + h:t * heads + h + 1, :], (rows, 128))
                part = lane_take(table, ids[t])
                total = part if total is None else total + part
            bias_ref[h, :, lanes] = jnp.where(ok, total, -1e30)

def make_bias(tables, boxes, pages, ids_dtype=f32):
    heads = tables.shape[1]
    n = pages.shape[0]
    rows = 64
    tab = jnp.pad(tables.astype(f32).reshape(3, 32, heads).transpose(0, 2, 1).reshape(3 * heads, 32), ((0, 0), (0, 96)))
    lane = jnp.arange(128, dtype=jnp.int32)
    steps = sum([(lane >= e).astype(jnp.int32) for e in EDGES])[None]
    return pl.pallas_call(functools.partial(bias_kernel, heads, rows, n),
        grid=(n // rows,),
        out_shape=(jax.ShapeDtypeStruct((heads, n, n), f32), jax.ShapeDtypeStruct((3, n, n), ids_dtype)),
        in_specs=[pl.BlockSpec((1, 128), lambda i: (0, 0)), pl.BlockSpec((3 * heads, 128), lambda i: (0, 0)),
                  pl.BlockSpec((rows, 2), lambda i: (i, 0)), pl.BlockSpec((2, n), lambda i: (0, 0)),
                  pl.BlockSpec((rows, 1), lambda i: (i, 0)), pl.BlockSpec((1, n), lambda i: (0, 0))],
        out_specs=(pl.BlockSpec((heads, rows, n), lambda i: (0, i, 0)), pl.BlockSpec((3, rows, n), lambda i: (0, i, 0))),
        compiler_params=pltpu.CompilerParams(vmem_limit_bytes=VM), name="layout_bias")(steps, tab, boxes.T, boxes, pages[:, None], pages[None])

def half_of(v, e):
    lane = lax.broadcasted_iota(jnp.int32, v.shape, 1)
    return jnp.where((lane >= 64) == (e == 1), v, jnp.zeros_like(v))

def join(a, b):
    lane = lax.broadcasted_iota(jnp.int32, a.shape, 1)
    return jnp.where(lane < 64, a, b)

def fwd_kernel(q_ref, k_ref, v_ref, bias_ref, o_ref, lse_ref):
    q, k, v = q_ref[...], k_ref[...], v_ref[...]
    outs, lses = [], []
    for e in range(2):
        s = lax.dot_general(half_of(q, e), k, NT, preferred_element_type=f32) + bias_ref[e]
        peak = jnp.max(s, axis=1, keepdims=True)
        p = jnp.exp(s - peak)
        total = jnp.sum(p, axis=1, keepdims=True)
        outs.append(jnp.dot(p.astype(bf16), v, preferred_element_type=f32) / total)
        lses.append(peak + jnp.log(total))
    o_ref[...] = join(*outs).astype(bf16)
    lse_ref[0] = jnp.concatenate(lses, axis=1)

def attn_fwd(qkv, bias, tq=256):
    n, width = qkv.shape[0], qkv.shape[1] // 3
    pairs = width // 128
    return pl.pallas_call(fwd_kernel, grid=(pairs, n // tq),
        out_shape=(jax.ShapeDtypeStruct((n, width), bf16), jax.ShapeDtypeStruct((pairs, n, 2), f32)),
        in_specs=[pl.BlockSpec((tq, 128), lambda p, i: (i, p)), pl.BlockSpec((n, 128), lambda p, i: (0, p + pairs)),
                  pl.BlockSpec((n, 128), lambda p, i: (0, p + 2 * pairs)), pl.BlockSpec((2, tq, n), lambda p, i: (p, i, 0))],
        out_specs=(pl.BlockSpec((tq, 128), lambda p, i: (i, p)), pl.BlockSpec((1, tq, 2), lambda p, i: (p, i, 0))),
        compiler_params=pltpu.CompilerParams(vmem_limit_bytes=VM), name="attention")(qkv, qkv, qkv, bias)

def bwd_kernel(q_ref, k_ref, v_ref, bias_ref, o_ref, do_ref, lse_ref, dq_ref, dk_ref, dv_ref, g_ref, dkt, dvt):
    i = pl.program_id(1)
    @pl.when(i == 0)
    def _():
        dkt[...] = jnp.zeros_like(dkt)
        dvt[...] = jnp.zeros_like(dvt)
    q, k, v, do = q_ref[...], k_ref[...], v_ref[...], do_ref[...]
    prod = do.astype(f32) * o_ref[...].astype(f32)
    dqs = []
    for e in range(2):
        qm, dom = half_of(q, e), half_of(do, e)
        s = lax.dot_general(qm, k, NT, preferred_element_type=f32) + bias_ref[e]
        p = jnp.exp(s - lse_ref[0, :, e:e + 1])
        dp = lax.dot_general(dom, v, NT, preferred_element_type=f32)
        inner = jnp.sum(half_of(prod, e), axis=1, keepdims=True)
        g = (p * (dp - inner)).astype(bf16)
        g_ref[e] = g
        dqs.append(jnp.dot(g, k, preferred_element_type=f32))
        dvt[...] += jnp.dot(dom.T, p.astype(bf16), preferred_element_type=f32)
        dkt[...] += jnp.dot(qm.T, g, preferred_element_type=f32)
    dq_ref[...] = join(*dqs).astype(bf16)
    @pl.when(i == pl.num_programs(1) - 1)
    def _():
        dk_ref[...] = dkt[...].T.astype(bf16)
        dv_ref[...] = dvt[...].T.astype(bf16)

def attn_bwd(qkv, bias, o, do, lse, tq=256):
    n, width = qkv.shape[0], qkv.shape[1] // 3
    pairs = width // 128
    tile = pl.BlockSpec((tq, 128), lambda p, i: (i, p))
    full = pl.BlockSpec((n, 128), lambda p, i: (0, p))
    return pl.pallas_call(bwd_kernel, grid=(pairs, n // tq),
        out_shape=(jax.ShapeDtypeStruct((n, width), bf16),) * 3 + (jax.ShapeDtypeStruct((2 * pairs, n, n), bf16),),
        in_specs=[tile, pl.BlockSpec((n, 128), lambda p, i: (0, p + pairs)), pl.BlockSpec((n, 128), lambda p, i: (0, p + 2 * pairs)), pl.BlockSpec((2, tq, n), lambda p, i: (p, i, 0)), tile, tile,
                  pl.BlockSpec((1, tq, 2), lambda p, i: (p, i, 0))],
        out_specs=(tile, full, full, pl.BlockSpec((2, tq, n), lambda p, i: (p, i, 0))),
        scratch_shapes=[pltpu.VMEM((128, n), f32), pltpu.VMEM((128, n), f32)],
        compiler_params=pltpu.CompilerParams(vmem_limit_bytes=VM), name="attention_back")(qkv, qkv, qkv, bias, o, do, lse)

def hist_kernel(heads, rows, n, g_ref, ids_ref, out_ref, gs):
    @pl.when(pl.program_id(0) == 0)
    def _():
        out_ref[...] = jnp.zeros_like(out_ref)
    for h in range(heads):
        for c in range(n // 128):
            gs[c, h * rows:(h + 1) * rows, :] = g_ref[h, :, c * 128:(c + 1) * 128].astype(f32)
    label = lax.broadcasted_iota(jnp.int32, (32, n), 0).astype(bf16)
    one, zero = jnp.ones((32, n), bf16), jnp.zeros((32, n), bf16)
    acc = jnp.zeros((heads, 96), f32)
    for r in range(rows):
        grow = jnp.concatenate([gs[c, pl.ds(r, heads, stride=rows), :] for c in range(n // 128)], axis=1).astype(bf16)
        hots = []
        for t in range(3):
            row = jnp.broadcast_to(ids_ref[t, r:r + 1, :], (32, n)).astype(bf16)
            hots.append(jnp.where(row == label, one, zero))
        acc = acc + lax.dot_general(grow, jnp.concatenate(hots, axis=0), NT, preferred_element_type=f32)
    out_ref[...] += acc

def table_hist(g, ids):
    heads, n, _ = g.shape
    rows = 16
    return pl.pallas_call(functools.partial(hist_kernel, heads, rows, n), grid=(n // rows,),
        out_shape=jax.ShapeDtypeStruct((heads, 96), f32),
        in_specs=[pl.BlockSpec((heads, rows, n), lambda i: (0, i, 0)), pl.BlockSpec((3, rows, n), lambda i: (0, i, 0))],
        out_specs=pl.BlockSpec((heads, 96), lambda i: (0, 0)),
        scratch_shapes=[pltpu.VMEM((n // 128, heads * rows, 128), f32)],
        compiler_params=pltpu.CompilerParams(vmem_limit_bytes=VM), name="table_grad")(g, ids)


def place():
    me = lax.axis_index("wide")
    return me // 4, (me // 2) % 2, me % 2

def wide_id(z, y, x):
    return {"wide": z * 4 + y * 2 + x}

def remote(src, dst, send, recv, target):
    return pltpu.make_async_remote_copy(src_ref=src, dst_ref=dst, send_sem=send, recv_sem=recv, device_id=target, device_id_type=MESH)

def greet(G, far):
    z, y, x = place()
    bar = pltpu.get_barrier_semaphore()
    sig = lambda t: pl.semaphore_signal(bar, inc=1, device_id=t, device_id_type=MESH)
    sig(wide_id(z, 1 - y, x)); sig(wide_id(z, y, 1 - x))
    if far:
        for k in range(1, G):
            sig(wide_id((z + k) % G, y, x))
        pl.semaphore_wait(bar, 2 + G - 1)
    else:
        @pl.when(z > 0)
        def _(): sig(wide_id(z - 1, y, x))
        @pl.when(z < G - 1)
        def _(): sig(wide_id(z + 1, y, x))
        pl.semaphore_wait(bar, 2 + (z > 0).astype(jnp.int32) + (z < G - 1).astype(jnp.int32))

class Gather:
    def __init__(self, G, cut, src, out, local_sem, zs, zr, ns, nr):
        self.G, self.src, self.out, self.local_sem = G, src, out, local_sem
        self.zs, self.zr, self.ns, self.nr = zs, zr, ns, nr
        self.half = (pl.ds(0, cut), pl.ds(cut, src.shape[1] - cut))
        self.z, self.y, self.x = place()
    def hop(self, own, zz, yy, xx, h, tgt, j):
        y, x = self.y, self.x
        target = wide_id(self.z, 1 - y, x) if tgt == "y" else wide_id(self.z, y, 1 - x)
        s = self.src.at[:, self.half[h]] if own else self.out.at[zz, yy, xx, :, self.half[h]]
        return remote(s, self.out.at[zz, yy, xx, :, self.half[h]], self.ns.at[zz * 6 + j], self.nr.at[zz * 6 + j], target)
    def first(self, zz, own=False):
        y, x = self.y, self.x
        return [self.hop(own, zz, y, x, 0, "y", 0), self.hop(own, zz, y, x, 1, "x", 1),
                self.hop(own, zz, y, x, 0, "x", 2), self.hop(own, zz, y, x, 1, "y", 3)]
    def second(self, zz):
        y, x = self.y, self.x
        return [self.hop(False, zz, 1 - y, x, 0, "x", 4), self.hop(False, zz, y, 1 - x, 1, "y", 5)]
    def relay(self, own, zz, step, way):
        s = self.src if own else self.out.at[zz, self.y, self.x]
        slot = way * (self.G - 1) + step
        target = wide_id(self.z + (1 if way == 0 else -1), self.y, self.x)
        return remote(s, self.out.at[zz, self.y, self.x], self.zs.at[slot], self.zr.at[slot], target)
    def can(self, way):
        return self.z < self.G - 1 if way == 0 else self.z > 0
    def source(self, d, way):
        return (self.z - d, self.z - d >= 0) if way == 0 else (self.z + d, self.z + d < self.G)
    def begin(self):
        pltpu.make_async_copy(self.src, self.out.at[self.z, self.y, self.x], self.local_sem).start()
        for way in range(2):
            @pl.when(self.can(way))
            def _(): self.relay(True, self.z, 0, way).start()
        for c in self.first(self.z, True): c.start()
    def turn(self, zz):
        y, x = self.y, self.x
        self.hop(False, zz, 1 - y, x, 0, "y", 0).wait_recv()
        self.hop(False, zz, y, 1 - x, 1, "x", 1).wait_recv()
        for c in self.second(zz): c.start()
    def step(self, d):
        for way in range(2):
            zz, there = self.source(d, way)
            @pl.when(there)
            def _():
                self.relay(False, zz, d - 1, way).wait_recv()
                @pl.when(self.can(way))
                def _():
                    self.relay(False, zz, d, way).start()
                for c in self.first(zz): c.start()
    def turns(self, d):
        if d == 0:
            self.turn(self.z)
            return
        for way in range(2):
            zz, there = self.source(d, way)
            @pl.when(there)
            def _(): self.turn(zz)
    def finish(self):
        y, x = self.y, self.x
        for zz in range(self.G):
            self.hop(False, zz, y, 1 - x, 0, "x", 2).wait_recv()
            self.hop(False, zz, 1 - y, x, 1, "y", 3).wait_recv()
            self.hop(False, zz, 1 - y, 1 - x, 0, "x", 4).wait_recv()
            self.hop(False, zz, 1 - y, 1 - x, 1, "y", 5).wait_recv()
            for c in self.first(zz) + self.second(zz): c.wait_send()
        for way in range(2):
            @pl.when(self.can(way))
            def _():
                self.relay(True, self.z, 0, way).wait_send()
                for d in range(1, self.G - 1):
                    zz, there = self.source(d, way)
                    @pl.when(there)
                    def _(): self.relay(False, zz, d, way).wait_send()
        pltpu.make_async_copy(self.src, self.out.at[self.z, self.y, self.x], self.local_sem).wait()

def gather_sems(G):
    D = pltpu.SemaphoreType.DMA
    return [D, D((2 * (G - 1),)), D((2 * (G - 1),)), D((6 * G,)), D((6 * G,))]

def cut_of(C):
    return (C // 128 + 1) // 2 * 128

def ag_kernel(G, cut, src, out, *sems):
    greet(G, False)
    a = Gather(G, cut, src, out, *sems)
    a.begin()
    a.turns(0)
    for d in range(1, G):
        a.step(d)
        a.turns(d)
    a.finish()

def gather(shard, wide, cid):
    R, C = shard.shape
    G = wide // 4
    out = pl.pallas_call(functools.partial(ag_kernel, G, cut_of(C)),
        out_shape=jax.ShapeDtypeStruct((G, 2, 2, R, C), shard.dtype),
        in_specs=[pl.BlockSpec(memory_space=pl.ANY)], out_specs=pl.BlockSpec(memory_space=pl.ANY),
        scratch_shapes=gather_sems(G),
        compiler_params=pltpu.CompilerParams(collective_id=cid, has_side_effects=True), name="gather")(shard)
    return out.reshape(wide * R, C)

class Scatter:
    def __init__(self, G, cut, part, r1a, r1b, o1a, o1b, r2a, r2b, r3, own, lsem, s1, v1, s2, v2, s3, v3):
        self.__dict__.update(locals())
        C = part.shape[-1]
        self.ha, self.hb = pl.ds(0, cut), pl.ds(cut, C - cut)
        self.z, self.y, self.x = place()
    def zk(self, k):
        return (self.z + k) % self.G
    def ynb(self): return wide_id(self.z, 1 - self.y, self.x)
    def xnb(self): return wide_id(self.z, self.y, 1 - self.x)
    def one(self, k):
        z = self.zk(k)
        return [remote(self.part.at[z, :, 1 - self.x, :, self.ha], self.r1a.at[k], self.s1.at[2 * k], self.v1.at[2 * k], self.xnb()),
                remote(self.part.at[z, 1 - self.y, :, :, self.hb], self.r1b.at[k], self.s1.at[2 * k + 1], self.v1.at[2 * k + 1], self.ynb())]
    def load(self, k):
        z = self.zk(k)
        return [pltpu.make_async_copy(self.part.at[z, :, self.x, :, self.ha], self.o1a.at[k], self.lsem.at[2 * k]),
                pltpu.make_async_copy(self.part.at[z, self.y, :, :, self.hb], self.o1b.at[k], self.lsem.at[2 * k + 1])]
    def two(self, k):
        return [remote(self.o1a.at[k, 1 - self.y], self.r2a.at[k], self.s2.at[2 * k], self.v2.at[2 * k], self.ynb()),
                remote(self.o1b.at[k, 1 - self.x], self.r2b.at[k], self.s2.at[2 * k + 1], self.v2.at[2 * k + 1], self.xnb())]
    def three(self, k):
        return remote(self.own.at[k], self.r3.at[k - 1], self.s3.at[k - 1], self.v3.at[k - 1], wide_id(self.zk(k), self.y, self.x))
    def order(self):
        ks = list(range(1, self.G))
        return sorted(ks, key=lambda k: min(k, self.G - k), reverse=True) + [0]
    def launch(self, k):
        for c in self.one(k) + self.load(k): c.start()
    def begin(self):
        for k in self.order()[:2]: self.launch(k)
    def add_one(self, k):
        R = self.part.shape[3]
        for c in self.one(k): c.wait_recv()
        for c in self.load(k): c.wait()
        step = min(16, R)
        for mine, got in ((self.o1a, self.r1a), (self.o1b, self.r1b)):
            @pl.loop(0, 2 * R // step)
            def _(i):
                j, r = i // (R // step), pl.ds(pl.multiple_of((i % (R // step)) * step, step), step)
                mine[k, j, r, :] = (mine[k, j, r, :].astype(f32) + got[k, j, r, :].astype(f32)).astype(bf16)
        for c in self.two(k): c.start()
        later = self.order()[self.order().index(k) + 2:]
        if later: self.launch(later[0])
    def add_two(self, k):
        R = self.part.shape[3]
        for c in self.two(k): c.wait_recv()
        step = min(16, R)
        for mine, got, me, cols in ((self.o1a, self.r2a, self.y, self.ha), (self.o1b, self.r2b, self.x, self.hb)):
            @pl.loop(0, R // step)
            def _(i):
                r = pl.ds(pl.multiple_of(i * step, step), step)
                self.own[k, r, cols] = (mine[k, me, r, :].astype(f32) + got[k, r, :].astype(f32)).astype(bf16)
        if k:
            self.three(k).start()
    def finish(self, out):
        R = self.part.shape[3]
        for k in range(1, self.G): self.three(k).wait_recv()
        step = min(16, R)
        @pl.loop(0, R // step)
        def _(i):
            r = pl.ds(pl.multiple_of(i * step, step), step)
            total = self.own[0, r, :].astype(f32)
            for k in range(self.G - 1):
                total = total + self.r3[k, r, :].astype(f32)
            out[r, :] = total
        for k in range(self.G):
            for c in self.one(k) + self.two(k): c.wait_send()
            if k: self.three(k).wait_send()

def scatter_scratch(G, R, C):
    cut = cut_of(C)
    D, V = pltpu.SemaphoreType.DMA, lambda *s: pltpu.VMEM(s, bf16)
    return [V(G, 2, R, cut), V(G, 2, R, C - cut), V(G, 2, R, cut), V(G, 2, R, C - cut), V(G, R, cut), V(G, R, C - cut),
            V(G - 1, R, C), V(G, R, C), D((2 * G,)), D((2 * G,)), D((2 * G,)), D((2 * G,)), D((2 * G,)), D((G - 1,)), D((G - 1,))]

def rs_kernel(G, cut, part, out, *scratch):
    greet(G, True)
    s = Scatter(G, cut, part, *scratch)
    s.begin()
    order = s.order()
    for n, k in enumerate(order):
        s.add_one(k)
        if n: s.add_two(order[n - 1])
    s.add_two(order[-1])
    s.finish(out)

def scatter(part, wide, cid):
    R, C, G = part.shape[0] // wide, part.shape[1], wide // 4
    return pl.pallas_call(functools.partial(rs_kernel, G, cut_of(C)),
        out_shape=jax.ShapeDtypeStruct((R, C), f32),
        in_specs=[pl.BlockSpec(memory_space=pl.ANY)], out_specs=pl.BlockSpec(memory_space=pltpu.VMEM),
        scratch_shapes=scatter_scratch(G, R, C),
        compiler_params=pltpu.CompilerParams(collective_id=cid, has_side_effects=True, vmem_limit_bytes=56 * 2**20), name="scatter")(part.reshape(G, 2, 2, R, C))

def sum_kernel(G, src, out, acc, got, gz, s, v, sz, vz):
    z, y, x = place()
    core = {"narrow": 1 - lax.axis_index("narrow")}
    ynb, xnb = wide_id(z, 1 - y, x), wide_id(z, y, 1 - x)
    far = [wide_id((z + k) % G, y, x) for k in range(1, G)]
    bar = pltpu.get_barrier_semaphore()
    for t in [core, ynb, xnb] + far:
        pl.semaphore_signal(bar, inc=1, device_id=t, device_id_type=MESH)
    pl.semaphore_wait(bar, 3 + len(far))
    acc[0] = src[...]
    for n, t in enumerate((core, xnb, ynb)):
        c = remote(acc.at[n], got.at[n], s.at[n], v.at[n], t)
        c.start()
        c.wait()
        acc[n + 1] = acc[n] + got[n]
    gz[z] = acc[3]
    sent = [remote(acc.at[3], gz.at[z], sz.at[k], vz.at[z], t) for k, t in enumerate(far)]
    for c in sent: c.start()
    for k in range(1, G):
        zz = (z + k) % G
        remote(acc.at[3], gz.at[zz], sz.at[k - 1], vz.at[zz], far[k - 1]).wait_recv()
    for c in sent: c.wait_send()
    total = gz[0]
    for k in range(1, G):
        total = total + gz[k]
    out[...] = total

def sum_all(part, wide, cid):
    G, rows = wide // 4, part.shape[0]
    D, V = pltpu.SemaphoreType.DMA, lambda k: pltpu.VMEM((k, rows, 128), f32)
    return pl.pallas_call(functools.partial(sum_kernel, G), out_shape=jax.ShapeDtypeStruct(part.shape, f32),
        in_specs=[pl.BlockSpec(memory_space=pltpu.VMEM)], out_specs=pl.BlockSpec(memory_space=pltpu.VMEM),
        scratch_shapes=[V(4), V(3), V(G), D((3,)), D((3,)), D((G - 1,)), D((G,))],
        compiler_params=pltpu.CompilerParams(collective_id=cid, has_side_effects=True), name="small_sums")(part)


epsilon = 1e-06


def norm_plain(values, gain_row):
    factor = lax.rsqrt(jnp.mean(values * values, axis=-1, keepdims=True) + epsilon)
    return values * factor * gain_row


def gated_unit(gate_pre, up_pre):
    return jax.nn.gelu(gate_pre, approximate=True) * up_pre


def times(a, b):
    return jnp.dot(a, b, preferred_element_type=f32)


def times_transposed(a, b):
    return lax.dot_general(a, b, NT, preferred_element_type=f32)


def transposed_times(a, b):
    return lax.dot_general(a, b, (((0,), (0,)), ((), ())), preferred_element_type=f32)


def swap(a):
    return lax.ppermute(a, "narrow", [(0, 1), (1, 0)])


def both(a):
    return a.astype(f32) + swap(a).astype(f32)


def local(tokens, cotangent, pages, boxes, gain_attn, gain_ffn, bias_tables, w_query, w_key, w_value, w_out, w_gate, w_up, w_down):
    wide, narrow = lax.axis_size("wide"), lax.axis_size("narrow")
    heads_all = bias_tables.shape[1]
    heads = heads_all // narrow
    rows = tokens.shape[0]
    core = lax.axis_index("narrow")
    tables = lax.dynamic_slice_in_dim(bias_tables, core * heads, heads, 1)
    inner, ff = w_query.shape[1], w_gate.shape[1]
    mine = lambda a: lax.dynamic_slice_in_dim(a, core * rows, rows, 0)

    all_tokens = lax.all_gather(tokens, "narrow", axis=0, tiled=True)
    all_cot = lax.all_gather(cotangent, "narrow", axis=0, tiled=True)
    bias, ids = make_bias(tables, boxes, pages)
    w_first = gather(jnp.concatenate([w_query, w_key, w_value], axis=1), wide, 1)
    w_second = gather(jnp.concatenate([w_out.T, w_gate, w_up, w_down.T], axis=1), wide, 2)
    full_out, full_gate, full_up, full_down = jnp.split(w_second, [inner, inner + ff, inner + 2 * ff], axis=1)

    x = all_tokens.astype(f32)
    gain_one, gain_two = gain_attn.astype(f32), gain_ffn.astype(f32)
    normed = norm_plain(x, gain_one).astype(bf16)
    qkv = times(normed, w_first).astype(bf16)
    attended, lse = attn_fwd(qkv, bias)
    hidden = x + both(times_transposed(attended, full_out).astype(bf16))
    normed_two = norm_plain(hidden, gain_two).astype(bf16)
    gate_pre, up_pre = times(normed_two, full_gate), times(normed_two, full_up)
    hidden_ff = gated_unit(gate_pre, up_pre).astype(bf16)
    down = times_transposed(hidden_ff, full_down).astype(bf16)
    output = (mine(hidden) + lax.psum_scatter(down, "narrow", scatter_dimension=0, tiled=True).astype(f32)).astype(bf16)

    grad_w_down = transposed_times(all_cot, hidden_ff)
    grad_ff = times(all_cot, full_down)
    _, gated_pull = jax.vjp(gated_unit, gate_pre, up_pre)
    grad_gate, grad_up = [g.astype(bf16) for g in gated_pull(grad_ff)]
    grad_w_gate = transposed_times(normed_two, grad_gate)
    grad_w_up = transposed_times(normed_two, grad_up)
    grad_two = both((times_transposed(grad_gate, full_gate) + times_transposed(grad_up, full_up)).astype(bf16))
    _, pull_two = jax.vjp(lambda h: norm_plain(h, gain_two), hidden)
    grad_hidden = all_cot.astype(f32) + pull_two(grad_two)[0]
    own_hidden = mine(hidden)
    grad_gain_two = jnp.sum(mine(grad_two) * own_hidden * lax.rsqrt(jnp.mean(own_hidden * own_hidden, axis=-1, keepdims=True) + epsilon), axis=0)
    grad_low = grad_hidden.astype(bf16)
    grad_w_out = transposed_times(grad_low, attended)
    second = jnp.concatenate([g.astype(bf16) for g in (grad_w_out, grad_w_gate, grad_w_up, grad_w_down)], axis=1)
    shard_second = scatter(second, wide, 3)
    grad_attended = times(grad_low, full_out).astype(bf16)
    dq, dk, dv, g = attn_bwd(qkv, bias, attended, grad_attended, lse)
    dqkv = jnp.concatenate([dq, dk, dv], axis=1)
    shard_first = scatter(transposed_times(normed, dqkv).astype(bf16), wide, 4)
    grad_normed = lax.psum_scatter(times_transposed(dqkv, w_first).astype(bf16), "narrow", scatter_dimension=0, tiled=True).astype(f32)
    own = tokens.astype(f32)
    _, pull_one = jax.vjp(norm_plain, own, gain_one)
    grad_tokens_norm, grad_gain_one = pull_one(grad_normed)
    grad_tokens = mine(grad_hidden) + grad_tokens_norm
    table_part = lax.dynamic_update_slice(jnp.zeros((bias_tables.shape[0], heads_all), f32), table_hist(g, ids).T, (jnp.int32(0), core * heads))
    sizes = [gain_one.size, gain_two.size, table_part.size]
    small = sum_all(jnp.concatenate([grad_gain_one, grad_gain_two, table_part.reshape(-1)]).reshape(-1, 128), wide, 5).reshape(-1)
    one, two, table = jnp.split(small, [sizes[0], sizes[0] + sizes[1]])
    s_query, s_key, s_value = jnp.split(shard_first, 3, axis=1)
    s_out, s_gate, s_up, s_down = jnp.split(shard_second, [inner, inner + ff, inner + 2 * ff], axis=1)
    return (output, grad_tokens, one, two, table.reshape(bias_tables.shape), s_query, s_key, s_value, s_out.T, s_gate, s_up, s_down.T)


def solution(mesh):
    rows, cols, tall = P(("wide", "narrow"), None), P("wide", "narrow"), P("narrow", "wide")
    in_specs = (rows, rows, P("wide"), P(None, "wide"), P(), P(), P(), cols, cols, cols, tall, cols, cols, tall)
    out_specs = (rows, rows, P(), P(), P(), cols, cols, cols, tall, cols, cols, tall)
    return jax.shard_map(local, mesh=mesh, in_specs=in_specs, out_specs=out_specs, check_vma=False)
```

```python
import functools

import jax
import jax.numpy as jnp
from jax import lax
from jax.experimental import pallas as pl
from jax.experimental.pallas import tpu as pltpu
from jax.sharding import PartitionSpec as P

f32, bf16 = jnp.float32, jnp.bfloat16
MESH = pl.DeviceIdType.MESH


EDGES = (1, 2, 3, 4, 5, 6, 7, 8, 12, 16, 23, 32, 46, 64, 91)
NT = (((1,), (1,)), ((), ()))
VM = 58 * 2**20


def params(cid):
    return pltpu.CompilerParams(collective_id=cid, has_side_effects=True, vmem_limit_bytes=VM)


def lane_take(table, idx):
    return jnp.take_along_axis(table, idx, axis=1, mode="promise_in_bounds")


def bias_tile(start, heads, rows, n, steps_ref, tab_ref, box_col, box_row, page_col, page_row, bias_ref, ids_ref):
    steps = jnp.broadcast_to(steps_ref[...], (rows, 128))
    allowed_col = jnp.broadcast_to(page_col[...] % 2, (rows, 128))
    cols = [jnp.broadcast_to(box_col[:, t:t + 1], (rows, 128)) for t in range(2)]
    own = lax.broadcasted_iota(jnp.int32, (rows, 128), 0) + start

    @pl.loop(0, n // 128)
    def _(c):
        lanes = pl.ds(pl.multiple_of(c * 128, 128), 128)
        lane_id = lax.broadcasted_iota(jnp.int32, (rows, 128), 1) + c * 128
        ids = []
        for t in range(3):
            gap = (lane_id - own) if t == 0 else (jnp.broadcast_to(box_row[t - 1:t, lanes], (rows, 128)) - cols[t - 1])
            size = jnp.abs(gap)
            if t > 0:
                size = size >> 2
            bucket = lane_take(steps, jnp.minimum(size, 91)) + jnp.where(gap > 0, 16, 0)
            ids.append(bucket)
            ids_ref[t, :, lanes] = bucket.astype(f32)
        ok = jnp.broadcast_to(page_row[:, lanes], (rows, 128)) == allowed_col
        for h in range(heads):
            total = None
            for t in range(3):
                table = jnp.broadcast_to(tab_ref[t * heads + h:t * heads + h + 1, :], (rows, 128))
                part = lane_take(table, ids[t])
                total = part if total is None else total + part
            bias_ref[h, :, lanes] = jnp.where(ok, total, -1e30)


def bias_gather_kernel(heads, rows, n, G, halves, count, *refs):
    ins, srcs = refs[:6], refs[6:6 + count]
    bias_ref, ids_ref = refs[6 + count:8 + count]
    outs, sems = refs[8 + count:8 + 2 * count], refs[8 + 2 * count:]
    now = pl.program_id(0)
    comm = Gather(G, halves, srcs, outs, *sems)
    beside(comm, n // rows, now, lambda: bias_tile(now * rows, heads, rows, n, *ins, bias_ref, ids_ref))


def bias_and_gather(tables, boxes, pages, shards, halves, wide, cid):
    heads, n, G, rows = tables.shape[1], pages.shape[0], wide // 4, 64
    tab = jnp.pad(tables.astype(f32).reshape(3, 32, heads).transpose(0, 2, 1).reshape(3 * heads, 32), ((0, 0), (0, 96)))
    lane = jnp.arange(128, dtype=jnp.int32)
    steps = sum([(lane >= e).astype(jnp.int32) for e in EDGES])[None]
    count = len(shards)
    outs = pl.pallas_call(functools.partial(bias_gather_kernel, heads, rows, n, G, halves, count),
        grid=(n // rows,),
        out_shape=(jax.ShapeDtypeStruct((heads, n, n), f32), jax.ShapeDtypeStruct((3, n, n), f32)) + gathered_shapes(shards, wide),
        in_specs=[pl.BlockSpec((1, 128), lambda i: (0, 0)), pl.BlockSpec((3 * heads, 128), lambda i: (0, 0)),
                  pl.BlockSpec((rows, 2), lambda i: (i, 0)), pl.BlockSpec((2, n), lambda i: (0, 0)),
                  pl.BlockSpec((rows, 1), lambda i: (i, 0)), pl.BlockSpec((1, n), lambda i: (0, 0))] + [ANY] * count,
        out_specs=(pl.BlockSpec((heads, rows, n), lambda i: (0, i, 0)), pl.BlockSpec((3, rows, n), lambda i: (0, i, 0))) + (ANY,) * count,
        scratch_shapes=gather_scratch(G, halves, count), compiler_params=params(cid), name="layout_bias_gather")(
            steps, tab, boxes.T, boxes, pages[:, None], pages[None], *shards)
    return outs[0], outs[1], [flat(a) for a in outs[2:]]


def half_of(v, e):
    lane = lax.broadcasted_iota(jnp.int32, v.shape, 1)
    return jnp.where((lane >= 64) == (e == 1), v, jnp.zeros_like(v))


def join(a, b):
    lane = lax.broadcasted_iota(jnp.int32, a.shape, 1)
    return jnp.where(lane < 64, a, b)


def fwd_tile(q_ref, k_ref, v_ref, bias_ref, o_ref, lse_ref):
    q, k, v = q_ref[...], k_ref[...], v_ref[...]
    outs, lses = [], []
    for e in range(2):
        s = lax.dot_general(half_of(q, e), k, NT, preferred_element_type=f32) + bias_ref[e]
        peak = jnp.max(s, axis=1, keepdims=True)
        p = jnp.exp(s - peak)
        total = jnp.sum(p, axis=1, keepdims=True)
        outs.append(jnp.dot(p.astype(bf16), v, preferred_element_type=f32) / total)
        lses.append(peak + jnp.log(total))
    o_ref[...] = join(*outs).astype(bf16)
    lse_ref[0] = jnp.concatenate(lses, axis=1)


def fwd_kernel(steps, tiles, G, halves, count, *refs):
    ins, srcs = refs[:4], refs[4:4 + count]
    mid = refs[4 + count:6 + count]
    outs, sems = refs[6 + count:6 + 2 * count], refs[6 + 2 * count:]
    now = pl.program_id(0) * tiles + pl.program_id(1)
    beside(Gather(G, halves, srcs, outs, *sems), steps, now, lambda: fwd_tile(*ins, *mid))


def attn_fwd_and_gather(qkv, bias, shards, halves, wide, cid, tq=256):
    n, width = qkv.shape[0], qkv.shape[1] // 3
    pairs, tiles, count, G = width // 128, n // tq, len(shards), wide // 4
    outs = pl.pallas_call(functools.partial(fwd_kernel, pairs * tiles, tiles, G, halves, count), grid=(pairs, tiles),
        out_shape=(jax.ShapeDtypeStruct((n, width), bf16), jax.ShapeDtypeStruct((pairs, n, 2), f32)) + gathered_shapes(shards, wide),
        in_specs=[pl.BlockSpec((tq, 128), lambda p, i: (i, p)), pl.BlockSpec((n, 128), lambda p, i: (0, p + pairs)),
                  pl.BlockSpec((n, 128), lambda p, i: (0, p + 2 * pairs)), pl.BlockSpec((2, tq, n), lambda p, i: (p, i, 0))] + [ANY] * count,
        out_specs=(pl.BlockSpec((tq, 128), lambda p, i: (i, p)), pl.BlockSpec((1, tq, 2), lambda p, i: (p, i, 0))) + (ANY,) * count,
        scratch_shapes=gather_scratch(G, halves, count), compiler_params=params(cid), name="attention_gather")(qkv, qkv, qkv, bias, *shards)
    return outs[0], outs[1], [flat(a) for a in outs[2:]]


def bwd_tile(first, last, q_ref, k_ref, v_ref, bias_ref, o_ref, do_ref, lse_ref, dq_ref, dk_ref, dv_ref, g_ref, dkt, dvt):
    @pl.when(first)
    def _():
        dkt[...] = jnp.zeros_like(dkt)
        dvt[...] = jnp.zeros_like(dvt)

    q, k, v, do = q_ref[...], k_ref[...], v_ref[...], do_ref[...]
    prod = do.astype(f32) * o_ref[...].astype(f32)
    dqs = []
    for e in range(2):
        qm, dom = half_of(q, e), half_of(do, e)
        s = lax.dot_general(qm, k, NT, preferred_element_type=f32) + bias_ref[e]
        p = jnp.exp(s - lse_ref[0, :, e:e + 1])
        dp = lax.dot_general(dom, v, NT, preferred_element_type=f32)
        inner = jnp.sum(half_of(prod, e), axis=1, keepdims=True)
        g = (p * (dp - inner)).astype(bf16)
        g_ref[e] = g
        dqs.append(jnp.dot(g, k, preferred_element_type=f32))
        dvt[...] += jnp.dot(dom.T, p.astype(bf16), preferred_element_type=f32)
        dkt[...] += jnp.dot(qm.T, g, preferred_element_type=f32)
    dq_ref[...] = join(*dqs).astype(bf16)

    @pl.when(last)
    def _():
        dk_ref[...] = dkt[...].T.astype(bf16)
        dv_ref[...] = dvt[...].T.astype(bf16)


def bwd_kernel(steps, tiles, G, halves, count, *refs):
    ins, parts = refs[:7], refs[7:7 + count]
    mid = refs[7 + count:11 + count]
    outs, accs, sems = refs[11 + count:11 + 2 * count], refs[11 + 2 * count:13 + 2 * count], refs[13 + 2 * count:]
    i = pl.program_id(1)
    comm = Scatter(G, halves, parts, outs, *sems)
    beside(comm, steps, pl.program_id(0) * tiles + i, lambda: bwd_tile(i == 0, i == tiles - 1, *ins, *mid, *accs))


def shard_shapes(parts, wide):
    return tuple(jax.ShapeDtypeStruct((p.shape[0] // wide, p.shape[1]), f32) for p in parts)


def attn_bwd_and_scatter(qkv, bias, o, do, lse, parts, halves, wide, cid, tq=256):
    n, width = qkv.shape[0], qkv.shape[1] // 3
    pairs, tiles, count, G = width // 128, n // tq, len(parts), wide // 4
    tile = pl.BlockSpec((tq, 128), lambda p, i: (i, p))
    full = pl.BlockSpec((n, 128), lambda p, i: (0, p))
    outs = pl.pallas_call(functools.partial(bwd_kernel, pairs * tiles, tiles, G, halves, count), grid=(pairs, tiles),
        out_shape=(jax.ShapeDtypeStruct((n, width), bf16),) * 3 + (jax.ShapeDtypeStruct((2 * pairs, n, n), bf16),) + shard_shapes(parts, wide),
        in_specs=[tile, pl.BlockSpec((n, 128), lambda p, i: (0, p + pairs)), pl.BlockSpec((n, 128), lambda p, i: (0, p + 2 * pairs)),
                  pl.BlockSpec((2, tq, n), lambda p, i: (p, i, 0)), tile, tile, pl.BlockSpec((1, tq, 2), lambda p, i: (p, i, 0))] + [ANY] * count,
        out_specs=(tile, full, full, pl.BlockSpec((2, tq, n), lambda p, i: (p, i, 0))) + (whole_vmem(),) * count,
        scratch_shapes=[pltpu.VMEM((128, n), f32), pltpu.VMEM((128, n), f32)] + scatter_scratch(G, halves, parts[0].shape[0] // wide),
        compiler_params=params(cid), name="attention_back_scatter")(qkv, qkv, qkv, bias, o, do, lse, *[spread(p, wide) for p in parts])
    return outs[:4], outs[4:]


def hist_tile(first, heads, rows, n, g_ref, ids_ref, out_ref, gs):
    @pl.when(first)
    def _():
        out_ref[...] = jnp.zeros_like(out_ref)

    for h in range(heads):
        for c in range(n // 128):
            gs[c, h * rows:(h + 1) * rows, :] = g_ref[h, :, c * 128:(c + 1) * 128].astype(f32)
    label = lax.broadcasted_iota(jnp.int32, (32, n), 0).astype(bf16)
    one, zero = jnp.ones((32, n), bf16), jnp.zeros((32, n), bf16)
    acc = jnp.zeros((heads, 96), f32)
    for r in range(rows):
        grow = jnp.concatenate([gs[c, pl.ds(r, heads, stride=rows), :] for c in range(n // 128)], axis=1).astype(bf16)
        hots = []
        for t in range(3):
            row = jnp.broadcast_to(ids_ref[t, r:r + 1, :], (32, n)).astype(bf16)
            hots.append(jnp.where(row == label, one, zero))
        acc = acc + lax.dot_general(grow, jnp.concatenate(hots, axis=0), NT, preferred_element_type=f32)
    out_ref[...] += acc


def hist_kernel(heads, rows, n, G, halves, count, *refs):
    ins, parts, out_ref = refs[:2], refs[2:2 + count], refs[2 + count]
    outs, gs, sems = refs[3 + count:3 + 2 * count], refs[3 + 2 * count], refs[4 + 2 * count:]
    now = pl.program_id(0)
    comm = Scatter(G, halves, parts, outs, *sems)
    beside(comm, n // rows, now, lambda: hist_tile(now == 0, heads, rows, n, *ins, out_ref, gs))


def hist_and_scatter(g, ids, parts, halves, wide, cid):
    heads, n, _ = g.shape
    rows, count, G = 16, len(parts), wide // 4
    outs = pl.pallas_call(functools.partial(hist_kernel, heads, rows, n, G, halves, count), grid=(n // rows,),
        out_shape=(jax.ShapeDtypeStruct((heads, 96), f32),) + shard_shapes(parts, wide),
        in_specs=[pl.BlockSpec((heads, rows, n), lambda i: (0, i, 0)), pl.BlockSpec((3, rows, n), lambda i: (0, i, 0))] + [ANY] * count,
        out_specs=(pl.BlockSpec((heads, 96), lambda i: (0, 0)),) + (whole_vmem(),) * count,
        scratch_shapes=[pltpu.VMEM((n // 128, heads * rows, 128), f32)] + scatter_scratch(G, halves, parts[0].shape[0] // wide),
        compiler_params=params(cid), name="table_grad_scatter")(g, ids, *[spread(p, wide) for p in parts])
    return outs[0], outs[1:]


D = pltpu.SemaphoreType.DMA


def place():
    me = lax.axis_index("wide")
    return me // 4, (me // 2) % 2, me % 2


def wide_id(z, y, x):
    return {"wide": z * 4 + y * 2 + x}


def remote(src, dst, send, recv, target):
    return pltpu.make_async_remote_copy(src_ref=src, dst_ref=dst, send_sem=send, recv_sem=recv, device_id=target, device_id_type=MESH)


def greet(G, far):
    z, y, x = place()
    bar = pltpu.get_barrier_semaphore()
    sig = lambda t: pl.semaphore_signal(bar, inc=1, device_id=t, device_id_type=MESH)
    sig(wide_id(z, 1 - y, x))
    sig(wide_id(z, y, 1 - x))
    if far:
        for k in range(1, G):
            sig(wide_id((z + k) % G, y, x))
        pl.semaphore_wait(bar, 2 + G - 1)
    else:
        @pl.when(z > 0)
        def _():
            sig(wide_id(z - 1, y, x))

        @pl.when(z < G - 1)
        def _():
            sig(wide_id(z + 1, y, x))

        pl.semaphore_wait(bar, 2 + (z > 0).astype(jnp.int32) + (z < G - 1).astype(jnp.int32))


class Gather:
    def __init__(self, G, halves, srcs, outs, local_sem, zs, zr, ns, nr):
        self.G, self.halves, self.srcs, self.outs, self.local_sem = G, halves, srcs, outs, local_sem
        self.zs, self.zr, self.ns, self.nr = zs, zr, ns, nr
        self.most = max(len(h) for h in halves)
        self.z, self.y, self.x = place()

    def hop(self, own, zz, yy, xx, h, way, j):
        target = wide_id(self.z, 1 - self.y, self.x) if way == "y" else wide_id(self.z, self.y, 1 - self.x)
        copies = []
        for n, (a, c, w) in enumerate(self.halves[h]):
            slot = (zz * 6 + j) * self.most + n
            dst = self.outs[a].at[zz, yy, xx, :, pl.ds(c, w)]
            copies.append(remote(self.srcs[a].at[:, pl.ds(c, w)] if own else dst, dst, self.ns.at[slot], self.nr.at[slot], target))
        return copies

    def second_stage(self, zz, own=False):
        return self.hop(own, zz, self.y, self.x, 0, "y", 0) + self.hop(own, zz, self.y, self.x, 1, "x", 1)

    def third_stage(self, zz, own=False):
        return self.hop(own, zz, self.y, self.x, 0, "x", 2) + self.hop(own, zz, self.y, self.x, 1, "y", 3)

    def last_stage(self, zz):
        return self.hop(False, zz, 1 - self.y, self.x, 0, "x", 4) + self.hop(False, zz, self.y, 1 - self.x, 1, "y", 5)

    def relay(self, own, zz, step, way):
        copies = []
        for a in range(len(self.srcs)):
            slot = (way * (self.G - 1) + step) * len(self.srcs) + a
            dst = self.outs[a].at[zz, self.y, self.x]
            copies.append(remote(self.srcs[a] if own else dst, dst, self.zs.at[slot], self.zr.at[slot],
                                 wide_id(self.z + (1 if way == 0 else -1), self.y, self.x)))
        return copies

    def can(self, way):
        return self.z < self.G - 1 if way == 0 else self.z > 0

    def source(self, d, way):
        return (self.z - d, self.z - d >= 0) if way == 0 else (self.z + d, self.z + d < self.G)

    def keep(self):
        return [pltpu.make_async_copy(s, o.at[self.z, self.y, self.x], self.local_sem.at[a]) for a, (s, o) in enumerate(zip(self.srcs, self.outs))]

    def begin(self):
        for way in range(2):
            @pl.when(self.can(way))
            def _():
                for c in self.relay(True, self.z, 0, way):
                    c.start()
        for c in self.second_stage(self.z, True) + self.third_stage(self.z, True) + self.keep():
            c.start()

    def turn(self, zz):
        for c in self.hop(False, zz, 1 - self.y, self.x, 0, "y", 0) + self.hop(False, zz, self.y, 1 - self.x, 1, "x", 1):
            c.wait_recv()
        for c in self.last_stage(zz):
            c.start()

    def step(self, d):
        for way in range(2):
            zz, there = self.source(d, way)

            @pl.when(there)
            def _():
                for c in self.relay(False, zz, d - 1, way):
                    c.wait_recv()

                @pl.when(self.can(way))
                def _():
                    for c in self.relay(False, zz, d, way):
                        c.start()

                for c in self.second_stage(zz):
                    c.start()
        for way in range(2):
            zz, there = self.source(d, way)

            @pl.when(there)
            def _():
                for c in self.third_stage(zz):
                    c.start()

    def turns(self, d):
        if d == 0:
            self.turn(self.z)
            return
        for way in range(2):
            zz, there = self.source(d, way)

            @pl.when(there)
            def _():
                self.turn(zz)

    def finish(self):
        y, x = self.y, self.x

        @pl.loop(0, self.G)
        def _(zz):
            for c in (self.hop(False, zz, y, 1 - x, 0, "x", 2) + self.hop(False, zz, 1 - y, x, 1, "y", 3)
                      + self.hop(False, zz, 1 - y, 1 - x, 0, "x", 4) + self.hop(False, zz, 1 - y, 1 - x, 1, "y", 5)):
                c.wait_recv()
            for c in self.second_stage(zz) + self.third_stage(zz) + self.last_stage(zz):
                c.wait_send()

        for way in range(2):
            @pl.when(self.can(way))
            def _():
                for c in self.relay(True, self.z, 0, way):
                    c.wait_send()
                for d in range(1, self.G - 1):
                    zz, there = self.source(d, way)

                    @pl.when(there)
                    def _():
                        for c in self.relay(False, zz, d, way):
                            c.wait_send()
        for c in self.keep():
            c.wait()

    def events(self):
        G = self.G
        first = lambda: (greet(G, False), self.begin())
        ev = [(0.0, first), (0.7, lambda: self.turns(0))]
        for d in range(1, G):
            ev += [(1.15 * d, functools.partial(self.step, d)), (1.3 * d + 1.2, functools.partial(self.turns, d))]
        return sorted(ev, key=lambda e: e[0]), self.finish


def gather_scratch(G, halves, arrays):
    most = max(len(h) for h in halves)
    return [D((arrays,)), D((2 * (G - 1) * arrays,)), D((2 * (G - 1) * arrays,)), D((6 * G * most,)), D((6 * G * most,))]


class Scatter:
    def __init__(self, G, halves, parts, outs, r1a, r1b, o1a, o1b, r2a, r2b, r3, own, lsem, s1, v1, s2, v2, s3, v3):
        self.__dict__.update(locals())
        self.most = max(len(h) for h in halves)
        self.wa, self.wb = [sum(p[2] for p in h) for h in halves]
        self.R = parts[0].shape[3]
        self.z, self.y, self.x = place()
        self.order = sorted(range(1, G), key=lambda k: min(k, G - k), reverse=True) + [0]

    def zk(self, k):
        return (self.z + k) % self.G

    def neighbour(self, way):
        return wide_id(self.z, 1 - self.y, self.x) if way == "y" else wide_id(self.z, self.y, 1 - self.x)

    def pieces(self, h):
        at, out = 0, []
        for n, (a, c, w) in enumerate(self.halves[h]):
            out.append((n, a, pl.ds(c, w), pl.ds(at, w)))
            at += w
        return out

    def one(self, k):
        z, cs = self.zk(k), []
        for n, a, src, dst in self.pieces(0):
            slot = (2 * k) * self.most + n
            cs.append(remote(self.parts[a].at[z, :, 1 - self.x, :, src], self.r1a.at[k, :, :, dst], self.s1.at[slot], self.v1.at[slot], self.neighbour("x")))
        for n, a, src, dst in self.pieces(1):
            slot = (2 * k + 1) * self.most + n
            cs.append(remote(self.parts[a].at[z, 1 - self.y, :, :, src], self.r1b.at[k, :, :, dst], self.s1.at[slot], self.v1.at[slot], self.neighbour("y")))
        return cs

    def load(self, k):
        z, cs = self.zk(k), []
        for n, a, src, dst in self.pieces(0):
            cs.append(pltpu.make_async_copy(self.parts[a].at[z, :, self.x, :, src], self.o1a.at[k, :, :, dst], self.lsem.at[(2 * k) * self.most + n]))
        for n, a, src, dst in self.pieces(1):
            cs.append(pltpu.make_async_copy(self.parts[a].at[z, self.y, :, :, src], self.o1b.at[k, :, :, dst], self.lsem.at[(2 * k + 1) * self.most + n]))
        return cs

    def two(self, k):
        return [remote(self.o1a.at[k, 1 - self.y], self.r2a.at[k], self.s2.at[2 * k], self.v2.at[2 * k], self.neighbour("y")),
                remote(self.o1b.at[k, 1 - self.x], self.r2b.at[k], self.s2.at[2 * k + 1], self.v2.at[2 * k + 1], self.neighbour("x"))]

    def three(self, k):
        return remote(self.own.at[k], self.r3.at[k - 1], self.s3.at[k - 1], self.v3.at[k - 1], wide_id(self.zk(k), self.y, self.x))

    def launch(self, k):
        for c in self.one(k) + self.load(k):
            c.start()

    def begin(self):
        for k in self.order[:2]:
            self.launch(k)

    def rows(self, count, body):
        step = min(16, count)

        @pl.loop(0, count // step)
        def _(i):
            body(pl.ds(pl.multiple_of(i * step, step), step))

    def add_one(self, n):
        k = self.order[n]
        for c in self.one(k):
            c.wait_recv()
        for c in self.load(k):
            c.wait()
        for mine, got in ((self.o1a, self.r1a), (self.o1b, self.r1b)):
            def body(r):
                for j in range(2):
                    mine[k, j, r, :] = (mine[k, j, r, :].astype(f32) + got[k, j, r, :].astype(f32)).astype(bf16)

            self.rows(self.R, body)
        for c in self.two(k):
            c.start()
        if n + 2 < self.G:
            self.launch(self.order[n + 2])

    def add_two(self, n):
        k = self.order[n]
        for c in self.two(k):
            c.wait_recv()

        def body(r):
            self.own[k, r, pl.ds(0, self.wa)] = (self.o1a[k, self.y, r, :].astype(f32) + self.r2a[k, r, :].astype(f32)).astype(bf16)
            self.own[k, r, pl.ds(self.wa, self.wb)] = (self.o1b[k, self.x, r, :].astype(f32) + self.r2b[k, r, :].astype(f32)).astype(bf16)

        self.rows(self.R, body)
        if k:
            self.three(k).start()

    def finish(self):
        self.add_two(self.G - 1)
        for k in range(1, self.G):
            self.three(k).wait_recv()

        def body(r):
            for h in range(2):
                for _, a, src, dst in self.pieces(h):
                    cols = pl.ds(dst.start + h * self.wa, dst.size)
                    total = self.own[0, r, cols].astype(f32)
                    for k in range(self.G - 1):
                        total = total + self.r3[k, r, cols].astype(f32)
                    self.outs[a][r, src] = total

        self.rows(self.R, body)
        for k in range(self.G):
            for c in self.one(k) + self.two(k):
                c.wait_send()
            if k:
                self.three(k).wait_send()

    def events(self):
        G = self.G
        first = lambda: (greet(G, True), self.begin())
        ev = [(0.0, first), (1.1, lambda: self.add_one(0))]
        for n in range(1, G):
            ev += [(1.5 * n + 0.65, functools.partial(self.add_one, n)), (1.5 * n + 1.1, functools.partial(self.add_two, n - 1))]
        return sorted(ev, key=lambda e: e[0]), self.finish


def scatter_scratch(G, halves, R):
    most = max(len(h) for h in halves)
    a, b = [sum(p[2] for p in h) for h in halves]
    V = lambda *s: pltpu.VMEM(s, bf16)
    return [V(G, 2, R, a), V(G, 2, R, b), V(G, 2, R, a), V(G, 2, R, b), V(G, R, a), V(G, R, b), V(G - 1, R, a + b), V(G, R, a + b),
            D((2 * G * most,)), D((2 * G * most,)), D((2 * G * most,)), D((2 * G,)), D((2 * G,)), D((G - 1,)), D((G - 1,))]


def beside(comm, steps, now, compute):
    events, finish = comm.events()
    units = 1.55 * comm.G
    for n in range(steps):
        here = [act for t, act in events if min(steps - 1, int(-(-t * steps // units))) == n]
        if here:
            @pl.when(now == n)
            def _():
                for act in here:
                    act()
    compute()

    @pl.when(now == steps - 1)
    def _():
        finish()


ANY = pl.BlockSpec(memory_space=pl.ANY)


def whole_vmem():
    return pl.BlockSpec(memory_space=pltpu.VMEM)


def spread(a, wide):
    return a.reshape(wide // 4, 2, 2, a.shape[0] // wide, a.shape[1])


def gathered_shapes(shards, wide):
    return tuple(jax.ShapeDtypeStruct((wide // 4, 2, 2) + s.shape, s.dtype) for s in shards)


def flat(a):
    return a.reshape(-1, a.shape[-1])


def sum_kernel(G, src, out, acc, got, gz, s, v, sz, vz):
    z, y, x = place()
    core = {"narrow": 1 - lax.axis_index("narrow")}
    ynb, xnb = wide_id(z, 1 - y, x), wide_id(z, y, 1 - x)
    far = [wide_id((z + k) % G, y, x) for k in range(1, G)]
    bar = pltpu.get_barrier_semaphore()
    for t in [core, ynb, xnb] + far:
        pl.semaphore_signal(bar, inc=1, device_id=t, device_id_type=MESH)
    pl.semaphore_wait(bar, 3 + len(far))
    acc[0] = src[...]
    for n, t in enumerate((core, xnb, ynb)):
        c = remote(acc.at[n], got.at[n], s.at[n], v.at[n], t)
        c.start()
        c.wait()
        acc[n + 1] = acc[n] + got[n]
    gz[z] = acc[3]
    sent = [remote(acc.at[3], gz.at[z], sz.at[k], vz.at[z], t) for k, t in enumerate(far)]
    for c in sent:
        c.start()
    for k in range(1, G):
        zz = (z + k) % G
        remote(acc.at[3], gz.at[zz], sz.at[k - 1], vz.at[zz], far[k - 1]).wait_recv()
    for c in sent:
        c.wait_send()
    total = gz[0]
    for k in range(1, G):
        total = total + gz[k]
    out[...] = total


def sum_all(part, wide, cid):
    G, rows = wide // 4, part.shape[0]
    V = lambda k: pltpu.VMEM((k, rows, 128), f32)
    return pl.pallas_call(functools.partial(sum_kernel, G), out_shape=jax.ShapeDtypeStruct(part.shape, f32),
        in_specs=[whole_vmem()], out_specs=whole_vmem(),
        scratch_shapes=[V(4), V(3), V(G), D((3,)), D((3,)), D((G - 1,)), D((G,))],
        compiler_params=pltpu.CompilerParams(collective_id=cid, has_side_effects=True), name="small_sums")(part)


epsilon = 1e-06


def norm_plain(values, gain_row):
    factor = lax.rsqrt(jnp.mean(values * values, axis=-1, keepdims=True) + epsilon)
    return values * factor * gain_row


def gated_unit(gate_pre, up_pre):
    return jax.nn.gelu(gate_pre, approximate=True) * up_pre


def times(a, b):
    return jnp.dot(a, b, preferred_element_type=f32)


def times_transposed(a, b):
    return lax.dot_general(a, b, NT, preferred_element_type=f32)


def transposed_times(a, b):
    return lax.dot_general(a, b, (((0,), (0,)), ((), ())), preferred_element_type=f32)


def swap(a):
    return lax.ppermute(a, "narrow", [(0, 1), (1, 0)])


def both(a):
    return a.astype(f32) + swap(a).astype(f32)


def local(tokens, cotangent, pages, boxes, gain_attn, gain_ffn, bias_tables, w_query, w_key, w_value, w_out, w_gate, w_up, w_down):
    wide, narrow = lax.axis_size("wide"), lax.axis_size("narrow")
    heads_all = bias_tables.shape[1]
    heads = heads_all // narrow
    rows = tokens.shape[0]
    core = lax.axis_index("narrow")
    tables = lax.dynamic_slice_in_dim(bias_tables, core * heads, heads, 1)
    inner, ff = w_query.shape[1], w_gate.shape[1]
    mine = lambda a: lax.dynamic_slice_in_dim(a, core * rows, rows, 0)

    all_tokens = lax.all_gather(tokens, "narrow", axis=0, tiled=True)
    all_cot = lax.all_gather(cotangent, "narrow", axis=0, tiled=True)
    keys_to = 2 * inner
    bias, ids, (w_first, full_out, full_gate, full_up) = bias_and_gather(
        tables, boxes, pages, [jnp.concatenate([w_query, w_key, w_value], axis=1), w_out.T, w_gate, w_up],
        (((2, 0, ff), (0, 0, keys_to)), ((3, 0, ff), (1, 0, inner), (0, keys_to, inner))), wide, 1)

    x = all_tokens.astype(f32)
    gain_one, gain_two = gain_attn.astype(f32), gain_ffn.astype(f32)
    normed = norm_plain(x, gain_one).astype(bf16)
    qkv = times(normed, w_first).astype(bf16)
    cut = (ff // 128 + 1) // 2 * 128
    attended, lse, (full_down,) = attn_fwd_and_gather(qkv, bias, [w_down.T], (((0, 0, cut),), ((0, cut, ff - cut),)), wide, 2)
    hidden = x + both(times_transposed(attended, full_out).astype(bf16))
    normed_two = norm_plain(hidden, gain_two).astype(bf16)
    gate_pre, up_pre = times(normed_two, full_gate), times(normed_two, full_up)
    hidden_ff = gated_unit(gate_pre, up_pre).astype(bf16)
    down = times_transposed(hidden_ff, full_down).astype(bf16)
    output = (mine(hidden) + lax.psum_scatter(down, "narrow", scatter_dimension=0, tiled=True).astype(f32)).astype(bf16)

    grad_w_down = transposed_times(all_cot, hidden_ff)
    grad_ff = times(all_cot, full_down)
    _, gated_pull = jax.vjp(gated_unit, gate_pre, up_pre)
    grad_gate, grad_up = [g.astype(bf16) for g in gated_pull(grad_ff)]
    grad_w_gate = transposed_times(normed_two, grad_gate)
    grad_w_up = transposed_times(normed_two, grad_up)
    grad_two = both((times_transposed(grad_gate, full_gate) + times_transposed(grad_up, full_up)).astype(bf16))
    _, pull_two = jax.vjp(lambda h: norm_plain(h, gain_two), hidden)
    grad_hidden = all_cot.astype(f32) + pull_two(grad_two)[0]
    own_hidden = mine(hidden)
    grad_gain_two = jnp.sum(mine(grad_two) * own_hidden * lax.rsqrt(jnp.mean(own_hidden * own_hidden, axis=-1, keepdims=True) + epsilon), axis=0)
    grad_low = grad_hidden.astype(bf16)
    grad_w_out = transposed_times(grad_low, attended)
    grad_attended = times(grad_low, full_out).astype(bf16)
    (dq, dk, dv, g), (s_down, s_out) = attn_bwd_and_scatter(
        qkv, bias, attended, grad_attended, lse, [grad_w_down.astype(bf16), grad_w_out.astype(bf16)],
        (((0, 0, keys_to),), ((0, keys_to, ff - keys_to), (1, 0, inner))), wide, 3)
    dqkv = jnp.concatenate([dq, dk, dv], axis=1)
    mid = 3 * inner // 2
    table_part, (s_gate, s_up, s_first) = hist_and_scatter(
        g, ids, [grad_w_gate.astype(bf16), grad_w_up.astype(bf16), transposed_times(normed, dqkv).astype(bf16)],
        (((0, 0, ff), (2, 0, mid)), ((1, 0, ff), (2, mid, mid))), wide, 4)
    grad_normed = lax.psum_scatter(times_transposed(dqkv, w_first).astype(bf16), "narrow", scatter_dimension=0, tiled=True).astype(f32)
    own = tokens.astype(f32)
    _, pull_one = jax.vjp(norm_plain, own, gain_one)
    grad_tokens_norm, grad_gain_one = pull_one(grad_normed)
    grad_tokens = mine(grad_hidden) + grad_tokens_norm
    table_part = lax.dynamic_update_slice(jnp.zeros((bias_tables.shape[0], heads_all), f32), table_part.T, (jnp.int32(0), core * heads))
    sizes = [gain_one.size, gain_two.size, table_part.size]
    small = sum_all(jnp.concatenate([grad_gain_one, grad_gain_two, table_part.reshape(-1)]).reshape(-1, 128), wide, 5).reshape(-1)
    one, two, table = jnp.split(small, [sizes[0], sizes[0] + sizes[1]])
    s_query, s_key, s_value = jnp.split(s_first, 3, axis=1)
    return (output, grad_tokens, one, two, table.reshape(bias_tables.shape), s_query, s_key, s_value, s_out.T, s_gate, s_up, s_down.T)


def solution(mesh):
    rows, cols, tall = P(("wide", "narrow"), None), P("wide", "narrow"), P("narrow", "wide")
    in_specs = (rows, rows, P("wide"), P(None, "wide"), P(), P(), P(), cols, cols, cols, tall, cols, cols, tall)
    out_specs = (rows, rows, P(), P(), P(), cols, cols, cols, tall, cols, cols, tall)
    return jax.shard_map(local, mesh=mesh, in_specs=in_specs, out_specs=out_specs, check_vma=False)
```

```python
import functools

import jax
import jax.numpy as jnp
from jax import lax
from jax.experimental import pallas as pl
from jax.experimental.pallas import tpu as pltpu
from jax.sharding import PartitionSpec as P

f32, bf16 = jnp.float32, jnp.bfloat16
MESH = pl.DeviceIdType.MESH


EDGES = (1, 2, 3, 4, 5, 6, 7, 8, 12, 16, 23, 32, 46, 64, 91)
NT = (((1,), (1,)), ((), ()))
VM = 58 * 2**20
TABLE_SCALE = 2047.0
TABLE_LIFT = 8192


def params(cid):
    return pltpu.CompilerParams(collective_id=cid, has_side_effects=True, vmem_limit_bytes=VM)


def lane_take(table, idx):
    return jnp.take_along_axis(table, idx, axis=1, mode="promise_in_bounds")


def buckets_of(gap, steps, shift):
    return lane_take(steps, jnp.minimum(jnp.abs(gap) >> shift, EDGES[-1])) + jnp.where(gap > 0, 16, 0)


def bias_tile(start, heads, rows, n, steps_ref, tab_ref, box_col, box_row, page_col, page_row, bias_ref, ids_ref, lin, lin_ids):
    steps = jnp.broadcast_to(steps_ref[...], (rows, 128))
    allowed_col = jnp.broadcast_to(page_col[...] % 2, (rows, 128))
    cols = [jnp.broadcast_to(box_col[:, t:t + 1], (rows, 128)) for t in range(2)]
    pairs = heads // 2
    table = lambda t, p: jnp.broadcast_to(tab_ref[t * pairs + p:t * pairs + p + 1, :], (rows, 128))
    unit = 1.0 / TABLE_SCALE

    @pl.when(start == 0)
    def _():
        @pl.loop(0, 8)
        def _(k):
            ids = buckets_of(lax.broadcasted_iota(jnp.int32, (rows, 128), 1) - lax.broadcasted_iota(jnp.int32, (rows, 128), 0) + (k - 4) * rows, steps, 0)
            lin_ids[k] = ids.astype(f32)
            for p in range(pairs):
                lin[k, p] = lane_take(table(0, p), ids)

    @pl.loop(0, n // 128)
    def _(c):
        lanes = pl.ds(pl.multiple_of(c * 128, 128), 128)
        near = jnp.clip((c * 128 - start) // rows + 4, 0, 7)
        ids_ref[0, :, lanes] = lin_ids[near]
        ids = []
        for t in range(2):
            ids.append(buckets_of(jnp.broadcast_to(box_row[t:t + 1, lanes], (rows, 128)) - cols[t], steps, 2))
            ids_ref[t + 1, :, lanes] = ids[t].astype(f32)
        ok = jnp.broadcast_to(page_row[:, lanes], (rows, 128)) == allowed_col
        for p in range(pairs):
            words = lin[near, p] + lane_take(table(1, p), ids[0]) + lane_take(table(2, p), ids[1])
            upper = (words >> 16).astype(f32) * unit
            lower = (words & 0xFFFF).astype(f32) * unit - 3 * TABLE_LIFT * unit
            bias_ref[2 * p, :, lanes] = jnp.where(ok, upper, -1e30)
            bias_ref[2 * p + 1, :, lanes] = jnp.where(ok, lower, -1e30)


def bias_gather_kernel(heads, rows, n, G, halves, count, *refs):
    ins, srcs = refs[:6], refs[6:6 + count]
    bias_ref, ids_ref = refs[6 + count:8 + count]
    outs, lins, sems = refs[8 + count:8 + 2 * count], refs[8 + 2 * count:10 + 2 * count], refs[10 + 2 * count:]
    now = pl.program_id(0)
    comm = Gather(G, halves, srcs, outs, *sems)
    beside(comm, n // rows, now, lambda: bias_tile(now * rows, heads, rows, n, *ins, bias_ref, ids_ref, *lins))


def bias_and_gather(tables, boxes, pages, shards, halves, wide, cid):
    heads, n, G, rows = tables.shape[1], pages.shape[0], wide // 4, 64
    fixed = jnp.round(tables.astype(f32) * TABLE_SCALE).astype(jnp.int32).reshape(3, 32, heads // 2, 2)
    words = fixed[..., 0] * 65536 + fixed[..., 1] + TABLE_LIFT
    tab = jnp.pad(words.transpose(0, 2, 1).reshape(3 * heads // 2, 32), ((0, 0), (0, 96)))
    lane = jnp.arange(128, dtype=jnp.int32)
    steps = sum([(lane >= e).astype(jnp.int32) for e in EDGES])[None]
    count = len(shards)
    outs = pl.pallas_call(functools.partial(bias_gather_kernel, heads, rows, n, G, halves, count),
        grid=(n // rows,),
        out_shape=(jax.ShapeDtypeStruct((heads, n, n), f32), jax.ShapeDtypeStruct((3, n, n), f32)) + gathered_shapes(shards, wide),
        in_specs=[pl.BlockSpec((1, 128), lambda i: (0, 0)), pl.BlockSpec((3 * heads // 2, 128), lambda i: (0, 0)),
                  pl.BlockSpec((rows, 2), lambda i: (i, 0)), pl.BlockSpec((2, n), lambda i: (0, 0)),
                  pl.BlockSpec((rows, 1), lambda i: (i, 0)), pl.BlockSpec((1, n), lambda i: (0, 0))] + [ANY] * count,
        out_specs=(pl.BlockSpec((heads, rows, n), lambda i: (0, i, 0)), pl.BlockSpec((3, rows, n), lambda i: (0, i, 0))) + (ANY,) * count,
        scratch_shapes=[pltpu.VMEM((8, heads // 2, rows, 128), jnp.int32), pltpu.VMEM((8, rows, 128), f32)] + gather_scratch(G, halves, count),
        compiler_params=params(cid), name="layout_bias_gather")(
            steps, tab, boxes.T, boxes, pages[:, None], pages[None], *shards)
    return outs[0], outs[1], [flat(a) for a in outs[2:]]


def half_of(v, e):
    lane = lax.broadcasted_iota(jnp.int32, v.shape, 1)
    return jnp.where((lane >= 64) == (e == 1), v, jnp.zeros_like(v))


def join(a, b):
    lane = lax.broadcasted_iota(jnp.int32, a.shape, 1)
    return jnp.where(lane < 64, a, b)


def fwd_tile(q_ref, k_ref, v_ref, bias_ref, o_ref, lse_ref):
    q, k, v = q_ref[...], k_ref[...], v_ref[...]
    outs, lses = [], []
    for e in range(2):
        s = lax.dot_general(half_of(q, e), k, NT, preferred_element_type=f32) + bias_ref[e]
        peak = jnp.max(s, axis=1, keepdims=True)
        p = jnp.exp(s - peak)
        total = jnp.sum(p, axis=1, keepdims=True)
        outs.append(jnp.dot(p.astype(bf16), v, preferred_element_type=f32) / total)
        lses.append(peak + jnp.log(total))
    o_ref[...] = join(*outs).astype(bf16)
    lse_ref[0] = jnp.concatenate(lses, axis=1)


def fwd_kernel(steps, tiles, G, halves, count, *refs):
    ins, srcs = refs[:4], refs[4:4 + count]
    mid = refs[4 + count:6 + count]
    outs, sems = refs[6 + count:6 + 2 * count], refs[6 + 2 * count:]
    now = pl.program_id(0) * tiles + pl.program_id(1)
    beside(Gather(G, halves, srcs, outs, *sems), steps, now, lambda: fwd_tile(*ins, *mid))


def attn_fwd_and_gather(qkv, bias, shards, halves, wide, cid, tq=256):
    n, width = qkv.shape[0], qkv.shape[1] // 3
    pairs, tiles, count, G = width // 128, n // tq, len(shards), wide // 4
    outs = pl.pallas_call(functools.partial(fwd_kernel, pairs * tiles, tiles, G, halves, count), grid=(pairs, tiles),
        out_shape=(jax.ShapeDtypeStruct((n, width), bf16), jax.ShapeDtypeStruct((pairs, n, 2), f32)) + gathered_shapes(shards, wide),
        in_specs=[pl.BlockSpec((tq, 128), lambda p, i: (i, p)), pl.BlockSpec((n, 128), lambda p, i: (0, p + pairs)),
                  pl.BlockSpec((n, 128), lambda p, i: (0, p + 2 * pairs)), pl.BlockSpec((2, tq, n), lambda p, i: (p, i, 0))] + [ANY] * count,
        out_specs=(pl.BlockSpec((tq, 128), lambda p, i: (i, p)), pl.BlockSpec((1, tq, 2), lambda p, i: (p, i, 0))) + (ANY,) * count,
        scratch_shapes=gather_scratch(G, halves, count), compiler_params=params(cid), name="attention_gather")(qkv, qkv, qkv, bias, *shards)
    return outs[0], outs[1], [flat(a) for a in outs[2:]]


def bwd_tile(first, last, q_ref, k_ref, v_ref, bias_ref, o_ref, do_ref, lse_ref, dq_ref, dk_ref, dv_ref, g_ref, dkt, dvt):
    @pl.when(first)
    def _():
        dkt[...] = jnp.zeros_like(dkt)
        dvt[...] = jnp.zeros_like(dvt)

    q, k, v, do = q_ref[...], k_ref[...], v_ref[...], do_ref[...]
    prod = do.astype(f32) * o_ref[...].astype(f32)
    dqs = []
    for e in range(2):
        qm, dom = half_of(q, e), half_of(do, e)
        s = lax.dot_general(qm, k, NT, preferred_element_type=f32) + bias_ref[e]
        p = jnp.exp(s - lse_ref[0, :, e:e + 1])
        dp = lax.dot_general(dom, v, NT, preferred_element_type=f32)
        inner = jnp.sum(half_of(prod, e), axis=1, keepdims=True)
        g = (p * (dp - inner)).astype(bf16)
        g_ref[e] = g
        dqs.append(jnp.dot(g, k, preferred_element_type=f32))
        dvt[...] += jnp.dot(dom.T, p.astype(bf16), preferred_element_type=f32)
        dkt[...] += jnp.dot(qm.T, g, preferred_element_type=f32)
    dq_ref[...] = join(*dqs).astype(bf16)

    @pl.when(last)
    def _():
        dk_ref[...] = dkt[...].T.astype(bf16)
        dv_ref[...] = dvt[...].T.astype(bf16)


def bwd_kernel(steps, tiles, G, halves, count, *refs):
    ins, parts = refs[:7], refs[7:7 + count]
    mid = refs[7 + count:11 + count]
    outs, accs, sems = refs[11 + count:11 + 2 * count], refs[11 + 2 * count:13 + 2 * count], refs[13 + 2 * count:]
    i = pl.program_id(1)
    comm = Scatter(G, halves, parts, outs, *sems)
    beside(comm, steps, pl.program_id(0) * tiles + i, lambda: bwd_tile(i == 0, i == tiles - 1, *ins, *mid, *accs))


def shard_shapes(parts, wide):
    return tuple(jax.ShapeDtypeStruct((p.shape[0] // wide, p.shape[1]), f32) for p in parts)


def attn_bwd_and_scatter(qkv, bias, o, do, lse, parts, halves, wide, cid, tq=256):
    n, width = qkv.shape[0], qkv.shape[1] // 3
    pairs, tiles, count, G = width // 128, n // tq, len(parts), wide // 4
    tile = pl.BlockSpec((tq, 128), lambda p, i: (i, p))
    full = pl.BlockSpec((n, 128), lambda p, i: (0, p))
    outs = pl.pallas_call(functools.partial(bwd_kernel, pairs * tiles, tiles, G, halves, count), grid=(pairs, tiles),
        out_shape=(jax.ShapeDtypeStruct((n, width), bf16),) * 3 + (jax.ShapeDtypeStruct((2 * pairs, n, n), bf16),) + shard_shapes(parts, wide),
        in_specs=[tile, pl.BlockSpec((n, 128), lambda p, i: (0, p + pairs)), pl.BlockSpec((n, 128), lambda p, i: (0, p + 2 * pairs)),
                  pl.BlockSpec((2, tq, n), lambda p, i: (p, i, 0)), tile, tile, pl.BlockSpec((1, tq, 2), lambda p, i: (p, i, 0))] + [ANY] * count,
        out_specs=(tile, full, full, pl.BlockSpec((2, tq, n), lambda p, i: (p, i, 0))) + (whole_vmem(),) * count,
        scratch_shapes=[pltpu.VMEM((128, n), f32), pltpu.VMEM((128, n), f32)] + scatter_scratch(G, halves, parts[0].shape[0] // wide),
        compiler_params=params(cid), name="attention_back_scatter")(qkv, qkv, qkv, bias, o, do, lse, *[spread(p, wide) for p in parts])
    return outs[:4], outs[4:]


def hist_tile(first, heads, rows, n, g_ref, ids_ref, out_ref, gs):
    @pl.when(first)
    def _():
        out_ref[...] = jnp.zeros_like(out_ref)

    for h in range(heads):
        for c in range(n // 128):
            gs[c, h * rows:(h + 1) * rows, :] = g_ref[h, :, c * 128:(c + 1) * 128].astype(f32)
    label = lax.broadcasted_iota(jnp.int32, (32, n), 0).astype(bf16)
    one, zero = jnp.ones((32, n), bf16), jnp.zeros((32, n), bf16)
    acc = jnp.zeros((heads, 96), f32)
    for r in range(rows):
        grow = jnp.concatenate([gs[c, pl.ds(r, heads, stride=rows), :] for c in range(n // 128)], axis=1).astype(bf16)
        hots = []
        for t in range(3):
            row = jnp.broadcast_to(ids_ref[t, r:r + 1, :], (32, n)).astype(bf16)
            hots.append(jnp.where(row == label, one, zero))
        acc = acc + lax.dot_general(grow, jnp.concatenate(hots, axis=0), NT, preferred_element_type=f32)
    out_ref[...] += acc


def hist_kernel(heads, rows, n, G, halves, count, *refs):
    ins, parts, out_ref = refs[:2], refs[2:2 + count], refs[2 + count]
    outs, gs, sems = refs[3 + count:3 + 2 * count], refs[3 + 2 * count], refs[4 + 2 * count:]
    now = pl.program_id(0)
    comm = Scatter(G, halves, parts, outs, *sems)
    beside(comm, n // rows, now, lambda: hist_tile(now == 0, heads, rows, n, *ins, out_ref, gs))


def hist_and_scatter(g, ids, parts, halves, wide, cid):
    heads, n, _ = g.shape
    rows, count, G = 16, len(parts), wide // 4
    outs = pl.pallas_call(functools.partial(hist_kernel, heads, rows, n, G, halves, count), grid=(n // rows,),
        out_shape=(jax.ShapeDtypeStruct((heads, 96), f32),) + shard_shapes(parts, wide),
        in_specs=[pl.BlockSpec((heads, rows, n), lambda i: (0, i, 0)), pl.BlockSpec((3, rows, n), lambda i: (0, i, 0))] + [ANY] * count,
        out_specs=(pl.BlockSpec((heads, 96), lambda i: (0, 0)),) + (whole_vmem(),) * count,
        scratch_shapes=[pltpu.VMEM((n // 128, heads * rows, 128), f32)] + scatter_scratch(G, halves, parts[0].shape[0] // wide),
        compiler_params=params(cid), name="table_grad_scatter")(g, ids, *[spread(p, wide) for p in parts])
    return outs[0], outs[1:]


D = pltpu.SemaphoreType.DMA


def place():
    me = lax.axis_index("wide")
    return me // 4, (me // 2) % 2, me % 2


def wide_id(z, y, x):
    return {"wide": z * 4 + y * 2 + x}


def remote(src, dst, send, recv, target):
    return pltpu.make_async_remote_copy(src_ref=src, dst_ref=dst, send_sem=send, recv_sem=recv, device_id=target, device_id_type=MESH)


def greet(G, far):
    z, y, x = place()
    bar = pltpu.get_barrier_semaphore()
    sig = lambda t: pl.semaphore_signal(bar, inc=1, device_id=t, device_id_type=MESH)
    sig(wide_id(z, 1 - y, x))
    sig(wide_id(z, y, 1 - x))
    if far:
        for k in range(1, G):
            sig(wide_id((z + k) % G, y, x))
        pl.semaphore_wait(bar, 2 + G - 1)
    else:
        @pl.when(z > 0)
        def _():
            sig(wide_id(z - 1, y, x))

        @pl.when(z < G - 1)
        def _():
            sig(wide_id(z + 1, y, x))

        pl.semaphore_wait(bar, 2 + (z > 0).astype(jnp.int32) + (z < G - 1).astype(jnp.int32))


class Gather:
    def __init__(self, G, halves, srcs, outs, local_sem, zs, zr, ns, nr):
        self.G, self.halves, self.srcs, self.outs, self.local_sem = G, halves, srcs, outs, local_sem
        self.zs, self.zr, self.ns, self.nr = zs, zr, ns, nr
        self.most = max(len(h) for h in halves)
        self.z, self.y, self.x = place()

    def hop(self, own, zz, yy, xx, h, way, j):
        target = wide_id(self.z, 1 - self.y, self.x) if way == "y" else wide_id(self.z, self.y, 1 - self.x)
        copies = []
        for n, (a, c, w) in enumerate(self.halves[h]):
            slot = (zz * 6 + j) * self.most + n
            dst = self.outs[a].at[zz, yy, xx, :, pl.ds(c, w)]
            copies.append(remote(self.srcs[a].at[:, pl.ds(c, w)] if own else dst, dst, self.ns.at[slot], self.nr.at[slot], target))
        return copies

    def second_stage(self, zz, own=False):
        return self.hop(own, zz, self.y, self.x, 0, "y", 0) + self.hop(own, zz, self.y, self.x, 1, "x", 1)

    def third_stage(self, zz, own=False):
        return self.hop(own, zz, self.y, self.x, 0, "x", 2) + self.hop(own, zz, self.y, self.x, 1, "y", 3)

    def last_stage(self, zz):
        return self.hop(False, zz, 1 - self.y, self.x, 0, "x", 4) + self.hop(False, zz, self.y, 1 - self.x, 1, "y", 5)

    def relay(self, own, zz, step, way):
        copies = []
        for a in range(len(self.srcs)):
            slot = (way * (self.G - 1) + step) * len(self.srcs) + a
            dst = self.outs[a].at[zz, self.y, self.x]
            copies.append(remote(self.srcs[a] if own else dst, dst, self.zs.at[slot], self.zr.at[slot],
                                 wide_id(self.z + (1 if way == 0 else -1), self.y, self.x)))
        return copies

    def can(self, way):
        return self.z < self.G - 1 if way == 0 else self.z > 0

    def source(self, d, way):
        return (self.z - d, self.z - d >= 0) if way == 0 else (self.z + d, self.z + d < self.G)

    def keep(self):
        return [pltpu.make_async_copy(s, o.at[self.z, self.y, self.x], self.local_sem.at[a]) for a, (s, o) in enumerate(zip(self.srcs, self.outs))]

    def begin(self):
        for way in range(2):
            @pl.when(self.can(way))
            def _():
                for c in self.relay(True, self.z, 0, way):
                    c.start()
        for c in self.second_stage(self.z, True) + self.third_stage(self.z, True) + self.keep():
            c.start()

    def turn(self, zz):
        for c in self.hop(False, zz, 1 - self.y, self.x, 0, "y", 0) + self.hop(False, zz, self.y, 1 - self.x, 1, "x", 1):
            c.wait_recv()
        for c in self.last_stage(zz):
            c.start()

    def step(self, d):
        for way in range(2):
            zz, there = self.source(d, way)

            @pl.when(there)
            def _():
                for c in self.relay(False, zz, d - 1, way):
                    c.wait_recv()

                @pl.when(self.can(way))
                def _():
                    for c in self.relay(False, zz, d, way):
                        c.start()

                for c in self.second_stage(zz):
                    c.start()
        for way in range(2):
            zz, there = self.source(d, way)

            @pl.when(there)
            def _():
                for c in self.third_stage(zz):
                    c.start()

    def turns(self, d):
        if d == 0:
            self.turn(self.z)
            return
        for way in range(2):
            zz, there = self.source(d, way)

            @pl.when(there)
            def _():
                self.turn(zz)

    def finish(self):
        y, x = self.y, self.x

        @pl.loop(0, self.G)
        def _(zz):
            for c in (self.hop(False, zz, y, 1 - x, 0, "x", 2) + self.hop(False, zz, 1 - y, x, 1, "y", 3)
                      + self.hop(False, zz, 1 - y, 1 - x, 0, "x", 4) + self.hop(False, zz, 1 - y, 1 - x, 1, "y", 5)):
                c.wait_recv()
            for c in self.second_stage(zz) + self.third_stage(zz) + self.last_stage(zz):
                c.wait_send()

        for way in range(2):
            @pl.when(self.can(way))
            def _():
                for c in self.relay(True, self.z, 0, way):
                    c.wait_send()
                for d in range(1, self.G - 1):
                    zz, there = self.source(d, way)

                    @pl.when(there)
                    def _():
                        for c in self.relay(False, zz, d, way):
                            c.wait_send()
        for c in self.keep():
            c.wait()

    def events(self):
        G = self.G
        first = lambda: (greet(G, False), self.begin())
        ev = [(0.0, first), (0.7, lambda: self.turns(0))]
        for d in range(1, G):
            ev += [(1.15 * d, functools.partial(self.step, d)), (1.3 * d + 1.2, functools.partial(self.turns, d))]
        return sorted(ev, key=lambda e: e[0]), self.finish


def gather_scratch(G, halves, arrays):
    most = max(len(h) for h in halves)
    return [D((arrays,)), D((2 * (G - 1) * arrays,)), D((2 * (G - 1) * arrays,)), D((6 * G * most,)), D((6 * G * most,))]


class Scatter:
    def __init__(self, G, halves, parts, outs, r1a, r1b, o1a, o1b, r2a, r2b, r3, own, lsem, s1, v1, s2, v2, s3, v3):
        self.__dict__.update(locals())
        self.most = max(len(h) for h in halves)
        self.wa, self.wb = [sum(p[2] for p in h) for h in halves]
        self.R = parts[0].shape[3]
        self.z, self.y, self.x = place()
        self.order = sorted(range(1, G), key=lambda k: min(k, G - k), reverse=True) + [0]

    def zk(self, k):
        return (self.z + k) % self.G

    def neighbour(self, way):
        return wide_id(self.z, 1 - self.y, self.x) if way == "y" else wide_id(self.z, self.y, 1 - self.x)

    def pieces(self, h):
        at, out = 0, []
        for n, (a, c, w) in enumerate(self.halves[h]):
            out.append((n, a, pl.ds(c, w), pl.ds(at, w)))
            at += w
        return out

    def one(self, k):
        z, cs = self.zk(k), []
        for n, a, src, dst in self.pieces(0):
            slot = (2 * k) * self.most + n
            cs.append(remote(self.parts[a].at[z, :, 1 - self.x, :, src], self.r1a.at[k, :, :, dst], self.s1.at[slot], self.v1.at[slot], self.neighbour("x")))
        for n, a, src, dst in self.pieces(1):
            slot = (2 * k + 1) * self.most + n
            cs.append(remote(self.parts[a].at[z, 1 - self.y, :, :, src], self.r1b.at[k, :, :, dst], self.s1.at[slot], self.v1.at[slot], self.neighbour("y")))
        return cs

    def load(self, k):
        z, cs = self.zk(k), []
        for n, a, src, dst in self.pieces(0):
            cs.append(pltpu.make_async_copy(self.parts[a].at[z, :, self.x, :, src], self.o1a.at[k, :, :, dst], self.lsem.at[(2 * k) * self.most + n]))
        for n, a, src, dst in self.pieces(1):
            cs.append(pltpu.make_async_copy(self.parts[a].at[z, self.y, :, :, src], self.o1b.at[k, :, :, dst], self.lsem.at[(2 * k + 1) * self.most + n]))
        return cs

    def two(self, k):
        return [remote(self.o1a.at[k, 1 - self.y], self.r2a.at[k], self.s2.at[2 * k], self.v2.at[2 * k], self.neighbour("y")),
                remote(self.o1b.at[k, 1 - self.x], self.r2b.at[k], self.s2.at[2 * k + 1], self.v2.at[2 * k + 1], self.neighbour("x"))]

    def three(self, k):
        return remote(self.own.at[k], self.r3.at[k - 1], self.s3.at[k - 1], self.v3.at[k - 1], wide_id(self.zk(k), self.y, self.x))

    def launch(self, k):
        for c in self.one(k) + self.load(k):
            c.start()

    def begin(self):
        for k in self.order[:2]:
            self.launch(k)

    def rows(self, count, body):
        step = min(16, count)

        @pl.loop(0, count // step)
        def _(i):
            body(pl.ds(pl.multiple_of(i * step, step), step))

    def add_one(self, n):
        k = self.order[n]
        for c in self.one(k):
            c.wait_recv()
        for c in self.load(k):
            c.wait()
        for mine, got in ((self.o1a, self.r1a), (self.o1b, self.r1b)):
            def body(r):
                for j in range(2):
                    mine[k, j, r, :] = (mine[k, j, r, :].astype(f32) + got[k, j, r, :].astype(f32)).astype(bf16)

            self.rows(self.R, body)
        for c in self.two(k):
            c.start()
        if n + 2 < self.G:
            self.launch(self.order[n + 2])

    def add_two(self, n):
        k = self.order[n]
        for c in self.two(k):
            c.wait_recv()

        def body(r):
            self.own[k, r, pl.ds(0, self.wa)] = (self.o1a[k, self.y, r, :].astype(f32) + self.r2a[k, r, :].astype(f32)).astype(bf16)
            self.own[k, r, pl.ds(self.wa, self.wb)] = (self.o1b[k, self.x, r, :].astype(f32) + self.r2b[k, r, :].astype(f32)).astype(bf16)

        self.rows(self.R, body)
        if k:
            self.three(k).start()

    def finish(self):
        self.add_two(self.G - 1)
        for k in range(1, self.G):
            self.three(k).wait_recv()

        def body(r):
            for h in range(2):
                for _, a, src, dst in self.pieces(h):
                    cols = pl.ds(dst.start + h * self.wa, dst.size)
                    total = self.own[0, r, cols].astype(f32)
                    for k in range(self.G - 1):
                        total = total + self.r3[k, r, cols].astype(f32)
                    self.outs[a][r, src] = total

        self.rows(self.R, body)
        for k in range(self.G):
            for c in self.one(k) + self.two(k):
                c.wait_send()
            if k:
                self.three(k).wait_send()

    def events(self):
        G = self.G
        first = lambda: (greet(G, True), self.begin())
        ev = [(0.0, first), (1.1, lambda: self.add_one(0))]
        for n in range(1, G):
            ev += [(1.5 * n + 0.65, functools.partial(self.add_one, n)), (1.5 * n + 1.1, functools.partial(self.add_two, n - 1))]
        return sorted(ev, key=lambda e: e[0]), self.finish


def scatter_scratch(G, halves, R):
    most = max(len(h) for h in halves)
    a, b = [sum(p[2] for p in h) for h in halves]
    V = lambda *s: pltpu.VMEM(s, bf16)
    return [V(G, 2, R, a), V(G, 2, R, b), V(G, 2, R, a), V(G, 2, R, b), V(G, R, a), V(G, R, b), V(G - 1, R, a + b), V(G, R, a + b),
            D((2 * G * most,)), D((2 * G * most,)), D((2 * G * most,)), D((2 * G,)), D((2 * G,)), D((G - 1,)), D((G - 1,))]


def beside(comm, steps, now, compute):
    events, finish = comm.events()
    units = 1.55 * comm.G
    for n in range(steps):
        here = [act for t, act in events if min(steps - 1, int(-(-t * steps // units))) == n]
        if here:
            @pl.when(now == n)
            def _():
                for act in here:
                    act()
    compute()

    @pl.when(now == steps - 1)
    def _():
        finish()


ANY = pl.BlockSpec(memory_space=pl.ANY)


def whole_vmem():
    return pl.BlockSpec(memory_space=pltpu.VMEM)


def spread(a, wide):
    return a.reshape(wide // 4, 2, 2, a.shape[0] // wide, a.shape[1])


def gathered_shapes(shards, wide):
    return tuple(jax.ShapeDtypeStruct((wide // 4, 2, 2) + s.shape, s.dtype) for s in shards)


def flat(a):
    return a.reshape(-1, a.shape[-1])


def sum_kernel(G, src, out, acc, got, gz, s, v, sz, vz):
    z, y, x = place()
    core = {"narrow": 1 - lax.axis_index("narrow")}
    ynb, xnb = wide_id(z, 1 - y, x), wide_id(z, y, 1 - x)
    far = [wide_id((z + k) % G, y, x) for k in range(1, G)]
    bar = pltpu.get_barrier_semaphore()
    for t in [core, ynb, xnb] + far:
        pl.semaphore_signal(bar, inc=1, device_id=t, device_id_type=MESH)
    pl.semaphore_wait(bar, 3 + len(far))
    acc[0] = src[...]
    for n, t in enumerate((core, xnb, ynb)):
        c = remote(acc.at[n], got.at[n], s.at[n], v.at[n], t)
        c.start()
        c.wait()
        acc[n + 1] = acc[n] + got[n]
    gz[z] = acc[3]
    sent = [remote(acc.at[3], gz.at[z], sz.at[k], vz.at[z], t) for k, t in enumerate(far)]
    for c in sent:
        c.start()
    for k in range(1, G):
        zz = (z + k) % G
        remote(acc.at[3], gz.at[zz], sz.at[k - 1], vz.at[zz], far[k - 1]).wait_recv()
    for c in sent:
        c.wait_send()
    total = gz[0]
    for k in range(1, G):
        total = total + gz[k]
    out[...] = total


def sum_all(part, wide, cid):
    G, rows = wide // 4, part.shape[0]
    V = lambda k: pltpu.VMEM((k, rows, 128), f32)
    return pl.pallas_call(functools.partial(sum_kernel, G), out_shape=jax.ShapeDtypeStruct(part.shape, f32),
        in_specs=[whole_vmem()], out_specs=whole_vmem(),
        scratch_shapes=[V(4), V(3), V(G), D((3,)), D((3,)), D((G - 1,)), D((G,))],
        compiler_params=pltpu.CompilerParams(collective_id=cid, has_side_effects=True), name="small_sums")(part)


epsilon = 1e-06


def norm_plain(values, gain_row):
    factor = lax.rsqrt(jnp.mean(values * values, axis=-1, keepdims=True) + epsilon)
    return values * factor * gain_row


def gated_unit(gate_pre, up_pre):
    return jax.nn.gelu(gate_pre, approximate=True) * up_pre


def times(a, b):
    return jnp.dot(a, b, preferred_element_type=f32)


def times_transposed(a, b):
    return lax.dot_general(a, b, NT, preferred_element_type=f32)


def transposed_times(a, b):
    return lax.dot_general(a, b, (((0,), (0,)), ((), ())), preferred_element_type=f32)


def swap(a):
    return lax.ppermute(a, "narrow", [(0, 1), (1, 0)])


def both(a):
    return a.astype(f32) + swap(a).astype(f32)


def local(tokens, cotangent, pages, boxes, gain_attn, gain_ffn, bias_tables, w_query, w_key, w_value, w_out, w_gate, w_up, w_down):
    wide, narrow = lax.axis_size("wide"), lax.axis_size("narrow")
    heads_all = bias_tables.shape[1]
    heads = heads_all // narrow
    rows = tokens.shape[0]
    core = lax.axis_index("narrow")
    tables = lax.dynamic_slice_in_dim(bias_tables, core * heads, heads, 1)
    inner, ff = w_query.shape[1], w_gate.shape[1]
    mine = lambda a: lax.dynamic_slice_in_dim(a, core * rows, rows, 0)

    all_tokens = lax.all_gather(tokens, "narrow", axis=0, tiled=True)
    all_cot = lax.all_gather(cotangent, "narrow", axis=0, tiled=True)
    early = inner // 4 * 3
    bias, ids, (w_first, full_out, full_gate) = bias_and_gather(
        tables, boxes, pages, [jnp.concatenate([w_query, w_key, w_value], axis=1), w_out.T, w_gate],
        (((2, 0, ff), (0, 0, early)), ((1, 0, inner), (0, early, 3 * inner - early))), wide, 1)

    x = all_tokens.astype(f32)
    gain_one, gain_two = gain_attn.astype(f32), gain_ffn.astype(f32)
    normed = norm_plain(x, gain_one).astype(bf16)
    qkv = times(normed, w_first).astype(bf16)
    attended, lse, (full_up, full_down) = attn_fwd_and_gather(qkv, bias, [w_up, w_down.T], (((0, 0, ff),), ((1, 0, ff),)), wide, 2)
    hidden = x + both(times_transposed(attended, full_out).astype(bf16))
    normed_two = norm_plain(hidden, gain_two).astype(bf16)
    gate_pre, up_pre = times(normed_two, full_gate), times(normed_two, full_up)
    hidden_ff = gated_unit(gate_pre, up_pre).astype(bf16)
    down = times_transposed(hidden_ff, full_down).astype(bf16)
    output = (mine(hidden) + lax.psum_scatter(down, "narrow", scatter_dimension=0, tiled=True).astype(f32)).astype(bf16)

    grad_w_down = transposed_times(all_cot, hidden_ff)
    grad_ff = times(all_cot, full_down)
    _, gated_pull = jax.vjp(gated_unit, gate_pre, up_pre)
    grad_gate, grad_up = [g.astype(bf16) for g in gated_pull(grad_ff)]
    grad_w_gate = transposed_times(normed_two, grad_gate)
    grad_w_up = transposed_times(normed_two, grad_up)
    grad_two = both((times_transposed(grad_gate, full_gate) + times_transposed(grad_up, full_up)).astype(bf16))
    _, pull_two = jax.vjp(lambda h: norm_plain(h, gain_two), hidden)
    grad_hidden = all_cot.astype(f32) + pull_two(grad_two)[0]
    own_hidden = mine(hidden)
    grad_gain_two = jnp.sum(mine(grad_two) * own_hidden * lax.rsqrt(jnp.mean(own_hidden * own_hidden, axis=-1, keepdims=True) + epsilon), axis=0)
    grad_low = grad_hidden.astype(bf16)
    grad_w_out = transposed_times(grad_low, attended)
    grad_attended = times(grad_low, full_out).astype(bf16)
    (dq, dk, dv, g), (s_down, s_out) = attn_bwd_and_scatter(
        qkv, bias, attended, grad_attended, lse, [grad_w_down.astype(bf16), grad_w_out.astype(bf16)],
        (((0, 0, 2 * inner),), ((0, 2 * inner, ff - 2 * inner), (1, 0, inner))), wide, 3)
    dqkv = jnp.concatenate([dq, dk, dv], axis=1)
    mid = 3 * inner // 2
    table_part, (s_gate, s_up, s_first) = hist_and_scatter(
        g, ids, [grad_w_gate.astype(bf16), grad_w_up.astype(bf16), transposed_times(normed, dqkv).astype(bf16)],
        (((0, 0, ff), (2, 0, mid)), ((1, 0, ff), (2, mid, mid))), wide, 4)
    grad_normed = lax.psum_scatter(times_transposed(dqkv, w_first).astype(bf16), "narrow", scatter_dimension=0, tiled=True).astype(f32)
    own = tokens.astype(f32)
    _, pull_one = jax.vjp(norm_plain, own, gain_one)
    grad_tokens_norm, grad_gain_one = pull_one(grad_normed)
    grad_tokens = mine(grad_hidden) + grad_tokens_norm
    table_part = lax.dynamic_update_slice(jnp.zeros((bias_tables.shape[0], heads_all), f32), table_part.T, (jnp.int32(0), core * heads))
    sizes = [gain_one.size, gain_two.size, table_part.size]
    small = sum_all(jnp.concatenate([grad_gain_one, grad_gain_two, table_part.reshape(-1)]).reshape(-1, 128), wide, 5).reshape(-1)
    one, two, table = jnp.split(small, [sizes[0], sizes[0] + sizes[1]])
    s_query, s_key, s_value = jnp.split(s_first, 3, axis=1)
    return (output, grad_tokens, one, two, table.reshape(bias_tables.shape), s_query, s_key, s_value, s_out.T, s_gate, s_up, s_down.T)


def solution(mesh):
    rows, cols, tall = P(("wide", "narrow"), None), P("wide", "narrow"), P("narrow", "wide")
    in_specs = (rows, rows, P("wide"), P(None, "wide"), P(), P(), P(), cols, cols, cols, tall, cols, cols, tall)
    out_specs = (rows, rows, P(), P(), P(), cols, cols, cols, tall, cols, cols, tall)
    return jax.shard_map(local, mesh=mesh, in_specs=in_specs, out_specs=out_specs, check_vma=False)
```

```python
import functools

import jax
import jax.numpy as jnp
from jax import lax
from jax.experimental import pallas as pl
from jax.experimental.pallas import tpu as pltpu
from jax.sharding import PartitionSpec as P

f32, bf16 = jnp.float32, jnp.bfloat16
MESH = pl.DeviceIdType.MESH


EDGES = (1, 2, 3, 4, 5, 6, 7, 8, 12, 16, 23, 32, 46, 64, 91)
NT = (((1,), (1,)), ((), ()))
VM = 58 * 2**20
TABLE_SCALE = 2047.0
TABLE_LIFT = 8192


def params(cid):
    return pltpu.CompilerParams(collective_id=cid, has_side_effects=True, vmem_limit_bytes=VM)


def lane_take(table, idx):
    return jnp.take_along_axis(table, idx, axis=1, mode="promise_in_bounds")


def buckets_of(gap, steps, shift):
    return lane_take(steps, jnp.minimum(jnp.abs(gap) >> shift, EDGES[-1])) + jnp.where(gap > 0, 16, 0)


def bias_tile(start, heads, rows, n, steps_ref, tab_ref, box_col, box_row, page_col, page_row, bias_ref, ids_ref, lin, lin_ids):
    steps = jnp.broadcast_to(steps_ref[...], (rows, 128))
    allowed_col = jnp.broadcast_to(page_col[...] % 2, (rows, 128))
    cols = [jnp.broadcast_to(box_col[:, t:t + 1], (rows, 128)) for t in range(2)]
    pairs = heads // 2
    table = lambda t, p: jnp.broadcast_to(tab_ref[t * pairs + p:t * pairs + p + 1, :], (rows, 128))
    unit = 1.0 / TABLE_SCALE

    @pl.when(start == 0)
    def _():
        @pl.loop(0, 8)
        def _(k):
            ids = buckets_of(lax.broadcasted_iota(jnp.int32, (rows, 128), 1) - lax.broadcasted_iota(jnp.int32, (rows, 128), 0) + (k - 4) * rows, steps, 0)
            lin_ids[k] = ids.astype(f32)
            for p in range(pairs):
                lin[k, p] = lane_take(table(0, p), ids)

    @pl.loop(0, n // 128)
    def _(c):
        lanes = pl.ds(pl.multiple_of(c * 128, 128), 128)
        near = jnp.clip((c * 128 - start) // rows + 4, 0, 7)
        ids_ref[0, :, lanes] = lin_ids[near]
        ids = []
        for t in range(2):
            ids.append(buckets_of(jnp.broadcast_to(box_row[t:t + 1, lanes], (rows, 128)) - cols[t], steps, 2))
            ids_ref[t + 1, :, lanes] = ids[t].astype(f32)
        ok = jnp.broadcast_to(page_row[:, lanes], (rows, 128)) == allowed_col
        for p in range(pairs):
            words = lin[near, p] + lane_take(table(1, p), ids[0]) + lane_take(table(2, p), ids[1])
            upper = (words >> 16).astype(f32) * unit
            lower = (words & 0xFFFF).astype(f32) * unit - 3 * TABLE_LIFT * unit
            bias_ref[2 * p, :, lanes] = jnp.where(ok, upper, -1e30)
            bias_ref[2 * p + 1, :, lanes] = jnp.where(ok, lower, -1e30)


def bias_gather_kernel(heads, rows, n, G, halves, count, *refs):
    ins, srcs = refs[:6], refs[6:6 + count]
    bias_ref, ids_ref = refs[6 + count:8 + count]
    outs, lins, sems = refs[8 + count:8 + 2 * count], refs[8 + 2 * count:10 + 2 * count], refs[10 + 2 * count:]
    now = pl.program_id(0)
    comm = Gather(G, halves, srcs, outs, *sems)
    beside(comm, n // rows, now, lambda: bias_tile(now * rows, heads, rows, n, *ins, bias_ref, ids_ref, *lins))


def bias_and_gather(tables, boxes, pages, shards, halves, wide, cid):
    heads, n, G, rows = tables.shape[1], pages.shape[0], wide // 4, 64
    fixed = jnp.round(tables.astype(f32) * TABLE_SCALE).astype(jnp.int32).reshape(3, 32, heads // 2, 2)
    words = fixed[..., 0] * 65536 + fixed[..., 1] + TABLE_LIFT
    tab = jnp.pad(words.transpose(0, 2, 1).reshape(3 * heads // 2, 32), ((0, 0), (0, 96)))
    lane = jnp.arange(128, dtype=jnp.int32)
    steps = sum([(lane >= e).astype(jnp.int32) for e in EDGES])[None]
    count = len(shards)
    outs = pl.pallas_call(functools.partial(bias_gather_kernel, heads, rows, n, G, halves, count),
        grid=(n // rows,),
        out_shape=(jax.ShapeDtypeStruct((heads, n, n), f32), jax.ShapeDtypeStruct((3, n, n), f32)) + gathered_shapes(shards, wide),
        in_specs=[pl.BlockSpec((1, 128), lambda i: (0, 0)), pl.BlockSpec((3 * heads // 2, 128), lambda i: (0, 0)),
                  pl.BlockSpec((rows, 2), lambda i: (i, 0)), pl.BlockSpec((2, n), lambda i: (0, 0)),
                  pl.BlockSpec((rows, 1), lambda i: (i, 0)), pl.BlockSpec((1, n), lambda i: (0, 0))] + [ANY] * count,
        out_specs=(pl.BlockSpec((heads, rows, n), lambda i: (0, i, 0)), pl.BlockSpec((3, rows, n), lambda i: (0, i, 0))) + (ANY,) * count,
        scratch_shapes=[pltpu.VMEM((8, heads // 2, rows, 128), jnp.int32), pltpu.VMEM((8, rows, 128), f32)] + gather_scratch(G, halves, count),
        compiler_params=params(cid), name="layout_bias_gather")(
            steps, tab, boxes.T, boxes, pages[:, None], pages[None], *shards)
    return outs[0], outs[1], [flat(a) for a in outs[2:]]


def half_of(v, e):
    lane = lax.broadcasted_iota(jnp.int32, v.shape, 1)
    return jnp.where((lane >= 64) == (e == 1), v, jnp.zeros_like(v))


def join(a, b):
    lane = lax.broadcasted_iota(jnp.int32, a.shape, 1)
    return jnp.where(lane < 64, a, b)


def fwd_tile(q_ref, k_ref, v_ref, bias_ref, o_ref, lse_ref):
    q, k, v = q_ref[...], k_ref[...], v_ref[...]
    outs, lses = [], []
    for e in range(2):
        s = lax.dot_general(half_of(q, e), k, NT, preferred_element_type=f32) + bias_ref[e]
        peak = jnp.max(s, axis=1, keepdims=True)
        p = jnp.exp(s - peak)
        total = jnp.sum(p, axis=1, keepdims=True)
        outs.append(jnp.dot(p.astype(bf16), v, preferred_element_type=f32) / total)
        lses.append(peak + jnp.log(total))
    o_ref[...] = join(*outs).astype(bf16)
    lse_ref[0] = jnp.concatenate(lses, axis=1)


def fwd_kernel(steps, tiles, G, halves, count, *refs):
    ins, srcs = refs[:4], refs[4:4 + count]
    mid = refs[4 + count:6 + count]
    outs, sems = refs[6 + count:6 + 2 * count], refs[6 + 2 * count:]
    now = pl.program_id(0) * tiles + pl.program_id(1)
    beside(Gather(G, halves, srcs, outs, *sems), steps, now, lambda: fwd_tile(*ins, *mid))


def attn_fwd_and_gather(qkv, bias, shards, halves, wide, cid, tq=256):
    n, width = qkv.shape[0], qkv.shape[1] // 3
    pairs, tiles, count, G = width // 128, n // tq, len(shards), wide // 4
    outs = pl.pallas_call(functools.partial(fwd_kernel, pairs * tiles, tiles, G, halves, count), grid=(pairs, tiles),
        out_shape=(jax.ShapeDtypeStruct((n, width), bf16), jax.ShapeDtypeStruct((pairs, n, 2), f32)) + gathered_shapes(shards, wide),
        in_specs=[pl.BlockSpec((tq, 128), lambda p, i: (i, p)), pl.BlockSpec((n, 128), lambda p, i: (0, p + pairs)),
                  pl.BlockSpec((n, 128), lambda p, i: (0, p + 2 * pairs)), pl.BlockSpec((2, tq, n), lambda p, i: (p, i, 0))] + [ANY] * count,
        out_specs=(pl.BlockSpec((tq, 128), lambda p, i: (i, p)), pl.BlockSpec((1, tq, 2), lambda p, i: (p, i, 0))) + (ANY,) * count,
        scratch_shapes=gather_scratch(G, halves, count), compiler_params=params(cid), name="attention_gather")(qkv, qkv, qkv, bias, *shards)
    return outs[0], outs[1], [flat(a) for a in outs[2:]]


def bwd_tile(first, last, q_ref, k_ref, v_ref, bias_ref, o_ref, do_ref, lse_ref, dq_ref, dk_ref, dv_ref, g_ref, dkt, dvt):
    @pl.when(first)
    def _():
        dkt[...] = jnp.zeros_like(dkt)
        dvt[...] = jnp.zeros_like(dvt)

    q, k, v, do = q_ref[...], k_ref[...], v_ref[...], do_ref[...]
    prod = do.astype(f32) * o_ref[...].astype(f32)
    dqs = []
    for e in range(2):
        qm, dom = half_of(q, e), half_of(do, e)
        s = lax.dot_general(qm, k, NT, preferred_element_type=f32) + bias_ref[e]
        p = jnp.exp(s - lse_ref[0, :, e:e + 1])
        dp = lax.dot_general(dom, v, NT, preferred_element_type=f32)
        inner = jnp.sum(half_of(prod, e), axis=1, keepdims=True)
        g = (p * (dp - inner)).astype(bf16)
        g_ref[e] = g
        dqs.append(jnp.dot(g, k, preferred_element_type=f32))
        dvt[...] += jnp.dot(dom.T, p.astype(bf16), preferred_element_type=f32)
        dkt[...] += jnp.dot(qm.T, g, preferred_element_type=f32)
    dq_ref[...] = join(*dqs).astype(bf16)

    @pl.when(last)
    def _():
        dk_ref[...] = dkt[...].T.astype(bf16)
        dv_ref[...] = dvt[...].T.astype(bf16)


def bwd_kernel(steps, tiles, G, halves, count, *refs):
    ins, parts = refs[:7], refs[7:7 + count]
    mid = refs[7 + count:11 + count]
    outs, accs, sems = refs[11 + count:11 + 2 * count], refs[11 + 2 * count:13 + 2 * count], refs[13 + 2 * count:]
    i = pl.program_id(1)
    comm = Scatter(G, halves, parts, outs, *sems)
    beside(comm, steps, pl.program_id(0) * tiles + i, lambda: bwd_tile(i == 0, i == tiles - 1, *ins, *mid, *accs))


def shard_shapes(parts, wide):
    return tuple(jax.ShapeDtypeStruct((p.shape[0] // wide, p.shape[1]), f32) for p in parts)


def attn_bwd_and_scatter(qkv, bias, o, do, lse, parts, halves, wide, cid, tq=256):
    n, width = qkv.shape[0], qkv.shape[1] // 3
    pairs, tiles, count, G = width // 128, n // tq, len(parts), wide // 4
    tile = pl.BlockSpec((tq, 128), lambda p, i: (i, p))
    full = pl.BlockSpec((n, 128), lambda p, i: (0, p))
    outs = pl.pallas_call(functools.partial(bwd_kernel, pairs * tiles, tiles, G, halves, count), grid=(pairs, tiles),
        out_shape=(jax.ShapeDtypeStruct((n, width), bf16),) * 3 + (jax.ShapeDtypeStruct((2 * pairs, n, n), bf16),) + shard_shapes(parts, wide),
        in_specs=[tile, pl.BlockSpec((n, 128), lambda p, i: (0, p + pairs)), pl.BlockSpec((n, 128), lambda p, i: (0, p + 2 * pairs)),
                  pl.BlockSpec((2, tq, n), lambda p, i: (p, i, 0)), tile, tile, pl.BlockSpec((1, tq, 2), lambda p, i: (p, i, 0))] + [ANY] * count,
        out_specs=(tile, full, full, pl.BlockSpec((2, tq, n), lambda p, i: (p, i, 0))) + (whole_vmem(),) * count,
        scratch_shapes=[pltpu.VMEM((128, n), f32), pltpu.VMEM((128, n), f32)] + scatter_scratch(G, halves, parts[0].shape[0] // wide),
        compiler_params=params(cid), name="attention_back_scatter")(qkv, qkv, qkv, bias, o, do, lse, *[spread(p, wide) for p in parts])
    return outs[:4], outs[4:]


def hist_tile(first, heads, rows, n, g_ref, ids_ref, out_ref, gs):
    @pl.when(first)
    def _():
        out_ref[...] = jnp.zeros_like(out_ref)

    for h in range(heads):
        for c in range(n // 128):
            gs[c, h * rows:(h + 1) * rows, :] = g_ref[h, :, c * 128:(c + 1) * 128].astype(f32)
    label = lax.broadcasted_iota(jnp.int32, (32, n), 0).astype(bf16)
    one, zero = jnp.ones((32, n), bf16), jnp.zeros((32, n), bf16)
    acc = jnp.zeros((heads, 96), f32)
    for r in range(rows):
        grow = jnp.concatenate([gs[c, pl.ds(r, heads, stride=rows), :] for c in range(n // 128)], axis=1).astype(bf16)
        hots = []
        for t in range(3):
            row = jnp.broadcast_to(ids_ref[t, r:r + 1, :], (32, n)).astype(bf16)
            hots.append(jnp.where(row == label, one, zero))
        acc = acc + lax.dot_general(grow, jnp.concatenate(hots, axis=0), NT, preferred_element_type=f32)
    out_ref[...] += acc


def hist_kernel(heads, rows, n, G, halves, count, *refs):
    ins, parts, out_ref = refs[:2], refs[2:2 + count], refs[2 + count]
    outs, gs, sems = refs[3 + count:3 + 2 * count], refs[3 + 2 * count], refs[4 + 2 * count:]
    now = pl.program_id(0)
    comm = Scatter(G, halves, parts, outs, *sems)
    beside(comm, n // rows, now, lambda: hist_tile(now == 0, heads, rows, n, *ins, out_ref, gs))


def hist_and_scatter(g, ids, parts, halves, wide, cid):
    heads, n, _ = g.shape
    rows, count, G = 16, len(parts), wide // 4
    outs = pl.pallas_call(functools.partial(hist_kernel, heads, rows, n, G, halves, count), grid=(n // rows,),
        out_shape=(jax.ShapeDtypeStruct((heads, 96), f32),) + shard_shapes(parts, wide),
        in_specs=[pl.BlockSpec((heads, rows, n), lambda i: (0, i, 0)), pl.BlockSpec((3, rows, n), lambda i: (0, i, 0))] + [ANY] * count,
        out_specs=(pl.BlockSpec((heads, 96), lambda i: (0, 0)),) + (whole_vmem(),) * count,
        scratch_shapes=[pltpu.VMEM((n // 128, heads * rows, 128), f32)] + scatter_scratch(G, halves, parts[0].shape[0] // wide),
        compiler_params=params(cid), name="table_grad_scatter")(g, ids, *[spread(p, wide) for p in parts])
    return outs[0], outs[1:]


D = pltpu.SemaphoreType.DMA


def place():
    me = lax.axis_index("wide")
    return me // 4, (me // 2) % 2, me % 2


def wide_id(z, y, x):
    return {"wide": z * 4 + y * 2 + x}


def remote(src, dst, send, recv, target):
    return pltpu.make_async_remote_copy(src_ref=src, dst_ref=dst, send_sem=send, recv_sem=recv, device_id=target, device_id_type=MESH)


def greet(G, far):
    z, y, x = place()
    bar = pltpu.get_barrier_semaphore()
    sig = lambda t: pl.semaphore_signal(bar, inc=1, device_id=t, device_id_type=MESH)
    sig(wide_id(z, 1 - y, x))
    sig(wide_id(z, y, 1 - x))
    if far:
        for k in range(1, G):
            sig(wide_id((z + k) % G, y, x))
        pl.semaphore_wait(bar, 2 + G - 1)
    else:
        @pl.when(z > 0)
        def _():
            sig(wide_id(z - 1, y, x))

        @pl.when(z < G - 1)
        def _():
            sig(wide_id(z + 1, y, x))

        pl.semaphore_wait(bar, 2 + (z > 0).astype(jnp.int32) + (z < G - 1).astype(jnp.int32))


class Gather:
    def __init__(self, G, halves, srcs, outs, local_sem, zs, zr, ns, nr):
        self.G, self.halves, self.srcs, self.outs, self.local_sem = G, halves, srcs, outs, local_sem
        self.zs, self.zr, self.ns, self.nr = zs, zr, ns, nr
        self.most = max(len(h) for h in halves)
        self.z, self.y, self.x = place()

    def hop(self, own, zz, yy, xx, h, way, j):
        target = wide_id(self.z, 1 - self.y, self.x) if way == "y" else wide_id(self.z, self.y, 1 - self.x)
        copies = []
        for n, (a, c, w) in enumerate(self.halves[h]):
            slot = (zz * 6 + j) * self.most + n
            dst = self.outs[a].at[zz, yy, xx, :, pl.ds(c, w)]
            copies.append(remote(self.srcs[a].at[:, pl.ds(c, w)] if own else dst, dst, self.ns.at[slot], self.nr.at[slot], target))
        return copies

    def second_stage(self, zz, own=False):
        return self.hop(own, zz, self.y, self.x, 0, "y", 0) + self.hop(own, zz, self.y, self.x, 1, "x", 1)

    def third_stage(self, zz, own=False):
        return self.hop(own, zz, self.y, self.x, 0, "x", 2) + self.hop(own, zz, self.y, self.x, 1, "y", 3)

    def last_stage(self, zz):
        return self.hop(False, zz, 1 - self.y, self.x, 0, "x", 4) + self.hop(False, zz, self.y, 1 - self.x, 1, "y", 5)

    def relay(self, own, zz, step, way):
        copies = []
        for a in range(len(self.srcs)):
            slot = (way * (self.G - 1) + step) * len(self.srcs) + a
            dst = self.outs[a].at[zz, self.y, self.x]
            copies.append(remote(self.srcs[a] if own else dst, dst, self.zs.at[slot], self.zr.at[slot],
                                 wide_id(self.z + (1 if way == 0 else -1), self.y, self.x)))
        return copies

    def can(self, way):
        return self.z < self.G - 1 if way == 0 else self.z > 0

    def source(self, d, way):
        return (self.z - d, self.z - d >= 0) if way == 0 else (self.z + d, self.z + d < self.G)

    def keep(self):
        return [pltpu.make_async_copy(s, o.at[self.z, self.y, self.x], self.local_sem.at[a]) for a, (s, o) in enumerate(zip(self.srcs, self.outs))]

    def begin(self):
        for way in range(2):
            @pl.when(self.can(way))
            def _():
                for c in self.relay(True, self.z, 0, way):
                    c.start()
        for c in self.second_stage(self.z, True) + self.third_stage(self.z, True) + self.keep():
            c.start()

    def turn(self, zz):
        for c in self.hop(False, zz, 1 - self.y, self.x, 0, "y", 0) + self.hop(False, zz, self.y, 1 - self.x, 1, "x", 1):
            c.wait_recv()
        for c in self.last_stage(zz):
            c.start()

    def step(self, d):
        for way in range(2):
            zz, there = self.source(d, way)

            @pl.when(there)
            def _():
                for c in self.relay(False, zz, d - 1, way):
                    c.wait_recv()

                @pl.when(self.can(way))
                def _():
                    for c in self.relay(False, zz, d, way):
                        c.start()

                for c in self.second_stage(zz):
                    c.start()
        for way in range(2):
            zz, there = self.source(d, way)

            @pl.when(there)
            def _():
                for c in self.third_stage(zz):
                    c.start()

    def turns(self, d):
        if d == 0:
            self.turn(self.z)
            return
        for way in range(2):
            zz, there = self.source(d, way)

            @pl.when(there)
            def _():
                self.turn(zz)

    def finish(self):
        y, x = self.y, self.x

        @pl.loop(0, self.G)
        def _(zz):
            for c in (self.hop(False, zz, y, 1 - x, 0, "x", 2) + self.hop(False, zz, 1 - y, x, 1, "y", 3)
                      + self.hop(False, zz, 1 - y, 1 - x, 0, "x", 4) + self.hop(False, zz, 1 - y, 1 - x, 1, "y", 5)):
                c.wait_recv()
            for c in self.second_stage(zz) + self.third_stage(zz) + self.last_stage(zz):
                c.wait_send()

        for way in range(2):
            @pl.when(self.can(way))
            def _():
                for c in self.relay(True, self.z, 0, way):
                    c.wait_send()
                for d in range(1, self.G - 1):
                    zz, there = self.source(d, way)

                    @pl.when(there)
                    def _():
                        for c in self.relay(False, zz, d, way):
                            c.wait_send()
        for c in self.keep():
            c.wait()

    def events(self):
        G = self.G
        first = lambda: (greet(G, False), self.begin())
        ev = [(0.0, first), (0.7, lambda: self.turns(0))]
        for d in range(1, G):
            ev += [(1.15 * d, functools.partial(self.step, d)), (1.3 * d + 1.2, functools.partial(self.turns, d))]
        return sorted(ev, key=lambda e: e[0]), self.finish


def gather_scratch(G, halves, arrays):
    most = max(len(h) for h in halves)
    return [D((arrays,)), D((2 * (G - 1) * arrays,)), D((2 * (G - 1) * arrays,)), D((6 * G * most,)), D((6 * G * most,))]


class Scatter:
    def __init__(self, G, halves, parts, outs, r1a, r1b, o1a, o1b, r2a, r2b, r3, own, lsem, s1, v1, s2, v2, s3, v3):
        self.__dict__.update(locals())
        self.most = max(len(h) for h in halves)
        self.wa, self.wb = [sum(p[2] for p in h) for h in halves]
        self.R = parts[0].shape[3]
        self.z, self.y, self.x = place()
        self.order = sorted(range(1, G), key=lambda k: min(k, G - k), reverse=True) + [0]

    def zk(self, k):
        return (self.z + k) % self.G

    def neighbour(self, way):
        return wide_id(self.z, 1 - self.y, self.x) if way == "y" else wide_id(self.z, self.y, 1 - self.x)

    def pieces(self, h):
        at, out = 0, []
        for n, (a, c, w) in enumerate(self.halves[h]):
            out.append((n, a, pl.ds(c, w), pl.ds(at, w)))
            at += w
        return out

    def one(self, k):
        z, cs = self.zk(k), []
        for n, a, src, dst in self.pieces(0):
            slot = (2 * k) * self.most + n
            cs.append(remote(self.parts[a].at[z, :, 1 - self.x, :, src], self.r1a.at[k, :, :, dst], self.s1.at[slot], self.v1.at[slot], self.neighbour("x")))
        for n, a, src, dst in self.pieces(1):
            slot = (2 * k + 1) * self.most + n
            cs.append(remote(self.parts[a].at[z, 1 - self.y, :, :, src], self.r1b.at[k, :, :, dst], self.s1.at[slot], self.v1.at[slot], self.neighbour("y")))
        return cs

    def load(self, k):
        z, cs = self.zk(k), []
        for n, a, src, dst in self.pieces(0):
            cs.append(pltpu.make_async_copy(self.parts[a].at[z, :, self.x, :, src], self.o1a.at[k, :, :, dst], self.lsem.at[(2 * k) * self.most + n]))
        for n, a, src, dst in self.pieces(1):
            cs.append(pltpu.make_async_copy(self.parts[a].at[z, self.y, :, :, src], self.o1b.at[k, :, :, dst], self.lsem.at[(2 * k + 1) * self.most + n]))
        return cs

    def two(self, k):
        return [remote(self.o1a.at[k, 1 - self.y], self.r2a.at[k], self.s2.at[2 * k], self.v2.at[2 * k], self.neighbour("y")),
                remote(self.o1b.at[k, 1 - self.x], self.r2b.at[k], self.s2.at[2 * k + 1], self.v2.at[2 * k + 1], self.neighbour("x"))]

    def three(self, k):
        return remote(self.own.at[k], self.r3.at[k - 1], self.s3.at[k - 1], self.v3.at[k - 1], wide_id(self.zk(k), self.y, self.x))

    def launch(self, k):
        for c in self.one(k) + self.load(k):
            c.start()

    def begin(self):
        for k in self.order[:2]:
            self.launch(k)

    def rows(self, count, body):
        step = min(16, count)

        @pl.loop(0, count // step)
        def _(i):
            body(pl.ds(pl.multiple_of(i * step, step), step))

    def add_one(self, n):
        k = self.order[n]
        for c in self.one(k):
            c.wait_recv()
        for c in self.load(k):
            c.wait()
        for mine, got in ((self.o1a, self.r1a), (self.o1b, self.r1b)):
            def body(r):
                for j in range(2):
                    mine[k, j, r, :] = (mine[k, j, r, :].astype(f32) + got[k, j, r, :].astype(f32)).astype(bf16)

            self.rows(self.R, body)
        for c in self.two(k):
            c.start()
        if n + 2 < self.G:
            self.launch(self.order[n + 2])

    def add_two(self, n):
        k = self.order[n]
        for c in self.two(k):
            c.wait_recv()

        def body(r):
            self.own[k, r, pl.ds(0, self.wa)] = (self.o1a[k, self.y, r, :].astype(f32) + self.r2a[k, r, :].astype(f32)).astype(bf16)
            self.own[k, r, pl.ds(self.wa, self.wb)] = (self.o1b[k, self.x, r, :].astype(f32) + self.r2b[k, r, :].astype(f32)).astype(bf16)

        self.rows(self.R, body)
        if k:
            self.three(k).start()

    def finish(self):
        self.add_two(self.G - 1)
        for k in range(1, self.G):
            self.three(k).wait_recv()

        def body(r):
            for h in range(2):
                for _, a, src, dst in self.pieces(h):
                    cols = pl.ds(dst.start + h * self.wa, dst.size)
                    total = self.own[0, r, cols].astype(f32)
                    for k in range(self.G - 1):
                        total = total + self.r3[k, r, cols].astype(f32)
                    self.outs[a][r, src] = total

        self.rows(self.R, body)
        for k in range(self.G):
            for c in self.one(k) + self.two(k):
                c.wait_send()
            if k:
                self.three(k).wait_send()

    def events(self):
        G = self.G
        first = lambda: (greet(G, True), self.begin())
        ev = [(0.0, first), (1.1, lambda: self.add_one(0))]
        for n in range(1, G):
            ev += [(1.5 * n + 0.65, functools.partial(self.add_one, n)), (1.5 * n + 1.1, functools.partial(self.add_two, n - 1))]
        return sorted(ev, key=lambda e: e[0]), self.finish


def scatter_scratch(G, halves, R):
    most = max(len(h) for h in halves)
    a, b = [sum(p[2] for p in h) for h in halves]
    V = lambda *s: pltpu.VMEM(s, bf16)
    return [V(G, 2, R, a), V(G, 2, R, b), V(G, 2, R, a), V(G, 2, R, b), V(G, R, a), V(G, R, b), V(G - 1, R, a + b), V(G, R, a + b),
            D((2 * G * most,)), D((2 * G * most,)), D((2 * G * most,)), D((2 * G,)), D((2 * G,)), D((G - 1,)), D((G - 1,))]


def beside(comm, steps, now, compute):
    events, finish = comm.events()
    units = 1.55 * comm.G
    for n in range(steps):
        here = [act for t, act in events if min(steps - 1, int(-(-t * steps // units))) == n]
        if here:
            @pl.when(now == n)
            def _():
                for act in here:
                    act()
    compute()

    @pl.when(now == steps - 1)
    def _():
        finish()


ANY = pl.BlockSpec(memory_space=pl.ANY)


def whole_vmem():
    return pl.BlockSpec(memory_space=pltpu.VMEM)


def spread(a, wide):
    return a.reshape(wide // 4, 2, 2, a.shape[0] // wide, a.shape[1])


def gathered_shapes(shards, wide):
    return tuple(jax.ShapeDtypeStruct((wide // 4, 2, 2) + s.shape, s.dtype) for s in shards)


def flat(a):
    return a.reshape(-1, a.shape[-1])


def sum_kernel(G, src, out, acc, got, gz, s, v, sz, vz):
    z, y, x = place()
    core = {"narrow": 1 - lax.axis_index("narrow")}
    ynb, xnb = wide_id(z, 1 - y, x), wide_id(z, y, 1 - x)
    far = [wide_id((z + k) % G, y, x) for k in range(1, G)]
    bar = pltpu.get_barrier_semaphore()
    for t in [core, ynb, xnb] + far:
        pl.semaphore_signal(bar, inc=1, device_id=t, device_id_type=MESH)
    pl.semaphore_wait(bar, 3 + len(far))
    acc[0] = src[...]
    for n, t in enumerate((core, xnb, ynb)):
        c = remote(acc.at[n], got.at[n], s.at[n], v.at[n], t)
        c.start()
        c.wait()
        acc[n + 1] = acc[n] + got[n]
    gz[z] = acc[3]
    sent = [remote(acc.at[3], gz.at[z], sz.at[k], vz.at[z], t) for k, t in enumerate(far)]
    for c in sent:
        c.start()
    for k in range(1, G):
        zz = (z + k) % G
        remote(acc.at[3], gz.at[zz], sz.at[k - 1], vz.at[zz], far[k - 1]).wait_recv()
    for c in sent:
        c.wait_send()
    total = gz[0]
    for k in range(1, G):
        total = total + gz[k]
    out[...] = total


def sum_all(part, wide, cid):
    G, rows = wide // 4, part.shape[0]
    V = lambda k: pltpu.VMEM((k, rows, 128), f32)
    return pl.pallas_call(functools.partial(sum_kernel, G), out_shape=jax.ShapeDtypeStruct(part.shape, f32),
        in_specs=[whole_vmem()], out_specs=whole_vmem(),
        scratch_shapes=[V(4), V(3), V(G), D((3,)), D((3,)), D((G - 1,)), D((G,))],
        compiler_params=pltpu.CompilerParams(collective_id=cid, has_side_effects=True), name="small_sums")(part)


TILE = 256


def nt(a, b):
    return lax.dot_general(a, b, NT, preferred_element_type=f32)


def nn(a, b):
    return jnp.dot(a, b, preferred_element_type=f32)


def gelu_and_slope(v):
    root = 0.7978845608028654
    square = v * v
    t = jnp.tanh(root * v * (1.0 + 0.044715 * square))
    half = 0.5 * (1.0 + t)
    return v * half, half + 0.5 * v * (1.0 - t * t) * root * (1.0 + 3 * 0.044715 * square)


def mid_kernel(att_h, tok_h, cot_h, wo_h, wg_h, wu_h, wd_h, gain_ref,
               gout_h, gg_h, gu_h, gd_h, y_ref, gh_ref, ga_ref, ggain_ref,
               att, tok, cot, wo, wg, wu, wd, part, other, back, hid, n2, n2t, cott, hff, gg, gu, ysend, yown, yother, stage,
               isem, osem, sp, vp, sb, vb, sy, vy):
    core = lax.axis_index("narrow")
    peer = {"narrow": 1 - core}
    n, d = tok.shape
    ff = wg.shape[1]
    tiles = n // TILE
    half = tiles // 2
    loads = [pltpu.make_async_copy(s, t, isem.at[k]) for k, (s, t) in enumerate(
        [(att_h, att), (wo_h, wo), (tok_h, tok), (wg_h, wg), (wu_h, wu), (wd_h, wd), (cot_h, cot)])]
    for c in loads:
        c.start()
    bar = pltpu.get_barrier_semaphore()
    pl.semaphore_signal(bar, inc=1, device_id=peer, device_id_type=MESH)
    pl.semaphore_wait(bar, 1)
    rows_of = lambda t: pl.ds(pl.multiple_of(t * TILE, TILE), TILE)
    send_part = lambda t: remote(part.at[rows_of(t)], other.at[rows_of(t)], sp.at[t], vp.at[t], peer)
    send_back = lambda t: remote(part.at[rows_of(t)], back.at[rows_of(t)], sb.at[t], vb.at[t], peer)
    send_y = lambda j: remote(ysend.at[rows_of(j)], yother.at[rows_of(j)], sy.at[j], vy.at[j], peer)
    gain = gain_ref[...]

    for c in loads[:2]:
        c.wait()

    @pl.loop(0, tiles)
    def _(t):
        part[rows_of(t), :] = nt(att[rows_of(t), :], wo[...]).astype(bf16)
        send_part(t).start()

    for c in loads[2:]:
        c.wait()

    chunks, at = [], 0
    while at < ff:
        w = min(384, ff - at)
        chunks.append((at, w))
        at += w

    @pl.loop(0, tiles)
    def _(s):
        t = (s + half * (1 - core)) % tiles
        r = rows_of(t)
        send_part(t).wait()
        h = tok[r, :].astype(f32) + (part[r, :].astype(f32) + other[r, :].astype(f32))
        hid[r, :] = h
        factor = lax.rsqrt(jnp.mean(h * h, axis=1, keepdims=True) + epsilon)
        low = (h * factor * gain).astype(bf16)
        n2[r, :] = low
        n2t[:, r] = low.T
        ct = cot[r, :]
        cott[:, r] = ct.T
        for at, w in chunks:
            cols = pl.ds(at, w)
            act, slope = gelu_and_slope(nn(low, wg[:, cols]))
            up = nn(low, wu[:, cols])
            gf = nn(ct, wd[:, cols])
            hff[r, cols] = (act * up).astype(bf16)
            gg[r, cols] = (gf * up * slope).astype(bf16)
            gu[r, cols] = (gf * act).astype(bf16)
        part[r, :] = (nt(gg[r, :], wg[...]) + nt(gu[r, :], wu[...])).astype(bf16)
        send_back(t).start()
        y = nt(hff[r, :], wd[...]).astype(bf16)

        @pl.when(s < half)
        def _():
            ysend[rows_of(s), :] = y
            send_y(s).start()

        @pl.when(s >= half)
        def _():
            yown[rows_of(s - half), :] = y

    def weight_grad(left, right, out, slot, width):
        @pl.loop(0, d // TILE)
        def _(k):
            b = k % 2
            copy = lambda kk: pltpu.make_async_copy(stage.at[kk % 2, :, pl.ds(0, width)], out.at[rows_of(kk)], osem.at[2 * slot + kk % 2])

            @pl.when(k >= 2)
            def _():
                copy(k - 2).wait()

            stage[b, :, pl.ds(0, width)] = nn(left[rows_of(k), :], right[...]).astype(bf16)
            copy(k).start()

        for k in range(d // TILE - 2, d // TILE):
            pltpu.make_async_copy(stage.at[k % 2, :, pl.ds(0, width)], out.at[rows_of(k)], osem.at[2 * slot + k % 2]).wait()

    weight_grad(cott, hff, gd_h, 0, ff)
    ggain_ref[...] = jnp.zeros_like(ggain_ref)

    @pl.loop(0, tiles)
    def _(s):
        t = (s + half * (1 - core)) % tiles
        r = rows_of(t)
        send_back(t).wait()
        total = part[r, :].astype(f32) + back[r, :].astype(f32)
        h = hid[r, :]
        factor = lax.rsqrt(jnp.mean(h * h, axis=1, keepdims=True) + epsilon)
        unit = h * factor
        g = gain * total
        gh = cot[r, :].astype(f32) + factor * (g - unit * jnp.mean(g * unit, axis=1, keepdims=True))
        low = gh.astype(bf16)
        cott[:, r] = low.T
        ga_ref[r, :] = nn(low, wo[...]).astype(bf16)

        @pl.when(s >= half)
        def _():
            j = rows_of(s - half)
            gh_ref[j, :] = gh
            ggain_ref[...] += jnp.sum(total * unit, axis=0, keepdims=True)
            send_y(s - half).wait()
            y_ref[j, :] = (h + (yown[j, :].astype(f32) + yother[j, :].astype(f32))).astype(bf16)

    weight_grad(n2t, gg, gg_h, 1, ff)
    weight_grad(n2t, gu, gu_h, 2, ff)
    weight_grad(cott, att, gout_h, 3, att.shape[1])


def middle(att, tok, cot, wo, wg, wu, wd, gain, cid):
    n, d = tok.shape
    units, ff = att.shape[1], wg.shape[1]
    B = lambda *s: pltpu.VMEM(s, bf16)
    sds = jax.ShapeDtypeStruct
    tiles = n // TILE
    return pl.pallas_call(mid_kernel,
        out_shape=(sds((d, units), bf16), sds((d, ff), bf16), sds((d, ff), bf16), sds((d, ff), bf16),
                   sds((n // 2, d), bf16), sds((n // 2, d), f32), sds((n, units), bf16), sds((1, d), f32)),
        in_specs=[ANY] * 7 + [whole_vmem()], out_specs=(ANY,) * 4 + (whole_vmem(),) * 4,
        scratch_shapes=[B(n, units), B(n, d), B(n, d), B(d, units), B(d, ff), B(d, ff), B(d, ff), B(n, d), B(n, d), B(n, d),
                        pltpu.VMEM((n, d), f32), B(n, d), B(d, n), B(d, n), B(n, ff), B(n, ff), B(n, ff),
                        B(n // 2, d), B(n // 2, d), B(n // 2, d), B(2, TILE, ff),
                        D((7,)), D((8,)), D((tiles,)), D((tiles,)), D((tiles,)), D((tiles,)), D((tiles // 2,)), D((tiles // 2,))],
        compiler_params=params(cid), name="feed_forward")(att, tok, cot, wo, wg, wu, wd, gain)


epsilon = 1e-06


def norm_plain(values, gain_row):
    factor = lax.rsqrt(jnp.mean(values * values, axis=-1, keepdims=True) + epsilon)
    return values * factor * gain_row


def times(a, b):
    return jnp.dot(a, b, preferred_element_type=f32)


def times_transposed(a, b):
    return lax.dot_general(a, b, NT, preferred_element_type=f32)


def transposed_times(a, b):
    return lax.dot_general(a, b, (((0,), (0,)), ((), ())), preferred_element_type=f32)


def local(tokens, cotangent, pages, boxes, gain_attn, gain_ffn, bias_tables, w_query, w_key, w_value, w_out, w_gate, w_up, w_down):
    wide, narrow = lax.axis_size("wide"), lax.axis_size("narrow")
    heads_all = bias_tables.shape[1]
    heads = heads_all // narrow
    rows = tokens.shape[0]
    core = lax.axis_index("narrow")
    tables = lax.dynamic_slice_in_dim(bias_tables, core * heads, heads, 1)
    inner, ff = w_query.shape[1], w_gate.shape[1]
    all_tokens = lax.all_gather(tokens, "narrow", axis=0, tiled=True)
    all_cot = lax.all_gather(cotangent, "narrow", axis=0, tiled=True)
    early = inner // 4 * 3
    bias, ids, (w_first, full_out, full_gate) = bias_and_gather(
        tables, boxes, pages, [jnp.concatenate([w_query, w_key, w_value], axis=1), w_out.T, w_gate],
        (((2, 0, ff), (0, 0, early)), ((1, 0, inner), (0, early, 3 * inner - early))), wide, 1)

    x = all_tokens.astype(f32)
    gain_one, gain_two = gain_attn.astype(f32), gain_ffn.astype(f32)
    normed = norm_plain(x, gain_one).astype(bf16)
    qkv = times(normed, w_first).astype(bf16)
    attended, lse, (full_up, full_down) = attn_fwd_and_gather(qkv, bias, [w_up, w_down.T], (((0, 0, ff),), ((1, 0, ff),)), wide, 2)
    grad_w_out, grad_w_gate, grad_w_up, grad_w_down, output, grad_hidden, grad_attended, grad_gain_two = middle(
        attended, all_tokens, all_cot, full_out, full_gate, full_up, full_down, gain_two[None], 6)
    (dq, dk, dv, g), (s_down, s_out) = attn_bwd_and_scatter(
        qkv, bias, attended, grad_attended, lse, [grad_w_down, grad_w_out],
        (((0, 0, 2 * inner),), ((0, 2 * inner, ff - 2 * inner), (1, 0, inner))), wide, 3)
    dqkv = jnp.concatenate([dq, dk, dv], axis=1)
    mid = 3 * inner // 2
    table_part, (s_gate, s_up, s_first) = hist_and_scatter(
        g, ids, [grad_w_gate, grad_w_up, transposed_times(normed, dqkv).astype(bf16)],
        (((0, 0, ff), (2, 0, mid)), ((1, 0, ff), (2, mid, mid))), wide, 4)
    grad_normed = lax.psum_scatter(times_transposed(dqkv, w_first).astype(bf16), "narrow", scatter_dimension=0, tiled=True).astype(f32)
    own = tokens.astype(f32)
    _, pull_one = jax.vjp(norm_plain, own, gain_one)
    grad_tokens_norm, grad_gain_one = pull_one(grad_normed)
    grad_tokens = grad_hidden + grad_tokens_norm
    table_part = lax.dynamic_update_slice(jnp.zeros((bias_tables.shape[0], heads_all), f32), table_part.T, (jnp.int32(0), core * heads))
    sizes = [gain_one.size, gain_two.size, table_part.size]
    small = sum_all(jnp.concatenate([grad_gain_one, grad_gain_two[0], table_part.reshape(-1)]).reshape(-1, 128), wide, 5).reshape(-1)
    one, two, table = jnp.split(small, [sizes[0], sizes[0] + sizes[1]])
    s_query, s_key, s_value = jnp.split(s_first, 3, axis=1)
    return (output, grad_tokens, one, two, table.reshape(bias_tables.shape), s_query, s_key, s_value, s_out.T, s_gate, s_up, s_down.T)


def solution(mesh):
    rows, cols, tall = P(("wide", "narrow"), None), P("wide", "narrow"), P("narrow", "wide")
    in_specs = (rows, rows, P("wide"), P(None, "wide"), P(), P(), P(), cols, cols, cols, tall, cols, cols, tall)
    out_specs = (rows, rows, P(), P(), P(), cols, cols, cols, tall, cols, cols, tall)
    return jax.shard_map(local, mesh=mesh, in_specs=in_specs, out_specs=out_specs, check_vma=False)
```

```python
import functools

import jax
import jax.numpy as jnp
from jax import lax
from jax.experimental import pallas as pl
from jax.experimental.pallas import tpu as pltpu
from jax.sharding import PartitionSpec as P

f32, bf16 = jnp.float32, jnp.bfloat16
MESH = pl.DeviceIdType.MESH


EDGES = (1, 2, 3, 4, 5, 6, 7, 8, 12, 16, 23, 32, 46, 64, 91)
NT = (((1,), (1,)), ((), ()))
VM = 58 * 2**20
TABLE_SCALE = 2047.0
TABLE_LIFT = 8192
TILE = 256
epsilon = 1e-06


def params(cid):
    return pltpu.CompilerParams(collective_id=cid, has_side_effects=True, vmem_limit_bytes=VM)


def lane_take(table, idx):
    return jnp.take_along_axis(table, idx, axis=1, mode="promise_in_bounds")


def buckets_of(gap, steps, shift):
    return lane_take(steps, jnp.minimum(jnp.abs(gap) >> shift, EDGES[-1])) + jnp.where(gap > 0, 16, 0)


def bias_tile(start, heads, rows, n, steps_ref, tab_ref, box_col, box_row, page_col, page_row, bias_ref, ids_ref, lin, lin_ids):
    steps = jnp.broadcast_to(steps_ref[...], (rows, 128))
    allowed_col = jnp.broadcast_to(page_col[...] % 2, (rows, 128))
    cols = [jnp.broadcast_to(box_col[:, t:t + 1], (rows, 128)) for t in range(2)]
    pairs = heads // 2
    table = lambda t, p: jnp.broadcast_to(tab_ref[t * pairs + p:t * pairs + p + 1, :], (rows, 128))
    unit = 1.0 / TABLE_SCALE

    @pl.when(start == 0)
    def _():
        @pl.loop(0, 8)
        def _(k):
            ids = buckets_of(lax.broadcasted_iota(jnp.int32, (rows, 128), 1) - lax.broadcasted_iota(jnp.int32, (rows, 128), 0) + (k - 4) * rows, steps, 0)
            lin_ids[k] = ids.astype(f32)
            for p in range(pairs):
                lin[k, p] = lane_take(table(0, p), ids)

    @pl.loop(0, n // 128)
    def _(c):
        lanes = pl.ds(pl.multiple_of(c * 128, 128), 128)
        near = jnp.clip((c * 128 - start) // rows + 4, 0, 7)
        ids_ref[0, :, lanes] = lin_ids[near]
        ids = []
        for t in range(2):
            ids.append(buckets_of(jnp.broadcast_to(box_row[t:t + 1, lanes], (rows, 128)) - cols[t], steps, 2))
            ids_ref[t + 1, :, lanes] = ids[t].astype(f32)
        ok = jnp.broadcast_to(page_row[:, lanes], (rows, 128)) == allowed_col
        for p in range(pairs):
            words = lin[near, p] + lane_take(table(1, p), ids[0]) + lane_take(table(2, p), ids[1])
            upper = (words >> 16).astype(f32) * unit
            lower = (words & 0xFFFF).astype(f32) * unit - 3 * TABLE_LIFT * unit
            bias_ref[2 * p, :, lanes] = jnp.where(ok, upper, -1e30)
            bias_ref[2 * p + 1, :, lanes] = jnp.where(ok, lower, -1e30)


def bias_gather_kernel(heads, rows, n, G, halves, count, *refs):
    ins, srcs = refs[:6], refs[6:6 + count]
    bias_ref, ids_ref = refs[6 + count:8 + count]
    outs, lins, sems = refs[8 + count:8 + 2 * count], refs[8 + 2 * count:10 + 2 * count], refs[10 + 2 * count:]
    now = pl.program_id(0)
    comm = Gather(G, halves, srcs, outs, *sems)
    beside(comm.events(), G, n // rows, now, lambda: bias_tile(now * rows, heads, rows, n, *ins, bias_ref, ids_ref, *lins))


def bias_and_gather(tables, boxes, pages, shards, halves, wide, cid):
    heads, n, G, rows = tables.shape[1], pages.shape[0], wide // 4, 64
    fixed = jnp.round(tables.astype(f32) * TABLE_SCALE).astype(jnp.int32).reshape(3, 32, heads // 2, 2)
    words = fixed[..., 0] * 65536 + fixed[..., 1] + TABLE_LIFT
    tab = jnp.pad(words.transpose(0, 2, 1).reshape(3 * heads // 2, 32), ((0, 0), (0, 96)))
    lane = jnp.arange(128, dtype=jnp.int32)
    steps = sum([(lane >= e).astype(jnp.int32) for e in EDGES])[None]
    count = len(shards)
    outs = pl.pallas_call(functools.partial(bias_gather_kernel, heads, rows, n, G, halves, count),
        grid=(n // rows,),
        out_shape=(jax.ShapeDtypeStruct((heads, n, n), f32), jax.ShapeDtypeStruct((3, n, n), f32)) + gathered_shapes(shards, wide),
        in_specs=[pl.BlockSpec((1, 128), lambda i: (0, 0)), pl.BlockSpec((3 * heads // 2, 128), lambda i: (0, 0)),
                  pl.BlockSpec((rows, 2), lambda i: (i, 0)), pl.BlockSpec((2, n), lambda i: (0, 0)),
                  pl.BlockSpec((rows, 1), lambda i: (i, 0)), pl.BlockSpec((1, n), lambda i: (0, 0))] + [ANY] * count,
        out_specs=(pl.BlockSpec((heads, rows, n), lambda i: (0, i, 0)), pl.BlockSpec((3, rows, n), lambda i: (0, i, 0))) + (ANY,) * count,
        scratch_shapes=[pltpu.VMEM((8, heads // 2, rows, 128), jnp.int32), pltpu.VMEM((8, rows, 128), f32)] + gather_scratch(G, halves, count),
        compiler_params=params(cid), name="layout_bias_gather")(
            steps, tab, boxes.T, boxes, pages[:, None], pages[None], *shards)
    return outs[0], outs[1], [flat(a) for a in outs[2:]]


def half_of(v, e):
    lane = lax.broadcasted_iota(jnp.int32, v.shape, 1)
    return jnp.where((lane >= 64) == (e == 1), v, jnp.zeros_like(v))


def join(a, b):
    lane = lax.broadcasted_iota(jnp.int32, a.shape, 1)
    return jnp.where(lane < 64, a, b)


def project(tok_ref, gain_ref, w_ref, normed, qkv):
    gain = gain_ref[...]

    @pl.loop(0, tok_ref.shape[0] // TILE)
    def _(t):
        r = pl.ds(pl.multiple_of(t * TILE, TILE), TILE)
        x = tok_ref[r, :].astype(f32)
        low = (x * lax.rsqrt(jnp.mean(x * x, axis=1, keepdims=True) + epsilon) * gain).astype(bf16)
        normed[r, :] = low
        qkv[r, :] = jnp.dot(low, w_ref[...], preferred_element_type=f32).astype(bf16)


def fwd_tile(p, i, tq, pairs, qkv, bias_ref, o_ref, lse_ref):
    cols = lambda k: pl.ds(pl.multiple_of((p + k * pairs) * 128, 128), 128)
    q, k, v = qkv[pl.ds(pl.multiple_of(i * tq, tq), tq), cols(0)], qkv[:, cols(1)], qkv[:, cols(2)]
    outs, lses = [], []
    for e in range(2):
        s = lax.dot_general(half_of(q, e), k, NT, preferred_element_type=f32) + bias_ref[e]
        peak = jnp.max(s, axis=1, keepdims=True)
        w = jnp.exp(s - peak)
        total = jnp.sum(w, axis=1, keepdims=True)
        outs.append(jnp.dot(w.astype(bf16), v, preferred_element_type=f32) / total)
        lses.append(peak + jnp.log(total))
    o_ref[...] = join(*outs).astype(bf16)
    lse_ref[0] = jnp.concatenate(lses, axis=1)


def fwd_kernel(pairs, tiles, G, halves, count, *refs):
    (tok, gain, w, bias_ref), srcs = refs[:4], refs[4:4 + count]
    o_ref, lse_ref, normed_h, qkv_h = refs[4 + count:8 + count]
    outs, (normed, qkv, keep), sems = refs[8 + count:8 + 2 * count], refs[8 + 2 * count:11 + 2 * count], refs[11 + 2 * count:]
    p, i = pl.program_id(0), pl.program_id(1)
    now, steps = p * tiles + i, pairs * tiles
    copies = lambda: [pltpu.make_async_copy(normed, normed_h, keep.at[0]), pltpu.make_async_copy(qkv, qkv_h, keep.at[1])]

    def compute():
        @pl.when(now == 0)
        def _():
            project(tok, gain, w, normed, qkv)
            for c in copies():
                c.start()

        fwd_tile(p, i, o_ref.shape[0], pairs, qkv, bias_ref, o_ref, lse_ref)

        @pl.when(now == steps - 1)
        def _():
            for c in copies():
                c.wait()

    beside(Gather(G, halves, srcs, outs, *sems).events(), G, steps, now, compute)


def attn_fwd_and_gather(tok, gain, w, bias, shards, halves, wide, cid, tq=256):
    n, d = tok.shape
    width = w.shape[1] // 3
    pairs, tiles, count, G = width // 128, n // tq, len(shards), wide // 4
    sds = jax.ShapeDtypeStruct
    const = lambda s: pl.BlockSpec(s, lambda p, i: (0, 0))
    outs = pl.pallas_call(functools.partial(fwd_kernel, pairs, tiles, G, halves, count), grid=(pairs, tiles),
        out_shape=(sds((n, width), bf16), sds((pairs, n, 2), f32), sds((n, d), bf16), sds((n, 3 * width), bf16)) + gathered_shapes(shards, wide),
        in_specs=[const((n, d)), const((1, d)), const(w.shape), pl.BlockSpec((2, tq, n), lambda p, i: (p, i, 0))] + [ANY] * count,
        out_specs=(pl.BlockSpec((tq, 128), lambda p, i: (i, p)), pl.BlockSpec((1, tq, 2), lambda p, i: (p, i, 0)), ANY, ANY) + (ANY,) * count,
        scratch_shapes=[pltpu.VMEM((n, d), bf16), pltpu.VMEM((n, 3 * width), bf16), D((2,))] + gather_scratch(G, halves, count),
        compiler_params=params(cid), name="attention_gather")(tok, gain, w, bias, *shards)
    return outs[:4], [flat(a) for a in outs[4:]]


def bwd_tile(p, i, last_tile, last, q_ref, k_ref, v_ref, bias_ref, o_ref, do_ref, lse_ref, normed_ref, wq_ref, wk_ref, wv_ref,
             g_ref, dwq_ref, dwk_ref, dwv_ref, dx_ref, dkt, dvt, dqkv, turned, dx):
    tq, n = q_ref.shape[0], k_ref.shape[0]
    rows = pl.ds(pl.multiple_of(i * tq, tq), tq)

    @pl.when(p == 0)
    def _():
        turned[:, rows] = normed_ref[rows, :].T
        dx[rows, :] = jnp.zeros((tq, dx.shape[1]), f32)

    @pl.when(i == 0)
    def _():
        dkt[...] = jnp.zeros_like(dkt)
        dvt[...] = jnp.zeros_like(dvt)

    q, k, v, do = q_ref[...], k_ref[...], v_ref[...], do_ref[...]
    prod = do.astype(f32) * o_ref[...].astype(f32)
    dqs = []
    for e in range(2):
        qm, dom = half_of(q, e), half_of(do, e)
        s = lax.dot_general(qm, k, NT, preferred_element_type=f32) + bias_ref[e]
        w = jnp.exp(s - lse_ref[0, :, e:e + 1])
        dp = lax.dot_general(dom, v, NT, preferred_element_type=f32)
        inner = jnp.sum(half_of(prod, e), axis=1, keepdims=True)
        g = (w * (dp - inner)).astype(bf16)
        g_ref[e] = g
        dqs.append(jnp.dot(g, k, preferred_element_type=f32))
        dvt[...] += jnp.dot(dom.T, w.astype(bf16), preferred_element_type=f32)
        dkt[...] += jnp.dot(qm.T, g, preferred_element_type=f32)
    dqkv[rows, 0:128] = join(*dqs).astype(bf16)

    @pl.when(last_tile)
    def _():
        dqkv[:, 128:256] = dkt[...].T.astype(bf16)
        dqkv[:, 256:384] = dvt[...].T.astype(bf16)

        @pl.loop(0, n // TILE)
        def _(t):
            r = pl.ds(pl.multiple_of(t * TILE, TILE), TILE)
            part = jnp.dot(turned[r, :], dqkv[...], preferred_element_type=f32).astype(bf16)
            dwq_ref[r, :], dwk_ref[r, :], dwv_ref[r, :] = part[:, 0:128], part[:, 128:256], part[:, 256:384]
            weights = jnp.concatenate([wq_ref[...], wk_ref[...], wv_ref[...]], axis=1)
            dx[r, :] += lax.dot_general(dqkv[r, :], weights, NT, preferred_element_type=f32)

        @pl.when(last)
        def _():
            dx_ref[...] = dx[...].astype(bf16)


def bwd_kernel(pairs, tiles, G, halves, count, *refs):
    ins, parts = refs[:11], refs[11:11 + count]
    mid = refs[11 + count:16 + count]
    outs, accs, sems = refs[16 + count:16 + 2 * count], refs[16 + 2 * count:21 + 2 * count], refs[21 + 2 * count:]
    p, i = pl.program_id(0), pl.program_id(1)
    comm = Scatter(G, halves, parts, outs, *sems)
    beside(comm.events(), G, pairs * tiles, p * tiles + i,
           lambda: bwd_tile(p, i, i == tiles - 1, p == pairs - 1, *ins, *mid, *accs))


def shard_shapes(parts, wide):
    return tuple(jax.ShapeDtypeStruct((p.shape[0] // wide, p.shape[1]), f32) for p in parts)


def attn_bwd_and_scatter(qkv, bias, o, do, lse, normed, w, parts, halves, wide, cid, tq=256):
    n, width, d = qkv.shape[0], qkv.shape[1] // 3, normed.shape[1]
    pairs, tiles, count, G = width // 128, n // tq, len(parts), wide // 4
    sds = jax.ShapeDtypeStruct
    tile = pl.BlockSpec((tq, 128), lambda p, i: (i, p))
    full = lambda rows, k: pl.BlockSpec((rows, 128), lambda p, i: (0, p + k * pairs))
    const = lambda s: pl.BlockSpec(s, lambda p, i: (0, 0))
    outs = pl.pallas_call(functools.partial(bwd_kernel, pairs, tiles, G, halves, count), grid=(pairs, tiles),
        out_shape=(sds((2 * pairs, n, n), bf16),) + (sds((d, width), bf16),) * 3 + (sds((n, d), bf16),) + shard_shapes(parts, wide),
        in_specs=[tile, full(n, 1), full(n, 2), pl.BlockSpec((2, tq, n), lambda p, i: (p, i, 0)), tile, tile,
                  pl.BlockSpec((1, tq, 2), lambda p, i: (p, i, 0)), const((n, d)), full(d, 0), full(d, 1), full(d, 2)] + [ANY] * count,
        out_specs=(pl.BlockSpec((2, tq, n), lambda p, i: (p, i, 0)),) + (full(d, 0),) * 3 + (const((n, d)),) + (whole_vmem(),) * count,
        scratch_shapes=[pltpu.VMEM((128, n), f32), pltpu.VMEM((128, n), f32), pltpu.VMEM((n, 384), bf16), pltpu.VMEM((d, n), bf16),
                        pltpu.VMEM((n, d), f32)] + scatter_scratch(G, halves, parts[0].shape[0] // wide),
        compiler_params=params(cid), name="attention_back_scatter")(
            qkv, qkv, qkv, bias, o, do, lse, normed, w, w, w, *[spread(p, wide) for p in parts])
    return outs[:5], outs[5:]


def hist_tile(first, heads, rows, n, g_ref, ids_ref, out_ref, gs):
    @pl.when(first)
    def _():
        out_ref[...] = jnp.zeros_like(out_ref)

    for h in range(heads):
        for c in range(n // 128):
            gs[c, h * rows:(h + 1) * rows, :] = g_ref[h, :, c * 128:(c + 1) * 128].astype(f32)
    label = lax.broadcasted_iota(jnp.int32, (32, n), 0).astype(bf16)
    one, zero = jnp.ones((32, n), bf16), jnp.zeros((32, n), bf16)
    acc = jnp.zeros((heads, 96), f32)
    for r in range(rows):
        grow = jnp.concatenate([gs[c, pl.ds(r, heads, stride=rows), :] for c in range(n // 128)], axis=1).astype(bf16)
        hots = []
        for t in range(3):
            row = jnp.broadcast_to(ids_ref[t, r:r + 1, :], (32, n)).astype(bf16)
            hots.append(jnp.where(row == label, one, zero))
        acc = acc + lax.dot_general(grow, jnp.concatenate(hots, axis=0), NT, preferred_element_type=f32)
    out_ref[...] += acc


def hist_kernel(heads, rows, n, G, halves, count, *refs):
    (g_ref, ids_ref, dx, tok, gh, gain_ref, gain_two), parts = refs[:7], refs[7:7 + count]
    small_ref, gt_ref = refs[7 + count:9 + count]
    outs, rest = refs[9 + count:9 + 2 * count], refs[9 + 2 * count:]
    (gs, table, got, pair_sem), sums, sems = rest[:4], rest[4:11], rest[11:]
    acc = sums[0]
    now, steps = pl.program_id(0), n // rows
    core = lax.axis_index("narrow")
    mine = tok.shape[0]
    d = tok.shape[1]
    comm = Scatter(G, halves, parts, outs, *sems)
    swap = lambda: remote(dx.at[pl.ds(pl.multiple_of((1 - core) * mine, mine), mine)], got, pair_sem.at[0], pair_sem.at[1], {"narrow": 1 - core})

    def compute():
        @pl.when(now == 0)
        def _():
            swap().start()
            acc[0] = jnp.zeros(acc.shape[1:], f32)
            for k in range(d // 128):
                acc[0, d // 128 + k:d // 128 + k + 1, :] = gain_two[:, k * 128:(k + 1) * 128]

        @pl.when(now == steps // 8)
        def _():
            swap().wait()

        for t in range(mine // TILE):
            @pl.when(now == steps // 8 + t)
            def _():
                r = pl.ds(t * TILE, TILE)
                x = tok[r, :].astype(f32)
                total = dx[pl.ds(pl.multiple_of(core * mine + t * TILE, TILE), TILE), :].astype(f32) + got[r, :].astype(f32)
                factor = lax.rsqrt(jnp.mean(x * x, axis=1, keepdims=True) + epsilon)
                unit = x * factor
                scaled = gain_ref[...] * total
                gt_ref[r, :] = gh[r, :] + factor * (scaled - unit * jnp.mean(scaled * unit, axis=1, keepdims=True))
                gain = jnp.sum(total * unit, axis=0, keepdims=True)
                for k in range(d // 128):
                    acc[0, k:k + 1, :] += gain[:, k * 128:(k + 1) * 128]

        hist_tile(now == 0, heads, rows, n, g_ref, ids_ref, table, gs)

    def reduce():
        acc[0, pl.ds(pl.multiple_of(2 * (d // 128) + core * heads, 8), heads), 0:96] = table[...]
        small_ref[...] = sum_everywhere(G, *sums)

    beside(comm.events(1), G, steps, now, compute, (reduce,))


def hist_and_scatter(g, ids, dx, tok, gh, gain, gain_two, parts, halves, wide, cid):
    heads, n, _ = g.shape
    rows, count, G, d = 16, len(parts), wide // 4, tok.shape[1]
    small = 2 * (d // 128) + 2 * heads
    sds = jax.ShapeDtypeStruct
    const = lambda s: pl.BlockSpec(s, lambda i: (0, 0))
    outs = pl.pallas_call(functools.partial(hist_kernel, heads, rows, n, G, halves, count), grid=(n // rows,),
        out_shape=(sds((small, 128), f32), sds(tok.shape, f32)) + shard_shapes(parts, wide),
        in_specs=[pl.BlockSpec((heads, rows, n), lambda i: (0, i, 0)), pl.BlockSpec((3, rows, n), lambda i: (0, i, 0)),
                  const(dx.shape), const(tok.shape), const(gh.shape), const(gain.shape), const(gain_two.shape)] + [ANY] * count,
        out_specs=(const((small, 128)), const(tok.shape)) + (whole_vmem(),) * count,
        scratch_shapes=[pltpu.VMEM((n // 128, heads * rows, 128), f32), pltpu.VMEM((heads, 96), f32), pltpu.VMEM(tok.shape, bf16), D((2,))]
        + sum_scratch(G, small) + scatter_scratch(G, halves, parts[0].shape[0] // wide),
        compiler_params=params(cid), name="table_grad_scatter")(g, ids, dx, tok, gh, gain, gain_two, *[spread(p, wide) for p in parts])
    return outs[0], outs[1], outs[2:]


D = pltpu.SemaphoreType.DMA


def place():
    me = lax.axis_index("wide")
    return me // 4, (me // 2) % 2, me % 2


def wide_id(z, y, x):
    return {"wide": z * 4 + y * 2 + x}


def remote(src, dst, send, recv, target):
    return pltpu.make_async_remote_copy(src_ref=src, dst_ref=dst, send_sem=send, recv_sem=recv, device_id=target, device_id_type=MESH)


def greet(G, far, pair=0):
    z, y, x = place()
    bar = pltpu.get_barrier_semaphore()
    sig = lambda t: pl.semaphore_signal(bar, inc=1, device_id=t, device_id_type=MESH)
    sig(wide_id(z, 1 - y, x))
    sig(wide_id(z, y, 1 - x))
    if pair:
        sig({"narrow": 1 - lax.axis_index("narrow")})
    if far:
        for k in range(1, G):
            sig(wide_id((z + k) % G, y, x))
        pl.semaphore_wait(bar, 2 + pair + G - 1)
    else:
        @pl.when(z > 0)
        def _():
            sig(wide_id(z - 1, y, x))

        @pl.when(z < G - 1)
        def _():
            sig(wide_id(z + 1, y, x))

        pl.semaphore_wait(bar, 2 + pair + (z > 0).astype(jnp.int32) + (z < G - 1).astype(jnp.int32))


class Gather:
    def __init__(self, G, halves, srcs, outs, local_sem, zs, zr, ns, nr):
        self.G, self.halves, self.srcs, self.outs, self.local_sem = G, halves, srcs, outs, local_sem
        self.zs, self.zr, self.ns, self.nr = zs, zr, ns, nr
        self.most = max(len(h) for h in halves)
        self.z, self.y, self.x = place()

    def hop(self, own, zz, yy, xx, h, way, j):
        target = wide_id(self.z, 1 - self.y, self.x) if way == "y" else wide_id(self.z, self.y, 1 - self.x)
        copies = []
        for n, (a, c, w) in enumerate(self.halves[h]):
            slot = (zz * 6 + j) * self.most + n
            dst = self.outs[a].at[zz, yy, xx, :, pl.ds(c, w)]
            copies.append(remote(self.srcs[a].at[:, pl.ds(c, w)] if own else dst, dst, self.ns.at[slot], self.nr.at[slot], target))
        return copies

    def second_stage(self, zz, own=False):
        return self.hop(own, zz, self.y, self.x, 0, "y", 0) + self.hop(own, zz, self.y, self.x, 1, "x", 1)

    def third_stage(self, zz, own=False):
        return self.hop(own, zz, self.y, self.x, 0, "x", 2) + self.hop(own, zz, self.y, self.x, 1, "y", 3)

    def last_stage(self, zz):
        return self.hop(False, zz, 1 - self.y, self.x, 0, "x", 4) + self.hop(False, zz, self.y, 1 - self.x, 1, "y", 5)

    def relay(self, own, zz, step, way):
        copies = []
        for a in range(len(self.srcs)):
            slot = (way * (self.G - 1) + step) * len(self.srcs) + a
            dst = self.outs[a].at[zz, self.y, self.x]
            copies.append(remote(self.srcs[a] if own else dst, dst, self.zs.at[slot], self.zr.at[slot],
                                 wide_id(self.z + (1 if way == 0 else -1), self.y, self.x)))
        return copies

    def can(self, way):
        return self.z < self.G - 1 if way == 0 else self.z > 0

    def source(self, d, way):
        return (self.z - d, self.z - d >= 0) if way == 0 else (self.z + d, self.z + d < self.G)

    def keep(self):
        return [pltpu.make_async_copy(s, o.at[self.z, self.y, self.x], self.local_sem.at[a]) for a, (s, o) in enumerate(zip(self.srcs, self.outs))]

    def begin(self):
        for way in range(2):
            @pl.when(self.can(way))
            def _():
                for c in self.relay(True, self.z, 0, way):
                    c.start()
        for c in self.second_stage(self.z, True) + self.third_stage(self.z, True) + self.keep():
            c.start()

    def turn(self, zz):
        for c in self.hop(False, zz, 1 - self.y, self.x, 0, "y", 0) + self.hop(False, zz, self.y, 1 - self.x, 1, "x", 1):
            c.wait_recv()
        for c in self.last_stage(zz):
            c.start()

    def step(self, d):
        for way in range(2):
            zz, there = self.source(d, way)

            @pl.when(there)
            def _():
                for c in self.relay(False, zz, d - 1, way):
                    c.wait_recv()

                @pl.when(self.can(way))
                def _():
                    for c in self.relay(False, zz, d, way):
                        c.start()

                for c in self.second_stage(zz):
                    c.start()
        for way in range(2):
            zz, there = self.source(d, way)

            @pl.when(there)
            def _():
                for c in self.third_stage(zz):
                    c.start()

    def turns(self, d):
        if d == 0:
            self.turn(self.z)
            return
        for way in range(2):
            zz, there = self.source(d, way)

            @pl.when(there)
            def _():
                self.turn(zz)

    def finish(self):
        y, x = self.y, self.x

        @pl.loop(0, self.G)
        def _(zz):
            for c in (self.hop(False, zz, y, 1 - x, 0, "x", 2) + self.hop(False, zz, 1 - y, x, 1, "y", 3)
                      + self.hop(False, zz, 1 - y, 1 - x, 0, "x", 4) + self.hop(False, zz, 1 - y, 1 - x, 1, "y", 5)):
                c.wait_recv()
            for c in self.second_stage(zz) + self.third_stage(zz) + self.last_stage(zz):
                c.wait_send()

        for way in range(2):
            @pl.when(self.can(way))
            def _():
                for c in self.relay(True, self.z, 0, way):
                    c.wait_send()
                for d in range(1, self.G - 1):
                    zz, there = self.source(d, way)

                    @pl.when(there)
                    def _():
                        for c in self.relay(False, zz, d, way):
                            c.wait_send()
        for c in self.keep():
            c.wait()

    def events(self):
        G = self.G
        first = lambda: (greet(G, False), self.begin())
        ev = [(0.0, first), (0.7, lambda: self.turns(0))]
        for d in range(1, G):
            ev += [(1.15 * d, functools.partial(self.step, d)), (1.3 * d + 1.2, functools.partial(self.turns, d))]
        return sorted(ev, key=lambda e: e[0]), self.finish


def gather_scratch(G, halves, arrays):
    most = max(len(h) for h in halves)
    return [D((arrays,)), D((2 * (G - 1) * arrays,)), D((2 * (G - 1) * arrays,)), D((6 * G * most,)), D((6 * G * most,))]


class Scatter:
    def __init__(self, G, halves, parts, outs, r1a, r1b, o1a, o1b, r2a, r2b, r3, own, lsem, s1, v1, s2, v2, s3, v3):
        self.__dict__.update(locals())
        self.most = max(len(h) for h in halves)
        self.wa, self.wb = [sum(p[2] for p in h) for h in halves]
        self.R = parts[0].shape[3]
        self.z, self.y, self.x = place()
        self.order = sorted(range(1, G), key=lambda k: min(k, G - k), reverse=True) + [0]

    def zk(self, k):
        return (self.z + k) % self.G

    def neighbour(self, way):
        return wide_id(self.z, 1 - self.y, self.x) if way == "y" else wide_id(self.z, self.y, 1 - self.x)

    def pieces(self, h):
        at, out = 0, []
        for n, (a, c, w) in enumerate(self.halves[h]):
            out.append((n, a, pl.ds(c, w), pl.ds(at, w)))
            at += w
        return out

    def one(self, k):
        z, cs = self.zk(k), []
        for n, a, src, dst in self.pieces(0):
            slot = (2 * k) * self.most + n
            cs.append(remote(self.parts[a].at[z, :, 1 - self.x, :, src], self.r1a.at[k, :, :, dst], self.s1.at[slot], self.v1.at[slot], self.neighbour("x")))
        for n, a, src, dst in self.pieces(1):
            slot = (2 * k + 1) * self.most + n
            cs.append(remote(self.parts[a].at[z, 1 - self.y, :, :, src], self.r1b.at[k, :, :, dst], self.s1.at[slot], self.v1.at[slot], self.neighbour("y")))
        return cs

    def load(self, k):
        z, cs = self.zk(k), []
        for n, a, src, dst in self.pieces(0):
            cs.append(pltpu.make_async_copy(self.parts[a].at[z, :, self.x, :, src], self.o1a.at[k, :, :, dst], self.lsem.at[(2 * k) * self.most + n]))
        for n, a, src, dst in self.pieces(1):
            cs.append(pltpu.make_async_copy(self.parts[a].at[z, self.y, :, :, src], self.o1b.at[k, :, :, dst], self.lsem.at[(2 * k + 1) * self.most + n]))
        return cs

    def two(self, k):
        return [remote(self.o1a.at[k, 1 - self.y], self.r2a.at[k], self.s2.at[2 * k], self.v2.at[2 * k], self.neighbour("y")),
                remote(self.o1b.at[k, 1 - self.x], self.r2b.at[k], self.s2.at[2 * k + 1], self.v2.at[2 * k + 1], self.neighbour("x"))]

    def three(self, k):
        return remote(self.own.at[k], self.r3.at[k - 1], self.s3.at[k - 1], self.v3.at[k - 1], wide_id(self.zk(k), self.y, self.x))

    def launch(self, k):
        for c in self.one(k) + self.load(k):
            c.start()

    def begin(self):
        for k in self.order[:2]:
            self.launch(k)

    def rows(self, count, body):
        step = min(16, count)

        @pl.loop(0, count // step)
        def _(i):
            body(pl.ds(pl.multiple_of(i * step, step), step))

    def add_one(self, n):
        k = self.order[n]
        for c in self.one(k):
            c.wait_recv()
        for c in self.load(k):
            c.wait()
        for mine, got in ((self.o1a, self.r1a), (self.o1b, self.r1b)):
            def body(r):
                for j in range(2):
                    mine[k, j, r, :] = (mine[k, j, r, :].astype(f32) + got[k, j, r, :].astype(f32)).astype(bf16)

            self.rows(self.R, body)
        for c in self.two(k):
            c.start()
        if n + 2 < self.G:
            self.launch(self.order[n + 2])

    def add_two(self, n):
        k = self.order[n]
        for c in self.two(k):
            c.wait_recv()

        def body(r):
            self.own[k, r, pl.ds(0, self.wa)] = (self.o1a[k, self.y, r, :].astype(f32) + self.r2a[k, r, :].astype(f32)).astype(bf16)
            self.own[k, r, pl.ds(self.wa, self.wb)] = (self.o1b[k, self.x, r, :].astype(f32) + self.r2b[k, r, :].astype(f32)).astype(bf16)

        self.rows(self.R, body)
        if k:
            self.three(k).start()

    def finish(self):
        self.add_two(self.G - 1)
        for k in range(1, self.G):
            self.three(k).wait_recv()

        def body(r):
            for h in range(2):
                for _, a, src, dst in self.pieces(h):
                    cols = pl.ds(dst.start + h * self.wa, dst.size)
                    total = self.own[0, r, cols].astype(f32)
                    for k in range(self.G - 1):
                        total = total + self.r3[k, r, cols].astype(f32)
                    self.outs[a][r, src] = total

        self.rows(self.R, body)
        for k in range(self.G):
            for c in self.one(k) + self.two(k):
                c.wait_send()
            if k:
                self.three(k).wait_send()

    def events(self, pair=0):
        G = self.G
        first = lambda: (greet(G, True, pair), self.begin())
        ev = [(0.0, first), (1.1, lambda: self.add_one(0))]
        for n in range(1, G):
            ev += [(1.5 * n + 0.65, functools.partial(self.add_one, n)), (1.5 * n + 1.1, functools.partial(self.add_two, n - 1))]
        return sorted(ev, key=lambda e: e[0]), self.finish


def scatter_scratch(G, halves, R):
    most = max(len(h) for h in halves)
    a, b = [sum(p[2] for p in h) for h in halves]
    V = lambda *s: pltpu.VMEM(s, bf16)
    return [V(G, 2, R, a), V(G, 2, R, b), V(G, 2, R, a), V(G, 2, R, b), V(G, R, a), V(G, R, b), V(G - 1, R, a + b), V(G, R, a + b),
            D((2 * G * most,)), D((2 * G * most,)), D((2 * G * most,)), D((2 * G,)), D((2 * G,)), D((G - 1,)), D((G - 1,))]


def beside(plan, G, steps, now, compute, late=()):
    events, finish = plan
    units = 1.55 * G
    for n in range(steps):
        here = [act for t, act in events if min(steps - 1, int(-(-t * steps // units))) == n]
        if here:
            @pl.when(now == n)
            def _():
                for act in here:
                    act()
    compute()

    @pl.when(now == steps - 1)
    def _():
        for act in late:
            act()
        finish()


ANY = pl.BlockSpec(memory_space=pl.ANY)


def whole_vmem():
    return pl.BlockSpec(memory_space=pltpu.VMEM)


def spread(a, wide):
    return a.reshape(wide // 4, 2, 2, a.shape[0] // wide, a.shape[1])


def gathered_shapes(shards, wide):
    return tuple(jax.ShapeDtypeStruct((wide // 4, 2, 2) + s.shape, s.dtype) for s in shards)


def flat(a):
    return a.reshape(-1, a.shape[-1])


def sum_everywhere(G, acc, got, gz, s, v, sz, vz):
    z, y, x = place()
    core = {"narrow": 1 - lax.axis_index("narrow")}
    for n, t in enumerate((core, wide_id(z, y, 1 - x), wide_id(z, 1 - y, x))):
        c = remote(acc.at[n], got.at[n], s.at[n], v.at[n], t)
        c.start()
        c.wait()
        acc[n + 1] = acc[n] + got[n]
    gz[z] = acc[3]
    far = [wide_id((z + k) % G, y, x) for k in range(1, G)]
    sent = [remote(acc.at[3], gz.at[z], sz.at[k], vz.at[z], t) for k, t in enumerate(far)]
    for c in sent:
        c.start()
    for k in range(1, G):
        zz = (z + k) % G
        remote(acc.at[3], gz.at[zz], sz.at[k - 1], vz.at[zz], far[k - 1]).wait_recv()
    for c in sent:
        c.wait_send()
    total = gz[0]
    for k in range(1, G):
        total = total + gz[k]
    return total


def sum_scratch(G, rows):
    V = lambda k: pltpu.VMEM((k, rows, 128), f32)
    return [V(4), V(3), V(G), D((3,)), D((3,)), D((G - 1,)), D((G,))]


def nt(a, b):
    return lax.dot_general(a, b, NT, preferred_element_type=f32)


def nn(a, b):
    return jnp.dot(a, b, preferred_element_type=f32)


def gelu_and_slope(v):
    root = 0.7978845608028654
    square = v * v
    t = jnp.tanh(root * v * (1.0 + 0.044715 * square))
    half = 0.5 * (1.0 + t)
    return v * half, half + 0.5 * v * (1.0 - t * t) * root * (1.0 + 3 * 0.044715 * square)


def mid_kernel(att_h, tok_h, cot_h, wo_h, wg_h, wu_h, wd_h, gain_ref,
               gout_h, gg_h, gu_h, gd_h, y_ref, gh_ref, ga_ref, ggain_ref,
               att, tok, cot, wo, wg, wu, wd, part, other, back, hid, n2, n2t, cott, hff, gg, gu, ysend, yown, yother, stage,
               isem, osem, sp, vp, sb, vb, sy, vy):
    core = lax.axis_index("narrow")
    peer = {"narrow": 1 - core}
    n, d = tok.shape
    ff = wg.shape[1]
    tiles = n // TILE
    half = tiles // 2
    loads = [pltpu.make_async_copy(s, t, isem.at[k]) for k, (s, t) in enumerate(
        [(att_h, att), (wo_h, wo), (tok_h, tok), (wg_h, wg), (wu_h, wu), (wd_h, wd), (cot_h, cot)])]
    for c in loads:
        c.start()
    bar = pltpu.get_barrier_semaphore()
    pl.semaphore_signal(bar, inc=1, device_id=peer, device_id_type=MESH)
    pl.semaphore_wait(bar, 1)
    rows_of = lambda t: pl.ds(pl.multiple_of(t * TILE, TILE), TILE)
    send_part = lambda t: remote(part.at[rows_of(t)], other.at[rows_of(t)], sp.at[t], vp.at[t], peer)
    send_back = lambda t: remote(part.at[rows_of(t)], back.at[rows_of(t)], sb.at[t], vb.at[t], peer)
    send_y = lambda j: remote(ysend.at[rows_of(j)], yother.at[rows_of(j)], sy.at[j], vy.at[j], peer)
    gain = gain_ref[...]

    for c in loads[:2]:
        c.wait()

    @pl.loop(0, tiles)
    def _(t):
        part[rows_of(t), :] = nt(att[rows_of(t), :], wo[...]).astype(bf16)
        send_part(t).start()

    for c in loads[2:]:
        c.wait()

    chunks, at = [], 0
    while at < ff:
        w = min(384, ff - at)
        chunks.append((at, w))
        at += w

    @pl.loop(0, tiles)
    def _(s):
        t = (s + half * (1 - core)) % tiles
        r = rows_of(t)
        send_part(t).wait()
        h = tok[r, :].astype(f32) + (part[r, :].astype(f32) + other[r, :].astype(f32))
        hid[r, :] = h
        factor = lax.rsqrt(jnp.mean(h * h, axis=1, keepdims=True) + epsilon)
        low = (h * factor * gain).astype(bf16)
        n2[r, :] = low
        n2t[:, r] = low.T
        ct = cot[r, :]
        cott[:, r] = ct.T
        for at, w in chunks:
            cols = pl.ds(at, w)
            act, slope = gelu_and_slope(nn(low, wg[:, cols]))
            up = nn(low, wu[:, cols])
            gf = nn(ct, wd[:, cols])
            hff[r, cols] = (act * up).astype(bf16)
            gg[r, cols] = (gf * up * slope).astype(bf16)
            gu[r, cols] = (gf * act).astype(bf16)
        part[r, :] = (nt(gg[r, :], wg[...]) + nt(gu[r, :], wu[...])).astype(bf16)
        send_back(t).start()
        y = nt(hff[r, :], wd[...]).astype(bf16)

        @pl.when(s < half)
        def _():
            ysend[rows_of(s), :] = y
            send_y(s).start()

        @pl.when(s >= half)
        def _():
            yown[rows_of(s - half), :] = y

    def weight_grad(left, right, out, slot, width):
        @pl.loop(0, d // TILE)
        def _(k):
            b = k % 2
            copy = lambda kk: pltpu.make_async_copy(stage.at[kk % 2, :, pl.ds(0, width)], out.at[rows_of(kk)], osem.at[2 * slot + kk % 2])

            @pl.when(k >= 2)
            def _():
                copy(k - 2).wait()

            stage[b, :, pl.ds(0, width)] = nn(left[rows_of(k), :], right[...]).astype(bf16)
            copy(k).start()

        for k in range(d // TILE - 2, d // TILE):
            pltpu.make_async_copy(stage.at[k % 2, :, pl.ds(0, width)], out.at[rows_of(k)], osem.at[2 * slot + k % 2]).wait()

    weight_grad(cott, hff, gd_h, 0, ff)
    ggain_ref[...] = jnp.zeros_like(ggain_ref)

    @pl.loop(0, tiles)
    def _(s):
        t = (s + half * (1 - core)) % tiles
        r = rows_of(t)
        send_back(t).wait()
        total = part[r, :].astype(f32) + back[r, :].astype(f32)
        h = hid[r, :]
        factor = lax.rsqrt(jnp.mean(h * h, axis=1, keepdims=True) + epsilon)
        unit = h * factor
        g = gain * total
        gh = cot[r, :].astype(f32) + factor * (g - unit * jnp.mean(g * unit, axis=1, keepdims=True))
        low = gh.astype(bf16)
        cott[:, r] = low.T
        ga_ref[r, :] = nn(low, wo[...]).astype(bf16)

        @pl.when(s >= half)
        def _():
            j = rows_of(s - half)
            gh_ref[j, :] = gh
            ggain_ref[...] += jnp.sum(total * unit, axis=0, keepdims=True)
            send_y(s - half).wait()
            y_ref[j, :] = (h + (yown[j, :].astype(f32) + yother[j, :].astype(f32))).astype(bf16)

    weight_grad(n2t, gg, gg_h, 1, ff)
    weight_grad(n2t, gu, gu_h, 2, ff)
    weight_grad(cott, att, gout_h, 3, att.shape[1])


def middle(att, tok, cot, wo, wg, wu, wd, gain, cid):
    n, d = tok.shape
    units, ff = att.shape[1], wg.shape[1]
    B = lambda *s: pltpu.VMEM(s, bf16)
    sds = jax.ShapeDtypeStruct
    tiles = n // TILE
    return pl.pallas_call(mid_kernel,
        out_shape=(sds((d, units), bf16), sds((d, ff), bf16), sds((d, ff), bf16), sds((d, ff), bf16),
                   sds((n // 2, d), bf16), sds((n // 2, d), f32), sds((n, units), bf16), sds((1, d), f32)),
        in_specs=[ANY] * 7 + [whole_vmem()], out_specs=(ANY,) * 4 + (whole_vmem(),) * 4,
        scratch_shapes=[B(n, units), B(n, d), B(n, d), B(d, units), B(d, ff), B(d, ff), B(d, ff), B(n, d), B(n, d), B(n, d),
                        pltpu.VMEM((n, d), f32), B(n, d), B(d, n), B(d, n), B(n, ff), B(n, ff), B(n, ff),
                        B(n // 2, d), B(n // 2, d), B(n // 2, d), B(2, TILE, ff),
                        D((7,)), D((8,)), D((tiles,)), D((tiles,)), D((tiles,)), D((tiles,)), D((tiles // 2,)), D((tiles // 2,))],
        compiler_params=params(cid), name="feed_forward")(att, tok, cot, wo, wg, wu, wd, gain)


def local(tokens, cotangent, pages, boxes, gain_attn, gain_ffn, bias_tables, w_query, w_key, w_value, w_out, w_gate, w_up, w_down):
    wide, narrow = lax.axis_size("wide"), lax.axis_size("narrow")
    heads_all = bias_tables.shape[1]
    heads = heads_all // narrow
    core = lax.axis_index("narrow")
    tables = lax.dynamic_slice_in_dim(bias_tables, core * heads, heads, 1)
    inner, ff, d = w_query.shape[1], w_gate.shape[1], tokens.shape[1]
    gain_one, gain_two = gain_attn.astype(f32)[None], gain_ffn.astype(f32)[None]

    all_tokens = lax.all_gather(tokens, "narrow", axis=0, tiled=True)
    all_cot = lax.all_gather(cotangent, "narrow", axis=0, tiled=True)
    early = inner // 4 * 3
    bias, ids, (w_first, full_out, full_gate) = bias_and_gather(
        tables, boxes, pages, [jnp.concatenate([w_query, w_key, w_value], axis=1), w_out.T, w_gate],
        (((2, 0, ff), (0, 0, early)), ((1, 0, inner), (0, early, 3 * inner - early))), wide, 1)
    (attended, lse, normed, qkv), (full_up, full_down) = attn_fwd_and_gather(
        all_tokens, gain_one, w_first, bias, [w_up, w_down.T], (((0, 0, ff),), ((1, 0, ff),)), wide, 2)
    grad_w_out, grad_w_gate, grad_w_up, grad_w_down, output, grad_hidden, grad_attended, grad_gain_two = middle(
        attended, all_tokens, all_cot, full_out, full_gate, full_up, full_down, gain_two, 3)
    (g, grad_w_query, grad_w_key, grad_w_value, grad_normed), (s_down, s_out) = attn_bwd_and_scatter(
        qkv, bias, attended, grad_attended, lse, normed, w_first, [grad_w_down, grad_w_out],
        (((0, 0, 2 * inner),), ((0, 2 * inner, ff - 2 * inner), (1, 0, inner))), wide, 4)
    half = inner // 2
    small, grad_tokens, (s_gate, s_up, s_query, s_key, s_value) = hist_and_scatter(
        g, ids, grad_normed, tokens, grad_hidden, gain_one, grad_gain_two,
        [grad_w_gate, grad_w_up, grad_w_query, grad_w_key, grad_w_value],
        (((0, 0, ff), (2, 0, inner), (3, 0, half)), ((1, 0, ff), (4, 0, inner), (3, half, half))), wide, 5)
    lines = d // 128
    one, two = small[:lines].reshape(d), small[lines:2 * lines].reshape(d)
    table = small[2 * lines:, :bias_tables.shape[0]].T
    return (output, grad_tokens, one, two, table, s_query, s_key, s_value, s_out.T, s_gate, s_up, s_down.T)


def solution(mesh):
    rows, cols, tall = P(("wide", "narrow"), None), P("wide", "narrow"), P("narrow", "wide")
    in_specs = (rows, rows, P("wide"), P(None, "wide"), P(), P(), P(), cols, cols, cols, tall, cols, cols, tall)
    out_specs = (rows, rows, P(), P(), P(), cols, cols, cols, tall, cols, cols, tall)
    return jax.shard_map(local, mesh=mesh, in_specs=in_specs, out_specs=out_specs, check_vma=False)
```

```python
import functools

import jax
import jax.numpy as jnp
from jax import lax
from jax.experimental import pallas as pl
from jax.experimental.pallas import tpu as pltpu
from jax.sharding import PartitionSpec as P

f32, bf16 = jnp.float32, jnp.bfloat16
MESH = pl.DeviceIdType.MESH


EDGES = (1, 2, 3, 4, 5, 6, 7, 8, 12, 16, 23, 32, 46, 64, 91)
NT = (((1,), (1,)), ((), ()))
VM = 58 * 2**20
TABLE_SCALE = 2047.0
TABLE_LIFT = 8192
TILE = 256
epsilon = 1e-06


def params(cid):
    return pltpu.CompilerParams(collective_id=cid, has_side_effects=True, vmem_limit_bytes=VM)


def lane_take(table, idx):
    return jnp.take_along_axis(table, idx, axis=1, mode="promise_in_bounds")


def buckets_of(gap, steps, shift):
    return lane_take(steps, jnp.minimum(jnp.abs(gap) >> shift, EDGES[-1])) + jnp.where(gap > 0, 16, 0)


def bias_tile(start, heads, rows, n, steps_ref, tab_ref, box_col, box_row, page_col, page_row, bias_ref, ids_ref, lin_ids, lin):
    steps = jnp.broadcast_to(steps_ref[...], (rows, 128))
    allowed_col = jnp.broadcast_to(page_col[...] % 2, (rows, 128))
    cols = [jnp.broadcast_to(box_col[:, t:t + 1], (rows, 128)) for t in range(2)]
    pairs = heads // 2
    table = lambda t, p: jnp.broadcast_to(tab_ref[t * pairs + p:t * pairs + p + 1, :], (rows, 128))
    unit = 1.0 / TABLE_SCALE

    @pl.when(start == 0)
    def _():
        @pl.loop(0, 8)
        def _(k):
            ids = buckets_of(lax.broadcasted_iota(jnp.int32, (rows, 128), 1) - lax.broadcasted_iota(jnp.int32, (rows, 128), 0) + (k - 4) * rows, steps, 0)
            lin_ids[k] = ids.astype(f32)
            for p in range(pairs):
                lin[k, p] = lane_take(table(0, p), ids)

    @pl.loop(0, n // 128)
    def _(c):
        lanes = pl.ds(pl.multiple_of(c * 128, 128), 128)
        near = jnp.clip((c * 128 - start) // rows + 4, 0, 7)
        ids = []
        for t in range(2):
            ids.append(buckets_of(jnp.broadcast_to(box_row[t:t + 1, lanes], (rows, 128)) - cols[t], steps, 2))
            ids_ref[t, :, lanes] = ids[t].astype(f32)
        ok = jnp.broadcast_to(page_row[:, lanes], (rows, 128)) == allowed_col
        for p in range(pairs):
            words = lin[near, p] + lane_take(table(1, p), ids[0]) + lane_take(table(2, p), ids[1])
            upper = (words >> 16).astype(f32) * unit
            lower = (words & 0xFFFF).astype(f32) * unit - 3 * TABLE_LIFT * unit
            bias_ref[2 * p, :, lanes] = jnp.where(ok, upper, -1e30)
            bias_ref[2 * p + 1, :, lanes] = jnp.where(ok, lower, -1e30)


def bias_gather_kernel(heads, rows, n, G, halves, count, *refs):
    ins, srcs = refs[:6], refs[6:6 + count]
    bias_ref, ids_ref, lin_ids = refs[6 + count:9 + count]
    outs, lin, sems = refs[9 + count:9 + 2 * count], refs[9 + 2 * count], refs[10 + 2 * count:]
    now = pl.program_id(0)
    comm = Gather(G, halves, srcs, outs, *sems)
    beside(comm.events(), G, n // rows, now, lambda: bias_tile(now * rows, heads, rows, n, *ins, bias_ref, ids_ref, lin_ids, lin))


def bias_and_gather(tables, boxes, pages, shards, halves, wide, cid):
    heads, n, G, rows = tables.shape[1], pages.shape[0], wide // 4, 64
    fixed = jnp.round(tables.astype(f32) * TABLE_SCALE).astype(jnp.int32).reshape(3, 32, heads // 2, 2)
    words = fixed[..., 0] * 65536 + fixed[..., 1] + TABLE_LIFT
    tab = jnp.pad(words.transpose(0, 2, 1).reshape(3 * heads // 2, 32), ((0, 0), (0, 96)))
    lane = jnp.arange(128, dtype=jnp.int32)
    steps = sum([(lane >= e).astype(jnp.int32) for e in EDGES])[None]
    count = len(shards)
    outs = pl.pallas_call(functools.partial(bias_gather_kernel, heads, rows, n, G, halves, count),
        grid=(n // rows,),
        out_shape=(jax.ShapeDtypeStruct((heads, n, n), f32), jax.ShapeDtypeStruct((2, n, n), f32), jax.ShapeDtypeStruct((8, rows, 128), f32)) + gathered_shapes(shards, wide),
        in_specs=[pl.BlockSpec((1, 128), lambda i: (0, 0)), pl.BlockSpec((3 * heads // 2, 128), lambda i: (0, 0)),
                  pl.BlockSpec((rows, 2), lambda i: (i, 0)), pl.BlockSpec((2, n), lambda i: (0, 0)),
                  pl.BlockSpec((rows, 1), lambda i: (i, 0)), pl.BlockSpec((1, n), lambda i: (0, 0))] + [ANY] * count,
        out_specs=(pl.BlockSpec((heads, rows, n), lambda i: (0, i, 0)), pl.BlockSpec((2, rows, n), lambda i: (0, i, 0)),
                   pl.BlockSpec((8, rows, 128), lambda i: (0, 0, 0))) + (ANY,) * count,
        scratch_shapes=[pltpu.VMEM((8, heads // 2, rows, 128), jnp.int32)] + gather_scratch(G, halves, count),
        compiler_params=params(cid), name="layout_bias_gather")(
            steps, tab, boxes.T, boxes, pages[:, None], pages[None], *shards)
    return outs[0], outs[1:3], outs[3:]


def half_of(v, e):
    lane = lax.broadcasted_iota(jnp.int32, v.shape, 1)
    return jnp.where((lane >= 64) == (e == 1), v, jnp.zeros_like(v))


def join(a, b):
    lane = lax.broadcasted_iota(jnp.int32, a.shape, 1)
    return jnp.where(lane < 64, a, b)


def project(tok_ref, gain_ref, w_ref, normed, qkv):
    gain = gain_ref[...]

    @pl.loop(0, tok_ref.shape[0] // TILE)
    def _(t):
        r = pl.ds(pl.multiple_of(t * TILE, TILE), TILE)
        x = tok_ref[r, :].astype(f32)
        low = (x * lax.rsqrt(jnp.mean(x * x, axis=1, keepdims=True) + epsilon) * gain).astype(bf16)
        normed[r, :] = low
        qkv[r, :] = jnp.dot(low, w_ref[...], preferred_element_type=f32).astype(bf16)


def fwd_tile(p, i, tq, pairs, qkv, bias_ref, o_ref, lse_ref):
    cols = lambda k: pl.ds(pl.multiple_of((p + k * pairs) * 128, 128), 128)
    q, k, v = qkv[pl.ds(pl.multiple_of(i * tq, tq), tq), cols(0)], qkv[:, cols(1)], qkv[:, cols(2)]
    outs, lses = [], []
    for e in range(2):
        s = lax.dot_general(half_of(q, e), k, NT, preferred_element_type=f32) + bias_ref[e]
        peak = jnp.max(s, axis=1, keepdims=True)
        w = jnp.exp(s - peak)
        total = jnp.sum(w, axis=1, keepdims=True)
        outs.append(jnp.dot(w.astype(bf16), v, preferred_element_type=f32) / total)
        lses.append(peak + jnp.log(total))
    o_ref[...] = join(*outs).astype(bf16)
    lse_ref[0] = jnp.concatenate(lses, axis=1)


def fwd_kernel(pairs, tiles, G, halves, count, *refs):
    (tok, gain, w, bias_ref), srcs = refs[:4], refs[4:4 + count]
    o_ref, lse_ref, normed_h, qkv_h = refs[4 + count:8 + count]
    outs, (normed, qkv, keep), sems = refs[8 + count:8 + 2 * count], refs[8 + 2 * count:11 + 2 * count], refs[11 + 2 * count:]
    p, i = pl.program_id(0), pl.program_id(1)
    now, steps = p * tiles + i, pairs * tiles
    copies = lambda: [pltpu.make_async_copy(normed, normed_h, keep.at[0]), pltpu.make_async_copy(qkv, qkv_h, keep.at[1])]

    def compute():
        @pl.when(now == 0)
        def _():
            project(tok, gain, w, normed, qkv)
            for c in copies():
                c.start()

        fwd_tile(p, i, o_ref.shape[0], pairs, qkv, bias_ref, o_ref, lse_ref)

        @pl.when(now == steps - 1)
        def _():
            for c in copies():
                c.wait()

    beside(Gather(G, halves, srcs, outs, *sems).events(), G, steps, now, compute)


def attn_fwd_and_gather(tok, gain, w, bias, shards, halves, wide, cid, tq=256):
    n, d = tok.shape
    width = w.shape[1] // 3
    pairs, tiles, count, G = width // 128, n // tq, len(shards), wide // 4
    sds = jax.ShapeDtypeStruct
    const = lambda s: pl.BlockSpec(s, lambda p, i: (0, 0))
    outs = pl.pallas_call(functools.partial(fwd_kernel, pairs, tiles, G, halves, count), grid=(pairs, tiles),
        out_shape=(sds((n, width), bf16), sds((pairs, n, 2), f32), sds((n, d), bf16), sds((n, 3 * width), bf16)) + gathered_shapes(shards, wide),
        in_specs=[const((n, d)), const((1, d)), const(w.shape), pl.BlockSpec((2, tq, n), lambda p, i: (p, i, 0))] + [ANY] * count,
        out_specs=(pl.BlockSpec((tq, 128), lambda p, i: (i, p)), pl.BlockSpec((1, tq, 2), lambda p, i: (p, i, 0)), ANY, ANY) + (ANY,) * count,
        scratch_shapes=[pltpu.VMEM((n, d), bf16), pltpu.VMEM((n, 3 * width), bf16), D((2,))] + gather_scratch(G, halves, count),
        compiler_params=params(cid), name="attention_gather")(tok, gain, w, bias, *shards)
    return outs[:4], outs[4:]


def band_sums(i, e, g_ref, band_ref, far_ref):
    tq, n = g_ref.shape[1], g_ref.shape[2]
    first = i * (tq // 128) - 1

    @pl.when(i == 0)
    def _():
        band_ref[e] = jnp.zeros(band_ref.shape[1:], f32)
        far_ref[e] = jnp.zeros(far_ref.shape[1:], f32)

    for m in range(tq // 128 + 2):
        @pl.when((first + m >= 0) & (first + m < n // 128))
        def _():
            band_ref[e, :, m * 128:(m + 1) * 128] += g_ref[e, :, pl.ds(pl.multiple_of((first + m) * 128, 128), 128)].astype(f32)

    for c in range(n // 128):
        @pl.when((c < first) | (c > first + tq // 128 + 1))
        def _():
            total = g_ref[e, 0:16, c * 128:(c + 1) * 128].astype(f32)
            for k in range(1, tq // 16):
                total = total + g_ref[e, k * 16:(k + 1) * 16, c * 128:(c + 1) * 128].astype(f32)
            far_ref[e, jnp.where(c < first, 0, 1)] += total


def bwd_tile(p, i, last_tile, last, q_ref, k_ref, v_ref, bias_ref, o_ref, do_ref, lse_ref, normed_ref, wq_ref, wk_ref, wv_ref,
             g_ref, band_ref, far_ref, dwq_ref, dwk_ref, dwv_ref, dx_ref, dkt, dvt, dqkv, turned, dx):
    tq, n = q_ref.shape[0], k_ref.shape[0]
    rows = pl.ds(pl.multiple_of(i * tq, tq), tq)

    @pl.when(p == 0)
    def _():
        turned[:, rows] = normed_ref[rows, :].T
        dx[rows, :] = jnp.zeros((tq, dx.shape[1]), f32)

    @pl.when(i == 0)
    def _():
        dkt[...] = jnp.zeros_like(dkt)
        dvt[...] = jnp.zeros_like(dvt)

    q, k, v, do = q_ref[...], k_ref[...], v_ref[...], do_ref[...]
    prod = do.astype(f32) * o_ref[...].astype(f32)
    dqs = []
    for e in range(2):
        qm, dom = half_of(q, e), half_of(do, e)
        s = lax.dot_general(qm, k, NT, preferred_element_type=f32) + bias_ref[e]
        w = jnp.exp(s - lse_ref[0, :, e:e + 1])
        dp = lax.dot_general(dom, v, NT, preferred_element_type=f32)
        inner = jnp.sum(half_of(prod, e), axis=1, keepdims=True)
        g = (w * (dp - inner)).astype(bf16)
        g_ref[e] = g
        dqs.append(jnp.dot(g, k, preferred_element_type=f32))
        dvt[...] += jnp.dot(dom.T, w.astype(bf16), preferred_element_type=f32)
        dkt[...] += jnp.dot(qm.T, g, preferred_element_type=f32)
        band_sums(i, e, g_ref, band_ref, far_ref)
    dqkv[rows, 0:128] = join(*dqs).astype(bf16)

    @pl.when(last_tile)
    def _():
        dqkv[:, 128:256] = dkt[...].T.astype(bf16)
        dqkv[:, 256:384] = dvt[...].T.astype(bf16)

        @pl.loop(0, n // TILE)
        def _(t):
            r = pl.ds(pl.multiple_of(t * TILE, TILE), TILE)
            part = jnp.dot(turned[r, :], dqkv[...], preferred_element_type=f32).astype(bf16)
            dwq_ref[r, :], dwk_ref[r, :], dwv_ref[r, :] = part[:, 0:128], part[:, 128:256], part[:, 256:384]
            weights = jnp.concatenate([wq_ref[...], wk_ref[...], wv_ref[...]], axis=1)
            dx[r, :] += lax.dot_general(dqkv[r, :], weights, NT, preferred_element_type=f32)

        @pl.when(last)
        def _():
            dx_ref[...] = dx[...].astype(bf16)


def bwd_kernel(pairs, tiles, G, halves, count, *refs):
    ins, parts = refs[:11], refs[11:11 + count]
    mid = refs[11 + count:18 + count]
    outs, accs, sems = refs[18 + count:18 + 2 * count], refs[18 + 2 * count:23 + 2 * count], refs[23 + 2 * count:]
    p, i = pl.program_id(0), pl.program_id(1)
    comm = Scatter(G, halves, parts, outs, *sems)
    beside(comm.events(), G, pairs * tiles, p * tiles + i,
           lambda: bwd_tile(p, i, i == tiles - 1, p == pairs - 1, *ins, *mid, *accs))


def shard_shapes(parts, wide):
    return tuple(jax.ShapeDtypeStruct((p.shape[0] // wide, p.shape[1]), f32) for p in parts)


def attn_bwd_and_scatter(qkv, bias, o, do, lse, normed, w, parts, halves, wide, cid, tq=256):
    n, width, d = qkv.shape[0], qkv.shape[1] // 3, normed.shape[1]
    pairs, tiles, count, G = width // 128, n // tq, len(parts), wide // 4
    sds = jax.ShapeDtypeStruct
    tile = pl.BlockSpec((tq, 128), lambda p, i: (i, p))
    full = lambda rows, k: pl.BlockSpec((rows, 128), lambda p, i: (0, p + k * pairs))
    const = lambda s: pl.BlockSpec(s, lambda p, i: (0, 0))
    outs = pl.pallas_call(functools.partial(bwd_kernel, pairs, tiles, G, halves, count), grid=(pairs, tiles),
        out_shape=(sds((2 * pairs, n, n), bf16), sds((2 * pairs, tq, tq + 256), f32), sds((2 * pairs, 2, 16, 128), f32)) + (sds((d, width), bf16),) * 3 + (sds((n, d), bf16),) + shard_shapes(parts, wide),
        in_specs=[tile, full(n, 1), full(n, 2), pl.BlockSpec((2, tq, n), lambda p, i: (p, i, 0)), tile, tile,
                  pl.BlockSpec((1, tq, 2), lambda p, i: (p, i, 0)), const((n, d)), full(d, 0), full(d, 1), full(d, 2)] + [ANY] * count,
        out_specs=(pl.BlockSpec((2, tq, n), lambda p, i: (p, i, 0)), pl.BlockSpec((2, tq, tq + 256), lambda p, i: (p, 0, 0)),
                   pl.BlockSpec((2, 2, 16, 128), lambda p, i: (p, 0, 0, 0))) + (full(d, 0),) * 3 + (const((n, d)),) + (whole_vmem(),) * count,
        scratch_shapes=[pltpu.VMEM((128, n), f32), pltpu.VMEM((128, n), f32), pltpu.VMEM((n, 384), bf16), pltpu.VMEM((d, n), bf16),
                        pltpu.VMEM((n, d), f32)] + scatter_scratch(G, halves, parts[0].shape[0] // wide),
        compiler_params=params(cid), name="attention_back_scatter")(
            qkv, qkv, qkv, bias, o, do, lse, normed, w, w, w, *parts)
    return outs[:7], outs[7:]


def rows_times_hots(src, ids, rows, heads, gs):
    n = src(0).shape[1]
    for h in range(heads):
        block = src(h)
        for c in range(n // 128):
            gs[c, h * rows:(h + 1) * rows, :] = block[:, c * 128:(c + 1) * 128]
    labels = [lax.broadcasted_iota(jnp.int32, (16, n), 0).astype(bf16) + float(k) for k in (0, 16)]
    one, zero = jnp.ones((16, n), bf16), jnp.zeros((16, n), bf16)
    total = jnp.zeros((heads, 32 * len(ids(0))), f32)
    for r in range(rows):
        grow = jnp.concatenate([gs[c, pl.ds(r, heads, stride=rows), :] for c in range(n // 128)], axis=1).astype(bf16)
        hots = []
        for one_row in ids(r):
            row = jnp.broadcast_to(one_row, (16, n)).astype(bf16)
            hots += [jnp.where(row == label, one, zero) for label in labels]
        total = total + lax.dot_general(grow, jnp.concatenate(hots, axis=0), NT, preferred_element_type=f32)
    return total


def hist_tile(now, heads, g_ref, ids_ref, band_ref, far_ref, lin_ids, table, gs):
    @pl.when(now == 0)
    def _():
        sides = [jnp.sum(jnp.sum(far_ref[:, k], axis=1), axis=1, keepdims=True) for k in range(2)]
        lane = lax.broadcasted_iota(jnp.int32, (heads, 128), 1)
        table[0] = jnp.where(lane == 15, sides[0], 0.0) + jnp.where(lane == 31, sides[1], 0.0)
        table[1] = jnp.zeros_like(table[1])

    big = g_ref.shape[1]

    @pl.loop(0, big // 16)
    def _(q):
        block = pl.ds(pl.multiple_of(q * 16, 16), 16)
        table[1, :, 0:64] += rows_times_hots(lambda h: g_ref[h, block, :].astype(f32), lambda r: [ids_ref.at[t, block][r:r + 1, :] for t in range(2)], 16, heads, gs)

    wide = band_ref.shape[2] // 128
    per = lin_ids.shape[1]
    a = now * 16 // per
    inside = pl.ds(pl.multiple_of(now * 16 % per, 16), 16)

    def band_ids(r):
        return [jnp.concatenate([lin_ids.at[jnp.clip((m - 1) * (128 // per) - a + 4, 0, 7), inside][r:r + 1, :] for m in range(wide)], axis=1)]

    table[0, :, 0:32] += rows_times_hots(lambda h: band_ref[h], band_ids, 16, heads, gs)


def hist_kernel(heads, rows, n, G, halves, count, *refs):
    (g_ref, ids_ref, band_ref, far_ref, lin_ids, dx, tok, gh, gain_ref, gain_two), parts = refs[:10], refs[10:10 + count]
    small_ref, gt_ref = refs[10 + count:12 + count]
    outs, rest = refs[12 + count:12 + 2 * count], refs[12 + 2 * count:]
    (gs, table, got, pair_sem), sums, sems = rest[:4], rest[4:11], rest[11:]
    acc = sums[0]
    now, steps = pl.program_id(0), n // rows
    core = lax.axis_index("narrow")
    mine = tok.shape[0]
    d = tok.shape[1]
    comm = Scatter(G, halves, parts, outs, *sems)
    swap = lambda: remote(dx.at[pl.ds(pl.multiple_of((1 - core) * mine, mine), mine)], got, pair_sem.at[0], pair_sem.at[1], {"narrow": 1 - core})

    def compute():
        @pl.when(now == 0)
        def _():
            swap().start()
            acc[0] = jnp.zeros(acc.shape[1:], f32)
            for k in range(d // 128):
                acc[0, d // 128 + k:d // 128 + k + 1, :] = gain_two[:, k * 128:(k + 1) * 128]

        @pl.when(now == steps // 8)
        def _():
            swap().wait()

        for t in range(mine // TILE):
            @pl.when(now == steps // 8 + t)
            def _():
                r = pl.ds(t * TILE, TILE)
                x = tok[r, :].astype(f32)
                total = dx[pl.ds(pl.multiple_of(core * mine + t * TILE, TILE), TILE), :].astype(f32) + got[r, :].astype(f32)
                factor = lax.rsqrt(jnp.mean(x * x, axis=1, keepdims=True) + epsilon)
                unit = x * factor
                scaled = gain_ref[...] * total
                gt_ref[r, :] = gh[r, :] + factor * (scaled - unit * jnp.mean(scaled * unit, axis=1, keepdims=True))
                gain = jnp.sum(total * unit, axis=0, keepdims=True)
                for k in range(d // 128):
                    acc[0, k:k + 1, :] += gain[:, k * 128:(k + 1) * 128]

        hist_tile(now, heads, g_ref, ids_ref, band_ref, far_ref, lin_ids, table, gs)

    def reduce():
        acc[0, pl.ds(pl.multiple_of(2 * (d // 128) + core * heads, 8), heads), 0:32] = table[0, :, 0:32]
        acc[0, pl.ds(pl.multiple_of(2 * (d // 128) + core * heads, 8), heads), 32:96] = table[1, :, 0:64]
        small_ref[...] = sum_everywhere(G, *sums)

    beside(comm.events(1), G, steps, now, compute, (reduce,))


def hist_and_scatter(g, band, far, ids, dx, tok, gh, gain, gain_two, parts, halves, wide, cid):
    heads, n, _ = g.shape
    rows, count, G, d = n // (band.shape[1] // 16), len(parts), wide // 4, tok.shape[1]
    box_ids, lin_ids = ids
    small = 2 * (d // 128) + 2 * heads
    sds = jax.ShapeDtypeStruct
    const = lambda s: pl.BlockSpec(s, lambda i: (0, 0))
    outs = pl.pallas_call(functools.partial(hist_kernel, heads, rows, n, G, halves, count), grid=(n // rows,),
        out_shape=(sds((small, 128), f32), sds(tok.shape, f32)) + shard_shapes(parts, wide),
        in_specs=[pl.BlockSpec((heads, rows, n), lambda i: (0, i, 0)), pl.BlockSpec((2, rows, n), lambda i: (0, i, 0)),
                  pl.BlockSpec((heads, 16, band.shape[2]), lambda i: (0, i, 0)), pl.BlockSpec(far.shape, lambda i: (0, 0, 0, 0)),
                  pl.BlockSpec(lin_ids.shape, lambda i: (0, 0, 0)), const(dx.shape), const(tok.shape), const(gh.shape), const(gain.shape), const(gain_two.shape)] + [ANY] * count,
        out_specs=(const((small, 128)), const(tok.shape)) + (whole_vmem(),) * count,
        scratch_shapes=[pltpu.VMEM((n // 128, heads * 16, 128), f32), pltpu.VMEM((2, heads, 128), f32), pltpu.VMEM(tok.shape, bf16), D((2,))]
        + sum_scratch(G, small) + scatter_scratch(G, halves, parts[0].shape[0] // wide),
        compiler_params=params(cid), name="table_grad_scatter")(g, box_ids, band, far, lin_ids, dx, tok, gh, gain, gain_two, *parts)
    return outs[0], outs[1], outs[2:]


D = pltpu.SemaphoreType.DMA


def place():
    me = lax.axis_index("wide")
    return me // 4, (me // 2) % 2, me % 2


def wide_id(z, y, x):
    return {"wide": z * 4 + y * 2 + x}


def shard_rows(z, y, x, R):
    return pl.ds(pl.multiple_of((z * 4 + y * 2 + x) * R, R), R)


def remote(src, dst, send, recv, target):
    return pltpu.make_async_remote_copy(src_ref=src, dst_ref=dst, send_sem=send, recv_sem=recv, device_id=target, device_id_type=MESH)


def greet(G, far, pair=0):
    z, y, x = place()
    bar = pltpu.get_barrier_semaphore()
    sig = lambda t: pl.semaphore_signal(bar, inc=1, device_id=t, device_id_type=MESH)
    sig(wide_id(z, 1 - y, x))
    sig(wide_id(z, y, 1 - x))
    if pair:
        sig({"narrow": 1 - lax.axis_index("narrow")})
    if far:
        for k in range(1, G):
            sig(wide_id((z + k) % G, y, x))
        pl.semaphore_wait(bar, 2 + pair + G - 1)
    else:
        @pl.when(z > 0)
        def _():
            sig(wide_id(z - 1, y, x))

        @pl.when(z < G - 1)
        def _():
            sig(wide_id(z + 1, y, x))

        pl.semaphore_wait(bar, 2 + pair + (z > 0).astype(jnp.int32) + (z < G - 1).astype(jnp.int32))


class Gather:
    def __init__(self, G, halves, srcs, outs, local_sem, zs, zr, ns, nr):
        self.G, self.halves, self.srcs, self.local_sem = G, halves, srcs, local_sem
        self.outs = [o if isinstance(o, tuple) else (o, 0, 0) for o in outs]
        self.widths = [sum(w for h in halves for a, _, w in h if a == k) for k in range(len(srcs))]
        self.zs, self.zr, self.ns, self.nr = zs, zr, ns, nr
        self.most = max(len(h) for h in halves)
        self.z, self.y, self.x = place()
        self.R = srcs[0].shape[0]

    def hop(self, own, zz, yy, xx, h, way, j):
        target = wide_id(self.z, 1 - self.y, self.x) if way == "y" else wide_id(self.z, self.y, 1 - self.x)
        copies = []
        for n, (a, c, w) in enumerate(self.halves[h]):
            slot = (zz * 6 + j) * self.most + n
            out, first, at = self.outs[a]
            dst = out.at[shard_rows(zz, yy, xx, self.R), pl.ds(first + c, w)]
            copies.append(remote(self.srcs[a].at[:, pl.ds(at + c, w)] if own else dst, dst, self.ns.at[slot], self.nr.at[slot], target))
        return copies

    def second_stage(self, zz, own=False):
        return self.hop(own, zz, self.y, self.x, 0, "y", 0) + self.hop(own, zz, self.y, self.x, 1, "x", 1)

    def third_stage(self, zz, own=False):
        return self.hop(own, zz, self.y, self.x, 0, "x", 2) + self.hop(own, zz, self.y, self.x, 1, "y", 3)

    def last_stage(self, zz):
        return self.hop(False, zz, 1 - self.y, self.x, 0, "x", 4) + self.hop(False, zz, self.y, 1 - self.x, 1, "y", 5)

    def relay(self, own, zz, step, way):
        copies = []
        for a in range(len(self.srcs)):
            slot = (way * (self.G - 1) + step) * len(self.srcs) + a
            dst = self.whole(a, zz)
            copies.append(remote(self.own(a) if own else dst, dst, self.zs.at[slot], self.zr.at[slot],
                                 wide_id(self.z + (1 if way == 0 else -1), self.y, self.x)))
        return copies

    def whole(self, a, zz):
        out, first, _ = self.outs[a]
        return out.at[shard_rows(zz, self.y, self.x, self.R), pl.ds(first, self.widths[a])]

    def own(self, a):
        return self.srcs[a].at[:, pl.ds(self.outs[a][2], self.widths[a])]

    def can(self, way):
        return self.z < self.G - 1 if way == 0 else self.z > 0

    def source(self, d, way):
        return (self.z - d, self.z - d >= 0) if way == 0 else (self.z + d, self.z + d < self.G)

    def keep(self):
        return [pltpu.make_async_copy(self.own(a), self.whole(a, self.z), self.local_sem.at[a]) for a in range(len(self.srcs))]

    def begin(self):
        for way in range(2):
            @pl.when(self.can(way))
            def _():
                for c in self.relay(True, self.z, 0, way):
                    c.start()
        for c in self.second_stage(self.z, True) + self.third_stage(self.z, True) + self.keep():
            c.start()

    def turn(self, zz):
        for c in self.hop(False, zz, 1 - self.y, self.x, 0, "y", 0) + self.hop(False, zz, self.y, 1 - self.x, 1, "x", 1):
            c.wait_recv()
        for c in self.last_stage(zz):
            c.start()

    def step(self, d):
        for way in range(2):
            zz, there = self.source(d, way)

            @pl.when(there)
            def _():
                for c in self.relay(False, zz, d - 1, way):
                    c.wait_recv()

                @pl.when(self.can(way))
                def _():
                    for c in self.relay(False, zz, d, way):
                        c.start()

                for c in self.second_stage(zz):
                    c.start()
        for way in range(2):
            zz, there = self.source(d, way)

            @pl.when(there)
            def _():
                for c in self.third_stage(zz):
                    c.start()

    def turns(self, d):
        if d == 0:
            self.turn(self.z)
            return
        for way in range(2):
            zz, there = self.source(d, way)

            @pl.when(there)
            def _():
                self.turn(zz)

    def finish(self):
        y, x = self.y, self.x

        @pl.loop(0, self.G)
        def _(zz):
            for c in (self.hop(False, zz, y, 1 - x, 0, "x", 2) + self.hop(False, zz, 1 - y, x, 1, "y", 3)
                      + self.hop(False, zz, 1 - y, 1 - x, 0, "x", 4) + self.hop(False, zz, 1 - y, 1 - x, 1, "y", 5)):
                c.wait_recv()
            for c in self.second_stage(zz) + self.third_stage(zz) + self.last_stage(zz):
                c.wait_send()

        for way in range(2):
            @pl.when(self.can(way))
            def _():
                for c in self.relay(True, self.z, 0, way):
                    c.wait_send()
                for d in range(1, self.G - 1):
                    zz, there = self.source(d, way)

                    @pl.when(there)
                    def _():
                        for c in self.relay(False, zz, d, way):
                            c.wait_send()
        for c in self.keep():
            c.wait()

    def events(self):
        G = self.G
        first = lambda: (greet(G, False), self.begin())
        ev = [(0.0, first), (0.7, lambda: self.turns(0))]
        for d in range(1, G):
            ev += [(1.15 * d, functools.partial(self.step, d)), (1.3 * d + 1.2, functools.partial(self.turns, d))]
        return sorted(ev, key=lambda e: e[0]), self.finish


def gather_scratch(G, halves, arrays):
    most = max(len(h) for h in halves)
    return [D((arrays,)), D((2 * (G - 1) * arrays,)), D((2 * (G - 1) * arrays,)), D((6 * G * most,)), D((6 * G * most,))]


class Scatter:
    def __init__(self, G, halves, parts, outs, r1a, r1b, o1a, o1b, r2a, r2b, r3, own, lsem, s1, v1, s2, v2, s3, v3):
        self.__dict__.update(locals())
        self.most = max(len(h) for h in halves)
        self.wa, self.wb = [sum(p[2] for p in h) for h in halves]
        self.R = parts[0].shape[0] // (4 * G)
        self.z, self.y, self.x = place()
        self.order = sorted(range(1, G), key=lambda k: min(k, G - k), reverse=True) + [0]

    def zk(self, k):
        return (self.z + k) % self.G

    def neighbour(self, way):
        return wide_id(self.z, 1 - self.y, self.x) if way == "y" else wide_id(self.z, self.y, 1 - self.x)

    def pieces(self, h):
        at, out = 0, []
        for n, (a, c, w) in enumerate(self.halves[h]):
            out.append((n, a, pl.ds(c, w), pl.ds(at, w)))
            at += w
        return out

    def sources(self, k, mine):
        z, y, x = self.zk(k), self.y, self.x
        for h in range(2):
            for n, a, src, dst in self.pieces(h):
                for j in range(2):
                    if h == 0:
                        rows = shard_rows(z, j, x if mine else 1 - x, self.R)
                    else:
                        rows = shard_rows(z, y if mine else 1 - y, j, self.R)
                    yield h, j, dst, ((2 * k + h) * self.most + n) * 2 + j, self.parts[a].at[rows, src]

    def one(self, k):
        return [remote(src, (self.r1a, self.r1b)[h].at[k, j, :, dst], self.s1.at[slot], self.v1.at[slot], self.neighbour("xy"[h]))
                for h, j, dst, slot, src in self.sources(k, False)]

    def load(self, k):
        return [pltpu.make_async_copy(src, (self.o1a, self.o1b)[h].at[k, j, :, dst], self.lsem.at[slot]) for h, j, dst, slot, src in self.sources(k, True)]

    def two(self, k):
        return [remote(self.o1a.at[k, 1 - self.y], self.r2a.at[k], self.s2.at[2 * k], self.v2.at[2 * k], self.neighbour("y")),
                remote(self.o1b.at[k, 1 - self.x], self.r2b.at[k], self.s2.at[2 * k + 1], self.v2.at[2 * k + 1], self.neighbour("x"))]

    def three(self, k):
        return remote(self.own.at[k], self.r3.at[k - 1], self.s3.at[k - 1], self.v3.at[k - 1], wide_id(self.zk(k), self.y, self.x))

    def launch(self, k):
        for c in self.one(k) + self.load(k):
            c.start()

    def begin(self):
        for k in self.order[:2]:
            self.launch(k)

    def rows(self, count, body):
        step = min(16, count)

        @pl.loop(0, count // step)
        def _(i):
            body(pl.ds(pl.multiple_of(i * step, step), step))

    def add_one(self, n):
        k = self.order[n]
        for c in self.one(k):
            c.wait_recv()
        for c in self.load(k):
            c.wait()
        for mine, got in ((self.o1a, self.r1a), (self.o1b, self.r1b)):
            def body(r):
                for j in range(2):
                    mine[k, j, r, :] = (mine[k, j, r, :].astype(f32) + got[k, j, r, :].astype(f32)).astype(bf16)

            self.rows(self.R, body)
        for c in self.two(k):
            c.start()
        if n + 2 < self.G:
            self.launch(self.order[n + 2])

    def add_two(self, n):
        k = self.order[n]
        for c in self.two(k):
            c.wait_recv()

        def body(r):
            self.own[k, r, pl.ds(0, self.wa)] = (self.o1a[k, self.y, r, :].astype(f32) + self.r2a[k, r, :].astype(f32)).astype(bf16)
            self.own[k, r, pl.ds(self.wa, self.wb)] = (self.o1b[k, self.x, r, :].astype(f32) + self.r2b[k, r, :].astype(f32)).astype(bf16)

        self.rows(self.R, body)
        if k:
            self.three(k).start()

    def finish(self):
        self.add_two(self.G - 1)
        for k in range(1, self.G):
            self.three(k).wait_recv()

        def body(r):
            for h in range(2):
                for _, a, src, dst in self.pieces(h):
                    cols = pl.ds(dst.start + h * self.wa, dst.size)
                    total = self.own[0, r, cols].astype(f32)
                    for k in range(self.G - 1):
                        total = total + self.r3[k, r, cols].astype(f32)
                    self.outs[a][r, src] = total

        self.rows(self.R, body)
        for k in range(self.G):
            for c in self.one(k) + self.two(k):
                c.wait_send()
            if k:
                self.three(k).wait_send()

    def events(self, pair=0):
        G = self.G
        first = lambda: (greet(G, True, pair), self.begin())
        ev = [(0.0, first), (1.1, lambda: self.add_one(0))]
        for n in range(1, G):
            ev += [(1.5 * n + 0.65, functools.partial(self.add_one, n)), (1.5 * n + 1.1, functools.partial(self.add_two, n - 1))]
        return sorted(ev, key=lambda e: e[0]), self.finish


def scatter_scratch(G, halves, R):
    most = max(len(h) for h in halves)
    a, b = [sum(p[2] for p in h) for h in halves]
    V = lambda *s: pltpu.VMEM(s, bf16)
    return [V(G, 2, R, a), V(G, 2, R, b), V(G, 2, R, a), V(G, 2, R, b), V(G, R, a), V(G, R, b), V(G - 1, R, a + b), V(G, R, a + b),
            D((4 * G * most,)), D((4 * G * most,)), D((4 * G * most,)), D((2 * G,)), D((2 * G,)), D((G - 1,)), D((G - 1,))]


def beside(plan, G, steps, now, compute, late=()):
    events, finish = plan
    units = 1.55 * G
    for n in range(steps):
        here = [act for t, act in events if min(steps - 1, int(-(-t * steps // units))) == n]
        if here:
            @pl.when(now == n)
            def _():
                for act in here:
                    act()
    compute()

    @pl.when(now == steps - 1)
    def _():
        for act in late:
            act()
        finish()


ANY = pl.BlockSpec(memory_space=pl.ANY)


def whole_vmem():
    return pl.BlockSpec(memory_space=pltpu.VMEM)


def gathered_shapes(shards, wide):
    return tuple(jax.ShapeDtypeStruct((wide * s.shape[0], s.shape[1]), s.dtype) for s in shards)


def sum_everywhere(G, acc, got, gz, s, v, sz, vz):
    z, y, x = place()
    core = {"narrow": 1 - lax.axis_index("narrow")}
    for n, t in enumerate((core, wide_id(z, y, 1 - x), wide_id(z, 1 - y, x))):
        c = remote(acc.at[n], got.at[n], s.at[n], v.at[n], t)
        c.start()
        c.wait()
        acc[n + 1] = acc[n] + got[n]
    gz[z] = acc[3]
    far = [wide_id((z + k) % G, y, x) for k in range(1, G)]
    sent = [remote(acc.at[3], gz.at[z], sz.at[k], vz.at[z], t) for k, t in enumerate(far)]
    for c in sent:
        c.start()
    for k in range(1, G):
        zz = (z + k) % G
        remote(acc.at[3], gz.at[zz], sz.at[k - 1], vz.at[zz], far[k - 1]).wait_recv()
    for c in sent:
        c.wait_send()
    total = gz[0]
    for k in range(1, G):
        total = total + gz[k]
    return total


def sum_scratch(G, rows):
    V = lambda k: pltpu.VMEM((k, rows, 128), f32)
    return [V(4), V(3), V(G), D((3,)), D((3,)), D((G - 1,)), D((G,))]


def nt(a, b):
    return lax.dot_general(a, b, NT, preferred_element_type=f32)


def nn(a, b):
    return jnp.dot(a, b, preferred_element_type=f32)


def gelu_and_slope(v):
    root = 0.7978845608028654
    square = v * v
    t = jnp.tanh(root * v * (1.0 + 0.044715 * square))
    half = 0.5 * (1.0 + t)
    return v * half, half + 0.5 * v * (1.0 - t * t) * root * (1.0 + 3 * 0.044715 * square)


def mid_kernel(G, cut, att_h, tok_h, cot_h, wo_h, wg_h, wu_h, wd_h, wd_shard, gain_ref,
               gout_h, gg_h, gu_h, gd_h, y_ref, gh_ref, ga_ref, ggain_ref, sd_ref,
               att, tok, cot, wo, wg, wu, wd, part, other, back, hid, n2t, cott, hff, gg, gu, ysend, yown, yother, stage,
               isem, osem, sp, vp, sb, vb, sy, vy, *sems):
    core = lax.axis_index("narrow")
    peer = {"narrow": 1 - core}
    n, d = tok.shape
    ff = wg.shape[1]
    tiles = n // TILE
    half = tiles // 2
    loads = [pltpu.make_async_copy(s, t, isem.at[k]) for k, (s, t) in enumerate(
        [(att_h, att), (wo_h, wo), (tok_h, tok), (wg_h, wg), (wu_h, wu), (cot_h, cot), (wd_h, wd.at[:, pl.ds(0, cut)])])]
    for c in loads:
        c.start()
    mid = cut + (ff - cut) // 256 * 128
    bring = Gather(G, (((0, 0, mid - cut),), ((0, mid - cut, ff - mid),)), [wd_shard], [(wd, cut, cut)], *sems[:5])
    give = Scatter(G, (((0, 0, cut),), ((0, cut, ff - cut),)), [gd_h], [sd_ref], *sems[5:])
    greet(G, True, 1)
    bring.begin()
    rows_of = lambda t: pl.ds(pl.multiple_of(t * TILE, TILE), TILE)
    send_part = lambda t: remote(part.at[rows_of(t)], other.at[rows_of(t)], sp.at[t], vp.at[t], peer)
    send_back = lambda t: remote(part.at[rows_of(t)], back.at[rows_of(t)], sb.at[t], vb.at[t], peer)
    send_y = lambda j: remote(ysend.at[rows_of(j)], yother.at[rows_of(j)], sy.at[j], vy.at[j], peer)
    gain = gain_ref[...]

    for c in loads[:2]:
        c.wait()

    def at_step(s, plan):
        for k, acts in plan.items():
            @pl.when(s == k)
            def _():
                for act in acts:
                    act()

    turns = [functools.partial(bring.turns, k) for k in range(G)]
    steps = [functools.partial(bring.step, k) for k in range(1, G)]

    @pl.loop(0, tiles)
    def _(t):
        part[rows_of(t), :] = nt(att[rows_of(t), :], wo[...]).astype(bf16)
        send_part(t).start()
        at_step(t, {1: turns[:1], 2: steps[:1]})

    for c in loads[2:]:
        c.wait()

    chunks, at = [], 0
    while at < ff:
        w = min(384, ff - at)
        chunks.append((at, w))
        at += w

    later = [act for pair in zip(turns[1:], steps[1:] + [lambda: None]) for act in pair]

    @pl.loop(0, tiles)
    def _(s):
        t = (s + half * (1 - core)) % tiles
        r = rows_of(t)
        send_part(t).wait()
        h = tok[r, :].astype(f32) + (part[r, :].astype(f32) + other[r, :].astype(f32))
        hid[r, :] = h
        factor = lax.rsqrt(jnp.mean(h * h, axis=1, keepdims=True) + epsilon)
        low = (h * factor * gain).astype(bf16)
        n2t[:, r] = low.T
        cott[:, r] = cot[r, :].T
        for at, w in chunks:
            cols = pl.ds(at, w)
            act, slope = gelu_and_slope(nn(low, wg[:, cols]))
            up = nn(low, wu[:, cols])
            hff[r, cols] = (act * up).astype(bf16)
            gg[r, cols] = (up * slope).astype(bf16)
            gu[r, cols] = act.astype(bf16)
        at_step(s, {1: later[:2], 2: later[2:4], 3: later[4:]})

    def weight_grad(left, right, out, slot, width):
        @pl.loop(0, d // TILE)
        def _(k):
            b = k % 2
            copy = lambda kk: pltpu.make_async_copy(stage.at[kk % 2, :, pl.ds(0, width)], out.at[rows_of(kk)], osem.at[2 * slot + kk % 2])

            @pl.when(k >= 2)
            def _():
                copy(k - 2).wait()

            stage[b, :, pl.ds(0, width)] = nn(left[rows_of(k), :], right[...]).astype(bf16)
            copy(k).start()

        for k in range(d // TILE - 2, d // TILE):
            pltpu.make_async_copy(stage.at[k % 2, :, pl.ds(0, width)], out.at[rows_of(k)], osem.at[2 * slot + k % 2]).wait()

    weight_grad(cott, hff, gd_h, 0, ff)
    give.begin()
    bring.finish()
    ones = [functools.partial(give.add_one, k) for k in range(G)]
    twos = [functools.partial(give.add_two, k) for k in range(G - 1)]

    @pl.loop(0, tiles)
    def _(s):
        t = (s + half * (1 - core)) % tiles
        r = rows_of(t)
        ct = cot[r, :]
        for at, w in chunks:
            cols = pl.ds(at, w)
            gf = nn(ct, wd[:, cols])
            gg[r, cols] = (gf * gg[r, cols].astype(f32)).astype(bf16)
            gu[r, cols] = (gf * gu[r, cols].astype(f32)).astype(bf16)
        part[r, :] = (nt(gg[r, :], wg[...]) + nt(gu[r, :], wu[...])).astype(bf16)
        send_back(t).start()
        y = nt(hff[r, :], wd[...]).astype(bf16)

        @pl.when(s < half)
        def _():
            ysend[rows_of(s), :] = y
            send_y(s).start()

        @pl.when(s >= half)
        def _():
            yown[rows_of(s - half), :] = y

        at_step(s, {0: ones[:1], 1: ones[1:2], 2: twos[:1], 3: ones[2:3] + twos[1:2]})

    ggain_ref[...] = jnp.zeros_like(ggain_ref)

    @pl.loop(0, tiles)
    def _(s):
        t = (s + half * (1 - core)) % tiles
        r = rows_of(t)
        send_back(t).wait()
        total = part[r, :].astype(f32) + back[r, :].astype(f32)
        h = hid[r, :]
        factor = lax.rsqrt(jnp.mean(h * h, axis=1, keepdims=True) + epsilon)
        unit = h * factor
        g = gain * total
        gh = cot[r, :].astype(f32) + factor * (g - unit * jnp.mean(g * unit, axis=1, keepdims=True))
        low = gh.astype(bf16)
        cott[:, r] = low.T
        ga_ref[r, :] = nn(low, wo[...]).astype(bf16)

        @pl.when(s >= half)
        def _():
            j = rows_of(s - half)
            gh_ref[j, :] = gh
            ggain_ref[...] += jnp.sum(total * unit, axis=0, keepdims=True)
            send_y(s - half).wait()
            y_ref[j, :] = (h + (yown[j, :].astype(f32) + yother[j, :].astype(f32))).astype(bf16)

        at_step(s, {2: ones[3:4]})

    weight_grad(n2t, gg, gg_h, 1, ff)
    for act in twos[2:3] + [act for pair in zip(ones[4:], twos[3:]) for act in pair]:
        act()
    weight_grad(n2t, gu, gu_h, 2, ff)
    weight_grad(cott, att, gout_h, 3, att.shape[1])
    give.finish()


def middle(att, tok, cot, wo, wg, wu, wd, wd_shard, gain, wide, cid):
    n, d = tok.shape
    units, ff, G, cut = att.shape[1], wg.shape[1], wide // 4, wd.shape[1]
    B = lambda *s: pltpu.VMEM(s, bf16)
    sds = jax.ShapeDtypeStruct
    tiles = n // TILE
    halves = (((0, 0, cut),), ((0, cut, ff - cut),))
    return pl.pallas_call(functools.partial(mid_kernel, G, cut),
        out_shape=(sds((d, units), bf16), sds((d, ff), bf16), sds((d, ff), bf16), sds((d, ff), bf16),
                   sds((n // 2, d), bf16), sds((n // 2, d), f32), sds((n, units), bf16), sds((1, d), f32), sds((d // wide, ff), f32)),
        in_specs=[ANY] * 8 + [whole_vmem()], out_specs=(ANY,) * 4 + (whole_vmem(),) * 5,
        scratch_shapes=[B(n, units), B(n, d), B(n, d), B(d, units), B(d, ff), B(d, ff), B(d, ff), B(n, d), B(n, d), B(n, d),
                        pltpu.VMEM((n, d), f32), B(d, n), B(d, n), B(n, ff), B(n, ff), B(n, ff),
                        B(n // 2, d), B(n // 2, d), B(n // 2, d), B(2, TILE, ff),
                        D((7,)), D((8,)), D((tiles,)), D((tiles,)), D((tiles,)), D((tiles,)), D((tiles // 2,)), D((tiles // 2,))]
        + gather_scratch(G, halves, 1) + scatter_scratch(G, halves, d // wide),
        compiler_params=params(cid), name="feed_forward")(att, tok, cot, wo, wg, wu, wd, wd_shard, gain)


def local(tokens, cotangent, pages, boxes, gain_attn, gain_ffn, bias_tables, w_query, w_key, w_value, w_out, w_gate, w_up, w_down):
    wide, narrow = lax.axis_size("wide"), lax.axis_size("narrow")
    heads_all = bias_tables.shape[1]
    heads = heads_all // narrow
    core = lax.axis_index("narrow")
    tables = lax.dynamic_slice_in_dim(bias_tables, core * heads, heads, 1)
    inner, ff, d = w_query.shape[1], w_gate.shape[1], tokens.shape[1]
    gain_one, gain_two = gain_attn.astype(f32)[None], gain_ffn.astype(f32)[None]

    all_tokens = lax.all_gather(tokens, "narrow", axis=0, tiled=True)
    all_cot = lax.all_gather(cotangent, "narrow", axis=0, tiled=True)
    early = inner // 4 * 3
    bias, ids, (w_first, full_out, full_gate) = bias_and_gather(
        tables, boxes, pages, [jnp.concatenate([w_query, w_key, w_value], axis=1), w_out.T, w_gate],
        (((2, 0, ff), (0, 0, early)), ((1, 0, inner), (0, early, 3 * inner - early))), wide, 1)
    down_shard = w_down.T
    cut = (ff // 128 + 1) // 2 * 128
    (attended, lse, normed, qkv), (full_up, most_down) = attn_fwd_and_gather(
        all_tokens, gain_one, w_first, bias, [w_up, down_shard[:, :cut]],
        (((0, 0, cut), (1, 0, cut - 384)), ((0, cut, ff - cut), (1, cut - 384, 384))), wide, 2)
    grad_w_out, grad_w_gate, grad_w_up, _, output, grad_hidden, grad_attended, grad_gain_two, s_down = middle(
        attended, all_tokens, all_cot, full_out, full_gate, full_up, most_down, down_shard, gain_two, wide, 3)
    (g, band, far, grad_w_query, grad_w_key, grad_w_value, grad_normed), (s_gate, s_out) = attn_bwd_and_scatter(
        qkv, bias, attended, grad_attended, lse, normed, w_first, [grad_w_gate, grad_w_out],
        (((0, 0, 2 * inner),), ((0, 2 * inner, ff - 2 * inner), (1, 0, inner))), wide, 4)
    small, grad_tokens, (s_up, s_query, s_key, s_value) = hist_and_scatter(
        g, band, far, ids, grad_normed, tokens, grad_hidden, gain_one, grad_gain_two, [grad_w_up, grad_w_query, grad_w_key, grad_w_value],
        (((0, 0, ff),), ((1, 0, inner), (2, 0, inner), (3, 0, inner))), wide, 5)
    lines = d // 128
    one, two = small[:lines].reshape(d), small[lines:2 * lines].reshape(d)
    table = small[2 * lines:, :bias_tables.shape[0]].T
    return (output, grad_tokens, one, two, table, s_query, s_key, s_value, s_out.T, s_gate, s_up, s_down.T)


def solution(mesh):
    rows, cols, tall = P(("wide", "narrow"), None), P("wide", "narrow"), P("narrow", "wide")
    in_specs = (rows, rows, P("wide"), P(None, "wide"), P(), P(), P(), cols, cols, cols, tall, cols, cols, tall)
    out_specs = (rows, rows, P(), P(), P(), cols, cols, cols, tall, cols, cols, tall)
    return jax.shard_map(local, mesh=mesh, in_specs=in_specs, out_specs=out_specs, check_vma=False)
```

```python
import functools

import jax
import jax.numpy as jnp
from jax import lax
from jax.experimental import pallas as pl
from jax.experimental.pallas import tpu as pltpu
from jax.sharding import PartitionSpec as P

f32, bf16 = jnp.float32, jnp.bfloat16
MESH = pl.DeviceIdType.MESH


EDGES = (1, 2, 3, 4, 5, 6, 7, 8, 12, 16, 23, 32, 46, 64, 91)
NT = (((1,), (1,)), ((), ()))
VM = 58 * 2**20
TABLE_SCALE = 2047.0
TABLE_LIFT = 8192
TILE = 256
epsilon = 1e-06


def params(cid):
    return pltpu.CompilerParams(collective_id=cid, has_side_effects=True, vmem_limit_bytes=VM)


def lane_take(table, idx):
    return jnp.take_along_axis(table, idx, axis=1, mode="promise_in_bounds")


def buckets_of(gap, steps, shift):
    return lane_take(steps, jnp.minimum(jnp.abs(gap) >> shift, EDGES[-1])) + jnp.where(gap > 0, 16, 0)


def bias_tile(start, heads, rows, n, steps_ref, tab_ref, box_col, box_row, page_col, page_row, bias_ref, ids_ref, lin_ids, lin):
    steps = jnp.broadcast_to(steps_ref[...], (rows, 128))
    allowed_col = jnp.broadcast_to(page_col[...] % 2, (rows, 128))
    cols = [jnp.broadcast_to(box_col[:, t:t + 1], (rows, 128)) for t in range(2)]
    pairs = heads // 2
    table = lambda t, p: jnp.broadcast_to(tab_ref[t * pairs + p:t * pairs + p + 1, :], (rows, 128))
    unit = 1.0 / TABLE_SCALE

    @pl.when(start == 0)
    def _():
        @pl.loop(0, 8)
        def _(k):
            ids = buckets_of(lax.broadcasted_iota(jnp.int32, (rows, 128), 1) - lax.broadcasted_iota(jnp.int32, (rows, 128), 0) + (k - 4) * rows, steps, 0)
            lin_ids[k] = ids.astype(f32)
            for p in range(pairs):
                lin[k, p] = lane_take(table(0, p), ids)

    @pl.loop(0, n // 128)
    def _(c):
        lanes = pl.ds(pl.multiple_of(c * 128, 128), 128)
        near = jnp.clip((c * 128 - start) // rows + 4, 0, 7)
        ids = []
        for t in range(2):
            ids.append(buckets_of(jnp.broadcast_to(box_row[t:t + 1, lanes], (rows, 128)) - cols[t], steps, 2))
            ids_ref[t, :, lanes] = ids[t].astype(f32)
        ok = jnp.broadcast_to(page_row[:, lanes], (rows, 128)) == allowed_col
        for p in range(pairs):
            words = lin[near, p] + lane_take(table(1, p), ids[0]) + lane_take(table(2, p), ids[1])
            upper = (words >> 16).astype(f32) * unit
            lower = (words & 0xFFFF).astype(f32) * unit - 3 * TABLE_LIFT * unit
            bias_ref[2 * p, :, lanes] = jnp.where(ok, upper, -1e30)
            bias_ref[2 * p + 1, :, lanes] = jnp.where(ok, lower, -1e30)


def bias_gather_kernel(heads, rows, n, G, halves, count, *refs):
    ins, srcs = refs[:6], refs[6:6 + count]
    bias_ref, ids_ref, lin_ids = refs[6 + count:9 + count]
    outs, lin, sems = refs[9 + count:9 + 2 * count], refs[9 + 2 * count], refs[10 + 2 * count:]
    now = pl.program_id(0)
    comm = Gather(G, halves, srcs, outs, *sems)
    beside(comm.events(), G, n // rows, now, lambda: bias_tile(now * rows, heads, rows, n, *ins, bias_ref, ids_ref, lin_ids, lin))


def bias_and_gather(tables, boxes, pages, shards, halves, wide, cid):
    heads, n, G, rows = tables.shape[1], pages.shape[0], wide // 4, 64
    fixed = jnp.round(tables.astype(f32) * TABLE_SCALE).astype(jnp.int32).reshape(3, 32, heads // 2, 2)
    words = fixed[..., 0] * 65536 + fixed[..., 1] + TABLE_LIFT
    tab = jnp.pad(words.transpose(0, 2, 1).reshape(3 * heads // 2, 32), ((0, 0), (0, 96)))
    lane = jnp.arange(128, dtype=jnp.int32)
    steps = sum([(lane >= e).astype(jnp.int32) for e in EDGES])[None]
    count = len(shards)
    outs = pl.pallas_call(functools.partial(bias_gather_kernel, heads, rows, n, G, halves, count),
        grid=(n // rows,),
        out_shape=(jax.ShapeDtypeStruct((heads, n, n), f32), jax.ShapeDtypeStruct((2, n, n), f32), jax.ShapeDtypeStruct((8, rows, 128), f32)) + gathered_shapes(shards, wide),
        in_specs=[pl.BlockSpec((1, 128), lambda i: (0, 0)), pl.BlockSpec((3 * heads // 2, 128), lambda i: (0, 0)),
                  pl.BlockSpec((rows, 2), lambda i: (i, 0)), pl.BlockSpec((2, n), lambda i: (0, 0)),
                  pl.BlockSpec((rows, 1), lambda i: (i, 0)), pl.BlockSpec((1, n), lambda i: (0, 0))] + [ANY] * count,
        out_specs=(pl.BlockSpec((heads, rows, n), lambda i: (0, i, 0)), pl.BlockSpec((2, rows, n), lambda i: (0, i, 0)),
                   pl.BlockSpec((8, rows, 128), lambda i: (0, 0, 0))) + (ANY,) * count,
        scratch_shapes=[pltpu.VMEM((8, heads // 2, rows, 128), jnp.int32)] + gather_scratch(G, halves, count),
        compiler_params=params(cid), name="layout_bias_gather")(
            steps, tab, boxes.T, boxes, pages[:, None], pages[None], *shards)
    return outs[0], outs[1:3], outs[3:]


def half_of(v, e):
    lane = lax.broadcasted_iota(jnp.int32, v.shape, 1)
    return jnp.where((lane >= 64) == (e == 1), v, jnp.zeros_like(v))


def join(a, b):
    lane = lax.broadcasted_iota(jnp.int32, a.shape, 1)
    return jnp.where(lane < 64, a, b)


def project(tok_ref, gain_ref, w_ref, normed, qkv):
    gain = gain_ref[...]

    @pl.loop(0, tok_ref.shape[0] // TILE)
    def _(t):
        r = pl.ds(pl.multiple_of(t * TILE, TILE), TILE)
        x = tok_ref[r, :].astype(f32)
        low = (x * lax.rsqrt(jnp.mean(x * x, axis=1, keepdims=True) + epsilon) * gain).astype(bf16)
        normed[r, :] = low
        qkv[r, :] = jnp.dot(low, w_ref[...], preferred_element_type=f32).astype(bf16)


def fwd_tile(p, i, tq, pairs, qkv, bias_ref, o_ref, lse_ref):
    cols = lambda k: pl.ds(pl.multiple_of((p + k * pairs) * 128, 128), 128)
    q, k, v = qkv[pl.ds(pl.multiple_of(i * tq, tq), tq), cols(0)], qkv[:, cols(1)], qkv[:, cols(2)]
    outs, lses = [], []
    for e in range(2):
        s = lax.dot_general(half_of(q, e), k, NT, preferred_element_type=f32) + bias_ref[e]
        peak = jnp.max(s, axis=1, keepdims=True)
        w = jnp.exp(s - peak)
        total = jnp.sum(w, axis=1, keepdims=True)
        outs.append(jnp.dot(w.astype(bf16), v, preferred_element_type=f32) / total)
        lses.append(peak + jnp.log(total))
    o_ref[...] = join(*outs).astype(bf16)
    lse_ref[0] = jnp.concatenate(lses, axis=1)


def fwd_kernel(pairs, tiles, G, halves, count, *refs):
    (tok, gain, w, bias_ref), srcs = refs[:4], refs[4:4 + count]
    o_ref, lse_ref, normed_h, qkv_h = refs[4 + count:8 + count]
    outs, (normed, qkv, keep), sems = refs[8 + count:8 + 2 * count], refs[8 + 2 * count:11 + 2 * count], refs[11 + 2 * count:]
    p, i = pl.program_id(0), pl.program_id(1)
    now, steps = p * tiles + i, pairs * tiles
    copies = lambda: [pltpu.make_async_copy(normed, normed_h, keep.at[0]), pltpu.make_async_copy(qkv, qkv_h, keep.at[1])]

    def compute():
        @pl.when(now == 0)
        def _():
            project(tok, gain, w, normed, qkv)
            for c in copies():
                c.start()

        fwd_tile(p, i, o_ref.shape[0], pairs, qkv, bias_ref, o_ref, lse_ref)

        @pl.when(now == steps - 1)
        def _():
            for c in copies():
                c.wait()

    beside(Gather(G, halves, srcs, outs, *sems).events(), G, steps, now, compute)


def attn_fwd_and_gather(tok, gain, w, bias, shards, halves, wide, cid, tq=256):
    n, d = tok.shape
    width = w.shape[1] // 3
    pairs, tiles, count, G = width // 128, n // tq, len(shards), wide // 4
    sds = jax.ShapeDtypeStruct
    const = lambda s: pl.BlockSpec(s, lambda p, i: (0, 0))
    outs = pl.pallas_call(functools.partial(fwd_kernel, pairs, tiles, G, halves, count), grid=(pairs, tiles),
        out_shape=(sds((n, width), bf16), sds((pairs, n, 2), f32), sds((n, d), bf16), sds((n, 3 * width), bf16)) + gathered_shapes(shards, wide),
        in_specs=[const((n, d)), const((1, d)), const(w.shape), pl.BlockSpec((2, tq, n), lambda p, i: (p, i, 0))] + [ANY] * count,
        out_specs=(pl.BlockSpec((tq, 128), lambda p, i: (i, p)), pl.BlockSpec((1, tq, 2), lambda p, i: (p, i, 0)), ANY, ANY) + (ANY,) * count,
        scratch_shapes=[pltpu.VMEM((n, d), bf16), pltpu.VMEM((n, 3 * width), bf16), D((2,))] + gather_scratch(G, halves, count),
        compiler_params=params(cid), name="attention_gather")(tok, gain, w, bias, *shards)
    return outs[:4], outs[4:]


def band_sums(i, e, g_ref, band_ref, far_ref):
    tq, n = g_ref.shape[1], g_ref.shape[2]
    first = i * (tq // 128) - 1

    @pl.when(i == 0)
    def _():
        band_ref[e] = jnp.zeros(band_ref.shape[1:], f32)
        far_ref[e] = jnp.zeros(far_ref.shape[1:], f32)

    for m in range(tq // 128 + 2):
        @pl.when((first + m >= 0) & (first + m < n // 128))
        def _():
            band_ref[e, :, m * 128:(m + 1) * 128] += g_ref[e, :, pl.ds(pl.multiple_of((first + m) * 128, 128), 128)].astype(f32)

    for c in range(n // 128):
        @pl.when((c < first) | (c > first + tq // 128 + 1))
        def _():
            total = g_ref[e, 0:16, c * 128:(c + 1) * 128].astype(f32)
            for k in range(1, tq // 16):
                total = total + g_ref[e, k * 16:(k + 1) * 16, c * 128:(c + 1) * 128].astype(f32)
            far_ref[e, jnp.where(c < first, 0, 1)] += total


def bwd_tile(p, pairs, i, last_tile, last, q_ref, k_ref, v_ref, bias_ref, o_ref, do_ref, lse_ref, normed_ref, w_ref,
             g_ref, band_ref, far_ref, dw_ref, dx_ref, dkt, dvt, dqkv, turned):
    tq, n = q_ref.shape[0], k_ref.shape[0]
    rows = pl.ds(pl.multiple_of(i * tq, tq), tq)

    @pl.when(p == 0)
    def _():
        turned[:, rows] = normed_ref[rows, :].T

    @pl.when(i == 0)
    def _():
        dkt[...] = jnp.zeros_like(dkt)
        dvt[...] = jnp.zeros_like(dvt)

    q, k, v, do = q_ref[...], k_ref[...], v_ref[...], do_ref[...]
    prod = do.astype(f32) * o_ref[...].astype(f32)
    dqs = []
    for e in range(2):
        qm, dom = half_of(q, e), half_of(do, e)
        s = lax.dot_general(qm, k, NT, preferred_element_type=f32) + bias_ref[e]
        w = jnp.exp(s - lse_ref[0, :, e:e + 1])
        dp = lax.dot_general(dom, v, NT, preferred_element_type=f32)
        inner = jnp.sum(half_of(prod, e), axis=1, keepdims=True)
        g = (w * (dp - inner)).astype(bf16)
        g_ref[e] = g
        dqs.append(jnp.dot(g, k, preferred_element_type=f32))
        dvt[...] += jnp.dot(dom.T, w.astype(bf16), preferred_element_type=f32)
        dkt[...] += jnp.dot(qm.T, g, preferred_element_type=f32)
        band_sums(i, e, g_ref, band_ref, far_ref)
    columns = lambda k: pl.ds(pl.multiple_of((p + k * pairs) * 128, 128), 128)
    dqkv[rows, columns(0)] = join(*dqs).astype(bf16)

    @pl.when(last_tile)
    def _():
        dqkv[:, columns(1)] = dkt[...].T.astype(bf16)
        dqkv[:, columns(2)] = dvt[...].T.astype(bf16)

        @pl.when(last)
        def _():
            @pl.loop(0, n // TILE)
            def _(t):
                r = pl.ds(pl.multiple_of(t * TILE, TILE), TILE)
                dw_ref[r, :] = jnp.dot(turned[r, :], dqkv[...], preferred_element_type=f32).astype(bf16)
                dx_ref[r, :] = lax.dot_general(dqkv[r, :], w_ref[...], NT, preferred_element_type=f32).astype(bf16)


def bwd_kernel(pairs, tiles, G, halves, count, *refs):
    ins, parts = refs[:9], refs[9:9 + count]
    mid = refs[9 + count:14 + count]
    outs, accs, sems = refs[14 + count:14 + 2 * count], refs[14 + 2 * count:18 + 2 * count], refs[18 + 2 * count:]
    p, i = pl.program_id(0), pl.program_id(1)
    comm = Scatter(G, halves, parts, outs, *sems)
    beside(comm.events(), G, pairs * tiles, p * tiles + i,
           lambda: bwd_tile(p, pairs, i, i == tiles - 1, p == pairs - 1, *ins, *mid, *accs))


def shard_shapes(parts, wide):
    return tuple(jax.ShapeDtypeStruct((p.shape[0] // wide, p.shape[1]), f32) for p in parts)


def attn_bwd_and_scatter(qkv, bias, o, do, lse, normed, w, parts, halves, wide, cid, tq=256):
    n, width, d = qkv.shape[0], qkv.shape[1] // 3, normed.shape[1]
    pairs, tiles, count, G = width // 128, n // tq, len(parts), wide // 4
    sds = jax.ShapeDtypeStruct
    tile = pl.BlockSpec((tq, 128), lambda p, i: (i, p))
    full = lambda rows, k: pl.BlockSpec((rows, 128), lambda p, i: (0, p + k * pairs))
    const = lambda s: pl.BlockSpec(s, lambda p, i: (0, 0))
    outs = pl.pallas_call(functools.partial(bwd_kernel, pairs, tiles, G, halves, count), grid=(pairs, tiles),
        out_shape=(sds((2 * pairs, n, n), bf16), sds((2 * pairs, tq, tq + 256), f32), sds((2 * pairs, 2, 16, 128), f32)) + (sds((d, 3 * width), bf16), sds((n, d), bf16)) + shard_shapes(parts, wide),
        in_specs=[tile, full(n, 1), full(n, 2), pl.BlockSpec((2, tq, n), lambda p, i: (p, i, 0)), tile, tile,
                  pl.BlockSpec((1, tq, 2), lambda p, i: (p, i, 0)), const((n, d)), const(w.shape)] + [ANY] * count,
        out_specs=(pl.BlockSpec((2, tq, n), lambda p, i: (p, i, 0)), pl.BlockSpec((2, tq, tq + 256), lambda p, i: (p, 0, 0)),
                   pl.BlockSpec((2, 2, 16, 128), lambda p, i: (p, 0, 0, 0))) + (const(w.shape), const((n, d))) + (whole_vmem(),) * count,
        scratch_shapes=[pltpu.VMEM((128, n), f32), pltpu.VMEM((128, n), f32), pltpu.VMEM((n, 3 * width), bf16), pltpu.VMEM((d, n), bf16)] + scatter_scratch(G, halves, parts[0].shape[0] // wide),
        compiler_params=params(cid), name="attention_back_scatter")(
            qkv, qkv, qkv, bias, o, do, lse, normed, w, *parts)
    return outs[:5], outs[5:]


def rows_times_hots(src, ids, rows, heads, gs):
    n = src(0).shape[1]
    for h in range(heads):
        block = src(h)
        for c in range(n // 128):
            gs[c, h * rows:(h + 1) * rows, :] = block[:, c * 128:(c + 1) * 128]
    labels = [lax.broadcasted_iota(jnp.int32, (16, n), 0).astype(bf16) + float(k) for k in (0, 16)]
    one, zero = jnp.ones((16, n), bf16), jnp.zeros((16, n), bf16)
    group = 4 // len(ids(0))
    total = jnp.zeros((heads * group, 128), f32)
    for first in range(0, rows, group):
        grow, hots = [], []
        for r in range(first, first + group):
            grow.append(jnp.concatenate([gs[c, pl.ds(r, heads, stride=rows), :] for c in range(n // 128)], axis=1))
            for one_row in ids(r):
                row = jnp.broadcast_to(one_row, (16, n)).astype(bf16)
                hots += [jnp.where(row == label, one, zero) for label in labels]
        total = total + lax.dot_general(jnp.concatenate(grow, axis=0).astype(bf16), jnp.concatenate(hots, axis=0), NT, preferred_element_type=f32)
    return total


def own_blocks(total, heads, width):
    out = total[0:heads, 0:width]
    for k in range(1, 128 // width):
        out = out + total[k * heads:(k + 1) * heads, k * width:(k + 1) * width]
    return out


def halves_times_hots(g_ref, ids_ref, block, heads, gs, low):
    rows, n = 16, g_ref.shape[2]
    for h in range(heads):
        for c in range(n // 128):
            gs[c, h * rows:(h + 1) * rows, :] = g_ref[h, block, c * 128:(c + 1) * 128].astype(f32)
    for t in range(2):
        ids = ids_ref[t, block, :]
        low[t] = jnp.where(ids >= 16.0, ids - 16.0, ids)
    label = lax.broadcasted_iota(jnp.int32, (16, n), 0).astype(bf16)
    one, zero = jnp.ones((16, n), bf16), jnp.zeros((16, n), bf16)
    total = jnp.zeros((64, 64), f32)
    for first in range(0, rows, 2):
        left, hots = [], []
        for r in range(first, first + 2):
            grow = jnp.concatenate([gs[c, pl.ds(r, heads, stride=rows), :] for c in range(n // 128)], axis=1)
            for t in range(2):
                upper = jnp.broadcast_to(ids_ref.at[t, block][r:r + 1, :], (heads, n)) >= 16.0
                left += [jnp.where(upper, 0.0, grow), jnp.where(upper, grow, 0.0)]
                row = jnp.broadcast_to(low[t, r:r + 1, :], (16, n)).astype(bf16)
                hots.append(jnp.where(row == label, one, zero))
        total = total + lax.dot_general(jnp.concatenate(left, axis=0).astype(bf16), jnp.concatenate(hots, axis=0), NT, preferred_element_type=f32)
    return total


def own_halves(total, heads):
    out = 0.0
    for k in range(2):
        part = lambda t, up: total[k * 32 + (2 * t + up) * heads:k * 32 + (2 * t + up + 1) * heads, k * 32 + t * 16:k * 32 + t * 16 + 16]
        out = out + jnp.concatenate([part(0, 0), part(0, 1), part(1, 0), part(1, 1)], axis=1)
    return out


def hist_tile(now, heads, g_ref, ids_ref, band_ref, far_ref, lin_ids, table, boxes, gs, low):
    @pl.when(now == 0)
    def _():
        sides = [jnp.sum(jnp.sum(far_ref[:, k], axis=1), axis=1, keepdims=True) for k in range(2)]
        lane = lax.broadcasted_iota(jnp.int32, (heads, 128), 1)
        table[...] = jnp.zeros_like(table)
        boxes[...] = jnp.zeros_like(boxes)
        table[0:heads, :] = jnp.where(lane == 15, sides[0], 0.0) + jnp.where(lane == 31, sides[1], 0.0)

    big = g_ref.shape[1]

    @pl.loop(0, big // 16)
    def _(q):
        block = pl.ds(pl.multiple_of(q * 16, 16), 16)
        boxes[...] += halves_times_hots(g_ref, ids_ref, block, heads, gs, low)

    wide = band_ref.shape[2] // 128
    per = lin_ids.shape[1]
    a = now * 16 // per
    inside = pl.ds(pl.multiple_of(now * 16 % per, 16), 16)

    def band_ids(r):
        return [jnp.concatenate([lin_ids.at[jnp.clip((m - 1) * (128 // per) - a + 4, 0, 7), inside][r:r + 1, :] for m in range(wide)], axis=1)]

    table[...] += rows_times_hots(lambda h: band_ref[h], band_ids, 16, heads, gs)


def hist_kernel(heads, rows, n, G, halves, count, *refs):
    (g_ref, ids_ref, band_ref, far_ref, lin_ids, dx, tok, gh, gain_ref, gain_two), parts = refs[:10], refs[10:10 + count]
    small_ref, gt_ref = refs[10 + count:12 + count]
    outs, rest = refs[12 + count:12 + 2 * count], refs[12 + 2 * count:]
    (gs, low, table, boxes, got, pair_sem), sums, sems = rest[:6], rest[6:13], rest[13:]
    acc = sums[0]
    now, steps = pl.program_id(0), n // rows
    core = lax.axis_index("narrow")
    mine = tok.shape[0]
    d = tok.shape[1]
    comm = Scatter(G, halves, parts, outs, *sems)
    swap = lambda: remote(dx.at[pl.ds(pl.multiple_of((1 - core) * mine, mine), mine)], got, pair_sem.at[0], pair_sem.at[1], {"narrow": 1 - core})

    def compute():
        @pl.when(now == 0)
        def _():
            swap().start()
            acc[0] = jnp.zeros(acc.shape[1:], f32)
            for k in range(d // 128):
                acc[0, d // 128 + k:d // 128 + k + 1, :] = gain_two[:, k * 128:(k + 1) * 128]

        @pl.when(now == steps // 8)
        def _():
            swap().wait()

        for t in range(mine // TILE):
            @pl.when(now == steps // 8 + t)
            def _():
                r = pl.ds(t * TILE, TILE)
                x = tok[r, :].astype(f32)
                total = dx[pl.ds(pl.multiple_of(core * mine + t * TILE, TILE), TILE), :].astype(f32) + got[r, :].astype(f32)
                factor = lax.rsqrt(jnp.mean(x * x, axis=1, keepdims=True) + epsilon)
                unit = x * factor
                scaled = gain_ref[...] * total
                gt_ref[r, :] = gh[r, :] + factor * (scaled - unit * jnp.mean(scaled * unit, axis=1, keepdims=True))
                gain = jnp.sum(total * unit, axis=0, keepdims=True)
                for k in range(d // 128):
                    acc[0, k:k + 1, :] += gain[:, k * 128:(k + 1) * 128]

        hist_tile(now, heads, g_ref, ids_ref, band_ref, far_ref, lin_ids, table, boxes, gs, low)

    def reduce():
        acc[0, pl.ds(pl.multiple_of(2 * (d // 128) + core * heads, 8), heads), 0:32] = own_blocks(table[...], heads, 32)
        acc[0, pl.ds(pl.multiple_of(2 * (d // 128) + core * heads, 8), heads), 32:96] = own_halves(boxes[...], heads)
        small_ref[...] = sum_everywhere(G, *sums)

    beside(comm.events(1), G, steps, now, compute, (reduce,))


def hist_and_scatter(g, band, far, ids, dx, tok, gh, gain, gain_two, parts, halves, wide, cid):
    heads, n, _ = g.shape
    rows, count, G, d = n // (band.shape[1] // 16), len(parts), wide // 4, tok.shape[1]
    box_ids, lin_ids = ids
    small = 2 * (d // 128) + 2 * heads
    sds = jax.ShapeDtypeStruct
    const = lambda s: pl.BlockSpec(s, lambda i: (0, 0))
    outs = pl.pallas_call(functools.partial(hist_kernel, heads, rows, n, G, halves, count), grid=(n // rows,),
        out_shape=(sds((small, 128), f32), sds(tok.shape, f32)) + shard_shapes(parts, wide),
        in_specs=[pl.BlockSpec((heads, rows, n), lambda i: (0, i, 0)), pl.BlockSpec((2, rows, n), lambda i: (0, i, 0)),
                  pl.BlockSpec((heads, 16, band.shape[2]), lambda i: (0, i, 0)), pl.BlockSpec(far.shape, lambda i: (0, 0, 0, 0)),
                  pl.BlockSpec(lin_ids.shape, lambda i: (0, 0, 0)), const(dx.shape), const(tok.shape), const(gh.shape), const(gain.shape), const(gain_two.shape)] + [ANY] * count,
        out_specs=(const((small, 128)), const(tok.shape)) + (whole_vmem(),) * count,
        scratch_shapes=[pltpu.VMEM((n // 128, heads * 16, 128), f32), pltpu.VMEM((2, 16, n), f32), pltpu.VMEM((4 * heads, 128), f32), pltpu.VMEM((64, 64), f32), pltpu.VMEM(tok.shape, bf16), D((2,))]
        + sum_scratch(G, small) + scatter_scratch(G, halves, parts[0].shape[0] // wide),
        compiler_params=params(cid), name="table_grad_scatter")(g, box_ids, band, far, lin_ids, dx, tok, gh, gain, gain_two, *parts)
    return outs[0], outs[1], outs[2:]


D = pltpu.SemaphoreType.DMA


def place():
    me = lax.axis_index("wide")
    return me // 4, (me // 2) % 2, me % 2


def wide_id(z, y, x):
    return {"wide": z * 4 + y * 2 + x}


def shard_rows(z, y, x, R):
    return pl.ds(pl.multiple_of((z * 4 + y * 2 + x) * R, R), R)


def remote(src, dst, send, recv, target):
    return pltpu.make_async_remote_copy(src_ref=src, dst_ref=dst, send_sem=send, recv_sem=recv, device_id=target, device_id_type=MESH)


def greet(G, far, pair=0):
    z, y, x = place()
    bar = pltpu.get_barrier_semaphore()
    sig = lambda t: pl.semaphore_signal(bar, inc=1, device_id=t, device_id_type=MESH)
    sig(wide_id(z, 1 - y, x))
    sig(wide_id(z, y, 1 - x))
    if pair:
        sig({"narrow": 1 - lax.axis_index("narrow")})
    if far:
        for k in range(1, G):
            sig(wide_id((z + k) % G, y, x))
        pl.semaphore_wait(bar, 2 + pair + G - 1)
    else:
        @pl.when(z > 0)
        def _():
            sig(wide_id(z - 1, y, x))

        @pl.when(z < G - 1)
        def _():
            sig(wide_id(z + 1, y, x))

        pl.semaphore_wait(bar, 2 + pair + (z > 0).astype(jnp.int32) + (z < G - 1).astype(jnp.int32))


class Gather:
    def __init__(self, G, halves, srcs, outs, local_sem, zs, zr, ns, nr):
        self.G, self.halves, self.srcs, self.local_sem = G, halves, srcs, local_sem
        self.outs = [o if isinstance(o, tuple) else (o, 0, 0) for o in outs]
        self.widths = [sum(w for h in halves for a, _, w in h if a == k) for k in range(len(srcs))]
        self.zs, self.zr, self.ns, self.nr = zs, zr, ns, nr
        self.most = max(len(h) for h in halves)
        self.z, self.y, self.x = place()
        self.R = srcs[0].shape[0]

    def hop(self, own, zz, yy, xx, h, way, j):
        target = wide_id(self.z, 1 - self.y, self.x) if way == "y" else wide_id(self.z, self.y, 1 - self.x)
        copies = []
        for n, (a, c, w) in enumerate(self.halves[h]):
            slot = (zz * 6 + j) * self.most + n
            out, first, at = self.outs[a]
            dst = out.at[shard_rows(zz, yy, xx, self.R), pl.ds(first + c, w)]
            copies.append(remote(self.srcs[a].at[:, pl.ds(at + c, w)] if own else dst, dst, self.ns.at[slot], self.nr.at[slot], target))
        return copies

    def second_stage(self, zz, own=False):
        return self.hop(own, zz, self.y, self.x, 0, "y", 0) + self.hop(own, zz, self.y, self.x, 1, "x", 1)

    def third_stage(self, zz, own=False):
        return self.hop(own, zz, self.y, self.x, 0, "x", 2) + self.hop(own, zz, self.y, self.x, 1, "y", 3)

    def last_stage(self, zz):
        return self.hop(False, zz, 1 - self.y, self.x, 0, "x", 4) + self.hop(False, zz, self.y, 1 - self.x, 1, "y", 5)

    def relay(self, own, zz, step, way):
        copies = []
        for a in range(len(self.srcs)):
            slot = (way * (self.G - 1) + step) * len(self.srcs) + a
            dst = self.whole(a, zz)
            copies.append(remote(self.own(a) if own else dst, dst, self.zs.at[slot], self.zr.at[slot],
                                 wide_id(self.z + (1 if way == 0 else -1), self.y, self.x)))
        return copies

    def whole(self, a, zz):
        out, first, _ = self.outs[a]
        return out.at[shard_rows(zz, self.y, self.x, self.R), pl.ds(first, self.widths[a])]

    def own(self, a):
        return self.srcs[a].at[:, pl.ds(self.outs[a][2], self.widths[a])]

    def can(self, way):
        return self.z < self.G - 1 if way == 0 else self.z > 0

    def source(self, d, way):
        return (self.z - d, self.z - d >= 0) if way == 0 else (self.z + d, self.z + d < self.G)

    def keep(self):
        return [pltpu.make_async_copy(self.own(a), self.whole(a, self.z), self.local_sem.at[a]) for a in range(len(self.srcs))]

    def begin(self):
        for way in range(2):
            @pl.when(self.can(way))
            def _():
                for c in self.relay(True, self.z, 0, way):
                    c.start()
        for c in self.second_stage(self.z, True) + self.third_stage(self.z, True) + self.keep():
            c.start()

    def turn(self, zz):
        for c in self.hop(False, zz, 1 - self.y, self.x, 0, "y", 0) + self.hop(False, zz, self.y, 1 - self.x, 1, "x", 1):
            c.wait_recv()
        for c in self.last_stage(zz):
            c.start()

    def step(self, d):
        for way in range(2):
            zz, there = self.source(d, way)

            @pl.when(there)
            def _():
                for c in self.relay(False, zz, d - 1, way):
                    c.wait_recv()

                @pl.when(self.can(way))
                def _():
                    for c in self.relay(False, zz, d, way):
                        c.start()

                for c in self.second_stage(zz):
                    c.start()
        for way in range(2):
            zz, there = self.source(d, way)

            @pl.when(there)
            def _():
                for c in self.third_stage(zz):
                    c.start()

    def turns(self, d):
        if d == 0:
            self.turn(self.z)
            return
        for way in range(2):
            zz, there = self.source(d, way)

            @pl.when(there)
            def _():
                self.turn(zz)

    def finish(self):
        y, x = self.y, self.x

        @pl.loop(0, self.G)
        def _(zz):
            for c in (self.hop(False, zz, y, 1 - x, 0, "x", 2) + self.hop(False, zz, 1 - y, x, 1, "y", 3)
                      + self.hop(False, zz, 1 - y, 1 - x, 0, "x", 4) + self.hop(False, zz, 1 - y, 1 - x, 1, "y", 5)):
                c.wait_recv()
            for c in self.second_stage(zz) + self.third_stage(zz) + self.last_stage(zz):
                c.wait_send()

        for way in range(2):
            @pl.when(self.can(way))
            def _():
                for c in self.relay(True, self.z, 0, way):
                    c.wait_send()
                for d in range(1, self.G - 1):
                    zz, there = self.source(d, way)

                    @pl.when(there)
                    def _():
                        for c in self.relay(False, zz, d, way):
                            c.wait_send()
        for c in self.keep():
            c.wait()

    def events(self):
        G = self.G
        first = lambda: (greet(G, False), self.begin())
        ev = [(0.0, first), (0.7, lambda: self.turns(0))]
        for d in range(1, G):
            ev += [(1.15 * d, functools.partial(self.step, d)), (1.3 * d + 1.2, functools.partial(self.turns, d))]
        return sorted(ev, key=lambda e: e[0]), self.finish


def gather_scratch(G, halves, arrays):
    most = max(len(h) for h in halves)
    return [D((arrays,)), D((2 * (G - 1) * arrays,)), D((2 * (G - 1) * arrays,)), D((6 * G * most,)), D((6 * G * most,))]


class Scatter:
    def __init__(self, G, halves, parts, outs, r1a, r1b, o1a, o1b, r2a, r2b, r3, own, lsem, s1, v1, s2, v2, s3, v3):
        self.__dict__.update(locals())
        self.most = max(len(h) for h in halves)
        self.wa, self.wb = [sum(p[2] for p in h) for h in halves]
        self.R = parts[0].shape[0] // (4 * G)
        self.z, self.y, self.x = place()
        self.order = sorted(range(1, G), key=lambda k: min(k, G - k), reverse=True) + [0]

    def zk(self, k):
        return (self.z + k) % self.G

    def neighbour(self, way):
        return wide_id(self.z, 1 - self.y, self.x) if way == "y" else wide_id(self.z, self.y, 1 - self.x)

    def pieces(self, h):
        at, out = 0, []
        for n, (a, c, w) in enumerate(self.halves[h]):
            out.append((n, a, pl.ds(c, w), pl.ds(at, w)))
            at += w
        return out

    def sources(self, k, mine):
        z, y, x = self.zk(k), self.y, self.x
        for h in range(2):
            for n, a, src, dst in self.pieces(h):
                for j in range(2):
                    if h == 0:
                        rows = shard_rows(z, j, x if mine else 1 - x, self.R)
                    else:
                        rows = shard_rows(z, y if mine else 1 - y, j, self.R)
                    yield h, j, dst, ((2 * k + h) * self.most + n) * 2 + j, self.parts[a].at[rows, src]

    def one(self, k):
        return [remote(src, (self.r1a, self.r1b)[h].at[k, j, :, dst], self.s1.at[slot], self.v1.at[slot], self.neighbour("xy"[h]))
                for h, j, dst, slot, src in self.sources(k, False)]

    def load(self, k):
        return [pltpu.make_async_copy(src, (self.o1a, self.o1b)[h].at[k, j, :, dst], self.lsem.at[slot]) for h, j, dst, slot, src in self.sources(k, True)]

    def two(self, k):
        return [remote(self.o1a.at[k, 1 - self.y], self.r2a.at[k], self.s2.at[2 * k], self.v2.at[2 * k], self.neighbour("y")),
                remote(self.o1b.at[k, 1 - self.x], self.r2b.at[k], self.s2.at[2 * k + 1], self.v2.at[2 * k + 1], self.neighbour("x"))]

    def three(self, k):
        return remote(self.own.at[k], self.r3.at[k - 1], self.s3.at[k - 1], self.v3.at[k - 1], wide_id(self.zk(k), self.y, self.x))

    def launch(self, k):
        for c in self.one(k) + self.load(k):
            c.start()

    def begin(self):
        for k in self.order[:2]:
            self.launch(k)

    def rows(self, count, body):
        step = min(16, count)

        @pl.loop(0, count // step)
        def _(i):
            body(pl.ds(pl.multiple_of(i * step, step), step))

    def add_one(self, n):
        k = self.order[n]
        for c in self.one(k):
            c.wait_recv()
        for c in self.load(k):
            c.wait()
        for mine, got in ((self.o1a, self.r1a), (self.o1b, self.r1b)):
            def body(r):
                for j in range(2):
                    mine[k, j, r, :] = (mine[k, j, r, :].astype(f32) + got[k, j, r, :].astype(f32)).astype(bf16)

            self.rows(self.R, body)
        for c in self.two(k):
            c.start()
        if n + 2 < self.G:
            self.launch(self.order[n + 2])

    def add_two(self, n):
        k = self.order[n]
        for c in self.two(k):
            c.wait_recv()

        def body(r):
            self.own[k, r, pl.ds(0, self.wa)] = (self.o1a[k, self.y, r, :].astype(f32) + self.r2a[k, r, :].astype(f32)).astype(bf16)
            self.own[k, r, pl.ds(self.wa, self.wb)] = (self.o1b[k, self.x, r, :].astype(f32) + self.r2b[k, r, :].astype(f32)).astype(bf16)

        self.rows(self.R, body)
        if k:
            self.three(k).start()

    def finish(self):
        self.add_two(self.G - 1)
        for k in range(1, self.G):
            self.three(k).wait_recv()

        def body(r):
            for h in range(2):
                for _, a, src, dst in self.pieces(h):
                    cols = pl.ds(dst.start + h * self.wa, dst.size)
                    total = self.own[0, r, cols].astype(f32)
                    for k in range(self.G - 1):
                        total = total + self.r3[k, r, cols].astype(f32)
                    self.outs[a][r, src] = total

        self.rows(self.R, body)
        for k in range(self.G):
            for c in self.one(k) + self.two(k):
                c.wait_send()
            if k:
                self.three(k).wait_send()

    def events(self, pair=0):
        G = self.G
        first = lambda: (greet(G, True, pair), self.begin())
        ev = [(0.0, first), (1.1, lambda: self.add_one(0))]
        for n in range(1, G):
            ev += [(1.5 * n + 0.65, functools.partial(self.add_one, n)), (1.5 * n + 1.1, functools.partial(self.add_two, n - 1))]
        return sorted(ev, key=lambda e: e[0]), self.finish


def scatter_scratch(G, halves, R):
    most = max(len(h) for h in halves)
    a, b = [sum(p[2] for p in h) for h in halves]
    V = lambda *s: pltpu.VMEM(s, bf16)
    return [V(G, 2, R, a), V(G, 2, R, b), V(G, 2, R, a), V(G, 2, R, b), V(G, R, a), V(G, R, b), V(G - 1, R, a + b), V(G, R, a + b),
            D((4 * G * most,)), D((4 * G * most,)), D((4 * G * most,)), D((2 * G,)), D((2 * G,)), D((G - 1,)), D((G - 1,))]


def beside(plan, G, steps, now, compute, late=()):
    events, finish = plan
    units = 1.55 * G
    for n in range(steps):
        here = [act for t, act in events if min(steps - 1, int(-(-t * steps // units))) == n]
        if here:
            @pl.when(now == n)
            def _():
                for act in here:
                    act()
    compute()

    @pl.when(now == steps - 1)
    def _():
        for act in late:
            act()
        finish()


ANY = pl.BlockSpec(memory_space=pl.ANY)


def whole_vmem():
    return pl.BlockSpec(memory_space=pltpu.VMEM)


def gathered_shapes(shards, wide):
    return tuple(jax.ShapeDtypeStruct((wide * s.shape[0], s.shape[1]), s.dtype) for s in shards)


def sum_everywhere(G, acc, got, gz, s, v, sz, vz):
    z, y, x = place()
    core = {"narrow": 1 - lax.axis_index("narrow")}
    for n, t in enumerate((core, wide_id(z, y, 1 - x), wide_id(z, 1 - y, x))):
        c = remote(acc.at[n], got.at[n], s.at[n], v.at[n], t)
        c.start()
        c.wait()
        acc[n + 1] = acc[n] + got[n]
    gz[z] = acc[3]
    far = [wide_id((z + k) % G, y, x) for k in range(1, G)]
    sent = [remote(acc.at[3], gz.at[z], sz.at[k], vz.at[z], t) for k, t in enumerate(far)]
    for c in sent:
        c.start()
    for k in range(1, G):
        zz = (z + k) % G
        remote(acc.at[3], gz.at[zz], sz.at[k - 1], vz.at[zz], far[k - 1]).wait_recv()
    for c in sent:
        c.wait_send()
    total = gz[0]
    for k in range(1, G):
        total = total + gz[k]
    return total


def sum_scratch(G, rows):
    V = lambda k: pltpu.VMEM((k, rows, 128), f32)
    return [V(4), V(3), V(G), D((3,)), D((3,)), D((G - 1,)), D((G,))]


def nt(a, b):
    return lax.dot_general(a, b, NT, preferred_element_type=f32)


def nn(a, b):
    return jnp.dot(a, b, preferred_element_type=f32)


def gelu_and_slope(v):
    root = 0.7978845608028654
    square = v * v
    t = jnp.tanh(root * v * (1.0 + 0.044715 * square))
    half = 0.5 * (1.0 + t)
    return v * half, half + 0.5 * v * (1.0 - t * t) * root * (1.0 + 3 * 0.044715 * square)


def mid_kernel(G, cut, att_h, tok_h, cot_h, wo_h, wg_h, wu_h, wd_h, wd_shard, gain_ref,
               gout_h, gg_h, gu_h, gd_h, y_ref, gh_ref, ga_ref, ggain_ref,
               att, tok, cot, wo, wg, wu, wd, part, other, back, hid, n2t, cott, hff, gg, gu, ysend, yown, yother, stage,
               isem, osem, sp, vp, sb, vb, sy, vy, *sems):
    core = lax.axis_index("narrow")
    peer = {"narrow": 1 - core}
    n, d = tok.shape
    ff = wg.shape[1]
    tiles = n // TILE
    half = tiles // 2
    loads = [pltpu.make_async_copy(s, t, isem.at[k]) for k, (s, t) in enumerate(
        [(att_h, att), (wo_h, wo), (tok_h, tok), (wg_h, wg), (wu_h, wu), (cot_h, cot), (wd_h, wd.at[:, pl.ds(0, cut)])])]
    for c in loads:
        c.start()
    mid = cut + (ff - cut) // 256 * 128
    bring = Gather(G, (((0, 0, mid - cut),), ((0, mid - cut, ff - mid),)), [wd_shard], [(wd, cut, cut)], *sems)
    greet(G, False, 1)
    bring.begin()
    rows_of = lambda t: pl.ds(pl.multiple_of(t * TILE, TILE), TILE)
    send_part = lambda t: remote(part.at[rows_of(t)], other.at[rows_of(t)], sp.at[t], vp.at[t], peer)
    send_back = lambda t: remote(part.at[rows_of(t)], back.at[rows_of(t)], sb.at[t], vb.at[t], peer)
    send_y = lambda j: remote(ysend.at[rows_of(j)], yother.at[rows_of(j)], sy.at[j], vy.at[j], peer)
    gain = gain_ref[...]

    for c in loads[:2]:
        c.wait()

    def at_step(s, plan):
        for k, acts in plan.items():
            @pl.when(s == k)
            def _():
                for act in acts:
                    act()

    turns = [functools.partial(bring.turns, k) for k in range(G)]
    steps = [functools.partial(bring.step, k) for k in range(1, G)]

    @pl.loop(0, tiles)
    def _(t):
        part[rows_of(t), :] = nt(att[rows_of(t), :], wo[...]).astype(bf16)
        send_part(t).start()
        at_step(t, {1: turns[:1], 2: steps[:1]})

    for c in loads[2:]:
        c.wait()

    chunks, at = [], 0
    while at < ff:
        w = min(384, ff - at)
        chunks.append((at, w))
        at += w

    later = [act for pair in zip(turns[1:], steps[1:] + [lambda: None]) for act in pair]

    @pl.loop(0, tiles)
    def _(s):
        t = (s + half * (1 - core)) % tiles
        r = rows_of(t)
        send_part(t).wait()
        h = tok[r, :].astype(f32) + (part[r, :].astype(f32) + other[r, :].astype(f32))
        hid[r, :] = h
        factor = lax.rsqrt(jnp.mean(h * h, axis=1, keepdims=True) + epsilon)
        low = (h * factor * gain).astype(bf16)
        n2t[:, r] = low.T
        cott[:, r] = cot[r, :].T
        for at, w in chunks:
            cols = pl.ds(at, w)
            act, slope = gelu_and_slope(nn(low, wg[:, cols]))
            up = nn(low, wu[:, cols])
            hff[r, cols] = (act * up).astype(bf16)
            gg[r, cols] = (up * slope).astype(bf16)
            gu[r, cols] = act.astype(bf16)
        at_step(s, {1: later[:2], 2: later[2:4], 3: later[4:]})

    def weight_grad(left, right, out, slot, width):
        @pl.loop(0, d // TILE)
        def _(k):
            b = k % 2
            copy = lambda kk: pltpu.make_async_copy(stage.at[kk % 2, :, pl.ds(0, width)], out.at[rows_of(kk)], osem.at[2 * slot + kk % 2])

            @pl.when(k >= 2)
            def _():
                copy(k - 2).wait()

            stage[b, :, pl.ds(0, width)] = nn(left[rows_of(k), :], right[...]).astype(bf16)
            copy(k).start()

        for k in range(d // TILE - 2, d // TILE):
            pltpu.make_async_copy(stage.at[k % 2, :, pl.ds(0, width)], out.at[rows_of(k)], osem.at[2 * slot + k % 2]).wait()

    weight_grad(cott, hff, gd_h, 0, ff)
    bring.finish()

    @pl.loop(0, tiles)
    def _(s):
        t = (s + half * (1 - core)) % tiles
        r = rows_of(t)
        ct = cot[r, :]
        for at, w in chunks:
            cols = pl.ds(at, w)
            gf = nn(ct, wd[:, cols])
            gg[r, cols] = (gf * gg[r, cols].astype(f32)).astype(bf16)
            gu[r, cols] = (gf * gu[r, cols].astype(f32)).astype(bf16)
        part[r, :] = (nt(gg[r, :], wg[...]) + nt(gu[r, :], wu[...])).astype(bf16)
        send_back(t).start()
        y = nt(hff[r, :], wd[...]).astype(bf16)

        @pl.when(s < half)
        def _():
            ysend[rows_of(s), :] = y
            send_y(s).start()

        @pl.when(s >= half)
        def _():
            yown[rows_of(s - half), :] = y

    ggain_ref[...] = jnp.zeros_like(ggain_ref)

    @pl.loop(0, tiles)
    def _(s):
        t = (s + half * (1 - core)) % tiles
        r = rows_of(t)
        send_back(t).wait()
        total = part[r, :].astype(f32) + back[r, :].astype(f32)
        h = hid[r, :]
        factor = lax.rsqrt(jnp.mean(h * h, axis=1, keepdims=True) + epsilon)
        unit = h * factor
        g = gain * total
        gh = cot[r, :].astype(f32) + factor * (g - unit * jnp.mean(g * unit, axis=1, keepdims=True))
        low = gh.astype(bf16)
        cott[:, r] = low.T
        ga_ref[r, :] = nn(low, wo[...]).astype(bf16)

        @pl.when(s >= half)
        def _():
            j = rows_of(s - half)
            gh_ref[j, :] = gh
            ggain_ref[...] += jnp.sum(total * unit, axis=0, keepdims=True)
            send_y(s - half).wait()
            y_ref[j, :] = (h + (yown[j, :].astype(f32) + yother[j, :].astype(f32))).astype(bf16)

    weight_grad(n2t, gg, gg_h, 1, ff)
    weight_grad(n2t, gu, gu_h, 2, ff)
    weight_grad(cott, att, gout_h, 3, att.shape[1])


def middle(att, tok, cot, wo, wg, wu, wd, wd_shard, gain, wide, cid):
    n, d = tok.shape
    units, ff, G, cut = att.shape[1], wg.shape[1], wide // 4, wd.shape[1]
    B = lambda *s: pltpu.VMEM(s, bf16)
    sds = jax.ShapeDtypeStruct
    tiles = n // TILE
    halves = (((0, 0, cut),), ((0, cut, ff - cut),))
    return pl.pallas_call(functools.partial(mid_kernel, G, cut),
        out_shape=(sds((d, units), bf16), sds((d, ff), bf16), sds((d, ff), bf16), sds((d, ff), bf16),
                   sds((n // 2, d), bf16), sds((n // 2, d), f32), sds((n, units), bf16), sds((1, d), f32)),
        in_specs=[ANY] * 8 + [whole_vmem()], out_specs=(ANY,) * 4 + (whole_vmem(),) * 4,
        scratch_shapes=[B(n, units), B(n, d), B(n, d), B(d, units), B(d, ff), B(d, ff), B(d, ff), B(n, d), B(n, d), B(n, d),
                        pltpu.VMEM((n, d), f32), B(d, n), B(d, n), B(n, ff), B(n, ff), B(n, ff),
                        B(n // 2, d), B(n // 2, d), B(n // 2, d), B(2, TILE, ff),
                        D((7,)), D((8,)), D((tiles,)), D((tiles,)), D((tiles,)), D((tiles,)), D((tiles // 2,)), D((tiles // 2,))]
        + gather_scratch(G, halves, 1),
        compiler_params=params(cid), name="feed_forward")(att, tok, cot, wo, wg, wu, wd, wd_shard, gain)


def local(tokens, cotangent, pages, boxes, gain_attn, gain_ffn, bias_tables, w_query, w_key, w_value, w_out, w_gate, w_up, w_down):
    wide, narrow = lax.axis_size("wide"), lax.axis_size("narrow")
    heads_all = bias_tables.shape[1]
    heads = heads_all // narrow
    core = lax.axis_index("narrow")
    tables = lax.dynamic_slice_in_dim(bias_tables, core * heads, heads, 1)
    inner, ff, d = w_query.shape[1], w_gate.shape[1], tokens.shape[1]
    gain_one, gain_two = gain_attn.astype(f32)[None], gain_ffn.astype(f32)[None]

    all_tokens = lax.all_gather(tokens, "narrow", axis=0, tiled=True)
    all_cot = lax.all_gather(cotangent, "narrow", axis=0, tiled=True)
    early = inner // 4 * 3
    bias, ids, (w_first, full_out, full_gate) = bias_and_gather(
        tables, boxes, pages, [jnp.concatenate([w_query, w_key, w_value], axis=1), w_out.T, w_gate],
        (((2, 0, ff), (0, 0, early)), ((1, 0, inner), (0, early, 3 * inner - early))), wide, 1)
    down_shard = w_down.T
    cut = (ff // 128 + 1) // 2 * 128
    (attended, lse, normed, qkv), (full_up, most_down) = attn_fwd_and_gather(
        all_tokens, gain_one, w_first, bias, [w_up, down_shard[:, :cut]],
        (((0, 0, cut), (1, 0, cut - 384)), ((0, cut, ff - cut), (1, cut - 384, 384))), wide, 2)
    grad_w_out, grad_w_gate, grad_w_up, grad_w_down, output, grad_hidden, grad_attended, grad_gain_two = middle(
        attended, all_tokens, all_cot, full_out, full_gate, full_up, most_down, down_shard, gain_two, wide, 3)
    (g, band, far, grad_w_first, grad_normed), (s_gate, s_down) = attn_bwd_and_scatter(
        qkv, bias, attended, grad_attended, lse, normed, w_first, [grad_w_gate, grad_w_down], (((0, 0, ff),), ((1, 0, ff),)), wide, 4)
    most = 2 * inner
    small, grad_tokens, (s_up, s_out, s_first) = hist_and_scatter(
        g, band, far, ids, grad_normed, tokens, grad_hidden, gain_one, grad_gain_two, [grad_w_up, grad_w_out, grad_w_first],
        (((0, 0, ff), (2, most, inner // 2)), ((1, 0, inner), (2, 0, most), (2, most + inner // 2, inner // 2))), wide, 5)
    s_query, s_key, s_value = jnp.split(s_first, 3, axis=1)
    lines = d // 128
    one, two = small[:lines].reshape(d), small[lines:2 * lines].reshape(d)
    table = small[2 * lines:, :bias_tables.shape[0]].T
    return (output, grad_tokens, one, two, table, s_query, s_key, s_value, s_out.T, s_gate, s_up, s_down.T)


def solution(mesh):
    rows, cols, tall = P(("wide", "narrow"), None), P("wide", "narrow"), P("narrow", "wide")
    in_specs = (rows, rows, P("wide"), P(None, "wide"), P(), P(), P(), cols, cols, cols, tall, cols, cols, tall)
    out_specs = (rows, rows, P(), P(), P(), cols, cols, cols, tall, cols, cols, tall)
    return jax.shard_map(local, mesh=mesh, in_specs=in_specs, out_specs=out_specs, check_vma=False)
```

```python
import functools

import jax
import jax.numpy as jnp
from jax import lax
from jax.experimental import pallas as pl
from jax.experimental.pallas import tpu as pltpu
from jax.sharding import PartitionSpec as P

f32, bf16 = jnp.float32, jnp.bfloat16
MESH = pl.DeviceIdType.MESH


EDGES = (1, 2, 3, 4, 5, 6, 7, 8, 12, 16, 23, 32, 46, 64, 91)
NT = (((1,), (1,)), ((), ()))
VM = 58 * 2**20
TABLE_SCALE = 2047.0
TABLE_LIFT = 8192
TILE = 256
epsilon = 1e-06


def params(cid):
    return pltpu.CompilerParams(collective_id=cid, has_side_effects=True, vmem_limit_bytes=VM)


def lane_take(table, idx):
    return jnp.take_along_axis(table, idx, axis=1, mode="promise_in_bounds")


def buckets_of(gap, steps, shift):
    return lane_take(steps, jnp.minimum(jnp.abs(gap) >> shift, EDGES[-1])) + jnp.where(gap > 0, 16, 0)


def bias_tile(start, heads, rows, n, steps_ref, tab_ref, box_col, box_row, page_col, page_row, bias_ref, ids_ref, lin_ids, lin):
    steps = jnp.broadcast_to(steps_ref[...], (rows, 128))
    allowed_col = jnp.broadcast_to(page_col[...] % 2, (rows, 128))
    cols = [jnp.broadcast_to(box_col[:, t:t + 1], (rows, 128)) for t in range(2)]
    pairs = heads // 2
    table = lambda t, p: jnp.broadcast_to(tab_ref[t * pairs + p:t * pairs + p + 1, :], (rows, 128))
    unit = 1.0 / TABLE_SCALE

    @pl.when(start == 0)
    def _():
        @pl.loop(0, 8)
        def _(k):
            ids = buckets_of(lax.broadcasted_iota(jnp.int32, (rows, 128), 1) - lax.broadcasted_iota(jnp.int32, (rows, 128), 0) + (k - 4) * rows, steps, 0)
            lin_ids[k] = ids.astype(f32)
            for p in range(pairs):
                lin[k, p] = lane_take(table(0, p), ids)

    @pl.loop(0, n // 128)
    def _(c):
        lanes = pl.ds(pl.multiple_of(c * 128, 128), 128)
        near = jnp.clip((c * 128 - start) // rows + 4, 0, 7)
        ids = []
        for t in range(2):
            ids.append(buckets_of(jnp.broadcast_to(box_row[t:t + 1, lanes], (rows, 128)) - cols[t], steps, 2))
            ids_ref[t, :, lanes] = ids[t].astype(f32)
        ok = jnp.broadcast_to(page_row[:, lanes], (rows, 128)) == allowed_col
        for p in range(pairs):
            words = lin[near, p] + lane_take(table(1, p), ids[0]) + lane_take(table(2, p), ids[1])
            upper = (words >> 16).astype(f32) * unit
            lower = (words & 0xFFFF).astype(f32) * unit - 3 * TABLE_LIFT * unit
            bias_ref[2 * p, :, lanes] = jnp.where(ok, upper, -1e30)
            bias_ref[2 * p + 1, :, lanes] = jnp.where(ok, lower, -1e30)


def bias_gather_kernel(heads, rows, n, G, halves, count, *refs):
    ins, srcs = refs[:6], refs[6:6 + count]
    bias_ref, ids_ref, lin_ids = refs[6 + count:9 + count]
    outs, lin, sems = refs[9 + count:9 + 2 * count], refs[9 + 2 * count], refs[10 + 2 * count:]
    now = pl.program_id(0)
    comm = Gather(G, halves, srcs, outs, *sems)
    beside(comm.events(), G, n // rows, now, lambda: bias_tile(now * rows, heads, rows, n, *ins, bias_ref, ids_ref, lin_ids, lin))


def bias_and_gather(tables, boxes, pages, shards, halves, wide, cid):
    heads, n, G, rows = tables.shape[1], pages.shape[0], wide // 4, 64
    fixed = jnp.round(tables.astype(f32) * TABLE_SCALE).astype(jnp.int32).reshape(3, 32, heads // 2, 2)
    words = fixed[..., 0] * 65536 + fixed[..., 1] + TABLE_LIFT
    tab = jnp.pad(words.transpose(0, 2, 1).reshape(3 * heads // 2, 32), ((0, 0), (0, 96)))
    lane = jnp.arange(128, dtype=jnp.int32)
    steps = sum([(lane >= e).astype(jnp.int32) for e in EDGES])[None]
    count = len(shards)
    outs = pl.pallas_call(functools.partial(bias_gather_kernel, heads, rows, n, G, halves, count),
        grid=(n // rows,),
        out_shape=(jax.ShapeDtypeStruct((heads, n, n), f32), jax.ShapeDtypeStruct((2, n, n), f32), jax.ShapeDtypeStruct((8, rows, 128), f32)) + gathered_shapes(shards, wide),
        in_specs=[pl.BlockSpec((1, 128), lambda i: (0, 0)), pl.BlockSpec((3 * heads // 2, 128), lambda i: (0, 0)),
                  pl.BlockSpec((rows, 2), lambda i: (i, 0)), pl.BlockSpec((2, n), lambda i: (0, 0)),
                  pl.BlockSpec((rows, 1), lambda i: (i, 0)), pl.BlockSpec((1, n), lambda i: (0, 0))] + [ANY] * count,
        out_specs=(pl.BlockSpec((heads, rows, n), lambda i: (0, i, 0)), pl.BlockSpec((2, rows, n), lambda i: (0, i, 0)),
                   pl.BlockSpec((8, rows, 128), lambda i: (0, 0, 0))) + (ANY,) * count,
        scratch_shapes=[pltpu.VMEM((8, heads // 2, rows, 128), jnp.int32)] + gather_scratch(G, halves, count),
        compiler_params=params(cid), name="layout_bias_gather")(
            steps, tab, boxes.T, boxes, pages[:, None], pages[None], *shards)
    return outs[0], outs[1:3], outs[3:]


def half_of(v, e):
    lane = lax.broadcasted_iota(jnp.int32, v.shape, 1)
    return jnp.where((lane >= 64) == (e == 1), v, jnp.zeros_like(v))


def join(a, b):
    lane = lax.broadcasted_iota(jnp.int32, a.shape, 1)
    return jnp.where(lane < 64, a, b)


def project(tok_ref, gain_ref, w_ref, normed, qkv):
    gain = gain_ref[...]

    @pl.loop(0, tok_ref.shape[0] // TILE)
    def _(t):
        r = pl.ds(pl.multiple_of(t * TILE, TILE), TILE)
        x = tok_ref[r, :].astype(f32)
        low = (x * lax.rsqrt(jnp.mean(x * x, axis=1, keepdims=True) + epsilon) * gain).astype(bf16)
        normed[r, :] = low
        qkv[r, :] = jnp.dot(low, w_ref[...], preferred_element_type=f32).astype(bf16)


def fwd_tile(p, i, tq, pairs, qkv, bias_ref, o_ref, lse_ref):
    cols = lambda k: pl.ds(pl.multiple_of((p + k * pairs) * 128, 128), 128)
    q, k, v = qkv[pl.ds(pl.multiple_of(i * tq, tq), tq), cols(0)], qkv[:, cols(1)], qkv[:, cols(2)]
    outs, lses = [], []
    for e in range(2):
        s = lax.dot_general(half_of(q, e), k, NT, preferred_element_type=f32) + bias_ref[e]
        peak = jnp.max(s, axis=1, keepdims=True)
        w = jnp.exp(s - peak)
        total = jnp.sum(w, axis=1, keepdims=True)
        outs.append(jnp.dot(w.astype(bf16), v, preferred_element_type=f32) / total)
        lses.append(peak + jnp.log(total))
    o_ref[...] = join(*outs).astype(bf16)
    lse_ref[0] = jnp.concatenate(lses, axis=1)


def fwd_kernel(pairs, tiles, G, halves, count, *refs):
    (tok, gain, w, bias_ref), srcs = refs[:4], refs[4:4 + count]
    o_ref, lse_ref, normed_h, qkv_h = refs[4 + count:8 + count]
    outs, (normed, qkv, keep), sems = refs[8 + count:8 + 2 * count], refs[8 + 2 * count:11 + 2 * count], refs[11 + 2 * count:]
    p, i = pl.program_id(0), pl.program_id(1)
    now, steps = p * tiles + i, pairs * tiles
    copies = lambda: [pltpu.make_async_copy(normed, normed_h, keep.at[0]), pltpu.make_async_copy(qkv, qkv_h, keep.at[1])]

    def compute():
        @pl.when(now == 0)
        def _():
            project(tok, gain, w, normed, qkv)
            for c in copies():
                c.start()

        fwd_tile(p, i, o_ref.shape[0], pairs, qkv, bias_ref, o_ref, lse_ref)

        @pl.when(now == steps - 1)
        def _():
            for c in copies():
                c.wait()

    beside(Gather(G, halves, srcs, outs, *sems).events(), G, steps, now, compute)


def attn_fwd_and_gather(tok, gain, w, bias, shards, halves, wide, cid, tq=256):
    n, d = tok.shape
    width = w.shape[1] // 3
    pairs, tiles, count, G = width // 128, n // tq, len(shards), wide // 4
    sds = jax.ShapeDtypeStruct
    const = lambda s: pl.BlockSpec(s, lambda p, i: (0, 0))
    outs = pl.pallas_call(functools.partial(fwd_kernel, pairs, tiles, G, halves, count), grid=(pairs, tiles),
        out_shape=(sds((n, width), bf16), sds((pairs, n, 2), f32), sds((n, d), bf16), sds((n, 3 * width), bf16)) + gathered_shapes(shards, wide),
        in_specs=[const((n, d)), const((1, d)), const(w.shape), pl.BlockSpec((2, tq, n), lambda p, i: (p, i, 0))] + [ANY] * count,
        out_specs=(pl.BlockSpec((tq, 128), lambda p, i: (i, p)), pl.BlockSpec((1, tq, 2), lambda p, i: (p, i, 0)), ANY, ANY) + (ANY,) * count,
        scratch_shapes=[pltpu.VMEM((n, d), bf16), pltpu.VMEM((n, 3 * width), bf16), D((2,))] + gather_scratch(G, halves, count),
        compiler_params=params(cid), name="attention_gather")(tok, gain, w, bias, *shards)
    return outs[:4], outs[4:]


def band_sums(i, e, g_ref, band_ref, far_ref):
    tq, n = g_ref.shape[1], g_ref.shape[2]
    first = i * (tq // 128) - 1

    @pl.when(i == 0)
    def _():
        band_ref[e] = jnp.zeros(band_ref.shape[1:], f32)
        far_ref[e] = jnp.zeros(far_ref.shape[1:], f32)

    for m in range(tq // 128 + 2):
        @pl.when((first + m >= 0) & (first + m < n // 128))
        def _():
            band_ref[e, :, m * 128:(m + 1) * 128] += g_ref[e, :, pl.ds(pl.multiple_of((first + m) * 128, 128), 128)].astype(f32)

    for c in range(n // 128):
        @pl.when((c < first) | (c > first + tq // 128 + 1))
        def _():
            total = g_ref[e, 0:16, c * 128:(c + 1) * 128].astype(f32)
            for k in range(1, tq // 16):
                total = total + g_ref[e, k * 16:(k + 1) * 16, c * 128:(c + 1) * 128].astype(f32)
            far_ref[e, jnp.where(c < first, 0, 1)] += total


def bwd_tile(p, pairs, i, last_tile, last, q_ref, k_ref, v_ref, bias_ref, o_ref, do_ref, lse_ref, normed_ref, w_ref,
             g_ref, band_ref, far_ref, dw_ref, dx_ref, dkt, dvt, dqkv, turned):
    tq, n = q_ref.shape[0], k_ref.shape[0]
    rows = pl.ds(pl.multiple_of(i * tq, tq), tq)

    @pl.when(p == 0)
    def _():
        turned[:, rows] = normed_ref[rows, :].T

    @pl.when(i == 0)
    def _():
        dkt[...] = jnp.zeros_like(dkt)
        dvt[...] = jnp.zeros_like(dvt)

    q, k, v, do = q_ref[...], k_ref[...], v_ref[...], do_ref[...]
    prod = do.astype(f32) * o_ref[...].astype(f32)
    dqs = []
    for e in range(2):
        qm, dom = half_of(q, e), half_of(do, e)
        s = lax.dot_general(qm, k, NT, preferred_element_type=f32) + bias_ref[e]
        w = jnp.exp(s - lse_ref[0, :, e:e + 1])
        dp = lax.dot_general(dom, v, NT, preferred_element_type=f32)
        inner = jnp.sum(half_of(prod, e), axis=1, keepdims=True)
        g = (w * (dp - inner)).astype(bf16)
        g_ref[e] = g
        dqs.append(jnp.dot(g, k, preferred_element_type=f32))
        dvt[...] += jnp.dot(dom.T, w.astype(bf16), preferred_element_type=f32)
        dkt[...] += jnp.dot(qm.T, g, preferred_element_type=f32)
        band_sums(i, e, g_ref, band_ref, far_ref)
    columns = lambda k: pl.ds(pl.multiple_of((p + k * pairs) * 128, 128), 128)
    dqkv[rows, columns(0)] = join(*dqs).astype(bf16)

    @pl.when(last_tile)
    def _():
        dqkv[:, columns(1)] = dkt[...].T.astype(bf16)
        dqkv[:, columns(2)] = dvt[...].T.astype(bf16)

        @pl.when(last)
        def _():
            @pl.loop(0, n // TILE)
            def _(t):
                r = pl.ds(pl.multiple_of(t * TILE, TILE), TILE)
                dw_ref[r, :] = jnp.dot(turned[r, :], dqkv[...], preferred_element_type=f32).astype(bf16)
                dx_ref[r, :] = lax.dot_general(dqkv[r, :], w_ref[...], NT, preferred_element_type=f32).astype(bf16)


def bwd_kernel(pairs, tiles, G, halves, count, *refs):
    ins, parts = refs[:9], refs[9:9 + count]
    mid = refs[9 + count:14 + count]
    outs, accs, sems = refs[14 + count:14 + 2 * count], refs[14 + 2 * count:18 + 2 * count], refs[18 + 2 * count:]
    p, i = pl.program_id(0), pl.program_id(1)
    comm = Scatter(G, halves, parts, outs, *sems)
    beside(comm.events(), G, pairs * tiles, p * tiles + i,
           lambda: bwd_tile(p, pairs, i, i == tiles - 1, p == pairs - 1, *ins, *mid, *accs))


def shard_shapes(parts, wide):
    return tuple(jax.ShapeDtypeStruct((p.shape[0] // wide, p.shape[1]), f32) for p in parts)


def attn_bwd_and_scatter(qkv, bias, o, do, lse, normed, w, parts, halves, wide, cid, tq=256):
    n, width, d = qkv.shape[0], qkv.shape[1] // 3, normed.shape[1]
    pairs, tiles, count, G = width // 128, n // tq, len(parts), wide // 4
    sds = jax.ShapeDtypeStruct
    tile = pl.BlockSpec((tq, 128), lambda p, i: (i, p))
    full = lambda rows, k: pl.BlockSpec((rows, 128), lambda p, i: (0, p + k * pairs))
    const = lambda s: pl.BlockSpec(s, lambda p, i: (0, 0))
    outs = pl.pallas_call(functools.partial(bwd_kernel, pairs, tiles, G, halves, count), grid=(pairs, tiles),
        out_shape=(sds((2 * pairs, n, n), bf16), sds((2 * pairs, tq, tq + 256), f32), sds((2 * pairs, 2, 16, 128), f32)) + (sds((d, 3 * width), bf16), sds((n, d), bf16)) + shard_shapes(parts, wide),
        in_specs=[tile, full(n, 1), full(n, 2), pl.BlockSpec((2, tq, n), lambda p, i: (p, i, 0)), tile, tile,
                  pl.BlockSpec((1, tq, 2), lambda p, i: (p, i, 0)), const((n, d)), const(w.shape)] + [ANY] * count,
        out_specs=(pl.BlockSpec((2, tq, n), lambda p, i: (p, i, 0)), pl.BlockSpec((2, tq, tq + 256), lambda p, i: (p, 0, 0)),
                   pl.BlockSpec((2, 2, 16, 128), lambda p, i: (p, 0, 0, 0))) + (const(w.shape), const((n, d))) + (whole_vmem(),) * count,
        scratch_shapes=[pltpu.VMEM((128, n), f32), pltpu.VMEM((128, n), f32), pltpu.VMEM((n, 3 * width), bf16), pltpu.VMEM((d, n), bf16)] + scatter_scratch(G, halves, parts[0].shape[0] // wide),
        compiler_params=params(cid), name="attention_back_scatter")(
            qkv, qkv, qkv, bias, o, do, lse, normed, w, *parts)
    return outs[:5], outs[5:]


def rows_times_hots(src, ids, rows, heads, gs):
    n = src(0).shape[1]
    for h in range(heads):
        block = src(h)
        for c in range(n // 128):
            gs[c, h * rows:(h + 1) * rows, :] = block[:, c * 128:(c + 1) * 128]
    labels = [lax.broadcasted_iota(jnp.int32, (16, n), 0).astype(bf16) + float(k) for k in (0, 16)]
    one, zero = jnp.ones((16, n), bf16), jnp.zeros((16, n), bf16)
    group = 4 // len(ids(0))
    total = jnp.zeros((heads * group, 128), f32)
    for first in range(0, rows, group):
        grow, hots = [], []
        for r in range(first, first + group):
            grow.append(jnp.concatenate([gs[c, pl.ds(r, heads, stride=rows), :] for c in range(n // 128)], axis=1))
            for one_row in ids(r):
                row = jnp.broadcast_to(one_row, (16, n)).astype(bf16)
                hots += [jnp.where(row == label, one, zero) for label in labels]
        total = total + lax.dot_general(jnp.concatenate(grow, axis=0).astype(bf16), jnp.concatenate(hots, axis=0), NT, preferred_element_type=f32)
    return total


def own_blocks(total, heads, width):
    out = total[0:heads, 0:width]
    for k in range(1, 128 // width):
        out = out + total[k * heads:(k + 1) * heads, k * width:(k + 1) * width]
    return out


def halves_times_hots(g_ref, ids_ref, block, heads, gs, low):
    rows, n = 16, g_ref.shape[2]
    for h in range(heads):
        for c in range(n // 128):
            gs[c, h * rows:(h + 1) * rows, :] = g_ref[h, block, c * 128:(c + 1) * 128].astype(f32)
    for t in range(2):
        ids = ids_ref[t, block, :]
        low[t] = jnp.where(ids >= 16.0, ids - 16.0, ids)
    label = lax.broadcasted_iota(jnp.int32, (16, n), 0).astype(bf16)
    one, zero = jnp.ones((16, n), bf16), jnp.zeros((16, n), bf16)
    total = jnp.zeros((64, 64), f32)
    for first in range(0, rows, 2):
        left, hots = [], []
        for r in range(first, first + 2):
            grow = jnp.concatenate([gs[c, pl.ds(r, heads, stride=rows), :] for c in range(n // 128)], axis=1)
            for t in range(2):
                upper = jnp.broadcast_to(ids_ref.at[t, block][r:r + 1, :], (heads, n)) >= 16.0
                left += [jnp.where(upper, 0.0, grow), jnp.where(upper, grow, 0.0)]
                row = jnp.broadcast_to(low[t, r:r + 1, :], (16, n)).astype(bf16)
                hots.append(jnp.where(row == label, one, zero))
        total = total + lax.dot_general(jnp.concatenate(left, axis=0).astype(bf16), jnp.concatenate(hots, axis=0), NT, preferred_element_type=f32)
    return total


def own_halves(total, heads):
    out = 0.0
    for k in range(2):
        part = lambda t, up: total[k * 32 + (2 * t + up) * heads:k * 32 + (2 * t + up + 1) * heads, k * 32 + t * 16:k * 32 + t * 16 + 16]
        out = out + jnp.concatenate([part(0, 0), part(0, 1), part(1, 0), part(1, 1)], axis=1)
    return out


def hist_tile(now, heads, g_ref, ids_ref, band_ref, far_ref, lin_ids, table, boxes, gs, low):
    @pl.when(now == 0)
    def _():
        sides = [jnp.sum(jnp.sum(far_ref[:, k], axis=1), axis=1, keepdims=True) for k in range(2)]
        lane = lax.broadcasted_iota(jnp.int32, (heads, 128), 1)
        table[...] = jnp.zeros_like(table)
        boxes[...] = jnp.zeros_like(boxes)
        table[0:heads, :] = jnp.where(lane == 15, sides[0], 0.0) + jnp.where(lane == 31, sides[1], 0.0)

    big = g_ref.shape[1]

    @pl.loop(0, big // 16)
    def _(q):
        block = pl.ds(pl.multiple_of(q * 16, 16), 16)
        boxes[...] += halves_times_hots(g_ref, ids_ref, block, heads, gs, low)

    wide = band_ref.shape[2] // 128
    per = lin_ids.shape[1]
    a = now * 16 // per
    inside = pl.ds(pl.multiple_of(now * 16 % per, 16), 16)

    def band_ids(r):
        return [jnp.concatenate([lin_ids.at[jnp.clip((m - 1) * (128 // per) - a + 4, 0, 7), inside][r:r + 1, :] for m in range(wide)], axis=1)]

    table[...] += rows_times_hots(lambda h: band_ref[h], band_ids, 16, heads, gs)


def hist_kernel(heads, rows, n, G, halves, count, *refs):
    (g_ref, ids_ref, band_ref, far_ref, lin_ids, dx, tok, gh, gain_ref, gain_two), parts = refs[:10], refs[10:10 + count]
    small_ref, gt_ref = refs[10 + count:12 + count]
    outs, rest = refs[12 + count:12 + 2 * count], refs[12 + 2 * count:]
    (gs, low, table, boxes, got, pair_sem), sums, sems = rest[:6], rest[6:13], rest[13:]
    acc = sums[0]
    now, steps = pl.program_id(0), n // rows
    core = lax.axis_index("narrow")
    mine = tok.shape[0]
    d = tok.shape[1]
    comm = Scatter(G, halves, parts, outs, *sems)
    swap = lambda: remote(dx.at[pl.ds(pl.multiple_of((1 - core) * mine, mine), mine)], got, pair_sem.at[0], pair_sem.at[1], {"narrow": 1 - core})

    def compute():
        @pl.when(now == 0)
        def _():
            swap().start()
            acc[0] = jnp.zeros(acc.shape[1:], f32)
            for k in range(d // 128):
                acc[0, d // 128 + k:d // 128 + k + 1, :] = gain_two[:, k * 128:(k + 1) * 128]

        @pl.when(now == steps // 8)
        def _():
            swap().wait()

        for t in range(mine // TILE):
            @pl.when(now == steps // 8 + t)
            def _():
                r = pl.ds(t * TILE, TILE)
                x = tok[r, :].astype(f32)
                total = dx[pl.ds(pl.multiple_of(core * mine + t * TILE, TILE), TILE), :].astype(f32) + got[r, :].astype(f32)
                factor = lax.rsqrt(jnp.mean(x * x, axis=1, keepdims=True) + epsilon)
                unit = x * factor
                scaled = gain_ref[...] * total
                gt_ref[r, :] = gh[r, :] + factor * (scaled - unit * jnp.mean(scaled * unit, axis=1, keepdims=True))
                gain = jnp.sum(total * unit, axis=0, keepdims=True)
                for k in range(d // 128):
                    acc[0, k:k + 1, :] += gain[:, k * 128:(k + 1) * 128]

        hist_tile(now, heads, g_ref, ids_ref, band_ref, far_ref, lin_ids, table, boxes, gs, low)

    def reduce():
        acc[0, pl.ds(pl.multiple_of(2 * (d // 128) + core * heads, 8), heads), 0:32] = own_blocks(table[...], heads, 32)
        acc[0, pl.ds(pl.multiple_of(2 * (d // 128) + core * heads, 8), heads), 32:96] = own_halves(boxes[...], heads)
        small_ref[...] = sum_everywhere(G, *sums)

    beside(comm.events(1), G, steps, now, compute, (reduce,))


def hist_and_scatter(g, band, far, ids, dx, tok, gh, gain, gain_two, parts, halves, wide, cid):
    heads, n, _ = g.shape
    rows, count, G, d = n // (band.shape[1] // 16), len(parts), wide // 4, tok.shape[1]
    box_ids, lin_ids = ids
    small = 2 * (d // 128) + 2 * heads
    sds = jax.ShapeDtypeStruct
    const = lambda s: pl.BlockSpec(s, lambda i: (0, 0))
    outs = pl.pallas_call(functools.partial(hist_kernel, heads, rows, n, G, halves, count), grid=(n // rows,),
        out_shape=(sds((small, 128), f32), sds(tok.shape, f32)) + shard_shapes(parts, wide),
        in_specs=[pl.BlockSpec((heads, rows, n), lambda i: (0, i, 0)), pl.BlockSpec((2, rows, n), lambda i: (0, i, 0)),
                  pl.BlockSpec((heads, 16, band.shape[2]), lambda i: (0, i, 0)), pl.BlockSpec(far.shape, lambda i: (0, 0, 0, 0)),
                  pl.BlockSpec(lin_ids.shape, lambda i: (0, 0, 0)), const(dx.shape), const(tok.shape), const(gh.shape), const(gain.shape), const(gain_two.shape)] + [ANY] * count,
        out_specs=(const((small, 128)), const(tok.shape)) + (whole_vmem(),) * count,
        scratch_shapes=[pltpu.VMEM((n // 128, heads * 16, 128), f32), pltpu.VMEM((2, 16, n), f32), pltpu.VMEM((4 * heads, 128), f32), pltpu.VMEM((64, 64), f32), pltpu.VMEM(tok.shape, bf16), D((2,))]
        + sum_scratch(G, small) + scatter_scratch(G, halves, parts[0].shape[0] // wide),
        compiler_params=params(cid), name="table_grad_scatter")(g, box_ids, band, far, lin_ids, dx, tok, gh, gain, gain_two, *parts)
    return outs[0], outs[1], outs[2:]


D = pltpu.SemaphoreType.DMA


def place():
    me = lax.axis_index("wide")
    return me // 4, (me // 2) % 2, me % 2


def wide_id(z, y, x):
    return {"wide": z * 4 + y * 2 + x}


def shard_rows(z, y, x, R):
    return pl.ds(pl.multiple_of((z * 4 + y * 2 + x) * R, R), R)


def remote(src, dst, send, recv, target):
    return pltpu.make_async_remote_copy(src_ref=src, dst_ref=dst, send_sem=send, recv_sem=recv, device_id=target, device_id_type=MESH)


def greet(G, far, pair=0):
    z, y, x = place()
    bar = pltpu.get_barrier_semaphore()
    sig = lambda t: pl.semaphore_signal(bar, inc=1, device_id=t, device_id_type=MESH)
    sig(wide_id(z, 1 - y, x))
    sig(wide_id(z, y, 1 - x))
    if pair:
        sig({"narrow": 1 - lax.axis_index("narrow")})
    if far:
        for k in range(1, G):
            sig(wide_id((z + k) % G, y, x))
        pl.semaphore_wait(bar, 2 + pair + G - 1)
    else:
        @pl.when(z > 0)
        def _():
            sig(wide_id(z - 1, y, x))

        @pl.when(z < G - 1)
        def _():
            sig(wide_id(z + 1, y, x))

        pl.semaphore_wait(bar, 2 + pair + (z > 0).astype(jnp.int32) + (z < G - 1).astype(jnp.int32))


class Gather:
    def __init__(self, G, halves, srcs, outs, local_sem, zs, zr, ns, nr):
        self.G, self.halves, self.srcs, self.local_sem = G, halves, srcs, local_sem
        self.outs = [o if isinstance(o, tuple) else (o, 0, 0) for o in outs]
        self.widths = [sum(w for h in halves for a, _, w in h if a == k) for k in range(len(srcs))]
        self.zs, self.zr, self.ns, self.nr = zs, zr, ns, nr
        self.most = max(len(h) for h in halves)
        self.z, self.y, self.x = place()
        self.R = srcs[0].shape[0]

    def hop(self, own, zz, yy, xx, h, way, j):
        target = wide_id(self.z, 1 - self.y, self.x) if way == "y" else wide_id(self.z, self.y, 1 - self.x)
        copies = []
        for n, (a, c, w) in enumerate(self.halves[h]):
            slot = (zz * 6 + j) * self.most + n
            out, first, at = self.outs[a]
            dst = out.at[shard_rows(zz, yy, xx, self.R), pl.ds(first + c, w)]
            copies.append(remote(self.srcs[a].at[:, pl.ds(at + c, w)] if own else dst, dst, self.ns.at[slot], self.nr.at[slot], target))
        return copies

    def second_stage(self, zz, own=False):
        return self.hop(own, zz, self.y, self.x, 0, "y", 0) + self.hop(own, zz, self.y, self.x, 1, "x", 1)

    def third_stage(self, zz, own=False):
        return self.hop(own, zz, self.y, self.x, 0, "x", 2) + self.hop(own, zz, self.y, self.x, 1, "y", 3)

    def last_stage(self, zz):
        return self.hop(False, zz, 1 - self.y, self.x, 0, "x", 4) + self.hop(False, zz, self.y, 1 - self.x, 1, "y", 5)

    def relay(self, own, zz, step, way):
        copies = []
        for a in range(len(self.srcs)):
            slot = (way * (self.G - 1) + step) * len(self.srcs) + a
            dst = self.whole(a, zz)
            copies.append(remote(self.own(a) if own else dst, dst, self.zs.at[slot], self.zr.at[slot],
                                 wide_id(self.z + (1 if way == 0 else -1), self.y, self.x)))
        return copies

    def whole(self, a, zz):
        out, first, _ = self.outs[a]
        return out.at[shard_rows(zz, self.y, self.x, self.R), pl.ds(first, self.widths[a])]

    def own(self, a):
        return self.srcs[a].at[:, pl.ds(self.outs[a][2], self.widths[a])]

    def can(self, way):
        return self.z < self.G - 1 if way == 0 else self.z > 0

    def source(self, d, way):
        return (self.z - d, self.z - d >= 0) if way == 0 else (self.z + d, self.z + d < self.G)

    def keep(self):
        return [pltpu.make_async_copy(self.own(a), self.whole(a, self.z), self.local_sem.at[a]) for a in range(len(self.srcs))]

    def begin(self):
        for way in range(2):
            @pl.when(self.can(way))
            def _():
                for c in self.relay(True, self.z, 0, way):
                    c.start()
        for c in self.second_stage(self.z, True) + self.third_stage(self.z, True) + self.keep():
            c.start()

    def turn(self, zz):
        for c in self.hop(False, zz, 1 - self.y, self.x, 0, "y", 0) + self.hop(False, zz, self.y, 1 - self.x, 1, "x", 1):
            c.wait_recv()
        for c in self.last_stage(zz):
            c.start()

    def step(self, d):
        for way in range(2):
            zz, there = self.source(d, way)

            @pl.when(there)
            def _():
                for c in self.relay(False, zz, d - 1, way):
                    c.wait_recv()

                @pl.when(self.can(way))
                def _():
                    for c in self.relay(False, zz, d, way):
                        c.start()

                for c in self.second_stage(zz):
                    c.start()
        for way in range(2):
            zz, there = self.source(d, way)

            @pl.when(there)
            def _():
                for c in self.third_stage(zz):
                    c.start()

    def turns(self, d):
        if d == 0:
            self.turn(self.z)
            return
        for way in range(2):
            zz, there = self.source(d, way)

            @pl.when(there)
            def _():
                self.turn(zz)

    def finish(self):
        y, x = self.y, self.x

        @pl.loop(0, self.G)
        def _(zz):
            for c in (self.hop(False, zz, y, 1 - x, 0, "x", 2) + self.hop(False, zz, 1 - y, x, 1, "y", 3)
                      + self.hop(False, zz, 1 - y, 1 - x, 0, "x", 4) + self.hop(False, zz, 1 - y, 1 - x, 1, "y", 5)):
                c.wait_recv()
            for c in self.second_stage(zz) + self.third_stage(zz) + self.last_stage(zz):
                c.wait_send()

        for way in range(2):
            @pl.when(self.can(way))
            def _():
                for c in self.relay(True, self.z, 0, way):
                    c.wait_send()
                for d in range(1, self.G - 1):
                    zz, there = self.source(d, way)

                    @pl.when(there)
                    def _():
                        for c in self.relay(False, zz, d, way):
                            c.wait_send()
        for c in self.keep():
            c.wait()

    def events(self):
        G = self.G
        first = lambda: (greet(G, False), self.begin())
        ev = [(0.0, first), (0.7, lambda: self.turns(0))]
        for d in range(1, G):
            ev += [(1.15 * d, functools.partial(self.step, d)), (1.3 * d + 1.2, functools.partial(self.turns, d))]
        return sorted(ev, key=lambda e: e[0]), self.finish


def gather_scratch(G, halves, arrays):
    most = max(len(h) for h in halves)
    return [D((arrays,)), D((2 * (G - 1) * arrays,)), D((2 * (G - 1) * arrays,)), D((6 * G * most,)), D((6 * G * most,))]


class Scatter:
    def __init__(self, G, halves, parts, outs, r1a, r1b, o1a, o1b, r2a, r2b, r3, own, lsem, s1, v1, s2, v2, s3, v3):
        self.__dict__.update(locals())
        self.most = max(len(h) for h in halves)
        self.wa, self.wb = [sum(p[2] for p in h) for h in halves]
        self.R = parts[0].shape[0] // (4 * G)
        self.z, self.y, self.x = place()
        self.order = sorted(range(1, G), key=lambda k: min(k, G - k), reverse=True) + [0]

    def zk(self, k):
        return (self.z + k) % self.G

    def neighbour(self, way):
        return wide_id(self.z, 1 - self.y, self.x) if way == "y" else wide_id(self.z, self.y, 1 - self.x)

    def pieces(self, h):
        at, out = 0, []
        for n, (a, c, w) in enumerate(self.halves[h]):
            out.append((n, a, pl.ds(c, w), pl.ds(at, w)))
            at += w
        return out

    def sources(self, k, mine):
        z, y, x = self.zk(k), self.y, self.x
        for h in range(2):
            for n, a, src, dst in self.pieces(h):
                for j in range(2):
                    if h == 0:
                        rows = shard_rows(z, j, x if mine else 1 - x, self.R)
                    else:
                        rows = shard_rows(z, y if mine else 1 - y, j, self.R)
                    yield h, j, dst, ((2 * k + h) * self.most + n) * 2 + j, self.parts[a].at[rows, src]

    def one(self, k):
        return [remote(src, (self.r1a, self.r1b)[h].at[k, j, :, dst], self.s1.at[slot], self.v1.at[slot], self.neighbour("xy"[h]))
                for h, j, dst, slot, src in self.sources(k, False)]

    def load(self, k):
        return [pltpu.make_async_copy(src, (self.o1a, self.o1b)[h].at[k, j, :, dst], self.lsem.at[slot]) for h, j, dst, slot, src in self.sources(k, True)]

    def two(self, k):
        return [remote(self.o1a.at[k, 1 - self.y], self.r2a.at[k], self.s2.at[2 * k], self.v2.at[2 * k], self.neighbour("y")),
                remote(self.o1b.at[k, 1 - self.x], self.r2b.at[k], self.s2.at[2 * k + 1], self.v2.at[2 * k + 1], self.neighbour("x"))]

    def three(self, k):
        return remote(self.own.at[k], self.r3.at[k - 1], self.s3.at[k - 1], self.v3.at[k - 1], wide_id(self.zk(k), self.y, self.x))

    def launch(self, k):
        for c in self.one(k) + self.load(k):
            c.start()

    def begin(self):
        for k in self.order[:2]:
            self.launch(k)

    def rows(self, count, body):
        step = min(16, count)

        @pl.loop(0, count // step)
        def _(i):
            body(pl.ds(pl.multiple_of(i * step, step), step))

    def add_one(self, n):
        k = self.order[n]
        for c in self.one(k):
            c.wait_recv()
        for c in self.load(k):
            c.wait()
        for mine, got in ((self.o1a, self.r1a), (self.o1b, self.r1b)):
            def body(r):
                for j in range(2):
                    mine[k, j, r, :] = (mine[k, j, r, :].astype(f32) + got[k, j, r, :].astype(f32)).astype(bf16)

            self.rows(self.R, body)
        for c in self.two(k):
            c.start()
        if n + 2 < self.G:
            self.launch(self.order[n + 2])

    def add_two(self, n):
        k = self.order[n]
        for c in self.two(k):
            c.wait_recv()

        def body(r):
            self.own[k, r, pl.ds(0, self.wa)] = (self.o1a[k, self.y, r, :].astype(f32) + self.r2a[k, r, :].astype(f32)).astype(bf16)
            self.own[k, r, pl.ds(self.wa, self.wb)] = (self.o1b[k, self.x, r, :].astype(f32) + self.r2b[k, r, :].astype(f32)).astype(bf16)

        self.rows(self.R, body)
        if k:
            self.three(k).start()

    def finish(self):
        self.add_two(self.G - 1)
        for k in range(1, self.G):
            self.three(k).wait_recv()

        def body(r):
            for h in range(2):
                for _, a, src, dst in self.pieces(h):
                    cols = pl.ds(dst.start + h * self.wa, dst.size)
                    total = self.own[0, r, cols].astype(f32)
                    for k in range(self.G - 1):
                        total = total + self.r3[k, r, cols].astype(f32)
                    self.outs[a][r, src] = total

        self.rows(self.R, body)
        for k in range(self.G):
            for c in self.one(k) + self.two(k):
                c.wait_send()
            if k:
                self.three(k).wait_send()

    def events(self, pair=0):
        G = self.G
        first = lambda: (greet(G, True, pair), self.begin())
        ev = [(0.0, first), (1.1, lambda: self.add_one(0))]
        for n in range(1, G):
            ev += [(1.5 * n + 0.65, functools.partial(self.add_one, n)), (1.5 * n + 1.1, functools.partial(self.add_two, n - 1))]
        return sorted(ev, key=lambda e: e[0]), self.finish


def scatter_scratch(G, halves, R):
    most = max(len(h) for h in halves)
    a, b = [sum(p[2] for p in h) for h in halves]
    V = lambda *s: pltpu.VMEM(s, bf16)
    return [V(G, 2, R, a), V(G, 2, R, b), V(G, 2, R, a), V(G, 2, R, b), V(G, R, a), V(G, R, b), V(G - 1, R, a + b), V(G, R, a + b),
            D((4 * G * most,)), D((4 * G * most,)), D((4 * G * most,)), D((2 * G,)), D((2 * G,)), D((G - 1,)), D((G - 1,))]


def beside(plan, G, steps, now, compute, late=()):
    events, finish = plan
    units = 1.55 * G
    for n in range(steps):
        here = [act for t, act in events if min(steps - 1, int(-(-t * steps // units))) == n]
        if here:
            @pl.when(now == n)
            def _():
                for act in here:
                    act()
    compute()

    @pl.when(now == steps - 1)
    def _():
        for act in late:
            act()
        finish()


ANY = pl.BlockSpec(memory_space=pl.ANY)


def whole_vmem():
    return pl.BlockSpec(memory_space=pltpu.VMEM)


def gathered_shapes(shards, wide):
    return tuple(jax.ShapeDtypeStruct((wide * s.shape[0], s.shape[1]), s.dtype) for s in shards)


def sum_everywhere(G, acc, got, gz, s, v, sz, vz):
    z, y, x = place()
    core = {"narrow": 1 - lax.axis_index("narrow")}
    for n, t in enumerate((core, wide_id(z, y, 1 - x), wide_id(z, 1 - y, x))):
        c = remote(acc.at[n], got.at[n], s.at[n], v.at[n], t)
        c.start()
        c.wait()
        acc[n + 1] = acc[n] + got[n]
    gz[z] = acc[3]
    far = [wide_id((z + k) % G, y, x) for k in range(1, G)]
    sent = [remote(acc.at[3], gz.at[z], sz.at[k], vz.at[z], t) for k, t in enumerate(far)]
    for c in sent:
        c.start()
    for k in range(1, G):
        zz = (z + k) % G
        remote(acc.at[3], gz.at[zz], sz.at[k - 1], vz.at[zz], far[k - 1]).wait_recv()
    for c in sent:
        c.wait_send()
    total = gz[0]
    for k in range(1, G):
        total = total + gz[k]
    return total


def sum_scratch(G, rows):
    V = lambda k: pltpu.VMEM((k, rows, 128), f32)
    return [V(4), V(3), V(G), D((3,)), D((3,)), D((G - 1,)), D((G,))]


def nt(a, b):
    return lax.dot_general(a, b, NT, preferred_element_type=f32)


def nn(a, b):
    return jnp.dot(a, b, preferred_element_type=f32)


def gelu_and_slope(v):
    root = 0.7978845608028654
    square = v * v
    t = jnp.tanh(root * v * (1.0 + 0.044715 * square))
    half = 0.5 * (1.0 + t)
    return v * half, half + 0.5 * v * (1.0 - t * t) * root * (1.0 + 3 * 0.044715 * square)


def mid_kernel(G, cut, att_h, tok_h, cot_h, wo_h, wg_h, wu_h, wd_h, wd_shard, gain_ref,
               gout_h, gg_h, gu_h, gd_h, y_ref, gh_ref, ga_ref, ggain_ref, sd_ref,
               att, tok, cot, wo, wg, wu, wd, part, other, back, hid, n2t, cott, hff, gg, gu, ysend, yown, yother, stage,
               isem, osem, sp, vp, sb, vb, sy, vy, *sems):
    core = lax.axis_index("narrow")
    peer = {"narrow": 1 - core}
    n, d = tok.shape
    ff = wg.shape[1]
    tiles = n // TILE
    half = tiles // 2
    loads = [pltpu.make_async_copy(s, t, isem.at[k]) for k, (s, t) in enumerate(
        [(att_h, att), (wo_h, wo), (tok_h, tok), (wg_h, wg), (wu_h, wu), (cot_h, cot), (wd_h, wd.at[:, pl.ds(0, cut)])])]
    for c in loads:
        c.start()
    part_cols = sd_ref.shape[1]
    mid = cut + (ff - cut) // 256 * 128
    bring = Gather(G, (((0, 0, mid - cut),), ((0, mid - cut, ff - mid),)), [wd_shard], [(wd, cut, cut)], *sems[:5])
    give = Scatter(G, (((0, 0, part_cols // 2),), ((0, part_cols // 2, part_cols // 2),)), [gd_h], [sd_ref], *sems[5:])
    greet(G, True, 1)
    bring.begin()
    rows_of = lambda t: pl.ds(pl.multiple_of(t * TILE, TILE), TILE)
    send_part = lambda t: remote(part.at[rows_of(t)], other.at[rows_of(t)], sp.at[t], vp.at[t], peer)
    send_back = lambda t: remote(part.at[rows_of(t)], back.at[rows_of(t)], sb.at[t], vb.at[t], peer)
    send_y = lambda j: remote(ysend.at[rows_of(j)], yother.at[rows_of(j)], sy.at[j], vy.at[j], peer)
    gain = gain_ref[...]

    for c in loads[:2]:
        c.wait()

    def at_step(s, plan):
        for k, acts in plan.items():
            @pl.when(s == k)
            def _():
                for act in acts:
                    act()

    turns = [functools.partial(bring.turns, k) for k in range(G)]
    steps = [functools.partial(bring.step, k) for k in range(1, G)]

    @pl.loop(0, tiles)
    def _(t):
        part[rows_of(t), :] = nt(att[rows_of(t), :], wo[...]).astype(bf16)
        send_part(t).start()
        at_step(t, {1: turns[:1], 2: steps[:1]})

    for c in loads[2:]:
        c.wait()

    chunks, at = [], 0
    while at < ff:
        w = min(384, ff - at)
        chunks.append((at, w))
        at += w

    later = [act for pair in zip(turns[1:], steps[1:] + [lambda: None]) for act in pair]

    @pl.loop(0, tiles)
    def _(s):
        t = (s + half * (1 - core)) % tiles
        r = rows_of(t)
        send_part(t).wait()
        h = tok[r, :].astype(f32) + (part[r, :].astype(f32) + other[r, :].astype(f32))
        hid[r, :] = h
        factor = lax.rsqrt(jnp.mean(h * h, axis=1, keepdims=True) + epsilon)
        low = (h * factor * gain).astype(bf16)
        n2t[:, r] = low.T
        cott[:, r] = cot[r, :].T
        for at, w in chunks:
            cols = pl.ds(at, w)
            act, slope = gelu_and_slope(nn(low, wg[:, cols]))
            up = nn(low, wu[:, cols])
            hff[r, cols] = (act * up).astype(bf16)
            gg[r, cols] = (up * slope).astype(bf16)
            gu[r, cols] = act.astype(bf16)
        at_step(s, {1: later[:2], 2: later[2:4], 3: later[4:]})

    def weight_grad(left, right, out, slot, width):
        rows = stage.shape[1]
        block = lambda k: pl.ds(k * rows, rows)
        copy = lambda k: pltpu.make_async_copy(stage.at[k % 2, :, pl.ds(0, width)], out.at[block(k)], osem.at[2 * slot + k % 2])
        count = d // rows
        for k in range(count):
            if k >= 2:
                copy(k - 2).wait()
            stage[k % 2, :, pl.ds(0, width)] = nn(left[block(k), :], right[...]).astype(bf16)
            copy(k).start()
        return [copy(k) for k in range(max(0, count - 2), count)]

    for c in weight_grad(cott, hff, gd_h, 0, ff):
        c.wait()
    give.begin()
    bring.finish()
    ones = [functools.partial(give.add_one, k) for k in range(G)]
    twos = [functools.partial(give.add_two, k) for k in range(G - 1)]

    @pl.loop(0, tiles)
    def _(s):
        t = (s + half * (1 - core)) % tiles
        r = rows_of(t)
        ct = cot[r, :]
        for at, w in chunks:
            cols = pl.ds(at, w)
            gf = nn(ct, wd[:, cols])
            gg[r, cols] = (gf * gg[r, cols].astype(f32)).astype(bf16)
            gu[r, cols] = (gf * gu[r, cols].astype(f32)).astype(bf16)
        part[r, :] = (nt(gg[r, :], wg[...]) + nt(gu[r, :], wu[...])).astype(bf16)
        send_back(t).start()
        y = nt(hff[r, :], wd[...]).astype(bf16)

        @pl.when(s < half)
        def _():
            ysend[rows_of(s), :] = y
            send_y(s).start()

        @pl.when(s >= half)
        def _():
            yown[rows_of(s - half), :] = y

        at_step(s, {0: ones[:1], 1: ones[1:2], 2: twos[:1] + ones[2:3], 3: twos[1:2]})

    ggain_ref[...] = jnp.zeros_like(ggain_ref)

    @pl.loop(0, tiles)
    def _(s):
        t = (s + half * (1 - core)) % tiles
        r = rows_of(t)
        send_back(t).wait()
        total = part[r, :].astype(f32) + back[r, :].astype(f32)
        h = hid[r, :]
        factor = lax.rsqrt(jnp.mean(h * h, axis=1, keepdims=True) + epsilon)
        unit = h * factor
        g = gain * total
        gh = cot[r, :].astype(f32) + factor * (g - unit * jnp.mean(g * unit, axis=1, keepdims=True))
        low = gh.astype(bf16)
        cott[:, r] = low.T
        ga_ref[r, :] = nn(low, wo[...]).astype(bf16)

        @pl.when(s >= half)
        def _():
            j = rows_of(s - half)
            gh_ref[j, :] = gh
            ggain_ref[...] += jnp.sum(total * unit, axis=0, keepdims=True)
            send_y(s - half).wait()
            y_ref[j, :] = (h + (yown[j, :].astype(f32) + yother[j, :].astype(f32))).astype(bf16)

        at_step(s, {0: ones[3:4], 3: twos[2:3]})

    for act in [act for pair in zip(ones[4:], twos[3:]) for act in pair]:
        act()
    for left, right, out, slot in ((n2t, gg, gg_h, 1), (n2t, gu, gu_h, 2), (cott, att, gout_h, 3)):
        for c in weight_grad(left, right, out, slot, right.shape[1]):
            c.wait()
    give.finish()


def middle(att, tok, cot, wo, wg, wu, wd, wd_shard, gain, here, wide, cid):
    n, d = tok.shape
    units, ff, G, cut = att.shape[1], wg.shape[1], wide // 4, wd.shape[1]
    B = lambda *s: pltpu.VMEM(s, bf16)
    sds = jax.ShapeDtypeStruct
    tiles = n // TILE
    halves = (((0, 0, cut),), ((0, cut, ff - cut),))
    return pl.pallas_call(functools.partial(mid_kernel, G, cut),
        out_shape=(sds((d, units), bf16), sds((d, ff), bf16), sds((d, ff), bf16), sds((d, ff), bf16),
                   sds((n // 2, d), bf16), sds((n // 2, d), f32), sds((n, units), bf16), sds((1, d), f32), sds((d // wide, here), f32)),
        in_specs=[ANY] * 8 + [whole_vmem()], out_specs=(ANY,) * 4 + (whole_vmem(),) * 5,
        scratch_shapes=[B(n, units), B(n, d), B(n, d), B(d, units), B(d, ff), B(d, ff), B(d, ff), B(n, d), B(n, d), B(n, d),
                        pltpu.VMEM((n, d), f32), B(d, n), B(d, n), B(n, ff), B(n, ff), B(n, ff),
                        B(n // 2, d), B(n // 2, d), B(n // 2, d), B(2, 512, ff),
                        D((7,)), D((8,)), D((tiles,)), D((tiles,)), D((tiles,)), D((tiles,)), D((tiles // 2,)), D((tiles // 2,))]
        + gather_scratch(G, halves, 1) + scatter_scratch(G, (((0, 0, here // 2),), ((0, here // 2, here // 2),)), d // wide),
        compiler_params=params(cid), name="feed_forward")(att, tok, cot, wo, wg, wu, wd, wd_shard, gain)


def local(tokens, cotangent, pages, boxes, gain_attn, gain_ffn, bias_tables, w_query, w_key, w_value, w_out, w_gate, w_up, w_down):
    wide, narrow = lax.axis_size("wide"), lax.axis_size("narrow")
    heads_all = bias_tables.shape[1]
    heads = heads_all // narrow
    core = lax.axis_index("narrow")
    tables = lax.dynamic_slice_in_dim(bias_tables, core * heads, heads, 1)
    inner, ff, d = w_query.shape[1], w_gate.shape[1], tokens.shape[1]
    gain_one, gain_two = gain_attn.astype(f32)[None], gain_ffn.astype(f32)[None]

    all_tokens = lax.all_gather(tokens, "narrow", axis=0, tiled=True)
    all_cot = lax.all_gather(cotangent, "narrow", axis=0, tiled=True)
    early = inner // 4 * 3
    bias, ids, (w_first, full_out, full_gate) = bias_and_gather(
        tables, boxes, pages, [jnp.concatenate([w_query, w_key, w_value], axis=1), w_out.T, w_gate],
        (((2, 0, ff), (0, 0, early)), ((1, 0, inner), (0, early, 3 * inner - early))), wide, 1)
    down_shard = w_down.T
    cut = (ff // 128 + 1) // 2 * 128
    (attended, lse, normed, qkv), (full_up, most_down) = attn_fwd_and_gather(
        all_tokens, gain_one, w_first, bias, [w_up, down_shard[:, :cut]],
        (((0, 0, cut), (1, 0, cut - 384)), ((0, cut, ff - cut), (1, cut - 384, 384))), wide, 2)
    here = 2 * inner
    grad_w_out, grad_w_gate, grad_w_up, grad_w_down, output, grad_hidden, grad_attended, grad_gain_two, s_down = middle(
        attended, all_tokens, all_cot, full_out, full_gate, full_up, most_down, down_shard, gain_two, here, wide, 3)
    even = (ff + inner + ff - here) // 2
    (g, band, far, grad_w_first, grad_normed), (s_gate, s_out, more_down) = attn_bwd_and_scatter(
        qkv, bias, attended, grad_attended, lse, normed, w_first, [grad_w_gate, grad_w_out, grad_w_down],
        (((0, 0, even),), ((0, even, ff - even), (1, 0, inner), (2, here, ff - here))), wide, 4)
    s_down = jnp.concatenate([s_down, more_down[:, here:]], axis=1)
    small, grad_tokens, (s_up, s_first) = hist_and_scatter(
        g, band, far, ids, grad_normed, tokens, grad_hidden, gain_one, grad_gain_two, [grad_w_up, grad_w_first],
        (((0, 0, ff),), ((1, 0, 3 * inner),)), wide, 5)
    s_query, s_key, s_value = jnp.split(s_first, 3, axis=1)
    lines = d // 128
    one, two = small[:lines].reshape(d), small[lines:2 * lines].reshape(d)
    table = small[2 * lines:, :bias_tables.shape[0]].T
    return (output, grad_tokens, one, two, table, s_query, s_key, s_value, s_out.T, s_gate, s_up, s_down.T)


def solution(mesh):
    rows, cols, tall = P(("wide", "narrow"), None), P("wide", "narrow"), P("narrow", "wide")
    in_specs = (rows, rows, P("wide"), P(None, "wide"), P(), P(), P(), cols, cols, cols, tall, cols, cols, tall)
    out_specs = (rows, rows, P(), P(), P(), cols, cols, cols, tall, cols, cols, tall)
    return jax.shard_map(local, mesh=mesh, in_specs=in_specs, out_specs=out_specs, check_vma=False)
```

```python
import functools

import jax
import jax.numpy as jnp
from jax import lax
from jax.experimental import pallas as pl
from jax.experimental.pallas import tpu as pltpu
from jax.sharding import PartitionSpec as P

f32, bf16 = jnp.float32, jnp.bfloat16
MESH = pl.DeviceIdType.MESH


EDGES = (1, 2, 3, 4, 5, 6, 7, 8, 12, 16, 23, 32, 46, 64, 91)
NT = (((1,), (1,)), ((), ()))
VM = 58 * 2**20
TABLE_SCALE = 2047.0
TABLE_LIFT = 8192
TILE = 256
epsilon = 1e-06


def params(cid):
    return pltpu.CompilerParams(collective_id=cid, has_side_effects=True, vmem_limit_bytes=VM)


def lane_take(table, idx):
    return jnp.take_along_axis(table, idx, axis=1, mode="promise_in_bounds")


def buckets_of(gap, steps, shift):
    return lane_take(steps, jnp.minimum(jnp.abs(gap) >> shift, EDGES[-1])) + jnp.where(gap > 0, 16, 0)


def bias_tile(start, heads, rows, n, tab_ref, box_row, page_row, bias_ref, ids_ref, lin_ids, lin, words_ref):
    lane = lax.broadcasted_iota(jnp.int32, (rows, 128), 1)
    down = lax.broadcasted_iota(jnp.int32, (rows, 128), 0)
    steps = sum([(lane >= e).astype(jnp.int32) for e in EDGES])
    pairs = heads // 2

    def column(row_ref, t):
        values = jnp.broadcast_to(row_ref[t:t + 1, pl.ds(pl.multiple_of(start // 128 * 128, 128), 128)], (rows, 128)).astype(f32)
        return jnp.broadcast_to(jnp.sum(jnp.where(lane == down + start % 128, values, 0.0), axis=1, keepdims=True), (rows, 128)).astype(jnp.int32)

    allowed_col = column(page_row, 0) % 2
    cols = [column(box_row, t) for t in range(2)]

    @pl.when(start == 0)
    def _():
        first = lax.axis_index("narrow") * heads
        row = lax.broadcasted_iota(jnp.int32, (heads, tab_ref.shape[0]), 0)
        wanted = first + jnp.where(row < pairs, 2 * row, 2 * (row - pairs) + 1)
        pick = jnp.where(lax.broadcasted_iota(jnp.int32, row.shape, 1) == wanted, 1.0, 0.0).astype(bf16)
        picked = jnp.dot(pick, tab_ref[...], preferred_element_type=f32)
        fixed = jnp.round(picked * TABLE_SCALE).astype(jnp.int32)
        words_ref[...] = jnp.zeros_like(words_ref)
        words_ref[0:pairs, 0:picked.shape[1]] = fixed[0:pairs] * 65536 + fixed[pairs:heads] + TABLE_LIFT

        @pl.loop(0, 8)
        def _(k):
            ids = buckets_of(lane - down + (k - 4) * rows, steps, 0)
            lin_ids[k] = ids.astype(f32)
            for p in range(pairs):
                lin[k, p] = lane_take(jnp.broadcast_to(words_ref[p:p + 1, :], (rows, 128)), ids)

    unit = 1.0 / TABLE_SCALE
    tables = [jnp.broadcast_to(words_ref[p:p + 1, :], (rows, 128)) for p in range(pairs)]

    @pl.loop(0, n // 128)
    def _(c):
        lanes = pl.ds(pl.multiple_of(c * 128, 128), 128)
        near = jnp.clip((c * 128 - start) // rows + 4, 0, 7)
        ids = []
        for t in range(2):
            ids.append(buckets_of(jnp.broadcast_to(box_row[t:t + 1, lanes], (rows, 128)) - cols[t], steps, 2))
            ids_ref[t, :, lanes] = ids[t].astype(f32)
        ok = jnp.broadcast_to(page_row[:, lanes], (rows, 128)) == allowed_col
        for p in range(pairs):
            words = lin[near, p] + lane_take(tables[p], ids[0] + 32) + lane_take(tables[p], ids[1] + 64)
            upper = (words >> 16).astype(f32) * unit
            lower = (words & 0xFFFF).astype(f32) * unit - 3 * TABLE_LIFT * unit
            bias_ref[2 * p, :, lanes] = jnp.where(ok, upper, -1e30)
            bias_ref[2 * p + 1, :, lanes] = jnp.where(ok, lower, -1e30)


def bias_gather_kernel(heads, rows, n, G, halves, count, into, *refs):
    ins, srcs = refs[:3], refs[3:3 + count]
    bias_ref, ids_ref, lin_ids = refs[3 + count:6 + count]
    kinds = len(set(k for k, _ in into))
    outs, scratch, sems = refs[6 + count:6 + count + kinds], refs[6 + count + kinds:8 + count + kinds], refs[8 + count + kinds:]
    now = pl.program_id(0)
    comm = Gather(G, halves, srcs, [(outs[k], c, 0) for k, c in into], *sems)
    beside(comm.events(), G, n // rows, now, lambda: bias_tile(now * rows, heads, rows, n, *ins, bias_ref, ids_ref, lin_ids, *scratch))


def bias_and_gather(tables, heads, boxes, pages, shards, into, halves, wide, cid):
    n, G, rows = pages.shape[0], wide // 4, 64
    count = len(shards)
    widths = [sum(a.shape[1] for a, (j, _) in zip(shards, into) if j == k) for k in sorted(set(k for k, _ in into))]
    outs = pl.pallas_call(functools.partial(bias_gather_kernel, heads, rows, n, G, halves, count, into),
        grid=(n // rows,),
        out_shape=(jax.ShapeDtypeStruct((heads, n, n), f32), jax.ShapeDtypeStruct((2, n, n), f32), jax.ShapeDtypeStruct((8, rows, 128), f32)) + gathered_shapes([(shards[0].shape[0], w) for w in widths], wide),
        in_specs=[pl.BlockSpec(tables.shape, lambda i: (0, 0)), pl.BlockSpec((2, n), lambda i: (0, 0)), pl.BlockSpec((1, n), lambda i: (0, 0))] + [ANY] * count,
        out_specs=(pl.BlockSpec((heads, rows, n), lambda i: (0, i, 0)), pl.BlockSpec((2, rows, n), lambda i: (0, i, 0)),
                   pl.BlockSpec((8, rows, 128), lambda i: (0, 0, 0))) + (ANY,) * len(widths),
        scratch_shapes=[pltpu.VMEM((8, heads // 2, rows, 128), jnp.int32), pltpu.VMEM((8, 128), jnp.int32)] + gather_scratch(G, halves, count),
        compiler_params=params(cid), name="layout_bias_gather")(
            tables, boxes, pages[None], *shards)
    return outs[0], outs[1:3], outs[3:]


def half_of(v, e):
    lane = lax.broadcasted_iota(jnp.int32, v.shape, 1)
    return jnp.where((lane >= 64) == (e == 1), v, jnp.zeros_like(v))


def join(a, b):
    lane = lax.broadcasted_iota(jnp.int32, a.shape, 1)
    return jnp.where(lane < 64, a, b)


def project(tok_ref, gain_ref, w_ref, normed, qkv):
    gain = gain_ref[0:1, :].astype(f32)

    @pl.loop(0, tok_ref.shape[0] // TILE)
    def _(t):
        r = pl.ds(pl.multiple_of(t * TILE, TILE), TILE)
        x = tok_ref[r, :].astype(f32)
        low = (x * lax.rsqrt(jnp.mean(x * x, axis=1, keepdims=True) + epsilon) * gain).astype(bf16)
        normed[r, :] = low
        qkv[r, :] = jnp.dot(low, w_ref[...], preferred_element_type=f32).astype(bf16)


def fwd_tile(p, i, tq, pairs, qkv, bias_ref, o_ref, lse_ref):
    cols = lambda k: pl.ds(pl.multiple_of((p + k * pairs) * 128, 128), 128)
    q, k, v = qkv[pl.ds(pl.multiple_of(i * tq, tq), tq), cols(0)], qkv[:, cols(1)], qkv[:, cols(2)]
    outs, lses = [], []
    for e in range(2):
        s = lax.dot_general(half_of(q, e), k, NT, preferred_element_type=f32) + bias_ref[e]
        peak = jnp.max(s, axis=1, keepdims=True)
        w = jnp.exp(s - peak)
        total = jnp.sum(w, axis=1, keepdims=True)
        outs.append(jnp.dot(w.astype(bf16), v, preferred_element_type=f32) / total)
        lses.append(peak + jnp.log(total))
    o_ref[...] = join(*outs).astype(bf16)
    lse_ref[0] = jnp.concatenate(lses, axis=1)


def fwd_kernel(pairs, tiles, G, halves, count, *refs):
    (tok, gain, w, bias_ref), srcs = refs[:4], refs[4:4 + count]
    o_ref, lse_ref, normed_h, qkv_h = refs[4 + count:8 + count]
    outs, (tok_s, w_s, normed, qkv, keep, load), sems = refs[8 + count:8 + 2 * count], refs[8 + 2 * count:14 + 2 * count], refs[14 + 2 * count:]
    p, i = pl.program_id(0), pl.program_id(1)
    now, steps = p * tiles + i, pairs * tiles
    copies = lambda: [pltpu.make_async_copy(normed, normed_h, keep.at[0]), pltpu.make_async_copy(qkv, qkv_h, keep.at[1])]

    loads = lambda: [pltpu.make_async_copy(tok, tok_s, load.at[0]), pltpu.make_async_copy(w, w_s, load.at[1])]

    def compute():
        @pl.when(now == 0)
        def _():
            for c in loads():
                c.wait()
            project(tok_s, gain, w_s, normed, qkv)
            for c in copies():
                c.start()

        fwd_tile(p, i, o_ref.shape[0], pairs, qkv, bias_ref, o_ref, lse_ref)

        @pl.when(now == steps - 1)
        def _():
            for c in copies():
                c.wait()

    beside(Gather(G, halves, srcs, outs, *sems).events(), G, steps, now, compute, early=[lambda: [c.start() for c in loads()]])


def attn_fwd_and_gather(tok, gain, w, bias, shards, widths, halves, wide, cid, tq=256):
    n, d = tok.shape
    width = w.shape[1] // 3
    pairs, tiles, count, G = width // 128, n // tq, len(shards), wide // 4
    sds = jax.ShapeDtypeStruct
    const = lambda s: pl.BlockSpec(s, lambda p, i: (0, 0))
    outs = pl.pallas_call(functools.partial(fwd_kernel, pairs, tiles, G, halves, count), grid=(pairs, tiles),
        out_shape=(sds((n, width), bf16), sds((pairs, n, 2), f32), sds((n, d), bf16), sds((n, 3 * width), bf16)) + gathered_shapes([(shards[0].shape[0], c) for c in widths], wide),
        in_specs=[ANY, const(gain.shape), ANY, pl.BlockSpec((2, tq, n), lambda p, i: (p, i, 0))] + [ANY] * count,
        out_specs=(pl.BlockSpec((tq, 128), lambda p, i: (i, p)), pl.BlockSpec((1, tq, 2), lambda p, i: (p, i, 0)), ANY, ANY) + (ANY,) * count,
        scratch_shapes=[pltpu.VMEM((n, d), bf16), pltpu.VMEM(w.shape, bf16), pltpu.VMEM((n, d), bf16), pltpu.VMEM((n, 3 * width), bf16), D((2,)), D((2,))] + gather_scratch(G, halves, count),
        compiler_params=params(cid), name="attention_gather")(tok, gain, w, bias, *shards)
    return outs[:4], outs[4:]


def band_sums(i, e, g_ref, band_ref, far_ref):
    tq, n = g_ref.shape[1], g_ref.shape[2]
    first = i * (tq // 128) - 1

    @pl.when(i == 0)
    def _():
        band_ref[e] = jnp.zeros(band_ref.shape[1:], f32)
        far_ref[e] = jnp.zeros(far_ref.shape[1:], f32)

    for m in range(tq // 128 + 2):
        @pl.when((first + m >= 0) & (first + m < n // 128))
        def _():
            band_ref[e, :, m * 128:(m + 1) * 128] += g_ref[e, :, pl.ds(pl.multiple_of((first + m) * 128, 128), 128)].astype(f32)

    for c in range(n // 128):
        @pl.when((c < first) | (c > first + tq // 128 + 1))
        def _():
            total = g_ref[e, 0:16, c * 128:(c + 1) * 128].astype(f32)
            for k in range(1, tq // 16):
                total = total + g_ref[e, k * 16:(k + 1) * 16, c * 128:(c + 1) * 128].astype(f32)
            far_ref[e, jnp.where(c < first, 0, 1)] += total


def bwd_tile(p, pairs, i, last_tile, last, q_ref, k_ref, v_ref, bias_ref, o_ref, do_ref, lse_ref, normed_ref, w_ref,
             g_ref, band_ref, far_ref, dw_ref, dx_ref, dkt, dvt, dqkv, turned):
    tq, n = q_ref.shape[0], k_ref.shape[0]
    rows = pl.ds(pl.multiple_of(i * tq, tq), tq)

    @pl.when(p == 0)
    def _():
        turned[:, rows] = normed_ref[rows, :].T

    @pl.when(i == 0)
    def _():
        dkt[...] = jnp.zeros_like(dkt)
        dvt[...] = jnp.zeros_like(dvt)

    q, k, v, do = q_ref[...], k_ref[...], v_ref[...], do_ref[...]
    prod = do.astype(f32) * o_ref[...].astype(f32)
    dqs = []
    for e in range(2):
        qm, dom = half_of(q, e), half_of(do, e)
        s = lax.dot_general(qm, k, NT, preferred_element_type=f32) + bias_ref[e]
        w = jnp.exp(s - lse_ref[0, :, e:e + 1])
        dp = lax.dot_general(dom, v, NT, preferred_element_type=f32)
        inner = jnp.sum(half_of(prod, e), axis=1, keepdims=True)
        g = (w * (dp - inner)).astype(bf16)
        g_ref[e] = g
        dqs.append(jnp.dot(g, k, preferred_element_type=f32))
        dvt[...] += jnp.dot(dom.T, w.astype(bf16), preferred_element_type=f32)
        dkt[...] += jnp.dot(qm.T, g, preferred_element_type=f32)
        band_sums(i, e, g_ref, band_ref, far_ref)
    columns = lambda k: pl.ds(pl.multiple_of((p + k * pairs) * 128, 128), 128)
    dqkv[rows, columns(0)] = join(*dqs).astype(bf16)

    @pl.when(last_tile)
    def _():
        dqkv[:, columns(1)] = dkt[...].T.astype(bf16)
        dqkv[:, columns(2)] = dvt[...].T.astype(bf16)

        @pl.when(last)
        def _():
            @pl.loop(0, n // TILE)
            def _(t):
                r = pl.ds(pl.multiple_of(t * TILE, TILE), TILE)
                dw_ref[r, :] = jnp.dot(turned[r, :], dqkv[...], preferred_element_type=f32).astype(bf16)
                dx_ref[r, :] = lax.dot_general(dqkv[r, :], w_ref[...], NT, preferred_element_type=f32).astype(bf16)


def bwd_kernel(pairs, tiles, G, halves, count, *refs):
    ins, parts = refs[:9], refs[9:9 + count]
    mid = refs[9 + count:14 + count]
    outs, accs, sems = refs[14 + count:14 + 2 * count], refs[14 + 2 * count:18 + 2 * count], refs[21 + 2 * count:]
    normed_s, w_s, load = refs[18 + 2 * count:21 + 2 * count]
    loads = [lambda: pltpu.make_async_copy(ins[7], normed_s, load.at[0]), lambda: pltpu.make_async_copy(ins[8], w_s, load.at[1])]
    p, i = pl.program_id(0), pl.program_id(1)
    comm = Scatter(G, halves, parts, outs, *sems)
    now, steps = p * tiles + i, pairs * tiles

    def compute():
        for n, step in ((0, 0), (1, steps - 1)):
            @pl.when(now == step)
            def _():
                loads[n]().wait()

        bwd_tile(p, pairs, i, i == tiles - 1, p == pairs - 1, *ins[:7], normed_s, w_s, *mid, *accs)

    beside(comm.events(), G, steps, now, compute, early=[lambda: [c().start() for c in loads]])


def shard_shapes(parts, wide):
    return tuple(jax.ShapeDtypeStruct((p.shape[0] // wide, p.shape[1]), f32) for p in parts)


def attn_bwd_and_scatter(qkv, bias, o, do, lse, normed, w, parts, halves, wide, cid, tq=256):
    n, width, d = qkv.shape[0], qkv.shape[1] // 3, normed.shape[1]
    pairs, tiles, count, G = width // 128, n // tq, len(parts), wide // 4
    sds = jax.ShapeDtypeStruct
    tile = pl.BlockSpec((tq, 128), lambda p, i: (i, p))
    full = lambda rows, k: pl.BlockSpec((rows, 128), lambda p, i: (0, p + k * pairs))
    const = lambda s: pl.BlockSpec(s, lambda p, i: (0, 0))
    outs = pl.pallas_call(functools.partial(bwd_kernel, pairs, tiles, G, halves, count), grid=(pairs, tiles),
        out_shape=(sds((2 * pairs, n, n), bf16), sds((2 * pairs, tq, tq + 256), f32), sds((2 * pairs, 2, 16, 128), f32)) + (sds((d, 3 * width), bf16), sds((n, d), bf16)) + shard_shapes(parts, wide),
        in_specs=[tile, full(n, 1), full(n, 2), pl.BlockSpec((2, tq, n), lambda p, i: (p, i, 0)), tile, tile,
                  pl.BlockSpec((1, tq, 2), lambda p, i: (p, i, 0)), ANY, ANY] + [ANY] * count,
        out_specs=(pl.BlockSpec((2, tq, n), lambda p, i: (p, i, 0)), pl.BlockSpec((2, tq, tq + 256), lambda p, i: (p, 0, 0)),
                   pl.BlockSpec((2, 2, 16, 128), lambda p, i: (p, 0, 0, 0))) + (const(w.shape), const((n, d))) + (whole_vmem(),) * count,
        scratch_shapes=[pltpu.VMEM((128, n), f32), pltpu.VMEM((128, n), f32), pltpu.VMEM((n, 3 * width), bf16), pltpu.VMEM((d, n), bf16),
                        pltpu.VMEM((n, d), bf16), pltpu.VMEM(w.shape, bf16), D((2,))] + scatter_scratch(G, halves, parts[0].shape[0] // wide),
        compiler_params=params(cid), name="attention_back_scatter")(
            qkv, qkv, qkv, bias, o, do, lse, normed, w, *parts)
    return outs[:5], outs[5:]


def rows_times_hots(src, ids, rows, heads, gs):
    n = src(0).shape[1]
    for h in range(heads):
        block = src(h)
        for c in range(n // 128):
            gs[c, h * rows:(h + 1) * rows, :] = block[:, c * 128:(c + 1) * 128]
    labels = [lax.broadcasted_iota(jnp.int32, (16, n), 0).astype(bf16) + float(k) for k in (0, 16)]
    one, zero = jnp.ones((16, n), bf16), jnp.zeros((16, n), bf16)
    group = 4 // len(ids(0))
    total = jnp.zeros((heads * group, 128), f32)
    for first in range(0, rows, group):
        grow, hots = [], []
        for r in range(first, first + group):
            grow.append(jnp.concatenate([gs[c, pl.ds(r, heads, stride=rows), :] for c in range(n // 128)], axis=1))
            for one_row in ids(r):
                row = jnp.broadcast_to(one_row, (16, n)).astype(bf16)
                hots += [jnp.where(row == label, one, zero) for label in labels]
        total = total + lax.dot_general(jnp.concatenate(grow, axis=0).astype(bf16), jnp.concatenate(hots, axis=0), NT, preferred_element_type=f32)
    return total


def own_blocks(total, heads, width):
    out = total[0:heads, 0:width]
    for k in range(1, 128 // width):
        out = out + total[k * heads:(k + 1) * heads, k * width:(k + 1) * width]
    return out


def halves_times_hots(g_ref, ids_ref, block, heads, gs, low):
    rows, n = 16, g_ref.shape[2]
    for h in range(heads):
        for c in range(n // 128):
            gs[c, h * rows:(h + 1) * rows, :] = g_ref[h, block, c * 128:(c + 1) * 128].astype(f32)
    for t in range(2):
        ids = ids_ref[t, block, :]
        low[t] = jnp.where(ids >= 16.0, ids - 16.0, ids)
    label = lax.broadcasted_iota(jnp.int32, (16, n), 0).astype(bf16)
    one, zero = jnp.ones((16, n), bf16), jnp.zeros((16, n), bf16)
    total = jnp.zeros((64, 64), f32)
    for first in range(0, rows, 2):
        left, hots = [], []
        for r in range(first, first + 2):
            grow = jnp.concatenate([gs[c, pl.ds(r, heads, stride=rows), :] for c in range(n // 128)], axis=1)
            for t in range(2):
                upper = jnp.broadcast_to(ids_ref.at[t, block][r:r + 1, :], (heads, n)) >= 16.0
                left += [jnp.where(upper, 0.0, grow), jnp.where(upper, grow, 0.0)]
                row = jnp.broadcast_to(low[t, r:r + 1, :], (16, n)).astype(bf16)
                hots.append(jnp.where(row == label, one, zero))
        total = total + lax.dot_general(jnp.concatenate(left, axis=0).astype(bf16), jnp.concatenate(hots, axis=0), NT, preferred_element_type=f32)
    return total


def own_halves(total, heads):
    out = 0.0
    for k in range(2):
        part = lambda t, up: total[k * 32 + (2 * t + up) * heads:k * 32 + (2 * t + up + 1) * heads, k * 32 + t * 16:k * 32 + t * 16 + 16]
        out = out + jnp.concatenate([part(0, 0), part(0, 1), part(1, 0), part(1, 1)], axis=1)
    return out


def hist_tile(now, heads, g_ref, ids_ref, band_ref, far_ref, lin_ids, table, boxes, gs, low):
    @pl.when(now == 0)
    def _():
        sides = [jnp.sum(jnp.sum(far_ref[:, k], axis=1), axis=1, keepdims=True) for k in range(2)]
        lane = lax.broadcasted_iota(jnp.int32, (heads, 128), 1)
        table[...] = jnp.zeros_like(table)
        boxes[...] = jnp.zeros_like(boxes)
        table[0:heads, :] = jnp.where(lane == 15, sides[0], 0.0) + jnp.where(lane == 31, sides[1], 0.0)

    big = g_ref.shape[1]

    @pl.loop(0, big // 16)
    def _(q):
        block = pl.ds(pl.multiple_of(q * 16, 16), 16)
        boxes[...] += halves_times_hots(g_ref, ids_ref, block, heads, gs, low)

    wide = band_ref.shape[2] // 128
    per = lin_ids.shape[1]
    a = now * 16 // per
    inside = pl.ds(pl.multiple_of(now * 16 % per, 16), 16)

    def band_ids(r):
        return [jnp.concatenate([lin_ids.at[jnp.clip((m - 1) * (128 // per) - a + 4, 0, 7), inside][r:r + 1, :] for m in range(wide)], axis=1)]

    table[...] += rows_times_hots(lambda h: band_ref[h], band_ids, 16, heads, gs)


def hist_kernel(heads, rows, n, G, halves, count, *refs):
    (g_ref, ids_ref, band_ref, far_ref, lin_ids, dx_h, tok_h, gh_h, gain_ref, gain_two), parts = refs[:10], refs[10:10 + count]
    small_ref, gt_ref = refs[10 + count:12 + count]
    outs, rest = refs[12 + count:12 + 2 * count], refs[12 + 2 * count:]
    (gs, low, table, boxes, got, dx, tok, gh, load, pair_sem), sums, sems = rest[:10], rest[10:17], rest[17:]
    acc = sums[0]
    now, steps = pl.program_id(0), n // rows
    core = lax.axis_index("narrow")
    mine = tok.shape[0]
    d = tok.shape[1]
    comm = Scatter(G, halves, parts, outs, *sems)
    loads = lambda: [pltpu.make_async_copy(dx_h.at[pl.ds(pl.multiple_of(core * mine, mine), mine)], dx, load.at[0]),
                     pltpu.make_async_copy(tok_h, tok, load.at[1]), pltpu.make_async_copy(gh_h, gh, load.at[2])]
    swap = lambda: remote(dx_h.at[pl.ds(pl.multiple_of((1 - core) * mine, mine), mine)], got, pair_sem.at[0], pair_sem.at[1], {"narrow": 1 - core})

    def compute():
        @pl.when(now == 0)
        def _():
            swap().start()
            acc[0] = jnp.zeros(acc.shape[1:], f32)
            for k in range(d // 128):
                acc[0, d // 128 + k:d // 128 + k + 1, :] = gain_two[:, k * 128:(k + 1) * 128]

        @pl.when(now == steps // 8)
        def _():
            swap().wait()
            for c in loads():
                c.wait()

        for t in range(mine // TILE):
            @pl.when(now == steps // 8 + t)
            def _():
                r = pl.ds(t * TILE, TILE)
                x = tok[r, :].astype(f32)
                total = dx[r, :].astype(f32) + got[r, :].astype(f32)
                factor = lax.rsqrt(jnp.mean(x * x, axis=1, keepdims=True) + epsilon)
                unit = x * factor
                scaled = gain_ref[0:1, :].astype(f32) * total
                gt_ref[r, :] = gh[r, :] + factor * (scaled - unit * jnp.mean(scaled * unit, axis=1, keepdims=True))
                gain = jnp.sum(total * unit, axis=0, keepdims=True)
                for k in range(d // 128):
                    acc[0, k:k + 1, :] += gain[:, k * 128:(k + 1) * 128]

        hist_tile(now, heads, g_ref, ids_ref, band_ref, far_ref, lin_ids, table, boxes, gs, low)

    def reduce():
        acc[0, pl.ds(pl.multiple_of(2 * (d // 128) + core * heads, 8), heads), 0:32] = own_blocks(table[...], heads, 32)
        acc[0, pl.ds(pl.multiple_of(2 * (d // 128) + core * heads, 8), heads), 32:96] = own_halves(boxes[...], heads)

    events, _ = comm.events(1)
    stages = sum_everywhere(G, small_ref, *sums)
    beside((events, lambda: None), G, steps, now, compute, [reduce] + [act for pair in zip(stages, comm.ending()) for act in pair],
           [lambda: [c.start() for c in loads()]])


def hist_and_scatter(g, band, far, ids, dx, tok, gh, gain, gain_two, parts, halves, wide, cid):
    heads, n, _ = g.shape
    rows, count, G, d = n // (band.shape[1] // 16), len(parts), wide // 4, tok.shape[1]
    box_ids, lin_ids = ids
    small = 2 * (d // 128) + 2 * heads
    sds = jax.ShapeDtypeStruct
    const = lambda s: pl.BlockSpec(s, lambda i: (0, 0))
    outs = pl.pallas_call(functools.partial(hist_kernel, heads, rows, n, G, halves, count), grid=(n // rows,),
        out_shape=(sds((small, 128), f32), sds(tok.shape, f32)) + shard_shapes(parts, wide),
        in_specs=[pl.BlockSpec((heads, rows, n), lambda i: (0, i, 0)), pl.BlockSpec((2, rows, n), lambda i: (0, i, 0)),
                  pl.BlockSpec((heads, 16, band.shape[2]), lambda i: (0, i, 0)), pl.BlockSpec(far.shape, lambda i: (0, 0, 0, 0)),
                  pl.BlockSpec(lin_ids.shape, lambda i: (0, 0, 0)), ANY, ANY, ANY, const(gain.shape), const(gain_two.shape)] + [ANY] * count,
        out_specs=(const((small, 128)), const(tok.shape)) + (whole_vmem(),) * count,
        scratch_shapes=[pltpu.VMEM((n // 128, heads * 16, 128), f32), pltpu.VMEM((2, 16, n), f32), pltpu.VMEM((4 * heads, 128), f32), pltpu.VMEM((64, 64), f32), pltpu.VMEM(tok.shape, bf16),
                        pltpu.VMEM(tok.shape, bf16), pltpu.VMEM(tok.shape, bf16), pltpu.VMEM(tok.shape, f32), D((3,)), D((2,))]
        + sum_scratch(G, small) + scatter_scratch(G, halves, parts[0].shape[0] // wide),
        compiler_params=params(cid), name="table_grad_scatter")(g, box_ids, band, far, lin_ids, dx, tok, gh, gain, gain_two, *parts)
    return outs[0], outs[1], outs[2:]


D = pltpu.SemaphoreType.DMA


def place():
    me = lax.axis_index("wide")
    return me // 4, (me // 2) % 2, me % 2


def wide_id(z, y, x):
    return {"wide": z * 4 + y * 2 + x}


def shard_rows(z, y, x, R):
    return pl.ds(pl.multiple_of((z * 4 + y * 2 + x) * R, R), R)


def remote(src, dst, send, recv, target):
    return pltpu.make_async_remote_copy(src_ref=src, dst_ref=dst, send_sem=send, recv_sem=recv, device_id=target, device_id_type=MESH)


def greet(G, far, pair=0):
    z, y, x = place()
    bar = pltpu.get_barrier_semaphore()
    sig = lambda t: pl.semaphore_signal(bar, inc=1, device_id=t, device_id_type=MESH)
    sig(wide_id(z, 1 - y, x))
    sig(wide_id(z, y, 1 - x))
    if pair:
        sig({"narrow": 1 - lax.axis_index("narrow")})
    if far:
        for k in range(1, G):
            sig(wide_id((z + k) % G, y, x))
        pl.semaphore_wait(bar, 2 + pair + G - 1)
    else:
        @pl.when(z > 0)
        def _():
            sig(wide_id(z - 1, y, x))

        @pl.when(z < G - 1)
        def _():
            sig(wide_id(z + 1, y, x))

        pl.semaphore_wait(bar, 2 + pair + (z > 0).astype(jnp.int32) + (z < G - 1).astype(jnp.int32))


class Gather:
    def __init__(self, G, halves, srcs, outs, local_sem, zs, zr, ns, nr):
        self.G, self.halves, self.srcs, self.local_sem = G, halves, srcs, local_sem
        self.outs = [o if isinstance(o, tuple) else (o, 0, 0) for o in outs]
        self.widths = [sum(w for h in halves for a, _, w in h if a == k) for k in range(len(srcs))]
        self.zs, self.zr, self.ns, self.nr = zs, zr, ns, nr
        self.most = max(len(h) for h in halves)
        self.z, self.y, self.x = place()
        self.R = srcs[0].shape[0]

    def hop(self, own, zz, yy, xx, h, way, j):
        target = wide_id(self.z, 1 - self.y, self.x) if way == "y" else wide_id(self.z, self.y, 1 - self.x)
        copies = []
        for n, (a, c, w) in enumerate(self.halves[h]):
            slot = (zz * 6 + j) * self.most + n
            out, first, at = self.outs[a]
            dst = out.at[shard_rows(zz, yy, xx, self.R), pl.ds(first + c, w)]
            copies.append(remote(self.srcs[a].at[:, pl.ds(at + c, w)] if own else dst, dst, self.ns.at[slot], self.nr.at[slot], target))
        return copies

    def second_stage(self, zz, own=False):
        return self.hop(own, zz, self.y, self.x, 0, "y", 0) + self.hop(own, zz, self.y, self.x, 1, "x", 1)

    def third_stage(self, zz, own=False):
        return self.hop(own, zz, self.y, self.x, 0, "x", 2) + self.hop(own, zz, self.y, self.x, 1, "y", 3)

    def last_stage(self, zz):
        return self.hop(False, zz, 1 - self.y, self.x, 0, "x", 4) + self.hop(False, zz, self.y, 1 - self.x, 1, "y", 5)

    def relay(self, own, zz, step, way):
        copies = []
        for a in range(len(self.srcs)):
            slot = (way * (self.G - 1) + step) * len(self.srcs) + a
            dst = self.whole(a, zz)
            copies.append(remote(self.own(a) if own else dst, dst, self.zs.at[slot], self.zr.at[slot],
                                 wide_id(self.z + (1 if way == 0 else -1), self.y, self.x)))
        return copies

    def whole(self, a, zz):
        out, first, _ = self.outs[a]
        return out.at[shard_rows(zz, self.y, self.x, self.R), pl.ds(first, self.widths[a])]

    def own(self, a):
        return self.srcs[a].at[:, pl.ds(self.outs[a][2], self.widths[a])]

    def can(self, way):
        return self.z < self.G - 1 if way == 0 else self.z > 0

    def source(self, d, way):
        return (self.z - d, self.z - d >= 0) if way == 0 else (self.z + d, self.z + d < self.G)

    def keep(self):
        return [pltpu.make_async_copy(self.own(a), self.whole(a, self.z), self.local_sem.at[a]) for a in range(len(self.srcs))]

    def begin(self):
        for way in range(2):
            @pl.when(self.can(way))
            def _():
                for c in self.relay(True, self.z, 0, way):
                    c.start()
        for c in self.second_stage(self.z, True) + self.third_stage(self.z, True) + self.keep():
            c.start()

    def turn(self, zz):
        for c in self.hop(False, zz, 1 - self.y, self.x, 0, "y", 0) + self.hop(False, zz, self.y, 1 - self.x, 1, "x", 1):
            c.wait_recv()
        for c in self.last_stage(zz):
            c.start()

    def step(self, d):
        for way in range(2):
            zz, there = self.source(d, way)

            @pl.when(there)
            def _():
                for c in self.relay(False, zz, d - 1, way):
                    c.wait_recv()

                @pl.when(self.can(way))
                def _():
                    for c in self.relay(False, zz, d, way):
                        c.start()

                for c in self.second_stage(zz):
                    c.start()
        for way in range(2):
            zz, there = self.source(d, way)

            @pl.when(there)
            def _():
                for c in self.third_stage(zz):
                    c.start()

    def turns(self, d):
        if d == 0:
            self.turn(self.z)
            return
        for way in range(2):
            zz, there = self.source(d, way)

            @pl.when(there)
            def _():
                self.turn(zz)

    def finish(self):
        y, x = self.y, self.x

        @pl.loop(0, self.G)
        def _(zz):
            for c in (self.hop(False, zz, y, 1 - x, 0, "x", 2) + self.hop(False, zz, 1 - y, x, 1, "y", 3)
                      + self.hop(False, zz, 1 - y, 1 - x, 0, "x", 4) + self.hop(False, zz, 1 - y, 1 - x, 1, "y", 5)):
                c.wait_recv()
            for c in self.second_stage(zz) + self.third_stage(zz) + self.last_stage(zz):
                c.wait_send()

        for way in range(2):
            @pl.when(self.can(way))
            def _():
                for c in self.relay(True, self.z, 0, way):
                    c.wait_send()
                for d in range(1, self.G - 1):
                    zz, there = self.source(d, way)

                    @pl.when(there)
                    def _():
                        for c in self.relay(False, zz, d, way):
                            c.wait_send()
        for c in self.keep():
            c.wait()

    def events(self):
        G = self.G
        first = lambda: (greet(G, False), self.begin())
        ev = [(0.0, first), (0.7, lambda: self.turns(0))]
        for d in range(1, G):
            ev += [(1.15 * d, functools.partial(self.step, d)), (1.3 * d + 1.2, functools.partial(self.turns, d))]
        return sorted(ev, key=lambda e: e[0]), self.finish


def gather_scratch(G, halves, arrays):
    most = max(len(h) for h in halves)
    return [D((arrays,)), D((2 * (G - 1) * arrays,)), D((2 * (G - 1) * arrays,)), D((6 * G * most,)), D((6 * G * most,))]


class Scatter:
    def __init__(self, G, halves, parts, outs, r1a, r1b, o1a, o1b, r2a, r2b, r3, own, lsem, s1, v1, s2, v2, s3, v3):
        self.__dict__.update(locals())
        self.most = max(len(h) for h in halves)
        self.wa, self.wb = [sum(p[2] for p in h) for h in halves]
        self.R = parts[0].shape[0] // (4 * G)
        self.z, self.y, self.x = place()
        self.order = sorted(range(1, G), key=lambda k: min(k, G - k), reverse=True) + [0]

    def zk(self, k):
        return (self.z + k) % self.G

    def neighbour(self, way):
        return wide_id(self.z, 1 - self.y, self.x) if way == "y" else wide_id(self.z, self.y, 1 - self.x)

    def pieces(self, h):
        at, out = 0, []
        for n, (a, c, w) in enumerate(self.halves[h]):
            out.append((n, a, pl.ds(c, w), pl.ds(at, w)))
            at += w
        return out

    def sources(self, k, mine):
        z, y, x = self.zk(k), self.y, self.x
        for h in range(2):
            for n, a, src, dst in self.pieces(h):
                for j in range(2):
                    if h == 0:
                        rows = shard_rows(z, j, x if mine else 1 - x, self.R)
                    else:
                        rows = shard_rows(z, y if mine else 1 - y, j, self.R)
                    yield h, j, dst, ((2 * k + h) * self.most + n) * 2 + j, self.parts[a].at[rows, src]

    def one(self, k):
        return [remote(src, (self.r1a, self.r1b)[h].at[k, j, :, dst], self.s1.at[slot], self.v1.at[slot], self.neighbour("xy"[h]))
                for h, j, dst, slot, src in self.sources(k, False)]

    def load(self, k):
        return [pltpu.make_async_copy(src, (self.o1a, self.o1b)[h].at[k, j, :, dst], self.lsem.at[slot]) for h, j, dst, slot, src in self.sources(k, True)]

    def two(self, k):
        return [remote(self.o1a.at[k, 1 - self.y], self.r2a.at[k], self.s2.at[2 * k], self.v2.at[2 * k], self.neighbour("y")),
                remote(self.o1b.at[k, 1 - self.x], self.r2b.at[k], self.s2.at[2 * k + 1], self.v2.at[2 * k + 1], self.neighbour("x"))]

    def three(self, k):
        return remote(self.own.at[k], self.r3.at[k - 1], self.s3.at[k - 1], self.v3.at[k - 1], wide_id(self.zk(k), self.y, self.x))

    def launch(self, k):
        for c in self.one(k) + self.load(k):
            c.start()

    def begin(self):
        for k in self.order[:2]:
            self.launch(k)

    def rows(self, count, body):
        step = min(16, count)

        @pl.loop(0, count // step)
        def _(i):
            body(pl.ds(pl.multiple_of(i * step, step), step))

    def add_one(self, n):
        k = self.order[n]
        for c in self.one(k):
            c.wait_recv()
        for c in self.load(k):
            c.wait()
        for mine, got in ((self.o1a, self.r1a), (self.o1b, self.r1b)):
            def body(r):
                for j in range(2):
                    mine[k, j, r, :] = (mine[k, j, r, :].astype(f32) + got[k, j, r, :].astype(f32)).astype(bf16)

            self.rows(self.R, body)
        for c in self.two(k):
            c.start()
        if n + 2 < self.G:
            self.launch(self.order[n + 2])

    def add_two(self, n):
        k = self.order[n]
        for c in self.two(k):
            c.wait_recv()

        def body(r):
            self.own[k, r, pl.ds(0, self.wa)] = (self.o1a[k, self.y, r, :].astype(f32) + self.r2a[k, r, :].astype(f32)).astype(bf16)
            self.own[k, r, pl.ds(self.wa, self.wb)] = (self.o1b[k, self.x, r, :].astype(f32) + self.r2b[k, r, :].astype(f32)).astype(bf16)

        self.rows(self.R, body)
        if k:
            self.three(k).start()

    def arrived(self):
        for k in range(1, self.G):
            self.three(k).wait_recv()

    def write_out(self):
        def body(r):
            for h in range(2):
                for _, a, src, dst in self.pieces(h):
                    cols = pl.ds(dst.start + h * self.wa, dst.size)
                    total = self.own[0, r, cols].astype(f32)
                    for k in range(self.G - 1):
                        total = total + self.r3[k, r, cols].astype(f32)
                    self.outs[a][r, src] = total

        self.rows(self.R, body)

    def all_sent(self):
        for k in range(self.G):
            for c in self.one(k) + self.two(k):
                c.wait_send()
            if k:
                self.three(k).wait_send()

    def ending(self):
        return [lambda: self.add_two(self.G - 1), self.arrived, self.write_out, self.all_sent, lambda: None]

    def finish(self):
        for act in self.ending():
            act()

    def events(self, pair=0):
        G = self.G
        first = lambda: (greet(G, True, pair), self.begin())
        ev = [(0.0, first), (1.1, lambda: self.add_one(0))]
        for n in range(1, G):
            ev += [(1.5 * n + 0.65, functools.partial(self.add_one, n)), (1.5 * n + 1.1, functools.partial(self.add_two, n - 1))]
        return sorted(ev, key=lambda e: e[0]), self.finish


def scatter_scratch(G, halves, R):
    most = max(len(h) for h in halves)
    a, b = [sum(p[2] for p in h) for h in halves]
    V = lambda *s: pltpu.VMEM(s, bf16)
    return [V(G, 2, R, a), V(G, 2, R, b), V(G, 2, R, a), V(G, 2, R, b), V(G, R, a), V(G, R, b), V(G - 1, R, a + b), V(G, R, a + b),
            D((4 * G * most,)), D((4 * G * most,)), D((4 * G * most,)), D((2 * G,)), D((2 * G,)), D((G - 1,)), D((G - 1,))]


def beside(plan, G, steps, now, compute, late=(), early=()):
    events, finish = plan
    units = 1.55 * G
    if early:
        @pl.when(now == 0)
        def _():
            for act in early:
                act()
    for n in range(steps):
        here = [act for t, act in events if min(steps - 1, int(-(-t * steps // units))) == n]
        if here:
            @pl.when(now == n)
            def _():
                for act in here:
                    act()
    compute()

    @pl.when(now == steps - 1)
    def _():
        for act in late:
            act()
        finish()


ANY = pl.BlockSpec(memory_space=pl.ANY)


def whole_vmem():
    return pl.BlockSpec(memory_space=pltpu.VMEM)


def gathered_shapes(shards, wide):
    return tuple(jax.ShapeDtypeStruct((wide * rows, columns), bf16) for rows, columns in shards)


def sum_everywhere(G, out, acc, got, gz, s, v, sz, vz):
    z, y, x = place()
    targets = [{"narrow": 1 - lax.axis_index("narrow")}, wide_id(z, y, 1 - x), wide_id(z, 1 - y, x)]
    near = lambda n: remote(acc.at[n], got.at[n], s.at[n], v.at[n], targets[n])
    far = lambda k, zz: remote(acc.at[3], gz.at[zz], sz.at[k - 1], vz.at[zz], wide_id((z + k) % G, y, x))

    def take(n):
        near(n).wait()
        acc[n + 1] = acc[n] + got[n]

    def next_near(n):
        if n:
            take(n - 1)
        near(n).start()

    def spread_far():
        take(2)
        gz[z] = acc[3]
        for k in range(1, G):
            far(k, z).start()

    def total():
        for k in range(1, G):
            far(k, (z + k) % G).wait_recv()
        for k in range(1, G):
            far(k, z).wait_send()
        value = gz[0]
        for k in range(1, G):
            value = value + gz[k]
        out[...] = value

    return [functools.partial(next_near, n) for n in range(3)] + [spread_far, total]


def sum_scratch(G, rows):
    V = lambda k: pltpu.VMEM((k, rows, 128), f32)
    return [V(4), V(3), V(G), D((3,)), D((3,)), D((G - 1,)), D((G,))]


def nt(a, b):
    return lax.dot_general(a, b, NT, preferred_element_type=f32)


def nn(a, b):
    return jnp.dot(a, b, preferred_element_type=f32)


def gelu_and_slope(v):
    root = 0.7978845608028654
    square = v * v
    t = jnp.tanh(root * v * (1.0 + 0.044715 * square))
    half = 0.5 * (1.0 + t)
    return v * half, half + 0.5 * v * (1.0 - t * t) * root * (1.0 + 3 * 0.044715 * square)


def mid_kernel(G, cut, att_h, tok_h, cot_h, wo_h, wg_h, wu_h, wd_h, wd_shard, gain_ref,
               gout_h, gg_h, gu_h, gd_h, y_ref, gh_ref, ga_ref, ggain_ref, sd_ref,
               att, tok, cot, wo, wg, wu, wd, part, other, back, hid, n2t, cott, hff, gg, gu, ysend, yown, yother, stage,
               isem, osem, sp, vp, sb, vb, sy, vy, *sems):
    core = lax.axis_index("narrow")
    peer = {"narrow": 1 - core}
    n, d = tok.shape
    ff = wg.shape[1]
    tiles = n // TILE
    half = tiles // 2
    loads = [pltpu.make_async_copy(s, t, isem.at[k]) for k, (s, t) in enumerate(
        [(att_h, att), (wo_h, wo), (tok_h, tok), (wg_h, wg), (wu_h, wu), (cot_h, cot), (wd_h, wd.at[:, pl.ds(0, cut)])])]
    for c in loads:
        c.start()
    part_cols = sd_ref.shape[1]
    mid = cut + (ff - cut) // 256 * 128
    bring = Gather(G, (((0, 0, mid - cut),), ((0, mid - cut, ff - mid),)), [wd_shard], [(wd, cut, cut)], *sems[:5])
    give = Scatter(G, (((0, 0, part_cols // 2),), ((0, part_cols // 2, part_cols // 2),)), [gd_h], [sd_ref], *sems[5:])
    greet(G, True, 1)
    bring.begin()
    rows_of = lambda t: pl.ds(pl.multiple_of(t * TILE, TILE), TILE)
    send_part = lambda t: remote(part.at[rows_of(t)], other.at[rows_of(t)], sp.at[t], vp.at[t], peer)
    send_back = lambda t: remote(part.at[rows_of(t)], back.at[rows_of(t)], sb.at[t], vb.at[t], peer)
    send_y = lambda j: remote(ysend.at[rows_of(j)], yother.at[rows_of(j)], sy.at[j], vy.at[j], peer)
    gain = gain_ref[1:2, :].astype(f32)

    for c in loads[:2]:
        c.wait()

    def at_step(s, plan):
        for k, acts in plan.items():
            @pl.when(s == k)
            def _():
                for act in acts:
                    act()

    turns = [functools.partial(bring.turns, k) for k in range(G)]
    steps = [functools.partial(bring.step, k) for k in range(1, G)]

    @pl.loop(0, tiles)
    def _(t):
        part[rows_of(t), :] = nt(att[rows_of(t), :], wo[...]).astype(bf16)
        send_part(t).start()
        at_step(t, {1: turns[:1], 2: steps[:1]})

    for c in loads[2:]:
        c.wait()

    chunks, at = [], 0
    while at < ff:
        w = min(384, ff - at)
        chunks.append((at, w))
        at += w

    later = [act for pair in zip(turns[1:], steps[1:] + [lambda: None]) for act in pair]

    @pl.loop(0, tiles)
    def _(s):
        t = (s + half * (1 - core)) % tiles
        r = rows_of(t)
        send_part(t).wait()
        h = tok[r, :].astype(f32) + (part[r, :].astype(f32) + other[r, :].astype(f32))
        hid[r, :] = h
        factor = lax.rsqrt(jnp.mean(h * h, axis=1, keepdims=True) + epsilon)
        low = (h * factor * gain).astype(bf16)
        n2t[:, r] = low.T
        cott[:, r] = cot[r, :].T
        for at, w in chunks:
            cols = pl.ds(at, w)
            act, slope = gelu_and_slope(nn(low, wg[:, cols]))
            up = nn(low, wu[:, cols])
            hff[r, cols] = (act * up).astype(bf16)
            gg[r, cols] = (up * slope).astype(bf16)
            gu[r, cols] = act.astype(bf16)
        at_step(s, {1: later[:2], 2: later[2:4], 3: later[4:]})

    def weight_grad(left, right, out, slot, width):
        rows = stage.shape[1]
        block = lambda k: pl.ds(k * rows, rows)
        copy = lambda k: pltpu.make_async_copy(stage.at[k % 2, :, pl.ds(0, width)], out.at[block(k)], osem.at[2 * slot + k % 2])
        count = d // rows
        for k in range(count):
            if k >= 2:
                copy(k - 2).wait()
            stage[k % 2, :, pl.ds(0, width)] = nn(left[block(k), :], right[...]).astype(bf16)
            copy(k).start()
        return [copy(k) for k in range(max(0, count - 2), count)]

    for c in weight_grad(cott, hff, gd_h, 0, ff):
        c.wait()
    give.begin()
    bring.finish()
    ones = [functools.partial(give.add_one, k) for k in range(G)]
    twos = [functools.partial(give.add_two, k) for k in range(G - 1)]

    @pl.loop(0, tiles)
    def _(s):
        t = (s + half * (1 - core)) % tiles
        r = rows_of(t)
        ct = cot[r, :]
        for at, w in chunks:
            cols = pl.ds(at, w)
            gf = nn(ct, wd[:, cols])
            gg[r, cols] = (gf * gg[r, cols].astype(f32)).astype(bf16)
            gu[r, cols] = (gf * gu[r, cols].astype(f32)).astype(bf16)
        part[r, :] = (nt(gg[r, :], wg[...]) + nt(gu[r, :], wu[...])).astype(bf16)
        send_back(t).start()
        y = nt(hff[r, :], wd[...]).astype(bf16)

        @pl.when(s < half)
        def _():
            ysend[rows_of(s), :] = y
            send_y(s).start()

        @pl.when(s >= half)
        def _():
            yown[rows_of(s - half), :] = y

        at_step(s, {0: ones[:1], 1: ones[1:2], 2: twos[:1] + ones[2:3], 3: twos[1:2]})

    ggain_ref[...] = jnp.zeros_like(ggain_ref)

    @pl.loop(0, tiles)
    def _(s):
        t = (s + half * (1 - core)) % tiles
        r = rows_of(t)
        send_back(t).wait()
        total = part[r, :].astype(f32) + back[r, :].astype(f32)
        h = hid[r, :]
        factor = lax.rsqrt(jnp.mean(h * h, axis=1, keepdims=True) + epsilon)
        unit = h * factor
        g = gain * total
        gh = cot[r, :].astype(f32) + factor * (g - unit * jnp.mean(g * unit, axis=1, keepdims=True))
        low = gh.astype(bf16)
        cott[:, r] = low.T
        ga_ref[r, :] = nn(low, wo[...]).astype(bf16)

        @pl.when(s >= half)
        def _():
            j = rows_of(s - half)
            gh_ref[j, :] = gh
            ggain_ref[...] += jnp.sum(total * unit, axis=0, keepdims=True)
            send_y(s - half).wait()
            y_ref[j, :] = (h + (yown[j, :].astype(f32) + yother[j, :].astype(f32))).astype(bf16)

        at_step(s, {0: ones[3:4], 3: twos[2:3]})

    for act in [act for pair in zip(ones[4:], twos[3:]) for act in pair]:
        act()
    for left, right, out, slot in ((n2t, gg, gg_h, 1), (n2t, gu, gu_h, 2), (cott, att, gout_h, 3)):
        for c in weight_grad(left, right, out, slot, right.shape[1]):
            c.wait()
    give.finish()


def middle(att, tok, cot, wo, wg, wu, wd, wd_shard, gain, here, wide, cid):
    n, d = tok.shape
    units, ff, G, cut = att.shape[1], wg.shape[1], wide // 4, wd.shape[1]
    B = lambda *s: pltpu.VMEM(s, bf16)
    sds = jax.ShapeDtypeStruct
    tiles = n // TILE
    halves = (((0, 0, cut),), ((0, cut, ff - cut),))
    return pl.pallas_call(functools.partial(mid_kernel, G, cut),
        out_shape=(sds((d, units), bf16), sds((d, ff), bf16), sds((d, ff), bf16), sds((d, ff), bf16),
                   sds((n // 2, d), bf16), sds((n // 2, d), f32), sds((n, units), bf16), sds((1, d), f32), sds((d // wide, here), f32)),
        in_specs=[ANY] * 8 + [whole_vmem()], out_specs=(ANY,) * 4 + (whole_vmem(),) * 5,
        scratch_shapes=[B(n, units), B(n, d), B(n, d), B(d, units), B(d, ff), B(d, ff), B(d, ff), B(n, d), B(n, d), B(n, d),
                        pltpu.VMEM((n, d), f32), B(d, n), B(d, n), B(n, ff), B(n, ff), B(n, ff),
                        B(n // 2, d), B(n // 2, d), B(n // 2, d), B(2, 512, ff),
                        D((7,)), D((8,)), D((tiles,)), D((tiles,)), D((tiles,)), D((tiles,)), D((tiles // 2,)), D((tiles // 2,))]
        + gather_scratch(G, halves, 1) + scatter_scratch(G, (((0, 0, here // 2),), ((0, here // 2, here // 2),)), d // wide),
        compiler_params=params(cid), name="feed_forward")(att, tok, cot, wo, wg, wu, wd, wd_shard, gain)


def local(tokens, cotangent, pages, boxes, gain_attn, gain_ffn, bias_tables, w_query, w_key, w_value, w_out, w_gate, w_up, w_down):
    wide, narrow = lax.axis_size("wide"), lax.axis_size("narrow")
    heads = bias_tables.shape[1] // narrow
    inner, ff, d = w_query.shape[1], w_gate.shape[1], tokens.shape[1]
    gains = jnp.stack([gain_attn, gain_ffn])

    all_tokens = lax.all_gather(tokens, "narrow", axis=0, tiled=True)
    all_cot = lax.all_gather(cotangent, "narrow", axis=0, tiled=True)
    early = inner // 4 * 3
    bias, ids, (w_first, full_out, full_gate) = bias_and_gather(
        bias_tables.T, heads, boxes, pages, [w_query, w_key, w_value, w_out.T, w_gate], ((0, 0), (0, inner), (0, 2 * inner), (1, 0), (2, 0)),
        (((4, 0, ff), (0, 0, early)), ((3, 0, inner), (0, early, inner - early), (1, 0, inner), (2, 0, inner))), wide, 1)
    down_shard = w_down.T
    cut = (ff // 128 + 1) // 2 * 128
    (attended, lse, normed, qkv), (full_up, most_down) = attn_fwd_and_gather(
        all_tokens, gains, w_first, bias, [w_up, down_shard], (ff, cut),
        (((0, 0, cut), (1, 0, cut - 384)), ((0, cut, ff - cut), (1, cut - 384, 384))), wide, 2)
    here = 2 * inner
    grad_w_out, grad_w_gate, grad_w_up, grad_w_down, output, grad_hidden, grad_attended, grad_gain_two, s_down = middle(
        attended, all_tokens, all_cot, full_out, full_gate, full_up, most_down, down_shard, gains, here, wide, 3)
    even = (ff + inner + ff - here) // 2
    (g, band, far, grad_w_first, grad_normed), (s_gate, s_out, more_down) = attn_bwd_and_scatter(
        qkv, bias, attended, grad_attended, lse, normed, w_first, [grad_w_gate, grad_w_out, grad_w_down],
        (((0, 0, even),), ((0, even, ff - even), (1, 0, inner), (2, here, ff - here))), wide, 4)
    s_down = jnp.concatenate([s_down, more_down[:, here:]], axis=1)
    small, grad_tokens, (s_up, s_first) = hist_and_scatter(
        g, band, far, ids, grad_normed, tokens, grad_hidden, gains, grad_gain_two, [grad_w_up, grad_w_first],
        (((0, 0, ff),), ((1, 0, 3 * inner),)), wide, 5)
    s_query, s_key, s_value = jnp.split(s_first, 3, axis=1)
    lines = d // 128
    one, two = small[:lines].reshape(d), small[lines:2 * lines].reshape(d)
    table = small[2 * lines:, :bias_tables.shape[0]].T
    return (output, grad_tokens, one, two, table, s_query, s_key, s_value, s_out.T, s_gate, s_up, s_down.T)


def solution(mesh):
    rows, cols, tall = P(("wide", "narrow"), None), P("wide", "narrow"), P("narrow", "wide")
    in_specs = (rows, rows, P("wide"), P(None, "wide"), P(), P(), P(), cols, cols, cols, tall, cols, cols, tall)
    out_specs = (rows, rows, P(), P(), P(), cols, cols, cols, tall, cols, cols, tall)
    return jax.shard_map(local, mesh=mesh, in_specs=in_specs, out_specs=out_specs, check_vma=False)
```

```python
import functools

import jax
import jax.numpy as jnp
from jax import lax
from jax.experimental import pallas as pl
from jax.experimental.pallas import tpu as pltpu
from jax.sharding import PartitionSpec as P

f32, bf16 = jnp.float32, jnp.bfloat16
MESH = pl.DeviceIdType.MESH


EDGES = (1, 2, 3, 4, 5, 6, 7, 8, 12, 16, 23, 32, 46, 64, 91)
NT = (((1,), (1,)), ((), ()))
VM = 58 * 2**20
TABLE_SCALE = 2047.0
TABLE_LIFT = 8192
TILE = 256
epsilon = 1e-06


def params(cid):
    return pltpu.CompilerParams(collective_id=cid, has_side_effects=True, vmem_limit_bytes=VM)


def lane_take(table, idx):
    return jnp.take_along_axis(table, idx, axis=1, mode="promise_in_bounds")


def buckets_of(gap, shift):
    size = jnp.minimum(jnp.abs(gap) >> shift, EDGES[-1])
    return jnp.where(size < 8, size, 33 - lax.clz(size * size)) + jnp.where(gap > 0, 16, 0)


def bias_tile(start, heads, rows, n, tab_ref, box_row, page_row, bias_ref, ids_ref, lin_ids, lin, words_ref):
    lane = lax.broadcasted_iota(jnp.int32, (rows, 128), 1)
    down = lax.broadcasted_iota(jnp.int32, (rows, 128), 0)
    pairs = heads // 2

    def column(row_ref, t):
        values = jnp.broadcast_to(row_ref[t:t + 1, pl.ds(pl.multiple_of(start // 128 * 128, 128), 128)], (rows, 128)).astype(f32)
        return jnp.broadcast_to(jnp.sum(jnp.where(lane == down + start % 128, values, 0.0), axis=1, keepdims=True), (rows, 128)).astype(jnp.int32)

    allowed_col = column(page_row, 0) % 2
    cols = [column(box_row, t) for t in range(2)]

    @pl.when(start == 0)
    def _():
        first = lax.axis_index("narrow") * heads
        row = lax.broadcasted_iota(jnp.int32, (heads, tab_ref.shape[0]), 0)
        wanted = first + jnp.where(row < pairs, 2 * row, 2 * (row - pairs) + 1)
        pick = jnp.where(lax.broadcasted_iota(jnp.int32, row.shape, 1) == wanted, 1.0, 0.0).astype(bf16)
        picked = jnp.dot(pick, tab_ref[...], preferred_element_type=f32)
        fixed = jnp.round(picked * TABLE_SCALE).astype(jnp.int32)
        words_ref[...] = jnp.zeros_like(words_ref)
        words_ref[0:pairs, 0:picked.shape[1]] = fixed[0:pairs] * 65536 + fixed[pairs:heads] + TABLE_LIFT

        @pl.loop(0, 8)
        def _(k):
            ids = buckets_of(lane - down + (k - 4) * rows, 0)
            lin_ids[k] = ids.astype(f32)
            for p in range(pairs):
                lin[k, p] = lane_take(jnp.broadcast_to(words_ref[p:p + 1, :], (rows, 128)), ids)

    unit = 1.0 / TABLE_SCALE
    tables = [jnp.broadcast_to(words_ref[p:p + 1, :], (rows, 128)) for p in range(pairs)]

    @pl.loop(0, n // 128)
    def _(c):
        lanes = pl.ds(pl.multiple_of(c * 128, 128), 128)
        near = jnp.clip((c * 128 - start) // rows + 4, 0, 7)
        ids = []
        for t in range(2):
            ids.append(buckets_of(jnp.broadcast_to(box_row[t:t + 1, lanes], (rows, 128)) - cols[t], 2))
            ids_ref[t, :, lanes] = ids[t].astype(f32)
        ok = jnp.broadcast_to(page_row[:, lanes], (rows, 128)) == allowed_col
        for p in range(pairs):
            words = lin[near, p] + lane_take(tables[p], ids[0] + 32) + lane_take(tables[p], ids[1] + 64)
            upper = (words >> 16).astype(f32) * unit
            lower = (words & 0xFFFF).astype(f32) * unit - 3 * TABLE_LIFT * unit
            bias_ref[2 * p, :, lanes] = jnp.where(ok, upper, -1e30)
            bias_ref[2 * p + 1, :, lanes] = jnp.where(ok, lower, -1e30)


def bias_gather_kernel(heads, rows, n, G, halves, count, into, *refs):
    ins, srcs = refs[:3], refs[3:3 + count]
    bias_ref, ids_ref, lin_ids = refs[3 + count:6 + count]
    kinds = len(set(k for k, _ in into))
    outs, scratch, sems = refs[6 + count:6 + count + kinds], refs[6 + count + kinds:8 + count + kinds], refs[8 + count + kinds:]
    now = pl.program_id(0)
    comm = Gather(G, halves, srcs, [(outs[k], c, 0) for k, c in into], *sems)
    beside(comm.events(), G, n // rows, now, lambda: bias_tile(now * rows, heads, rows, n, *ins, bias_ref, ids_ref, lin_ids, *scratch))


def bias_and_gather(tables, heads, boxes, pages, shards, into, halves, wide, cid):
    n, G, rows = pages.shape[0], wide // 4, 64
    count = len(shards)
    widths = [sum(a.shape[1] for a, (j, _) in zip(shards, into) if j == k) for k in sorted(set(k for k, _ in into))]
    outs = pl.pallas_call(functools.partial(bias_gather_kernel, heads, rows, n, G, halves, count, into),
        grid=(n // rows,),
        out_shape=(jax.ShapeDtypeStruct((heads, n, n), f32), jax.ShapeDtypeStruct((2, n, n), f32), jax.ShapeDtypeStruct((8, rows, 128), f32)) + gathered_shapes([(shards[0].shape[0], w) for w in widths], wide),
        in_specs=[pl.BlockSpec(tables.shape, lambda i: (0, 0)), pl.BlockSpec((2, n), lambda i: (0, 0)), pl.BlockSpec((1, n), lambda i: (0, 0))] + [ANY] * count,
        out_specs=(pl.BlockSpec((heads, rows, n), lambda i: (0, i, 0)), pl.BlockSpec((2, rows, n), lambda i: (0, i, 0)),
                   pl.BlockSpec((8, rows, 128), lambda i: (0, 0, 0))) + (ANY,) * len(widths),
        scratch_shapes=[pltpu.VMEM((8, heads // 2, rows, 128), jnp.int32), pltpu.VMEM((8, 128), jnp.int32)] + gather_scratch(G, halves, count),
        compiler_params=params(cid), name="layout_bias_gather")(
            tables, boxes, pages[None], *shards)
    return outs[0], outs[1:3], outs[3:]


def half_of(v, e):
    lane = lax.broadcasted_iota(jnp.int32, v.shape, 1)
    return jnp.where((lane >= 64) == (e == 1), v, jnp.zeros_like(v))


def join(a, b):
    lane = lax.broadcasted_iota(jnp.int32, a.shape, 1)
    return jnp.where(lane < 64, a, b)


def project(tok_ref, gain_ref, w_ref, normed, qkv, between):
    gain = gain_ref[0:1, :].astype(f32)

    @pl.loop(0, tok_ref.shape[0] // TILE)
    def _(t):
        r = pl.ds(pl.multiple_of(t * TILE, TILE), TILE)
        x = tok_ref[r, :].astype(f32)
        low = (x * lax.rsqrt(jnp.mean(x * x, axis=1, keepdims=True) + epsilon) * gain).astype(bf16)
        normed[r, :] = low
        qkv[r, :] = jnp.dot(low, w_ref[...], preferred_element_type=f32).astype(bf16)
        for k, act in between:
            pl.when(t == k)(act)


def fwd_tile(p, i, tq, pairs, qkv, bias_ref, o_ref, lse_ref):
    cols = lambda k: pl.ds(pl.multiple_of((p + k * pairs) * 128, 128), 128)
    q, k, v = qkv[pl.ds(pl.multiple_of(i * tq, tq), tq), cols(0)], qkv[:, cols(1)], qkv[:, cols(2)]
    outs, lses = [], []
    for e in range(2):
        s = lax.dot_general(half_of(q, e), k, NT, preferred_element_type=f32) + bias_ref[e]
        peak = jnp.max(s, axis=1, keepdims=True)
        w = jnp.exp(s - peak)
        total = jnp.sum(w, axis=1, keepdims=True)
        outs.append(jnp.dot(w.astype(bf16), v, preferred_element_type=f32) / total)
        lses.append(peak + jnp.log(total))
    o_ref[...] = join(*outs).astype(bf16)
    lse_ref[0] = jnp.concatenate(lses, axis=1)


def fwd_kernel(pairs, tiles, G, halves, count, *refs):
    (tok, gain, w, bias_ref), srcs = refs[:4], refs[4:4 + count]
    o_ref, lse_ref, normed_h, qkv_h = refs[4 + count:8 + count]
    outs, (tok_s, w_s, normed, qkv, keep, load), sems = refs[8 + count:8 + 2 * count], refs[8 + 2 * count:14 + 2 * count], refs[14 + 2 * count:]
    p, i = pl.program_id(0), pl.program_id(1)
    now, steps = p * tiles + i, pairs * tiles
    copies = lambda: [pltpu.make_async_copy(normed, normed_h, keep.at[0]), pltpu.make_async_copy(qkv, qkv_h, keep.at[1])]

    events, finish = Gather(G, halves, srcs, outs, *sems).events()
    loads = lambda: [pltpu.make_async_copy(tok, tok_s, load.at[0]), pltpu.make_async_copy(w, w_s, load.at[1])]

    def compute():
        @pl.when(now == 0)
        def _():
            for c in loads():
                c.wait()
            project(tok_s, gain, w_s, normed, qkv, [(1, events[1][1]), (3, events[2][1])])
            for c in copies():
                c.start()

        fwd_tile(p, i, o_ref.shape[0], pairs, qkv, bias_ref, o_ref, lse_ref)

        @pl.when(now == steps - 1)
        def _():
            for c in copies():
                c.wait()

    beside((events[:1] + events[3:], finish), G, steps, now, compute, early=[lambda: [c.start() for c in loads()]], pace=0.36, lead=1.7)


def attn_fwd_and_gather(tok, gain, w, bias, shards, widths, halves, wide, cid, tq=256):
    n, d = tok.shape
    width = w.shape[1] // 3
    pairs, tiles, count, G = width // 128, n // tq, len(shards), wide // 4
    sds = jax.ShapeDtypeStruct
    const = lambda s: pl.BlockSpec(s, lambda p, i: (0, 0))
    outs = pl.pallas_call(functools.partial(fwd_kernel, pairs, tiles, G, halves, count), grid=(pairs, tiles),
        out_shape=(sds((n, width), bf16), sds((pairs, n, 2), f32), sds((n, d), bf16), sds((n, 3 * width), bf16)) + gathered_shapes([(shards[0].shape[0], c) for c in widths], wide),
        in_specs=[ANY, const(gain.shape), ANY, pl.BlockSpec((2, tq, n), lambda p, i: (p, i, 0))] + [ANY] * count,
        out_specs=(pl.BlockSpec((tq, 128), lambda p, i: (i, p)), pl.BlockSpec((1, tq, 2), lambda p, i: (p, i, 0)), ANY, ANY) + (ANY,) * count,
        scratch_shapes=[pltpu.VMEM((n, d), bf16), pltpu.VMEM(w.shape, bf16), pltpu.VMEM((n, d), bf16), pltpu.VMEM((n, 3 * width), bf16), D((2,)), D((2,))] + gather_scratch(G, halves, count),
        compiler_params=params(cid), name="attention_gather")(tok, gain, w, bias, *shards)
    return outs[:4], outs[4:]


def band_sums(i, e, g_ref, band_ref, far_ref):
    tq, n = g_ref.shape[1], g_ref.shape[2]
    first = i * (tq // 128) - 1

    @pl.when(i == 0)
    def _():
        band_ref[e] = jnp.zeros(band_ref.shape[1:], f32)
        far_ref[e] = jnp.zeros(far_ref.shape[1:], f32)

    for m in range(tq // 128 + 2):
        @pl.when((first + m >= 0) & (first + m < n // 128))
        def _():
            band_ref[e, :, m * 128:(m + 1) * 128] += g_ref[e, :, pl.ds(pl.multiple_of((first + m) * 128, 128), 128)].astype(f32)

    for c in range(n // 128):
        @pl.when((c < first) | (c > first + tq // 128 + 1))
        def _():
            total = g_ref[e, 0:16, c * 128:(c + 1) * 128].astype(f32)
            for k in range(1, tq // 16):
                total = total + g_ref[e, k * 16:(k + 1) * 16, c * 128:(c + 1) * 128].astype(f32)
            far_ref[e, jnp.where(c < first, 0, 1)] += total


def bwd_tile(p, pairs, i, last_tile, last, q_ref, k_ref, v_ref, bias_ref, o_ref, do_ref, lse_ref, normed_ref, w_ref,
             g_ref, band_ref, far_ref, dw_ref, dx_ref, dkt, dvt, dqkv, turned):
    tq, n = q_ref.shape[0], k_ref.shape[0]
    rows = pl.ds(pl.multiple_of(i * tq, tq), tq)

    @pl.when(p == 0)
    def _():
        turned[:, rows] = normed_ref[rows, :].T

    @pl.when(i == 0)
    def _():
        dkt[...] = jnp.zeros_like(dkt)
        dvt[...] = jnp.zeros_like(dvt)

    q, k, v, do = q_ref[...], k_ref[...], v_ref[...], do_ref[...]
    prod = do.astype(f32) * o_ref[...].astype(f32)
    dqs = []
    for e in range(2):
        qm, dom = half_of(q, e), half_of(do, e)
        s = lax.dot_general(qm, k, NT, preferred_element_type=f32) + bias_ref[e]
        w = jnp.exp(s - lse_ref[0, :, e:e + 1])
        dp = lax.dot_general(dom, v, NT, preferred_element_type=f32)
        inner = jnp.sum(half_of(prod, e), axis=1, keepdims=True)
        g = (w * (dp - inner)).astype(bf16)
        g_ref[e] = g
        dqs.append(jnp.dot(g, k, preferred_element_type=f32))
        dvt[...] += jnp.dot(dom.T, w.astype(bf16), preferred_element_type=f32)
        dkt[...] += jnp.dot(qm.T, g, preferred_element_type=f32)
        band_sums(i, e, g_ref, band_ref, far_ref)
    columns = lambda k: pl.ds(pl.multiple_of((p + k * pairs) * 128, 128), 128)
    dqkv[rows, columns(0)] = join(*dqs).astype(bf16)

    @pl.when(last_tile)
    def _():
        dqkv[:, columns(1)] = dkt[...].T.astype(bf16)
        dqkv[:, columns(2)] = dvt[...].T.astype(bf16)

        @pl.when(last)
        def _():
            @pl.loop(0, n // TILE)
            def _(t):
                r = pl.ds(pl.multiple_of(t * TILE, TILE), TILE)
                dw_ref[r, :] = jnp.dot(turned[r, :], dqkv[...], preferred_element_type=f32).astype(bf16)
                dx_ref[r, :] = lax.dot_general(dqkv[r, :], w_ref[...], NT, preferred_element_type=f32).astype(bf16)


def bwd_kernel(pairs, tiles, G, halves, count, *refs):
    ins, parts = refs[:9], refs[9:9 + count]
    mid = refs[9 + count:14 + count]
    outs, accs, sems = refs[14 + count:14 + 2 * count], refs[14 + 2 * count:18 + 2 * count], refs[21 + 2 * count:]
    normed_s, w_s, load = refs[18 + 2 * count:21 + 2 * count]
    loads = [lambda: pltpu.make_async_copy(ins[7], normed_s, load.at[0]), lambda: pltpu.make_async_copy(ins[8], w_s, load.at[1])]
    p, i = pl.program_id(0), pl.program_id(1)
    comm = Scatter(G, halves, parts, outs, *sems)
    now, steps = p * tiles + i, pairs * tiles

    def compute():
        for n, step in ((0, 0), (1, steps - 1)):
            @pl.when(now == step)
            def _():
                loads[n]().wait()

        bwd_tile(p, pairs, i, i == tiles - 1, p == pairs - 1, *ins[:7], normed_s, w_s, *mid, *accs)

    beside(comm.events(), G, steps, now, compute, early=[lambda: [c().start() for c in loads]])


def shard_shapes(parts, wide):
    return tuple(jax.ShapeDtypeStruct((p.shape[0] // wide, p.shape[1]), f32) for p in parts)


def attn_bwd_and_scatter(qkv, bias, o, do, lse, normed, w, parts, halves, wide, cid, tq=256):
    n, width, d = qkv.shape[0], qkv.shape[1] // 3, normed.shape[1]
    pairs, tiles, count, G = width // 128, n // tq, len(parts), wide // 4
    sds = jax.ShapeDtypeStruct
    tile = pl.BlockSpec((tq, 128), lambda p, i: (i, p))
    full = lambda rows, k: pl.BlockSpec((rows, 128), lambda p, i: (0, p + k * pairs))
    const = lambda s: pl.BlockSpec(s, lambda p, i: (0, 0))
    outs = pl.pallas_call(functools.partial(bwd_kernel, pairs, tiles, G, halves, count), grid=(pairs, tiles),
        out_shape=(sds((2 * pairs, n, n), bf16), sds((2 * pairs, tq, tq + 256), f32), sds((2 * pairs, 2, 16, 128), f32)) + (sds((d, 3 * width), bf16), sds((n, d), bf16)) + shard_shapes(parts, wide),
        in_specs=[tile, full(n, 1), full(n, 2), pl.BlockSpec((2, tq, n), lambda p, i: (p, i, 0)), tile, tile,
                  pl.BlockSpec((1, tq, 2), lambda p, i: (p, i, 0)), ANY, ANY] + [ANY] * count,
        out_specs=(pl.BlockSpec((2, tq, n), lambda p, i: (p, i, 0)), pl.BlockSpec((2, tq, tq + 256), lambda p, i: (p, 0, 0)),
                   pl.BlockSpec((2, 2, 16, 128), lambda p, i: (p, 0, 0, 0))) + (const(w.shape), const((n, d))) + (whole_vmem(),) * count,
        scratch_shapes=[pltpu.VMEM((128, n), f32), pltpu.VMEM((128, n), f32), pltpu.VMEM((n, 3 * width), bf16), pltpu.VMEM((d, n), bf16),
                        pltpu.VMEM((n, d), bf16), pltpu.VMEM(w.shape, bf16), D((2,))] + scatter_scratch(G, halves, parts[0].shape[0] // wide),
        compiler_params=params(cid), name="attention_back_scatter")(
            qkv, qkv, qkv, bias, o, do, lse, normed, w, *parts)
    return outs[:5], outs[5:]


def rows_times_hots(src, ids, rows, heads, gs):
    n = src(0).shape[1]
    for h in range(heads):
        block = src(h)
        for c in range(n // 128):
            gs[c, h * rows:(h + 1) * rows, :] = block[:, c * 128:(c + 1) * 128]
    labels = [lax.broadcasted_iota(jnp.int32, (16, n), 0).astype(bf16) + float(k) for k in (0, 16)]
    one, zero = jnp.ones((16, n), bf16), jnp.zeros((16, n), bf16)
    group = 4 // len(ids(0))
    total = jnp.zeros((heads * group, 128), f32)
    for first in range(0, rows, group):
        grow, hots = [], []
        for r in range(first, first + group):
            grow.append(jnp.concatenate([gs[c, pl.ds(r, heads, stride=rows), :] for c in range(n // 128)], axis=1))
            for one_row in ids(r):
                row = jnp.broadcast_to(one_row, (16, n)).astype(bf16)
                hots += [jnp.where(row == label, one, zero) for label in labels]
        total = total + lax.dot_general(jnp.concatenate(grow, axis=0).astype(bf16), jnp.concatenate(hots, axis=0), NT, preferred_element_type=f32)
    return total


def own_blocks(total, heads, width):
    out = total[0:heads, 0:width]
    for k in range(1, 128 // width):
        out = out + total[k * heads:(k + 1) * heads, k * width:(k + 1) * width]
    return out


def halves_times_hots(g_ref, ids_ref, block, heads, gs, low):
    rows, n = 16, g_ref.shape[2]
    for h in range(heads):
        for c in range(n // 128):
            gs[c, h * rows:(h + 1) * rows, :] = g_ref[h, block, c * 128:(c + 1) * 128].astype(f32)
    for t in range(2):
        ids = ids_ref[t, block, :]
        low[t] = jnp.where(ids >= 16.0, ids - 16.0, ids)
    label = lax.broadcasted_iota(jnp.int32, (16, n), 0).astype(bf16)
    one, zero = jnp.ones((16, n), bf16), jnp.zeros((16, n), bf16)
    total = jnp.zeros((64, 64), f32)
    for first in range(0, rows, 2):
        left, hots = [], []
        for r in range(first, first + 2):
            grow = jnp.concatenate([gs[c, pl.ds(r, heads, stride=rows), :] for c in range(n // 128)], axis=1)
            for t in range(2):
                upper = jnp.broadcast_to(ids_ref.at[t, block][r:r + 1, :], (heads, n)) >= 16.0
                left += [jnp.where(upper, 0.0, grow), jnp.where(upper, grow, 0.0)]
                row = jnp.broadcast_to(low[t, r:r + 1, :], (16, n)).astype(bf16)
                hots.append(jnp.where(row == label, one, zero))
        total = total + lax.dot_general(jnp.concatenate(left, axis=0).astype(bf16), jnp.concatenate(hots, axis=0), NT, preferred_element_type=f32)
    return total


def own_halves(total, heads):
    out = 0.0
    for k in range(2):
        part = lambda t, up: total[k * 32 + (2 * t + up) * heads:k * 32 + (2 * t + up + 1) * heads, k * 32 + t * 16:k * 32 + t * 16 + 16]
        out = out + jnp.concatenate([part(0, 0), part(0, 1), part(1, 0), part(1, 1)], axis=1)
    return out


def hist_tile(now, heads, g_ref, ids_ref, band_ref, far_ref, lin_ids, table, boxes, gs, low):
    @pl.when(now == 0)
    def _():
        sides = [jnp.sum(jnp.sum(far_ref[:, k], axis=1), axis=1, keepdims=True) for k in range(2)]
        lane = lax.broadcasted_iota(jnp.int32, (heads, 128), 1)
        table[...] = jnp.zeros_like(table)
        boxes[...] = jnp.zeros_like(boxes)
        table[0:heads, :] = jnp.where(lane == 15, sides[0], 0.0) + jnp.where(lane == 31, sides[1], 0.0)

    big = g_ref.shape[1]

    @pl.loop(0, big // 16)
    def _(q):
        block = pl.ds(pl.multiple_of(q * 16, 16), 16)
        boxes[...] += halves_times_hots(g_ref, ids_ref, block, heads, gs, low)

    wide = band_ref.shape[2] // 128
    per = lin_ids.shape[1]
    a = now * 16 // per
    inside = pl.ds(pl.multiple_of(now * 16 % per, 16), 16)

    def band_ids(r):
        return [jnp.concatenate([lin_ids.at[jnp.clip((m - 1) * (128 // per) - a + 4, 0, 7), inside][r:r + 1, :] for m in range(wide)], axis=1)]

    table[...] += rows_times_hots(lambda h: band_ref[h], band_ids, 16, heads, gs)


def hist_kernel(heads, rows, n, G, halves, count, *refs):
    (g_ref, ids_ref, band_ref, far_ref, lin_ids, dx_h, tok_h, gh_h, gain_ref, gain_two), parts = refs[:10], refs[10:10 + count]
    small_ref, gt_ref = refs[10 + count:12 + count]
    outs, rest = refs[12 + count:12 + 2 * count], refs[12 + 2 * count:]
    (gs, low, table, boxes, got, dx, tok, gh, load, pair_sem), sums, sems = rest[:10], rest[10:17], rest[17:]
    acc = sums[0]
    now, steps = pl.program_id(0), n // rows
    core = lax.axis_index("narrow")
    mine = tok.shape[0]
    d = tok.shape[1]
    comm = Scatter(G, halves, parts, outs, *sems)
    loads = lambda: [pltpu.make_async_copy(dx_h.at[pl.ds(pl.multiple_of(core * mine, mine), mine)], dx, load.at[0]),
                     pltpu.make_async_copy(tok_h, tok, load.at[1]), pltpu.make_async_copy(gh_h, gh, load.at[2])]
    swap = lambda: remote(dx_h.at[pl.ds(pl.multiple_of((1 - core) * mine, mine), mine)], got, pair_sem.at[0], pair_sem.at[1], {"narrow": 1 - core})

    def compute():
        @pl.when(now == 0)
        def _():
            swap().start()
            acc[0] = jnp.zeros(acc.shape[1:], f32)
            for k in range(d // 128):
                acc[0, d // 128 + k:d // 128 + k + 1, :] = gain_two[:, k * 128:(k + 1) * 128]

        @pl.when(now == steps // 8)
        def _():
            swap().wait()
            for c in loads():
                c.wait()

        for t in range(mine // TILE):
            @pl.when(now == steps // 8 + t)
            def _():
                r = pl.ds(t * TILE, TILE)
                x = tok[r, :].astype(f32)
                total = dx[r, :].astype(f32) + got[r, :].astype(f32)
                factor = lax.rsqrt(jnp.mean(x * x, axis=1, keepdims=True) + epsilon)
                unit = x * factor
                scaled = gain_ref[0:1, :].astype(f32) * total
                gt_ref[r, :] = gh[r, :] + factor * (scaled - unit * jnp.mean(scaled * unit, axis=1, keepdims=True))
                gain = jnp.sum(total * unit, axis=0, keepdims=True)
                for k in range(d // 128):
                    acc[0, k:k + 1, :] += gain[:, k * 128:(k + 1) * 128]

        hist_tile(now, heads, g_ref, ids_ref, band_ref, far_ref, lin_ids, table, boxes, gs, low)

    def reduce():
        acc[0, pl.ds(pl.multiple_of(2 * (d // 128) + core * heads, 8), heads), 0:32] = own_blocks(table[...], heads, 32)
        acc[0, pl.ds(pl.multiple_of(2 * (d // 128) + core * heads, 8), heads), 32:96] = own_halves(boxes[...], heads)

    events, _ = comm.events(1)
    stages = sum_everywhere(G, small_ref, *sums)
    beside((events, lambda: None), G, steps, now, compute, [reduce] + [act for pair in zip(stages, comm.ending()) for act in pair],
           [lambda: [c.start() for c in loads()]], pace=0.3875)


def hist_and_scatter(g, band, far, ids, dx, tok, gh, gain, gain_two, parts, halves, wide, cid):
    heads, n, _ = g.shape
    rows, count, G, d = n // (band.shape[1] // 16), len(parts), wide // 4, tok.shape[1]
    box_ids, lin_ids = ids
    small = 2 * (d // 128) + 2 * heads
    sds = jax.ShapeDtypeStruct
    const = lambda s: pl.BlockSpec(s, lambda i: (0, 0))
    outs = pl.pallas_call(functools.partial(hist_kernel, heads, rows, n, G, halves, count), grid=(n // rows,),
        out_shape=(sds((small, 128), f32), sds(tok.shape, f32)) + shard_shapes(parts, wide),
        in_specs=[pl.BlockSpec((heads, rows, n), lambda i: (0, i, 0)), pl.BlockSpec((2, rows, n), lambda i: (0, i, 0)),
                  pl.BlockSpec((heads, 16, band.shape[2]), lambda i: (0, i, 0)), pl.BlockSpec(far.shape, lambda i: (0, 0, 0, 0)),
                  pl.BlockSpec(lin_ids.shape, lambda i: (0, 0, 0)), ANY, ANY, ANY, const(gain.shape), const(gain_two.shape)] + [ANY] * count,
        out_specs=(const((small, 128)), const(tok.shape)) + (whole_vmem(),) * count,
        scratch_shapes=[pltpu.VMEM((n // 128, heads * 16, 128), f32), pltpu.VMEM((2, 16, n), f32), pltpu.VMEM((4 * heads, 128), f32), pltpu.VMEM((64, 64), f32), pltpu.VMEM(tok.shape, bf16),
                        pltpu.VMEM(tok.shape, bf16), pltpu.VMEM(tok.shape, bf16), pltpu.VMEM(tok.shape, f32), D((3,)), D((2,))]
        + sum_scratch(G, small) + scatter_scratch(G, halves, parts[0].shape[0] // wide),
        compiler_params=params(cid), name="table_grad_scatter")(g, box_ids, band, far, lin_ids, dx, tok, gh, gain, gain_two, *parts)
    return outs[0], outs[1], outs[2:]


D = pltpu.SemaphoreType.DMA
AHEAD = 2


def place():
    me = lax.axis_index("wide")
    return me // 4, (me // 2) % 2, me % 2


def wide_id(z, y, x):
    return {"wide": z * 4 + y * 2 + x}


def shard_rows(z, y, x, R):
    return pl.ds(pl.multiple_of((z * 4 + y * 2 + x) * R, R), R)


def remote(src, dst, send, recv, target):
    return pltpu.make_async_remote_copy(src_ref=src, dst_ref=dst, send_sem=send, recv_sem=recv, device_id=target, device_id_type=MESH)


def greet(G, far, pair=0):
    z, y, x = place()
    bar = pltpu.get_barrier_semaphore()
    sig = lambda t: pl.semaphore_signal(bar, inc=1, device_id=t, device_id_type=MESH)
    sig(wide_id(z, 1 - y, x))
    sig(wide_id(z, y, 1 - x))
    if pair:
        sig({"narrow": 1 - lax.axis_index("narrow")})
    if far:
        for k in range(1, G):
            sig(wide_id((z + k) % G, y, x))
        pl.semaphore_wait(bar, 2 + pair + G - 1)
    else:
        @pl.when(z > 0)
        def _():
            sig(wide_id(z - 1, y, x))

        @pl.when(z < G - 1)
        def _():
            sig(wide_id(z + 1, y, x))

        pl.semaphore_wait(bar, 2 + pair + (z > 0).astype(jnp.int32) + (z < G - 1).astype(jnp.int32))


class Gather:
    def __init__(self, G, halves, srcs, outs, local_sem, zs, zr, ns, nr):
        self.G, self.halves, self.srcs, self.local_sem = G, halves, srcs, local_sem
        self.outs = [o if isinstance(o, tuple) else (o, 0, 0) for o in outs]
        self.widths = [sum(w for h in halves for a, _, w in h if a == k) for k in range(len(srcs))]
        self.zs, self.zr, self.ns, self.nr = zs, zr, ns, nr
        self.most = max(len(h) for h in halves)
        self.z, self.y, self.x = place()
        self.R = srcs[0].shape[0]

    def hop(self, own, zz, yy, xx, h, way, j):
        target = wide_id(self.z, 1 - self.y, self.x) if way == "y" else wide_id(self.z, self.y, 1 - self.x)
        copies = []
        for n, (a, c, w) in enumerate(self.halves[h]):
            slot = (zz * 6 + j) * self.most + n
            out, first, at = self.outs[a]
            dst = out.at[shard_rows(zz, yy, xx, self.R), pl.ds(first + c, w)]
            copies.append(remote(self.srcs[a].at[:, pl.ds(at + c, w)] if own else dst, dst, self.ns.at[slot], self.nr.at[slot], target))
        return copies

    def second_stage(self, zz, own=False):
        return self.hop(own, zz, self.y, self.x, 0, "y", 0) + self.hop(own, zz, self.y, self.x, 1, "x", 1)

    def third_stage(self, zz, own=False):
        return self.hop(own, zz, self.y, self.x, 0, "x", 2) + self.hop(own, zz, self.y, self.x, 1, "y", 3)

    def last_stage(self, zz):
        return self.hop(False, zz, 1 - self.y, self.x, 0, "x", 4) + self.hop(False, zz, self.y, 1 - self.x, 1, "y", 5)

    def relay(self, own, zz, step, way):
        copies = []
        for a in range(len(self.srcs)):
            slot = (way * (self.G - 1) + step) * len(self.srcs) + a
            dst = self.whole(a, zz)
            copies.append(remote(self.own(a) if own else dst, dst, self.zs.at[slot], self.zr.at[slot],
                                 wide_id(self.z + (1 if way == 0 else -1), self.y, self.x)))
        return copies

    def whole(self, a, zz):
        out, first, _ = self.outs[a]
        return out.at[shard_rows(zz, self.y, self.x, self.R), pl.ds(first, self.widths[a])]

    def own(self, a):
        return self.srcs[a].at[:, pl.ds(self.outs[a][2], self.widths[a])]

    def can(self, way):
        return self.z < self.G - 1 if way == 0 else self.z > 0

    def source(self, d, way):
        return (self.z - d, self.z - d >= 0) if way == 0 else (self.z + d, self.z + d < self.G)

    def keep(self):
        return [pltpu.make_async_copy(self.own(a), self.whole(a, self.z), self.local_sem.at[a]) for a in range(len(self.srcs))]

    def begin(self):
        for way in range(2):
            @pl.when(self.can(way))
            def _():
                for c in self.relay(True, self.z, 0, way):
                    c.start()
        for c in self.second_stage(self.z, True) + self.third_stage(self.z, True) + self.keep():
            c.start()

    def turn(self, zz):
        for c in self.hop(False, zz, 1 - self.y, self.x, 0, "y", 0) + self.hop(False, zz, self.y, 1 - self.x, 1, "x", 1):
            c.wait_recv()
        for c in self.last_stage(zz):
            c.start()

    def step(self, d):
        for way in range(2):
            zz, there = self.source(d, way)

            @pl.when(there)
            def _():
                for c in self.relay(False, zz, d - 1, way):
                    c.wait_recv()

                @pl.when(self.can(way))
                def _():
                    for c in self.relay(False, zz, d, way):
                        c.start()

                for c in self.second_stage(zz):
                    c.start()
        for way in range(2):
            zz, there = self.source(d, way)

            @pl.when(there)
            def _():
                for c in self.third_stage(zz):
                    c.start()

    def turns(self, d):
        if d == 0:
            self.turn(self.z)
            return
        for way in range(2):
            zz, there = self.source(d, way)

            @pl.when(there)
            def _():
                self.turn(zz)

    def finish(self):
        y, x = self.y, self.x

        @pl.loop(0, self.G)
        def _(zz):
            for c in (self.hop(False, zz, y, 1 - x, 0, "x", 2) + self.hop(False, zz, 1 - y, x, 1, "y", 3)
                      + self.hop(False, zz, 1 - y, 1 - x, 0, "x", 4) + self.hop(False, zz, 1 - y, 1 - x, 1, "y", 5)):
                c.wait_recv()
            for c in self.second_stage(zz) + self.third_stage(zz) + self.last_stage(zz):
                c.wait_send()

        for way in range(2):
            @pl.when(self.can(way))
            def _():
                for c in self.relay(True, self.z, 0, way):
                    c.wait_send()
                for d in range(1, self.G - 1):
                    zz, there = self.source(d, way)

                    @pl.when(there)
                    def _():
                        for c in self.relay(False, zz, d, way):
                            c.wait_send()
        for c in self.keep():
            c.wait()

    def events(self):
        G = self.G
        first = lambda: (greet(G, False), self.begin())
        ev = [(0.0, first), (0.7, lambda: self.turns(0))]
        for d in range(1, G):
            ev += [(1.15 * d, functools.partial(self.step, d)), (1.3 * d + 1.2, functools.partial(self.turns, d))]
        return sorted(ev, key=lambda e: e[0]), self.finish


def gather_scratch(G, halves, arrays):
    most = max(len(h) for h in halves)
    return [D((arrays,)), D((2 * (G - 1) * arrays,)), D((2 * (G - 1) * arrays,)), D((6 * G * most,)), D((6 * G * most,))]


class Scatter:
    def __init__(self, G, halves, parts, outs, r1a, r1b, o1a, o1b, r2a, r2b, r3, own, lsem, s1, v1, s2, v2, s3, v3):
        self.__dict__.update(locals())
        self.most = max(len(h) for h in halves)
        self.wa, self.wb = [sum(p[2] for p in h) for h in halves]
        self.R = parts[0].shape[0] // (4 * G)
        self.z, self.y, self.x = place()
        self.order = sorted(range(1, G), key=lambda k: min(k, G - k), reverse=True) + [0]

    def zk(self, k):
        return (self.z + k) % self.G

    def neighbour(self, way):
        return wide_id(self.z, 1 - self.y, self.x) if way == "y" else wide_id(self.z, self.y, 1 - self.x)

    def pieces(self, h):
        at, out = 0, []
        for n, (a, c, w) in enumerate(self.halves[h]):
            out.append((n, a, pl.ds(c, w), pl.ds(at, w)))
            at += w
        return out

    def sources(self, k, mine):
        z, y, x = self.zk(k), self.y, self.x
        for h in range(2):
            for n, a, src, dst in self.pieces(h):
                for j in range(2):
                    if h == 0:
                        rows = shard_rows(z, j, x if mine else 1 - x, self.R)
                    else:
                        rows = shard_rows(z, y if mine else 1 - y, j, self.R)
                    yield h, j, dst, ((2 * k + h) * self.most + n) * 2 + j, self.parts[a].at[rows, src]

    def one(self, k):
        return [remote(src, (self.r1a, self.r1b)[h].at[k, j, :, dst], self.s1.at[slot], self.v1.at[slot], self.neighbour("xy"[h]))
                for h, j, dst, slot, src in self.sources(k, False)]

    def load(self, k):
        return [pltpu.make_async_copy(src, (self.o1a, self.o1b)[h].at[k, j, :, dst], self.lsem.at[slot]) for h, j, dst, slot, src in self.sources(k, True)]

    def two(self, k):
        return [remote(self.o1a.at[k, 1 - self.y], self.r2a.at[k], self.s2.at[2 * k], self.v2.at[2 * k], self.neighbour("y")),
                remote(self.o1b.at[k, 1 - self.x], self.r2b.at[k], self.s2.at[2 * k + 1], self.v2.at[2 * k + 1], self.neighbour("x"))]

    def three(self, k):
        return remote(self.own.at[k], self.r3.at[k - 1], self.s3.at[k - 1], self.v3.at[k - 1], wide_id(self.zk(k), self.y, self.x))

    def launch(self, k):
        for c in self.one(k) + self.load(k):
            c.start()

    def begin(self):
        for k in self.order[:AHEAD]:
            self.launch(k)

    def rows(self, count, body):
        step = min(16, count)

        @pl.loop(0, count // step)
        def _(i):
            body(pl.ds(pl.multiple_of(i * step, step), step))

    def add_one(self, n):
        k = self.order[n]
        for c in self.one(k):
            c.wait_recv()
        for c in self.load(k):
            c.wait()
        for mine, got in ((self.o1a, self.r1a), (self.o1b, self.r1b)):
            def body(r):
                for j in range(2):
                    mine[k, j, r, :] = (mine[k, j, r, :].astype(f32) + got[k, j, r, :].astype(f32)).astype(bf16)

            self.rows(self.R, body)
        for c in self.two(k):
            c.start()
        if n + AHEAD < self.G:
            self.launch(self.order[n + AHEAD])

    def add_two(self, n):
        k = self.order[n]
        for c in self.two(k):
            c.wait_recv()

        def body(r):
            self.own[k, r, pl.ds(0, self.wa)] = (self.o1a[k, self.y, r, :].astype(f32) + self.r2a[k, r, :].astype(f32)).astype(bf16)
            self.own[k, r, pl.ds(self.wa, self.wb)] = (self.o1b[k, self.x, r, :].astype(f32) + self.r2b[k, r, :].astype(f32)).astype(bf16)

        self.rows(self.R, body)
        if k:
            self.three(k).start()

    def arrived(self):
        for k in range(1, self.G):
            self.three(k).wait_recv()

    def write_out(self):
        def body(r):
            for h in range(2):
                for _, a, src, dst in self.pieces(h):
                    cols = pl.ds(dst.start + h * self.wa, dst.size)
                    total = self.own[0, r, cols].astype(f32)
                    for k in range(self.G - 1):
                        total = total + self.r3[k, r, cols].astype(f32)
                    self.outs[a][r, src] = total

        self.rows(self.R, body)

    def all_sent(self):
        for k in range(self.G):
            for c in self.one(k) + self.two(k):
                c.wait_send()
            if k:
                self.three(k).wait_send()

    def ending(self):
        return [lambda: self.add_two(self.G - 1), self.arrived, self.write_out, self.all_sent, lambda: None]

    def finish(self):
        for act in self.ending():
            act()

    def events(self, pair=0):
        G = self.G
        first = lambda: (greet(G, True, pair), self.begin())
        ev = [(0.0, first), (1.1, lambda: self.add_one(0))]
        for n in range(1, G):
            ev += [(1.5 * n + 0.65, functools.partial(self.add_one, n)), (1.5 * n + 1.1, functools.partial(self.add_two, n - 1))]
        return sorted(ev, key=lambda e: e[0]), self.finish


def scatter_scratch(G, halves, R):
    most = max(len(h) for h in halves)
    a, b = [sum(p[2] for p in h) for h in halves]
    V = lambda *s: pltpu.VMEM(s, bf16)
    return [V(G, 2, R, a), V(G, 2, R, b), V(G, 2, R, a), V(G, 2, R, b), V(G, R, a), V(G, R, b), V(G - 1, R, a + b), V(G, R, a + b),
            D((4 * G * most,)), D((4 * G * most,)), D((4 * G * most,)), D((2 * G,)), D((2 * G,)), D((G - 1,)), D((G - 1,))]


def beside(plan, G, steps, now, compute, late=(), early=(), pace=0.3875, lead=0.0):
    events, finish = plan
    if early:
        @pl.when(now == 0)
        def _():
            for act in early:
                act()
    for n in range(steps):
        here = [act for t, act in events if min(steps - 1, max(0, int(-((lead - t) // pace)))) == n]
        if here:
            @pl.when(now == n)
            def _():
                for act in here:
                    act()
    compute()

    @pl.when(now == steps - 1)
    def _():
        for act in late:
            act()
        finish()


ANY = pl.BlockSpec(memory_space=pl.ANY)


def whole_vmem():
    return pl.BlockSpec(memory_space=pltpu.VMEM)


def gathered_shapes(shards, wide):
    return tuple(jax.ShapeDtypeStruct((wide * rows, columns), bf16) for rows, columns in shards)


def sum_everywhere(G, out, acc, got, gz, s, v, sz, vz):
    z, y, x = place()
    targets = [{"narrow": 1 - lax.axis_index("narrow")}, wide_id(z, y, 1 - x), wide_id(z, 1 - y, x)]
    near = lambda n: remote(acc.at[n], got.at[n], s.at[n], v.at[n], targets[n])
    far = lambda k, zz: remote(acc.at[3], gz.at[zz], sz.at[k - 1], vz.at[zz], wide_id((z + k) % G, y, x))

    def take(n):
        near(n).wait()
        acc[n + 1] = acc[n] + got[n]

    def next_near(n):
        if n:
            take(n - 1)
        near(n).start()

    def spread_far():
        take(2)
        gz[z] = acc[3]
        for k in range(1, G):
            far(k, z).start()

    def total():
        for k in range(1, G):
            far(k, (z + k) % G).wait_recv()
        for k in range(1, G):
            far(k, z).wait_send()
        value = gz[0]
        for k in range(1, G):
            value = value + gz[k]
        out[...] = value

    return [functools.partial(next_near, n) for n in range(3)] + [spread_far, total]


def sum_scratch(G, rows):
    V = lambda k: pltpu.VMEM((k, rows, 128), f32)
    return [V(4), V(3), V(G), D((3,)), D((3,)), D((G - 1,)), D((G,))]


def nt(a, b):
    return lax.dot_general(a, b, NT, preferred_element_type=f32)


def nn(a, b):
    return jnp.dot(a, b, preferred_element_type=f32)


def gelu_and_slope(v):
    root = 0.7978845608028654
    square = v * v
    t = jnp.tanh(root * v * (1.0 + 0.044715 * square))
    half = 0.5 * (1.0 + t)
    return v * half, half + 0.5 * v * (1.0 - t * t) * root * (1.0 + 3 * 0.044715 * square)


def mid_kernel(G, cut, att_h, tok_h, cot_h, wo_h, wg_h, wu_h, wd_h, wd_shard, gain_ref,
               gout_h, gg_h, gu_h, gd_h, y_ref, gh_ref, ga_ref, ggain_ref, sd_ref,
               att, tok, cot, wo, wg, wu, wd, part, other, back, hid, n2t, cott, hff, gg, gu, yother, stage,
               isem, osem, sp, vp, sb, vb, sy, vy, *sems):
    core = lax.axis_index("narrow")
    peer = {"narrow": 1 - core}
    n, d = tok.shape
    ff = wg.shape[1]
    tiles = n // TILE
    half = tiles // 2
    loads = [pltpu.make_async_copy(s, t, isem.at[k]) for k, (s, t) in enumerate(
        [(att_h, att), (wo_h, wo), (tok_h, tok), (wg_h, wg), (wu_h, wu), (cot_h, cot), (wd_h, wd.at[:, pl.ds(0, cut)])])]
    for c in loads:
        c.start()
    part_cols = sd_ref.shape[1]
    mid = cut + (ff - cut) // 256 * 128
    bring = Gather(G, (((0, 0, mid - cut),), ((0, mid - cut, ff - mid),)), [wd_shard], [(wd, cut, cut)], *sems[:5])
    give = Scatter(G, (((0, 0, part_cols // 2),), ((0, part_cols // 2, part_cols // 2),)), [gd_h], [sd_ref], *sems[5:])
    greet(G, True, 1)
    bring.begin()
    rows_of = lambda t: pl.ds(pl.multiple_of(t * TILE, TILE), TILE)
    kept = lambda j: rows_of(j + half)
    send_part = lambda t: remote(part.at[rows_of(t)], other.at[rows_of(t)], sp.at[t], vp.at[t], peer)
    send_back = lambda t: remote(part.at[rows_of(t)], back.at[rows_of(t)], sb.at[t], vb.at[t], peer)
    send_y = lambda j: remote(tok.at[rows_of(j)], yother.at[rows_of(j)], sy.at[j], vy.at[j], peer)
    gain = gain_ref[1:2, :].astype(f32)

    for c in loads[:2]:
        c.wait()

    def at_step(s, plan):
        for k, acts in plan.items():
            @pl.when(s == k)
            def _():
                for act in acts:
                    act()

    turns = [functools.partial(bring.turns, k) for k in range(G)]
    steps = [functools.partial(bring.step, k) for k in range(1, G)]

    @pl.loop(0, tiles)
    def _(t):
        part[rows_of(t), :] = nt(att[rows_of(t), :], wo[...]).astype(bf16)
        send_part(t).start()

    for c in loads[2:]:
        c.wait()

    chunks, at = [], 0
    while at < ff:
        w = min(384, ff - at)
        chunks.append((at, w))
        at += w

    later = [act for pair in zip(turns[1:], steps[1:] + [lambda: None]) for act in pair]

    @pl.loop(0, tiles)
    def _(s):
        t = (s + half * (1 - core)) % tiles
        r = rows_of(t)
        send_part(t).wait()
        h = tok[r, :].astype(f32) + (part[r, :].astype(f32) + other[r, :].astype(f32))
        hid[r, :] = h
        factor = lax.rsqrt(jnp.mean(h * h, axis=1, keepdims=True) + epsilon)
        low = (h * factor * gain).astype(bf16)
        n2t[:, r] = low.T
        cott[:, r] = cot[r, :].T
        for at, w in chunks:
            cols = pl.ds(at, w)
            act, slope = gelu_and_slope(nn(low, wg[:, cols]))
            up = nn(low, wu[:, cols])
            hff[r, cols] = (act * up).astype(bf16)
            gg[r, cols] = (up * slope).astype(bf16)
            gu[r, cols] = act.astype(bf16)
        at_step(s, {0: turns[:1] + steps[:1], 1: later[:2], 2: later[2:4], 3: later[4:]})

    def weight_grad(left, right, out, slot, width):
        rows = stage.shape[1]
        block = lambda k: pl.ds(k * rows, rows)
        copy = lambda k: pltpu.make_async_copy(stage.at[k % 2, :, pl.ds(0, width)], out.at[block(k)], osem.at[2 * slot + k % 2])
        count = d // rows
        for k in range(count):
            if k >= 2:
                copy(k - 2).wait()
            stage[k % 2, :, pl.ds(0, width)] = nn(left[block(k), :], right[...]).astype(bf16)
            copy(k).start()
        return [copy(k) for k in range(max(0, count - 2), count)]

    for c in weight_grad(cott, hff, gd_h, 0, ff):
        c.wait()
    give.begin()
    bring.finish()
    ones = [functools.partial(give.add_one, k) for k in range(G)]
    twos = [functools.partial(give.add_two, k) for k in range(G - 1)]

    @pl.loop(0, tiles)
    def _(s):
        t = (s + half * (1 - core)) % tiles
        r = rows_of(t)
        ct = cot[r, :]
        for at, w in chunks:
            cols = pl.ds(at, w)
            gf = nn(ct, wd[:, cols])
            gg[r, cols] = (gf * gg[r, cols].astype(f32)).astype(bf16)
            gu[r, cols] = (gf * gu[r, cols].astype(f32)).astype(bf16)
        part[r, :] = (nt(gg[r, :], wg[...]) + nt(gu[r, :], wu[...])).astype(bf16)
        send_back(t).start()
        y = nt(hff[r, :], wd[...]).astype(bf16)

        @pl.when(s < half)
        def _():
            tok[rows_of(s), :] = y
            send_y(s).start()

        @pl.when(s >= half)
        def _():
            tok[rows_of(s), :] = y

        at_step(s, {1: ones[:1], 2: ones[1:2], 3: twos[:1]})

    ggain_ref[...] = jnp.zeros_like(ggain_ref)

    @pl.loop(0, tiles)
    def _(s):
        t = (s + half * (1 - core)) % tiles
        r = rows_of(t)
        send_back(t).wait()
        total = part[r, :].astype(f32) + back[r, :].astype(f32)
        h = hid[r, :]
        factor = lax.rsqrt(jnp.mean(h * h, axis=1, keepdims=True) + epsilon)
        unit = h * factor
        g = gain * total
        gh = cot[r, :].astype(f32) + factor * (g - unit * jnp.mean(g * unit, axis=1, keepdims=True))
        low = gh.astype(bf16)
        cott[:, r] = low.T
        ga_ref[r, :] = nn(low, wo[...]).astype(bf16)

        @pl.when(s >= half)
        def _():
            j = rows_of(s - half)
            gh_ref[j, :] = gh
            ggain_ref[...] += jnp.sum(total * unit, axis=0, keepdims=True)
            send_y(s - half).wait()
            y_ref[j, :] = (h + (tok[kept(s - half), :].astype(f32) + yother[j, :].astype(f32))).astype(bf16)

        at_step(s, {0: ones[2:3], 1: twos[1:2], 3: ones[3:4]})

    for left, right, out, slot in ((n2t, gg, gg_h, 1), (n2t, gu, gu_h, 2), (cott, att, gout_h, 3)):
        if slot == 2:
            for act in twos[2:3] + [act for pair in zip(ones[4:], twos[3:]) for act in pair]:
                act()
        for c in weight_grad(left, right, out, slot, right.shape[1]):
            c.wait()
    give.finish()


def middle(att, tok, cot, wo, wg, wu, wd, wd_shard, gain, here, wide, cid):
    n, d = tok.shape
    units, ff, G, cut = att.shape[1], wg.shape[1], wide // 4, wd.shape[1]
    B = lambda *s: pltpu.VMEM(s, bf16)
    sds = jax.ShapeDtypeStruct
    tiles = n // TILE
    halves = (((0, 0, cut),), ((0, cut, ff - cut),))
    return pl.pallas_call(functools.partial(mid_kernel, G, cut),
        out_shape=(sds((d, units), bf16), sds((d, ff), bf16), sds((d, ff), bf16), sds((d, ff), bf16),
                   sds((n // 2, d), bf16), sds((n // 2, d), f32), sds((n, units), bf16), sds((1, d), f32), sds((d // wide, here), f32)),
        in_specs=[ANY] * 8 + [whole_vmem()], out_specs=(ANY,) * 4 + (whole_vmem(),) * 5,
        scratch_shapes=[B(n, units), B(n, d), B(n, d), B(d, units), B(d, ff), B(d, ff), B(d, ff), B(n, d), B(n, d), B(n, d),
                        pltpu.VMEM((n, d), f32), B(d, n), B(d, n), B(n, ff), B(n, ff), B(n, ff),
                        B(n // 2, d), B(2, 512, ff),
                        D((7,)), D((8,)), D((tiles,)), D((tiles,)), D((tiles,)), D((tiles,)), D((tiles // 2,)), D((tiles // 2,))]
        + gather_scratch(G, halves, 1) + scatter_scratch(G, (((0, 0, here // 2),), ((0, here // 2, here // 2),)), d // wide),
        compiler_params=params(cid), name="feed_forward")(att, tok, cot, wo, wg, wu, wd, wd_shard, gain)


def local(tokens, cotangent, pages, boxes, gain_attn, gain_ffn, bias_tables, w_query, w_key, w_value, w_out, w_gate, w_up, w_down):
    wide, narrow = lax.axis_size("wide"), lax.axis_size("narrow")
    heads = bias_tables.shape[1] // narrow
    inner, ff, d = w_query.shape[1], w_gate.shape[1], tokens.shape[1]
    gains = jnp.stack([gain_attn, gain_ffn])

    all_tokens = lax.all_gather(tokens, "narrow", axis=0, tiled=True)
    all_cot = lax.all_gather(cotangent, "narrow", axis=0, tiled=True)
    early = inner // 4 * 3
    bias, ids, (w_first, full_out, full_gate) = bias_and_gather(
        bias_tables.T, heads, boxes, pages, [w_query, w_key, w_value, w_out.T, w_gate], ((0, 0), (0, inner), (0, 2 * inner), (1, 0), (2, 0)),
        (((4, 0, ff), (0, 0, early)), ((3, 0, inner), (0, early, inner - early), (1, 0, inner), (2, 0, inner))), wide, 1)
    down_shard = w_down.T
    cut = (ff // 128 + 1) // 2 * 128
    (attended, lse, normed, qkv), (full_up, most_down) = attn_fwd_and_gather(
        all_tokens, gains, w_first, bias, [w_up, down_shard], (ff, cut),
        (((0, 0, cut), (1, 0, cut - 384)), ((0, cut, ff - cut), (1, cut - 384, 384))), wide, 2)
    here, upto = ff // 256 * 256, ff // 256 * 256 - 128
    grad_w_out, grad_w_gate, grad_w_up, grad_w_down, output, grad_hidden, grad_attended, grad_gain_two, s_down = middle(
        attended, all_tokens, all_cot, full_out, full_gate, full_up, most_down, down_shard, gains, here, wide, 3)
    even = (ff + inner + ff - here + ff - upto) // 2
    (g, band, far, grad_w_first, grad_normed), (s_gate, s_out, more_down, more_up) = attn_bwd_and_scatter(
        qkv, bias, attended, grad_attended, lse, normed, w_first, [grad_w_gate, grad_w_out, grad_w_down, grad_w_up],
        (((0, 0, even),), ((0, even, ff - even), (1, 0, inner), (2, here, ff - here), (3, upto, ff - upto))), wide, 4)
    s_down = jnp.concatenate([s_down, more_down[:, here:]], axis=1)
    small, grad_tokens, (s_up, s_first) = hist_and_scatter(
        g, band, far, ids, grad_normed, tokens, grad_hidden, gains, grad_gain_two, [grad_w_up, grad_w_first],
        (((0, 0, upto), (1, 0, 128)), ((1, 128, 3 * inner - 128),)), wide, 5)
    s_up = jnp.concatenate([s_up[:, :upto], more_up[:, upto:]], axis=1)
    s_query, s_key, s_value = jnp.split(s_first, 3, axis=1)
    lines = d // 128
    one, two = small[:lines].reshape(d), small[lines:2 * lines].reshape(d)
    table = small[2 * lines:, :bias_tables.shape[0]].T
    return (output, grad_tokens, one, two, table, s_query, s_key, s_value, s_out.T, s_gate, s_up, s_down.T)


def solution(mesh):
    rows, cols, tall = P(("wide", "narrow"), None), P("wide", "narrow"), P("narrow", "wide")
    in_specs = (rows, rows, P("wide"), P(None, "wide"), P(), P(), P(), cols, cols, cols, tall, cols, cols, tall)
    out_specs = (rows, rows, P(), P(), P(), cols, cols, cols, tall, cols, cols, tall)
    return jax.shard_map(local, mesh=mesh, in_specs=in_specs, out_specs=out_specs, check_vma=False)
```

```python
import functools

import jax
import jax.numpy as jnp
from jax import lax
from jax.experimental import pallas as pl
from jax.experimental.pallas import tpu as pltpu
from jax.sharding import PartitionSpec as P

f32, bf16 = jnp.float32, jnp.bfloat16
MESH = pl.DeviceIdType.MESH


EDGES = (1, 2, 3, 4, 5, 6, 7, 8, 12, 16, 23, 32, 46, 64, 91)
NT = (((1,), (1,)), ((), ()))
VM = 58 * 2**20
TABLE_SCALE = 2047.0
TABLE_LIFT = 8192
TILE = 256
epsilon = 1e-06


def params(cid):
    return pltpu.CompilerParams(collective_id=cid, has_side_effects=True, vmem_limit_bytes=VM)


def lane_take(table, idx):
    return jnp.take_along_axis(table, idx, axis=1, mode="promise_in_bounds")


def buckets_of(gap, shift):
    size = jnp.minimum(jnp.abs(gap) >> shift, EDGES[-1])
    return jnp.where(size < 8, size, 33 - lax.clz(size * size)) + jnp.where(gap > 0, 16, 0)


def bias_tile(start, heads, rows, n, tab_ref, box_row, page_row, bias_ref, ids_ref, lin_ids, lin, words_ref):
    lane = lax.broadcasted_iota(jnp.int32, (rows, 128), 1)
    down = lax.broadcasted_iota(jnp.int32, (rows, 128), 0)
    pairs = heads // 2

    def column(row_ref, t):
        values = jnp.broadcast_to(row_ref[t:t + 1, pl.ds(pl.multiple_of(start // 128 * 128, 128), 128)], (rows, 128)).astype(f32)
        return jnp.broadcast_to(jnp.sum(jnp.where(lane == down + start % 128, values, 0.0), axis=1, keepdims=True), (rows, 128)).astype(jnp.int32)

    allowed_col = column(page_row, 0) % 2
    cols = [column(box_row, t) for t in range(2)]

    @pl.when(start == 0)
    def _():
        first = lax.axis_index("narrow") * heads
        row = lax.broadcasted_iota(jnp.int32, (heads, tab_ref.shape[0]), 0)
        wanted = first + jnp.where(row < pairs, 2 * row, 2 * (row - pairs) + 1)
        pick = jnp.where(lax.broadcasted_iota(jnp.int32, row.shape, 1) == wanted, 1.0, 0.0).astype(bf16)
        picked = jnp.dot(pick, tab_ref[...], preferred_element_type=f32)
        fixed = jnp.round(picked * TABLE_SCALE).astype(jnp.int32)
        words_ref[...] = jnp.zeros_like(words_ref)
        words_ref[0:pairs, 0:picked.shape[1]] = fixed[0:pairs] * 65536 + fixed[pairs:heads] + TABLE_LIFT

        @pl.loop(0, 8)
        def _(k):
            ids = buckets_of(lane - down + (k - 4) * rows, 0)
            lin_ids[k] = ids.astype(f32)
            for p in range(pairs):
                lin[k, p] = lane_take(jnp.broadcast_to(words_ref[p:p + 1, :], (rows, 128)), ids)

    unit = 1.0 / TABLE_SCALE
    tables = [jnp.broadcast_to(words_ref[p:p + 1, :], (rows, 128)) for p in range(pairs)]

    @pl.loop(0, n // 128)
    def _(c):
        lanes = pl.ds(pl.multiple_of(c * 128, 128), 128)
        near = jnp.clip((c * 128 - start) // rows + 4, 0, 7)
        ids = []
        for t in range(2):
            ids.append(buckets_of(jnp.broadcast_to(box_row[t:t + 1, lanes], (rows, 128)) - cols[t], 2))
            ids_ref[t, :, lanes] = ids[t].astype(f32)
        ok = jnp.broadcast_to(page_row[:, lanes], (rows, 128)) == allowed_col
        for p in range(pairs):
            words = lin[near, p] + lane_take(tables[p], ids[0] + 32) + lane_take(tables[p], ids[1] + 64)
            upper = (words >> 16).astype(f32) * unit
            lower = (words & 0xFFFF).astype(f32) * unit - 3 * TABLE_LIFT * unit
            bias_ref[2 * p, :, lanes] = jnp.where(ok, upper, -1e30)
            bias_ref[2 * p + 1, :, lanes] = jnp.where(ok, lower, -1e30)


def bias_gather_kernel(heads, rows, n, G, halves, count, into, *refs):
    ins, srcs = refs[:3], refs[3:3 + count]
    bias_ref, ids_ref, lin_ids = refs[3 + count:6 + count]
    kinds = len(set(k for k, _ in into))
    outs, scratch, sems = refs[6 + count:6 + count + kinds], refs[6 + count + kinds:8 + count + kinds], refs[8 + count + kinds:]
    now = pl.program_id(0)
    comm = Gather(G, halves, srcs, [(outs[k], c, 0) for k, c in into], *sems)
    beside(comm.events(), G, n // rows, now, lambda: bias_tile(now * rows, heads, rows, n, *ins, bias_ref, ids_ref, lin_ids, *scratch))


def bias_and_gather(tables, heads, boxes, pages, shards, into, halves, wide, cid):
    n, G, rows = pages.shape[0], wide // 4, 64
    count = len(shards)
    widths = [sum(a.shape[1] for a, (j, _) in zip(shards, into) if j == k) for k in sorted(set(k for k, _ in into))]
    outs = pl.pallas_call(functools.partial(bias_gather_kernel, heads, rows, n, G, halves, count, into),
        grid=(n // rows,),
        out_shape=(jax.ShapeDtypeStruct((heads, n, n), f32), jax.ShapeDtypeStruct((2, n, n), f32), jax.ShapeDtypeStruct((8, rows, 128), f32)) + gathered_shapes([(shards[0].shape[0], w) for w in widths], wide),
        in_specs=[pl.BlockSpec(tables.shape, lambda i: (0, 0)), pl.BlockSpec((2, n), lambda i: (0, 0)), pl.BlockSpec((1, n), lambda i: (0, 0))] + [ANY] * count,
        out_specs=(pl.BlockSpec((heads, rows, n), lambda i: (0, i, 0)), pl.BlockSpec((2, rows, n), lambda i: (0, i, 0)),
                   pl.BlockSpec((8, rows, 128), lambda i: (0, 0, 0))) + (ANY,) * len(widths),
        scratch_shapes=[pltpu.VMEM((8, heads // 2, rows, 128), jnp.int32), pltpu.VMEM((8, 128), jnp.int32)] + gather_scratch(G, halves, count),
        compiler_params=params(cid), name="layout_bias_gather")(
            tables, boxes, pages[None], *shards)
    return outs[0], outs[1:3], outs[3:]


def half_of(v, e):
    lane = lax.broadcasted_iota(jnp.int32, v.shape, 1)
    return jnp.where((lane >= 64) == (e == 1), v, jnp.zeros_like(v))


def join(a, b):
    lane = lax.broadcasted_iota(jnp.int32, a.shape, 1)
    return jnp.where(lane < 64, a, b)


def project(tok_ref, gain_ref, w_ref, normed, qkv, between):
    gain = gain_ref[0:1, :].astype(f32)

    @pl.loop(0, tok_ref.shape[0] // TILE)
    def _(t):
        r = pl.ds(pl.multiple_of(t * TILE, TILE), TILE)
        x = tok_ref[r, :].astype(f32)
        low = (x * lax.rsqrt(jnp.mean(x * x, axis=1, keepdims=True) + epsilon) * gain).astype(bf16)
        normed[r, :] = low
        qkv[r, :] = jnp.dot(low, w_ref[...], preferred_element_type=f32).astype(bf16)
        for k, act in between:
            pl.when(t == k)(act)


def fwd_tile(p, i, tq, pairs, qkv, bias_ref, o_ref, lse_ref):
    cols = lambda k: pl.ds(pl.multiple_of((p + k * pairs) * 128, 128), 128)
    q, k, v = qkv[pl.ds(pl.multiple_of(i * tq, tq), tq), cols(0)], qkv[:, cols(1)], qkv[:, cols(2)]
    outs, lses = [], []
    for e in range(2):
        s = lax.dot_general(half_of(q, e), k, NT, preferred_element_type=f32) + bias_ref[e]
        peak = jnp.max(s, axis=1, keepdims=True)
        w = jnp.exp(s - peak)
        total = jnp.sum(w, axis=1, keepdims=True)
        outs.append(jnp.dot(w.astype(bf16), v, preferred_element_type=f32) / total)
        lses.append(peak + jnp.log(total))
    o_ref[...] = join(*outs).astype(bf16)
    lse_ref[0] = jnp.concatenate(lses, axis=1)


def fwd_kernel(pairs, tiles, G, halves, count, *refs):
    (tok, gain, w, bias_ref), srcs = refs[:4], refs[4:4 + count]
    o_ref, lse_ref, normed_h, qkv_h = refs[4 + count:8 + count]
    outs, (tok_s, w_s, normed, qkv, keep, load), sems = refs[8 + count:8 + 2 * count], refs[8 + 2 * count:14 + 2 * count], refs[14 + 2 * count:]
    p, i = pl.program_id(0), pl.program_id(1)
    now, steps = p * tiles + i, pairs * tiles
    copies = lambda: [pltpu.make_async_copy(normed, normed_h, keep.at[0]), pltpu.make_async_copy(qkv, qkv_h, keep.at[1])]

    events, finish = Gather(G, halves, srcs, outs, *sems).events()
    loads = lambda: [pltpu.make_async_copy(tok, tok_s, load.at[0]), pltpu.make_async_copy(w, w_s, load.at[1])]

    def compute():
        @pl.when(now == 0)
        def _():
            for c in loads():
                c.wait()
            project(tok_s, gain, w_s, normed, qkv, [(1, events[1][1]), (3, events[2][1])])
            for c in copies():
                c.start()

        fwd_tile(p, i, o_ref.shape[0], pairs, qkv, bias_ref, o_ref, lse_ref)

        @pl.when(now == steps - 1)
        def _():
            for c in copies():
                c.wait()

    beside((events[:1] + events[3:], finish), G, steps, now, compute, early=[lambda: [c.start() for c in loads()]], pace=0.36, lead=1.7)


def attn_fwd_and_gather(tok, gain, w, bias, shards, widths, halves, wide, cid, tq=256):
    n, d = tok.shape
    width = w.shape[1] // 3
    pairs, tiles, count, G = width // 128, n // tq, len(shards), wide // 4
    sds = jax.ShapeDtypeStruct
    const = lambda s: pl.BlockSpec(s, lambda p, i: (0, 0))
    outs = pl.pallas_call(functools.partial(fwd_kernel, pairs, tiles, G, halves, count), grid=(pairs, tiles),
        out_shape=(sds((n, width), bf16), sds((pairs, n, 2), f32), sds((n, d), bf16), sds((n, 3 * width), bf16)) + gathered_shapes([(shards[0].shape[0], c) for c in widths], wide),
        in_specs=[ANY, const(gain.shape), ANY, pl.BlockSpec((2, tq, n), lambda p, i: (p, i, 0))] + [ANY] * count,
        out_specs=(pl.BlockSpec((tq, 128), lambda p, i: (i, p)), pl.BlockSpec((1, tq, 2), lambda p, i: (p, i, 0)), ANY, ANY) + (ANY,) * count,
        scratch_shapes=[pltpu.VMEM((n, d), bf16), pltpu.VMEM(w.shape, bf16), pltpu.VMEM((n, d), bf16), pltpu.VMEM((n, 3 * width), bf16), D((2,)), D((2,))] + gather_scratch(G, halves, count),
        compiler_params=params(cid), name="attention_gather")(tok, gain, w, bias, *shards)
    return outs[:4], outs[4:]


def band_sums(i, e, g_ref, band_ref, far_ref):
    tq, n = g_ref.shape[1], g_ref.shape[2]
    first = i * (tq // 128) - 1

    @pl.when(i == 0)
    def _():
        band_ref[e] = jnp.zeros(band_ref.shape[1:], f32)
        far_ref[e] = jnp.zeros(far_ref.shape[1:], f32)

    for m in range(tq // 128 + 2):
        @pl.when((first + m >= 0) & (first + m < n // 128))
        def _():
            band_ref[e, :, m * 128:(m + 1) * 128] += g_ref[e, :, pl.ds(pl.multiple_of((first + m) * 128, 128), 128)].astype(f32)

    for c in range(n // 128):
        @pl.when((c < first) | (c > first + tq // 128 + 1))
        def _():
            total = g_ref[e, 0:16, c * 128:(c + 1) * 128].astype(f32)
            for k in range(1, tq // 16):
                total = total + g_ref[e, k * 16:(k + 1) * 16, c * 128:(c + 1) * 128].astype(f32)
            far_ref[e, jnp.where(c < first, 0, 1)] += total


def bwd_tile(p, pairs, i, last_tile, last, q_ref, k_ref, v_ref, bias_ref, o_ref, do_ref, lse_ref, normed_ref, w_ref,
             g_ref, band_ref, far_ref, dw_ref, dx_ref, dkt, dvt, dqkv, turned):
    tq, n = q_ref.shape[0], k_ref.shape[0]
    rows = pl.ds(pl.multiple_of(i * tq, tq), tq)

    @pl.when(p == 0)
    def _():
        turned[:, rows] = normed_ref[rows, :].T

    @pl.when(i == 0)
    def _():
        dkt[...] = jnp.zeros_like(dkt)
        dvt[...] = jnp.zeros_like(dvt)

    q, k, v, do = q_ref[...], k_ref[...], v_ref[...], do_ref[...]
    prod = do.astype(f32) * o_ref[...].astype(f32)
    dqs = []
    for e in range(2):
        qm, dom = half_of(q, e), half_of(do, e)
        s = lax.dot_general(qm, k, NT, preferred_element_type=f32) + bias_ref[e]
        w = jnp.exp(s - lse_ref[0, :, e:e + 1])
        dp = lax.dot_general(dom, v, NT, preferred_element_type=f32)
        inner = jnp.sum(half_of(prod, e), axis=1, keepdims=True)
        g = (w * (dp - inner)).astype(bf16)
        g_ref[e] = g
        dqs.append(jnp.dot(g, k, preferred_element_type=f32))
        dvt[...] += jnp.dot(dom.T, w.astype(bf16), preferred_element_type=f32)
        dkt[...] += jnp.dot(qm.T, g, preferred_element_type=f32)
        band_sums(i, e, g_ref, band_ref, far_ref)
    columns = lambda k: pl.ds(pl.multiple_of((p + k * pairs) * 128, 128), 128)
    dqkv[rows, columns(0)] = join(*dqs).astype(bf16)

    @pl.when(last_tile)
    def _():
        dqkv[:, columns(1)] = dkt[...].T.astype(bf16)
        dqkv[:, columns(2)] = dvt[...].T.astype(bf16)

        @pl.when(last)
        def _():
            @pl.loop(0, n // TILE)
            def _(t):
                r = pl.ds(pl.multiple_of(t * TILE, TILE), TILE)
                dw_ref[r, :] = jnp.dot(turned[r, :], dqkv[...], preferred_element_type=f32).astype(bf16)
                dx_ref[r, :] = lax.dot_general(dqkv[r, :], w_ref[...], NT, preferred_element_type=f32).astype(bf16)


def bwd_kernel(pairs, tiles, G, halves, count, *refs):
    ins, parts = refs[:9], refs[9:9 + count]
    mid = refs[9 + count:14 + count]
    outs, accs, sems = refs[14 + count:14 + 2 * count], refs[14 + 2 * count:18 + 2 * count], refs[21 + 2 * count:]
    normed_s, w_s, load = refs[18 + 2 * count:21 + 2 * count]
    loads = [lambda: pltpu.make_async_copy(ins[7], normed_s, load.at[0]), lambda: pltpu.make_async_copy(ins[8], w_s, load.at[1])]
    p, i = pl.program_id(0), pl.program_id(1)
    comm = Scatter(G, halves, parts, outs, *sems)
    now, steps = p * tiles + i, pairs * tiles

    def compute():
        for n, step in ((0, 0), (1, steps - 1)):
            @pl.when(now == step)
            def _():
                loads[n]().wait()

        bwd_tile(p, pairs, i, i == tiles - 1, p == pairs - 1, *ins[:7], normed_s, w_s, *mid, *accs)

    beside(comm.events(), G, steps, now, compute, early=[lambda: [c().start() for c in loads]], pace=0.36)


def shard_shapes(parts, wide):
    return tuple(jax.ShapeDtypeStruct((p.shape[0] // wide, p.shape[1]), f32) for p in parts)


def attn_bwd_and_scatter(qkv, bias, o, do, lse, normed, w, parts, halves, wide, cid, tq=256):
    n, width, d = qkv.shape[0], qkv.shape[1] // 3, normed.shape[1]
    pairs, tiles, count, G = width // 128, n // tq, len(parts), wide // 4
    sds = jax.ShapeDtypeStruct
    tile = pl.BlockSpec((tq, 128), lambda p, i: (i, p))
    full = lambda rows, k: pl.BlockSpec((rows, 128), lambda p, i: (0, p + k * pairs))
    const = lambda s: pl.BlockSpec(s, lambda p, i: (0, 0))
    outs = pl.pallas_call(functools.partial(bwd_kernel, pairs, tiles, G, halves, count), grid=(pairs, tiles),
        out_shape=(sds((2 * pairs, n, n), bf16), sds((2 * pairs, tq, tq + 256), f32), sds((2 * pairs, 2, 16, 128), f32)) + (sds((d, 3 * width), bf16), sds((n, d), bf16)) + shard_shapes(parts, wide),
        in_specs=[tile, full(n, 1), full(n, 2), pl.BlockSpec((2, tq, n), lambda p, i: (p, i, 0)), tile, tile,
                  pl.BlockSpec((1, tq, 2), lambda p, i: (p, i, 0)), ANY, ANY] + [ANY] * count,
        out_specs=(pl.BlockSpec((2, tq, n), lambda p, i: (p, i, 0)), pl.BlockSpec((2, tq, tq + 256), lambda p, i: (p, 0, 0)),
                   pl.BlockSpec((2, 2, 16, 128), lambda p, i: (p, 0, 0, 0))) + (const(w.shape), const((n, d))) + (whole_vmem(),) * count,
        scratch_shapes=[pltpu.VMEM((128, n), f32), pltpu.VMEM((128, n), f32), pltpu.VMEM((n, 3 * width), bf16), pltpu.VMEM((d, n), bf16),
                        pltpu.VMEM((n, d), bf16), pltpu.VMEM(w.shape, bf16), D((2,))] + scatter_scratch(G, halves, parts[0].shape[0] // wide),
        compiler_params=params(cid), name="attention_back_scatter")(
            qkv, qkv, qkv, bias, o, do, lse, normed, w, *parts)
    return outs[:5], outs[5:]


def rows_times_hots(src, ids, rows, heads, gs):
    n = src(0).shape[1]
    for h in range(heads):
        block = src(h)
        for c in range(n // 128):
            gs[c, h * rows:(h + 1) * rows, :] = block[:, c * 128:(c + 1) * 128]
    labels = [lax.broadcasted_iota(jnp.int32, (16, n), 0).astype(bf16) + float(k) for k in (0, 16)]
    one, zero = jnp.ones((16, n), bf16), jnp.zeros((16, n), bf16)
    group = 4 // len(ids(0))
    total = jnp.zeros((heads * group, 128), f32)
    for first in range(0, rows, group):
        grow, hots = [], []
        for r in range(first, first + group):
            grow.append(jnp.concatenate([gs[c, pl.ds(r, heads, stride=rows), :] for c in range(n // 128)], axis=1))
            for one_row in ids(r):
                row = jnp.broadcast_to(one_row, (16, n)).astype(bf16)
                hots += [jnp.where(row == label, one, zero) for label in labels]
        total = total + lax.dot_general(jnp.concatenate(grow, axis=0).astype(bf16), jnp.concatenate(hots, axis=0), NT, preferred_element_type=f32)
    return total


def own_blocks(total, heads, width):
    out = total[0:heads, 0:width]
    for k in range(1, 128 // width):
        out = out + total[k * heads:(k + 1) * heads, k * width:(k + 1) * width]
    return out


def halves_times_hots(g_ref, ids_ref, block, heads, gs, low):
    rows, n = 16, g_ref.shape[2]
    for h in range(heads):
        for c in range(n // 128):
            gs[c, h * rows:(h + 1) * rows, :] = g_ref[h, block, c * 128:(c + 1) * 128].astype(f32)
    for t in range(2):
        ids = ids_ref[t, block, :]
        low[t] = jnp.where(ids >= 16.0, ids - 16.0, ids)
    label = lax.broadcasted_iota(jnp.int32, (16, n), 0).astype(bf16)
    one, zero = jnp.ones((16, n), bf16), jnp.zeros((16, n), bf16)
    total = jnp.zeros((64, 64), f32)
    for first in range(0, rows, 2):
        left, hots = [], []
        for r in range(first, first + 2):
            grow = jnp.concatenate([gs[c, pl.ds(r, heads, stride=rows), :] for c in range(n // 128)], axis=1)
            for t in range(2):
                upper = jnp.broadcast_to(ids_ref.at[t, block][r:r + 1, :], (heads, n)) >= 16.0
                left += [jnp.where(upper, 0.0, grow), jnp.where(upper, grow, 0.0)]
                row = jnp.broadcast_to(low[t, r:r + 1, :], (16, n)).astype(bf16)
                hots.append(jnp.where(row == label, one, zero))
        total = total + lax.dot_general(jnp.concatenate(left, axis=0).astype(bf16), jnp.concatenate(hots, axis=0), NT, preferred_element_type=f32)
    return total


def own_halves(total, heads):
    out = 0.0
    for k in range(2):
        part = lambda t, up: total[k * 32 + (2 * t + up) * heads:k * 32 + (2 * t + up + 1) * heads, k * 32 + t * 16:k * 32 + t * 16 + 16]
        out = out + jnp.concatenate([part(0, 0), part(0, 1), part(1, 0), part(1, 1)], axis=1)
    return out


def hist_tile(now, heads, g_ref, ids_ref, band_ref, far_ref, lin_ids, table, boxes, gs, low):
    @pl.when(now == 0)
    def _():
        sides = [jnp.sum(jnp.sum(far_ref[:, k], axis=1), axis=1, keepdims=True) for k in range(2)]
        lane = lax.broadcasted_iota(jnp.int32, (heads, 128), 1)
        table[...] = jnp.zeros_like(table)
        boxes[...] = jnp.zeros_like(boxes)
        table[0:heads, :] = jnp.where(lane == 15, sides[0], 0.0) + jnp.where(lane == 31, sides[1], 0.0)

    big = g_ref.shape[1]

    @pl.loop(0, big // 16)
    def _(q):
        block = pl.ds(pl.multiple_of(q * 16, 16), 16)
        boxes[...] += halves_times_hots(g_ref, ids_ref, block, heads, gs, low)

    wide = band_ref.shape[2] // 128
    per = lin_ids.shape[1]
    a = now * 16 // per
    inside = pl.ds(pl.multiple_of(now * 16 % per, 16), 16)

    def band_ids(r):
        return [jnp.concatenate([lin_ids.at[jnp.clip((m - 1) * (128 // per) - a + 4, 0, 7), inside][r:r + 1, :] for m in range(wide)], axis=1)]

    table[...] += rows_times_hots(lambda h: band_ref[h], band_ids, 16, heads, gs)


def hist_kernel(heads, rows, n, G, halves, count, *refs):
    (g_ref, ids_ref, band_ref, far_ref, lin_ids, dx_h, tok_h, gh_h, gain_ref, gain_two), parts = refs[:10], refs[10:10 + count]
    small_ref, gt_ref = refs[10 + count:12 + count]
    outs, rest = refs[12 + count:12 + 2 * count], refs[12 + 2 * count:]
    (gs, low, table, boxes, got, dx, tok, gh, load, pair_sem), sums, sems = rest[:10], rest[10:17], rest[17:]
    acc = sums[0]
    now, steps = pl.program_id(0), n // rows
    core = lax.axis_index("narrow")
    mine = tok.shape[0]
    d = tok.shape[1]
    comm = Scatter(G, halves, parts, outs, *sems)
    loads = lambda: [pltpu.make_async_copy(dx_h.at[pl.ds(pl.multiple_of(core * mine, mine), mine)], dx, load.at[0]),
                     pltpu.make_async_copy(tok_h, tok, load.at[1]), pltpu.make_async_copy(gh_h, gh, load.at[2])]
    swap = lambda: remote(dx_h.at[pl.ds(pl.multiple_of((1 - core) * mine, mine), mine)], got, pair_sem.at[0], pair_sem.at[1], {"narrow": 1 - core})

    def compute():
        @pl.when(now == 0)
        def _():
            swap().start()
            acc[0] = jnp.zeros(acc.shape[1:], f32)
            for k in range(d // 128):
                acc[0, d // 128 + k:d // 128 + k + 1, :] = gain_two[:, k * 128:(k + 1) * 128]

        @pl.when(now == steps // 8)
        def _():
            swap().wait()
            for c in loads():
                c.wait()

        for t in range(mine // TILE):
            @pl.when(now == steps // 8 + t)
            def _():
                r = pl.ds(t * TILE, TILE)
                x = tok[r, :].astype(f32)
                total = dx[r, :].astype(f32) + got[r, :].astype(f32)
                factor = lax.rsqrt(jnp.mean(x * x, axis=1, keepdims=True) + epsilon)
                unit = x * factor
                scaled = gain_ref[0:1, :].astype(f32) * total
                gt_ref[r, :] = gh[r, :] + factor * (scaled - unit * jnp.mean(scaled * unit, axis=1, keepdims=True))
                gain = jnp.sum(total * unit, axis=0, keepdims=True)
                for k in range(d // 128):
                    acc[0, k:k + 1, :] += gain[:, k * 128:(k + 1) * 128]

        hist_tile(now, heads, g_ref, ids_ref, band_ref, far_ref, lin_ids, table, boxes, gs, low)

    def reduce():
        acc[0, pl.ds(pl.multiple_of(2 * (d // 128) + core * heads, 8), heads), 0:32] = own_blocks(table[...], heads, 32)
        acc[0, pl.ds(pl.multiple_of(2 * (d // 128) + core * heads, 8), heads), 32:96] = own_halves(boxes[...], heads)

    events, _ = comm.events(1)
    stages = sum_everywhere(G, small_ref, *sums)
    beside((events, lambda: None), G, steps, now, compute, [reduce] + [act for pair in zip(stages, comm.ending()) for act in pair],
           [lambda: [c.start() for c in loads()]], pace=0.3875)


def hist_and_scatter(g, band, far, ids, dx, tok, gh, gain, gain_two, parts, halves, wide, cid):
    heads, n, _ = g.shape
    rows, count, G, d = n // (band.shape[1] // 16), len(parts), wide // 4, tok.shape[1]
    box_ids, lin_ids = ids
    small = 2 * (d // 128) + 2 * heads
    sds = jax.ShapeDtypeStruct
    const = lambda s: pl.BlockSpec(s, lambda i: (0, 0))
    outs = pl.pallas_call(functools.partial(hist_kernel, heads, rows, n, G, halves, count), grid=(n // rows,),
        out_shape=(sds((small, 128), f32), sds(tok.shape, f32)) + shard_shapes(parts, wide),
        in_specs=[pl.BlockSpec((heads, rows, n), lambda i: (0, i, 0)), pl.BlockSpec((2, rows, n), lambda i: (0, i, 0)),
                  pl.BlockSpec((heads, 16, band.shape[2]), lambda i: (0, i, 0)), pl.BlockSpec(far.shape, lambda i: (0, 0, 0, 0)),
                  pl.BlockSpec(lin_ids.shape, lambda i: (0, 0, 0)), ANY, ANY, ANY, const(gain.shape), const(gain_two.shape)] + [ANY] * count,
        out_specs=(const((small, 128)), const(tok.shape)) + (whole_vmem(),) * count,
        scratch_shapes=[pltpu.VMEM((n // 128, heads * 16, 128), f32), pltpu.VMEM((2, 16, n), f32), pltpu.VMEM((4 * heads, 128), f32), pltpu.VMEM((64, 64), f32), pltpu.VMEM(tok.shape, bf16),
                        pltpu.VMEM(tok.shape, bf16), pltpu.VMEM(tok.shape, bf16), pltpu.VMEM(tok.shape, f32), D((3,)), D((2,))]
        + sum_scratch(G, small) + scatter_scratch(G, halves, parts[0].shape[0] // wide),
        compiler_params=params(cid), name="table_grad_scatter")(g, box_ids, band, far, lin_ids, dx, tok, gh, gain, gain_two, *parts)
    return outs[0], outs[1], outs[2:]


D = pltpu.SemaphoreType.DMA
AHEAD = 2


def place():
    me = lax.axis_index("wide")
    return me // 4, (me // 2) % 2, me % 2


def wide_id(z, y, x):
    return {"wide": z * 4 + y * 2 + x}


def shard_rows(z, y, x, R):
    return pl.ds(pl.multiple_of((z * 4 + y * 2 + x) * R, R), R)


def remote(src, dst, send, recv, target):
    return pltpu.make_async_remote_copy(src_ref=src, dst_ref=dst, send_sem=send, recv_sem=recv, device_id=target, device_id_type=MESH)


def greet(G, far, pair=0):
    z, y, x = place()
    bar = pltpu.get_barrier_semaphore()
    sig = lambda t: pl.semaphore_signal(bar, inc=1, device_id=t, device_id_type=MESH)
    sig(wide_id(z, 1 - y, x))
    sig(wide_id(z, y, 1 - x))
    if pair:
        sig({"narrow": 1 - lax.axis_index("narrow")})
    if far:
        for k in range(1, G):
            sig(wide_id((z + k) % G, y, x))
        pl.semaphore_wait(bar, 2 + pair + G - 1)
    else:
        @pl.when(z > 0)
        def _():
            sig(wide_id(z - 1, y, x))

        @pl.when(z < G - 1)
        def _():
            sig(wide_id(z + 1, y, x))

        pl.semaphore_wait(bar, 2 + pair + (z > 0).astype(jnp.int32) + (z < G - 1).astype(jnp.int32))


class Gather:
    def __init__(self, G, halves, srcs, outs, local_sem, zs, zr, ns, nr):
        self.G, self.halves, self.srcs, self.local_sem = G, halves, srcs, local_sem
        self.outs = [o if isinstance(o, tuple) else (o, 0, 0) for o in outs]
        self.widths = [sum(w for h in halves for a, _, w in h if a == k) for k in range(len(srcs))]
        self.zs, self.zr, self.ns, self.nr = zs, zr, ns, nr
        self.most = max(len(h) for h in halves)
        self.z, self.y, self.x = place()
        self.R = srcs[0].shape[0]

    def hop(self, own, zz, yy, xx, h, way, j):
        target = wide_id(self.z, 1 - self.y, self.x) if way == "y" else wide_id(self.z, self.y, 1 - self.x)
        copies = []
        for n, (a, c, w) in enumerate(self.halves[h]):
            slot = (zz * 6 + j) * self.most + n
            out, first, at = self.outs[a]
            dst = out.at[shard_rows(zz, yy, xx, self.R), pl.ds(first + c, w)]
            copies.append(remote(self.srcs[a].at[:, pl.ds(at + c, w)] if own else dst, dst, self.ns.at[slot], self.nr.at[slot], target))
        return copies

    def second_stage(self, zz, own=False):
        return self.hop(own, zz, self.y, self.x, 0, "y", 0) + self.hop(own, zz, self.y, self.x, 1, "x", 1)

    def third_stage(self, zz, own=False):
        return self.hop(own, zz, self.y, self.x, 0, "x", 2) + self.hop(own, zz, self.y, self.x, 1, "y", 3)

    def last_stage(self, zz):
        return self.hop(False, zz, 1 - self.y, self.x, 0, "x", 4) + self.hop(False, zz, self.y, 1 - self.x, 1, "y", 5)

    def relay(self, own, zz, step, way):
        copies = []
        for a in range(len(self.srcs)):
            slot = (way * (self.G - 1) + step) * len(self.srcs) + a
            dst = self.whole(a, zz)
            copies.append(remote(self.own(a) if own else dst, dst, self.zs.at[slot], self.zr.at[slot],
                                 wide_id(self.z + (1 if way == 0 else -1), self.y, self.x)))
        return copies

    def whole(self, a, zz):
        out, first, _ = self.outs[a]
        return out.at[shard_rows(zz, self.y, self.x, self.R), pl.ds(first, self.widths[a])]

    def own(self, a):
        return self.srcs[a].at[:, pl.ds(self.outs[a][2], self.widths[a])]

    def can(self, way):
        return self.z < self.G - 1 if way == 0 else self.z > 0

    def source(self, d, way):
        return (self.z - d, self.z - d >= 0) if way == 0 else (self.z + d, self.z + d < self.G)

    def keep(self):
        return [pltpu.make_async_copy(self.own(a), self.whole(a, self.z), self.local_sem.at[a]) for a in range(len(self.srcs))]

    def begin(self):
        for way in range(2):
            @pl.when(self.can(way))
            def _():
                for c in self.relay(True, self.z, 0, way):
                    c.start()
        for c in self.second_stage(self.z, True) + self.third_stage(self.z, True) + self.keep():
            c.start()

    def turn(self, zz):
        for c in self.hop(False, zz, 1 - self.y, self.x, 0, "y", 0) + self.hop(False, zz, self.y, 1 - self.x, 1, "x", 1):
            c.wait_recv()
        for c in self.last_stage(zz):
            c.start()

    def step(self, d):
        for way in range(2):
            zz, there = self.source(d, way)

            @pl.when(there)
            def _():
                for c in self.relay(False, zz, d - 1, way):
                    c.wait_recv()

                @pl.when(self.can(way))
                def _():
                    for c in self.relay(False, zz, d, way):
                        c.start()

                for c in self.second_stage(zz):
                    c.start()
        for way in range(2):
            zz, there = self.source(d, way)

            @pl.when(there)
            def _():
                for c in self.third_stage(zz):
                    c.start()

    def turns(self, d):
        if d == 0:
            self.turn(self.z)
            return
        for way in range(2):
            zz, there = self.source(d, way)

            @pl.when(there)
            def _():
                self.turn(zz)

    def finish(self):
        y, x = self.y, self.x

        @pl.loop(0, self.G)
        def _(zz):
            for c in (self.hop(False, zz, y, 1 - x, 0, "x", 2) + self.hop(False, zz, 1 - y, x, 1, "y", 3)
                      + self.hop(False, zz, 1 - y, 1 - x, 0, "x", 4) + self.hop(False, zz, 1 - y, 1 - x, 1, "y", 5)):
                c.wait_recv()
            for c in self.second_stage(zz) + self.third_stage(zz) + self.last_stage(zz):
                c.wait_send()

        for way in range(2):
            @pl.when(self.can(way))
            def _():
                for c in self.relay(True, self.z, 0, way):
                    c.wait_send()
                for d in range(1, self.G - 1):
                    zz, there = self.source(d, way)

                    @pl.when(there)
                    def _():
                        for c in self.relay(False, zz, d, way):
                            c.wait_send()
        for c in self.keep():
            c.wait()

    def events(self):
        G = self.G
        first = lambda: (greet(G, False), self.begin())
        ev = [(0.0, first), (0.7, lambda: self.turns(0))]
        for d in range(1, G):
            ev += [(1.15 * d, functools.partial(self.step, d)), (1.3 * d + 1.2, functools.partial(self.turns, d))]
        return sorted(ev, key=lambda e: e[0]), self.finish


def gather_scratch(G, halves, arrays):
    most = max(len(h) for h in halves)
    return [D((arrays,)), D((2 * (G - 1) * arrays,)), D((2 * (G - 1) * arrays,)), D((6 * G * most,)), D((6 * G * most,))]


class Scatter:
    def __init__(self, G, halves, parts, outs, r1a, r1b, o1a, o1b, r2a, r2b, r3, own, lsem, s1, v1, s2, v2, s3, v3):
        self.__dict__.update(locals())
        self.most = max(len(h) for h in halves)
        self.wa, self.wb = [sum(p[2] for p in h) for h in halves]
        self.R = parts[0].shape[0] // (4 * G)
        self.z, self.y, self.x = place()
        self.order = sorted(range(1, G), key=lambda k: min(k, G - k), reverse=True) + [0]

    def zk(self, k):
        return (self.z + k) % self.G

    def neighbour(self, way):
        return wide_id(self.z, 1 - self.y, self.x) if way == "y" else wide_id(self.z, self.y, 1 - self.x)

    def pieces(self, h):
        at, out = 0, []
        for n, (a, c, w) in enumerate(self.halves[h]):
            out.append((n, a, pl.ds(c, w), pl.ds(at, w)))
            at += w
        return out

    def sources(self, k, mine):
        z, y, x = self.zk(k), self.y, self.x
        for h in range(2):
            for n, a, src, dst in self.pieces(h):
                for j in range(2):
                    if h == 0:
                        rows = shard_rows(z, j, x if mine else 1 - x, self.R)
                    else:
                        rows = shard_rows(z, y if mine else 1 - y, j, self.R)
                    yield h, j, dst, ((2 * k + h) * self.most + n) * 2 + j, self.parts[a].at[rows, src]

    def one(self, k):
        return [remote(src, (self.r1a, self.r1b)[h].at[k, j, :, dst], self.s1.at[slot], self.v1.at[slot], self.neighbour("xy"[h]))
                for h, j, dst, slot, src in self.sources(k, False)]

    def load(self, k):
        return [pltpu.make_async_copy(src, (self.o1a, self.o1b)[h].at[k, j, :, dst], self.lsem.at[slot]) for h, j, dst, slot, src in self.sources(k, True)]

    def two(self, k):
        return [remote(self.o1a.at[k, 1 - self.y], self.r2a.at[k], self.s2.at[2 * k], self.v2.at[2 * k], self.neighbour("y")),
                remote(self.o1b.at[k, 1 - self.x], self.r2b.at[k], self.s2.at[2 * k + 1], self.v2.at[2 * k + 1], self.neighbour("x"))]

    def three(self, k):
        return remote(self.own.at[k], self.r3.at[k - 1], self.s3.at[k - 1], self.v3.at[k - 1], wide_id(self.zk(k), self.y, self.x))

    def launch(self, k):
        for c in self.one(k) + self.load(k):
            c.start()

    def begin(self):
        for k in self.order[:AHEAD]:
            self.launch(k)

    def rows(self, count, body):
        step = min(16, count)

        @pl.loop(0, count // step)
        def _(i):
            body(pl.ds(pl.multiple_of(i * step, step), step))

    def add_one(self, n):
        k = self.order[n]
        for c in self.one(k):
            c.wait_recv()
        for c in self.load(k):
            c.wait()
        for mine, got in ((self.o1a, self.r1a), (self.o1b, self.r1b)):
            def body(r):
                for j in range(2):
                    mine[k, j, r, :] = (mine[k, j, r, :].astype(f32) + got[k, j, r, :].astype(f32)).astype(bf16)

            self.rows(self.R, body)
        for c in self.two(k):
            c.start()
        if n + AHEAD < self.G:
            self.launch(self.order[n + AHEAD])

    def add_two(self, n):
        k = self.order[n]
        for c in self.two(k):
            c.wait_recv()

        def body(r):
            self.own[k, r, pl.ds(0, self.wa)] = (self.o1a[k, self.y, r, :].astype(f32) + self.r2a[k, r, :].astype(f32)).astype(bf16)
            self.own[k, r, pl.ds(self.wa, self.wb)] = (self.o1b[k, self.x, r, :].astype(f32) + self.r2b[k, r, :].astype(f32)).astype(bf16)

        self.rows(self.R, body)
        if k:
            self.three(k).start()

    def arrived(self):
        for k in range(1, self.G):
            self.three(k).wait_recv()

    def write_out(self):
        def body(r):
            for h in range(2):
                for _, a, src, dst in self.pieces(h):
                    cols = pl.ds(dst.start + h * self.wa, dst.size)
                    total = self.own[0, r, cols].astype(f32)
                    for k in range(self.G - 1):
                        total = total + self.r3[k, r, cols].astype(f32)
                    self.outs[a][r, src] = total

        self.rows(self.R, body)

    def all_sent(self):
        for k in range(self.G):
            for c in self.one(k) + self.two(k):
                c.wait_send()
            if k:
                self.three(k).wait_send()

    def ending(self):
        return [lambda: self.add_two(self.G - 1), self.arrived, self.write_out, self.all_sent, lambda: None]

    def finish(self):
        for act in self.ending():
            act()

    def events(self, pair=0):
        G = self.G
        first = lambda: (greet(G, True, pair), self.begin())
        ev = [(0.0, first), (1.1, lambda: self.add_one(0))]
        for n in range(1, G):
            ev += [(1.5 * n + 0.65, functools.partial(self.add_one, n)), (1.5 * n + 1.1, functools.partial(self.add_two, n - 1))]
        return sorted(ev, key=lambda e: e[0]), self.finish


def scatter_scratch(G, halves, R):
    most = max(len(h) for h in halves)
    a, b = [sum(p[2] for p in h) for h in halves]
    V = lambda *s: pltpu.VMEM(s, bf16)
    return [V(G, 2, R, a), V(G, 2, R, b), V(G, 2, R, a), V(G, 2, R, b), V(G, R, a), V(G, R, b), V(G - 1, R, a + b), V(G, R, a + b),
            D((4 * G * most,)), D((4 * G * most,)), D((4 * G * most,)), D((2 * G,)), D((2 * G,)), D((G - 1,)), D((G - 1,))]


def beside(plan, G, steps, now, compute, late=(), early=(), pace=0.3875, lead=0.0):
    events, finish = plan
    if early:
        @pl.when(now == 0)
        def _():
            for act in early:
                act()
    for n in range(steps):
        here = [act for t, act in events if min(steps - 1, max(0, int(-((lead - t) // pace)))) == n]
        if here:
            @pl.when(now == n)
            def _():
                for act in here:
                    act()
    compute()

    @pl.when(now == steps - 1)
    def _():
        for act in late:
            act()
        finish()


ANY = pl.BlockSpec(memory_space=pl.ANY)


def whole_vmem():
    return pl.BlockSpec(memory_space=pltpu.VMEM)


def gathered_shapes(shards, wide):
    return tuple(jax.ShapeDtypeStruct((wide * rows, columns), bf16) for rows, columns in shards)


def sum_everywhere(G, out, acc, got, gz, s, v, sz, vz):
    z, y, x = place()
    targets = [{"narrow": 1 - lax.axis_index("narrow")}, wide_id(z, y, 1 - x), wide_id(z, 1 - y, x)]
    near = lambda n: remote(acc.at[n], got.at[n], s.at[n], v.at[n], targets[n])
    far = lambda k, zz: remote(acc.at[3], gz.at[zz], sz.at[k - 1], vz.at[zz], wide_id((z + k) % G, y, x))

    def take(n):
        near(n).wait()
        acc[n + 1] = acc[n] + got[n]

    def next_near(n):
        if n:
            take(n - 1)
        near(n).start()

    def spread_far():
        take(2)
        gz[z] = acc[3]
        for k in range(1, G):
            far(k, z).start()

    def total():
        for k in range(1, G):
            far(k, (z + k) % G).wait_recv()
        for k in range(1, G):
            far(k, z).wait_send()
        value = gz[0]
        for k in range(1, G):
            value = value + gz[k]
        out[...] = value

    return [functools.partial(next_near, n) for n in range(3)] + [spread_far, total]


def sum_scratch(G, rows):
    V = lambda k: pltpu.VMEM((k, rows, 128), f32)
    return [V(4), V(3), V(G), D((3,)), D((3,)), D((G - 1,)), D((G,))]


def nt(a, b):
    return lax.dot_general(a, b, NT, preferred_element_type=f32)


def nn(a, b):
    return jnp.dot(a, b, preferred_element_type=f32)


def gelu_and_slope(v):
    root = 0.7978845608028654
    square = v * v
    t = jnp.tanh(root * v * (1.0 + 0.044715 * square))
    half = 0.5 * (1.0 + t)
    return v * half, half + 0.5 * v * (1.0 - t * t) * root * (1.0 + 3 * 0.044715 * square)


def mid_kernel(G, cut, att_h, tok_h, cot_h, wo_h, wg_h, wu_h, wd_h, wd_shard, gain_ref,
               gout_h, gg_h, gu_h, gd_h, y_ref, gh_ref, ga_ref, ggain_ref, sd_ref,
               att, tok, cot, wo, wg, wu, wd, part, other, back, hid, n2t, cott, hff, gg, gu, yother, stage,
               isem, osem, sp, vp, sb, vb, sy, vy, *sems):
    core = lax.axis_index("narrow")
    peer = {"narrow": 1 - core}
    n, d = tok.shape
    ff = wg.shape[1]
    tiles = n // TILE
    half = tiles // 2
    loads = [pltpu.make_async_copy(s, t, isem.at[k]) for k, (s, t) in enumerate(
        [(att_h, att), (wo_h, wo), (tok_h, tok), (wg_h, wg), (wu_h, wu), (cot_h, cot), (wd_h, wd.at[:, pl.ds(0, cut)])])]
    for c in loads:
        c.start()
    part_cols = sd_ref.shape[1]
    mid = cut + (ff - cut) // 256 * 128
    bring = Gather(G, (((0, 0, mid - cut),), ((0, mid - cut, ff - mid),)), [wd_shard], [(wd, cut, cut)], *sems[:5])
    give = Scatter(G, (((0, 0, part_cols // 2),), ((0, part_cols // 2, part_cols // 2),)), [gd_h], [sd_ref], *sems[5:])
    greet(G, True, 1)
    bring.begin()
    rows_of = lambda t: pl.ds(pl.multiple_of(t * TILE, TILE), TILE)
    kept = lambda j: rows_of(j + half)
    send_part = lambda t: remote(part.at[rows_of(t)], other.at[rows_of(t)], sp.at[t], vp.at[t], peer)
    send_back = lambda t: remote(part.at[rows_of(t)], back.at[rows_of(t)], sb.at[t], vb.at[t], peer)
    send_y = lambda j: remote(tok.at[rows_of(j)], yother.at[rows_of(j)], sy.at[j], vy.at[j], peer)
    gain = gain_ref[1:2, :].astype(f32)

    for c in loads[:2]:
        c.wait()

    def at_step(s, plan):
        for k, acts in plan.items():
            @pl.when(s == k)
            def _():
                for act in acts:
                    act()

    turns = [functools.partial(bring.turns, k) for k in range(G)]
    steps = [functools.partial(bring.step, k) for k in range(1, G)]

    @pl.loop(0, tiles)
    def _(t):
        part[rows_of(t), :] = nt(att[rows_of(t), :], wo[...]).astype(bf16)
        send_part(t).start()

    for c in loads[2:]:
        c.wait()

    chunks, at = [], 0
    while at < ff:
        w = min(384, ff - at)
        chunks.append((at, w))
        at += w

    later = [act for pair in zip(turns[1:], steps[1:] + [lambda: None]) for act in pair]

    @pl.loop(0, tiles)
    def _(s):
        t = (s + half * (1 - core)) % tiles
        r = rows_of(t)
        send_part(t).wait()
        h = tok[r, :].astype(f32) + (part[r, :].astype(f32) + other[r, :].astype(f32))
        hid[r, :] = h
        factor = lax.rsqrt(jnp.mean(h * h, axis=1, keepdims=True) + epsilon)
        low = (h * factor * gain).astype(bf16)
        n2t[:, r] = low.T
        cott[:, r] = cot[r, :].T
        for at, w in chunks:
            cols = pl.ds(at, w)
            act, slope = gelu_and_slope(nn(low, wg[:, cols]))
            up = nn(low, wu[:, cols])
            hff[r, cols] = (act * up).astype(bf16)
            gg[r, cols] = (up * slope).astype(bf16)
            gu[r, cols] = act.astype(bf16)
        at_step(s, {0: turns[:1] + steps[:1], 1: later[:2], 2: later[2:4], 3: later[4:]})

    def weight_grad(left, right, out, slot, width):
        rows = stage.shape[1]
        block = lambda k: pl.ds(k * rows, rows)
        copy = lambda k: pltpu.make_async_copy(stage.at[k % 2, :, pl.ds(0, width)], out.at[block(k)], osem.at[2 * slot + k % 2])
        count = d // rows
        for k in range(count):
            if k >= 2:
                copy(k - 2).wait()
            stage[k % 2, :, pl.ds(0, width)] = nn(left[block(k), :], right[...]).astype(bf16)
            copy(k).start()
        return [copy(k) for k in range(max(0, count - 2), count)]

    for c in weight_grad(cott, hff, gd_h, 0, ff):
        c.wait()
    give.begin()
    bring.finish()
    ones = [functools.partial(give.add_one, k) for k in range(G)]
    twos = [functools.partial(give.add_two, k) for k in range(G - 1)]

    @pl.loop(0, tiles)
    def _(s):
        t = (s + half * (1 - core)) % tiles
        r = rows_of(t)
        ct = cot[r, :]
        for at, w in chunks:
            cols = pl.ds(at, w)
            gf = nn(ct, wd[:, cols])
            gg[r, cols] = (gf * gg[r, cols].astype(f32)).astype(bf16)
            gu[r, cols] = (gf * gu[r, cols].astype(f32)).astype(bf16)
        part[r, :] = (nt(gg[r, :], wg[...]) + nt(gu[r, :], wu[...])).astype(bf16)
        send_back(t).start()
        y = nt(hff[r, :], wd[...]).astype(bf16)

        @pl.when(s < half)
        def _():
            tok[rows_of(s), :] = y
            send_y(s).start()

        @pl.when(s >= half)
        def _():
            tok[rows_of(s), :] = y

        at_step(s, {1: ones[:1], 2: ones[1:2], 3: twos[:1]})

    ggain_ref[...] = jnp.zeros_like(ggain_ref)

    @pl.loop(0, tiles)
    def _(s):
        t = (s + half * (1 - core)) % tiles
        r = rows_of(t)
        send_back(t).wait()
        total = part[r, :].astype(f32) + back[r, :].astype(f32)
        h = hid[r, :]
        factor = lax.rsqrt(jnp.mean(h * h, axis=1, keepdims=True) + epsilon)
        unit = h * factor
        g = gain * total
        gh = cot[r, :].astype(f32) + factor * (g - unit * jnp.mean(g * unit, axis=1, keepdims=True))
        low = gh.astype(bf16)
        cott[:, r] = low.T
        ga_ref[r, :] = nn(low, wo[...]).astype(bf16)

        @pl.when(s >= half)
        def _():
            j = rows_of(s - half)
            gh_ref[j, :] = gh
            ggain_ref[...] += jnp.sum(total * unit, axis=0, keepdims=True)
            send_y(s - half).wait()
            y_ref[j, :] = (h + (tok[kept(s - half), :].astype(f32) + yother[j, :].astype(f32))).astype(bf16)

        at_step(s, {0: ones[2:3], 1: twos[1:2], 3: ones[3:4]})

    for left, right, out, slot in ((n2t, gg, gg_h, 1), (n2t, gu, gu_h, 2), (cott, att, gout_h, 3)):
        if slot == 2:
            for act in twos[2:3] + [act for pair in zip(ones[4:], twos[3:]) for act in pair]:
                act()
        for c in weight_grad(left, right, out, slot, right.shape[1]):
            c.wait()
    give.finish()


def middle(att, tok, cot, wo, wg, wu, wd, wd_shard, gain, here, wide, cid):
    n, d = tok.shape
    units, ff, G, cut = att.shape[1], wg.shape[1], wide // 4, wd.shape[1]
    B = lambda *s: pltpu.VMEM(s, bf16)
    sds = jax.ShapeDtypeStruct
    tiles = n // TILE
    halves = (((0, 0, cut),), ((0, cut, ff - cut),))
    return pl.pallas_call(functools.partial(mid_kernel, G, cut),
        out_shape=(sds((d, units), bf16), sds((d, ff), bf16), sds((d, ff), bf16), sds((d, ff), bf16),
                   sds((n // 2, d), bf16), sds((n // 2, d), f32), sds((n, units), bf16), sds((1, d), f32), sds((d // wide, here), f32)),
        in_specs=[ANY] * 8 + [whole_vmem()], out_specs=(ANY,) * 4 + (whole_vmem(),) * 5,
        scratch_shapes=[B(n, units), B(n, d), B(n, d), B(d, units), B(d, ff), B(d, ff), B(d, ff), B(n, d), B(n, d), B(n, d),
                        pltpu.VMEM((n, d), f32), B(d, n), B(d, n), B(n, ff), B(n, ff), B(n, ff),
                        B(n // 2, d), B(2, 512, ff),
                        D((7,)), D((8,)), D((tiles,)), D((tiles,)), D((tiles,)), D((tiles,)), D((tiles // 2,)), D((tiles // 2,))]
        + gather_scratch(G, halves, 1) + scatter_scratch(G, (((0, 0, here // 2),), ((0, here // 2, here // 2),)), d // wide),
        compiler_params=params(cid), name="feed_forward")(att, tok, cot, wo, wg, wu, wd, wd_shard, gain)


def local(tokens, cotangent, pages, boxes, gain_attn, gain_ffn, bias_tables, w_query, w_key, w_value, w_out, w_gate, w_up, w_down):
    wide, narrow = lax.axis_size("wide"), lax.axis_size("narrow")
    heads = bias_tables.shape[1] // narrow
    inner, ff, d = w_query.shape[1], w_gate.shape[1], tokens.shape[1]
    gains = jnp.stack([gain_attn, gain_ffn])

    all_tokens = lax.all_gather(tokens, "narrow", axis=0, tiled=True)
    all_cot = lax.all_gather(cotangent, "narrow", axis=0, tiled=True)
    early = inner // 4 * 3
    bias, ids, (w_first, full_out, full_gate) = bias_and_gather(
        bias_tables.T, heads, boxes, pages, [w_query, w_key, w_value, w_out.T, w_gate], ((0, 0), (0, inner), (0, 2 * inner), (1, 0), (2, 0)),
        (((4, 0, ff), (0, 0, early)), ((3, 0, inner), (0, early, inner - early), (1, 0, inner), (2, 0, inner))), wide, 1)
    down_shard = w_down.T
    cut = (ff // 128 + 1) // 2 * 128
    (attended, lse, normed, qkv), (full_up, most_down) = attn_fwd_and_gather(
        all_tokens, gains, w_first, bias, [w_up, down_shard], (ff, cut),
        (((0, 0, cut), (1, 0, cut - 384)), ((0, cut, ff - cut), (1, cut - 384, 384))), wide, 2)
    here, upto = ff // 256 * 256, ff // 256 * 256 - 128
    grad_w_out, grad_w_gate, grad_w_up, grad_w_down, output, grad_hidden, grad_attended, grad_gain_two, s_down = middle(
        attended, all_tokens, all_cot, full_out, full_gate, full_up, most_down, down_shard, gains, here, wide, 3)
    even = (ff + inner + ff - here + ff - upto) // 2
    (g, band, far, grad_w_first, grad_normed), (s_gate, s_out, more_down, more_up) = attn_bwd_and_scatter(
        qkv, bias, attended, grad_attended, lse, normed, w_first, [grad_w_gate, grad_w_out, grad_w_down, grad_w_up],
        (((0, 0, even),), ((0, even, ff - even), (1, 0, inner), (2, here, ff - here), (3, upto, ff - upto))), wide, 4)
    s_down = jnp.concatenate([s_down, more_down[:, here:]], axis=1)
    small, grad_tokens, (s_up, s_first) = hist_and_scatter(
        g, band, far, ids, grad_normed, tokens, grad_hidden, gains, grad_gain_two, [grad_w_up, grad_w_first],
        (((0, 0, upto), (1, 0, 128)), ((1, 128, 3 * inner - 128),)), wide, 5)
    s_up = jnp.concatenate([s_up[:, :upto], more_up[:, upto:]], axis=1)
    s_query, s_key, s_value = jnp.split(s_first, 3, axis=1)
    lines = d // 128
    one, two = small[:lines].reshape(d), small[lines:2 * lines].reshape(d)
    table = small[2 * lines:, :bias_tables.shape[0]].T
    return (output, grad_tokens, one, two, table, s_query, s_key, s_value, s_out.T, s_gate, s_up, s_down.T)


def solution(mesh):
    rows, cols, tall = P(("wide", "narrow"), None), P("wide", "narrow"), P("narrow", "wide")
    in_specs = (rows, rows, P("wide"), P(None, "wide"), P(), P(), P(), cols, cols, cols, tall, cols, cols, tall)
    out_specs = (rows, rows, P(), P(), P(), cols, cols, cols, tall, cols, cols, tall)
    return jax.shard_map(local, mesh=mesh, in_specs=in_specs, out_specs=out_specs, check_vma=False)
```
